32 devices in a mesh: seq: 4 (over y, x), fsdp: 8 (over z, core).
Axes of the slice: x: 2, y: 2, z: 4, core: 2. Of those that a mesh axis runs over, the one named last changes fastest.
Arguments:
- tokens: bfloat16 [8, 2048, 1024], P('fsdp', 'seq'), may hold values from -6 to 6
- prompt_lens: int32 [8], P('fsdp'), may hold values from 512 to 1024, as said below
- cont_lens: int32 [8, 2], P('fsdp'), may hold values from 256 to 512, as said below
- gain_one: bfloat16 [1024], P('fsdp'), may hold values from 0.5 to 1.5
- shift_one: bfloat16 [1024], P('fsdp'), may hold values from -4 to 4
- w_qkv: bfloat16 [1024, 3072], P('fsdp'), may hold values from -0.25 to 0.25
- bias_qv: bfloat16 [2048], P('fsdp'), may hold values from -4 to 4
- w_out: bfloat16 [1024, 1024], P('fsdp'), may hold values from -0.375 to 0.375
- bias_out: bfloat16 [1024], P('fsdp'), may hold values from -4 to 4
- gain_two: bfloat16 [1024], P('fsdp'), may hold values from 0.5 to 1.5
- shift_two: bfloat16 [1024], P('fsdp'), may hold values from -4 to 4
- w_fc: bfloat16 [1024, 4096], P('fsdp'), may hold values from -0.1875 to 0.1875
- bias_fc: bfloat16 [4096], P('fsdp'), may hold values from -4 to 4
- w_proj: bfloat16 [4096, 1024], P('fsdp'), may hold values from -0.1875 to 0.1875
- bias_proj: bfloat16 [1024], P('fsdp'), may hold values from -4 to 4
- cotangent: bfloat16 [8, 2048, 1024], P('fsdp', 'seq'), may hold values from -6 to 6
Outputs:
- output: bfloat16 [8, 2048, 1024], P('fsdp', 'seq')
- input_grad: float32 [8, 2048, 1024], P('fsdp', 'seq')
- grad_gain_one: float32 [1024], P('fsdp')
- grad_shift_one: float32 [1024], P('fsdp')
- grad_w_qkv: float32 [1024, 3072], P('fsdp')
- grad_bias_qv: float32 [2048], P('fsdp')
- grad_w_out: float32 [1024, 1024], P('fsdp')
- grad_bias_out: float32 [1024], P('fsdp')
- grad_gain_two: float32 [1024], P('fsdp')
- grad_shift_two: float32 [1024], P('fsdp')
- grad_w_fc: float32 [1024, 4096], P('fsdp')
- grad_bias_fc: float32 [4096], P('fsdp')
- grad_w_proj: float32 [4096, 1024], P('fsdp')
- grad_bias_proj: float32 [1024], P('fsdp')
The draws below stay inside these ranges and needn't reach their ends.
Inputs may be any that keep to these rules, and one draw needn't show every extreme that they name: `prompt_lens`: group 0's prompt has all 1024 tokens live. `cont_lens`: the first continuation of every group has all 512 tokens live.
All inputs are finite; a program needn't handle non-finite values.
Results may differ from the reference program's by a relative error of at most 0.02.
Values may be sent and summed in bfloat16 or wider, within the bound.
No kernel may reach another device: no remote copies, remote signals or barrier semaphores. Data moves between devices by JAX's collectives and lax.ppermute only.
A program may use at most 256 MiB of HBM per device.

```python
import jax
import jax.numpy as jnp
from jax import lax

D = 1024
H = 16
HD = 64
FF = 4096
PROMPT = 1024
CONTLEN = 512
CONTS = 2
GLEN = 2048
GROUPS = 8


def draw_prompt_lens(key, part):
    drawn = jax.random.randint(key, (GROUPS,), PROMPT // 2, PROMPT + 1)
    return jnp.where(jnp.arange(GROUPS) == 0, PROMPT, drawn).astype(jnp.int32)


def draw_cont_lens(key, part):
    drawn = jax.random.randint(key, (GROUPS, CONTS), CONTLEN // 2, CONTLEN + 1)
    return jnp.where(jnp.arange(CONTS)[None, :] == 0, CONTLEN, drawn).astype(jnp.int32)


def shard_levels(stream_key, shape, cuts, smallest, high):
    def one(dim, parts):
        steps = jax.random.uniform(jax.random.fold_in(jax.random.fold_in(stream_key, 6), dim), (parts,), jnp.float32, smallest / len(cuts), high / len(cuts))
        return jnp.repeat(jnp.exp(steps), shape[dim] // parts).reshape((-1,) + (1,) * (len(shape) - dim - 1))

    loudness = one(*cuts[0])
    for cut in cuts[1:]:
        loudness = loudness * one(*cut)
    return loudness


def noise(rng, extent, scale, reach, cuts=(), held_as=jnp.bfloat16):
    level = shard_levels(rng, extent, cuts, -0.22, 0.18) if cuts else 1.0
    entries = jax.random.normal(rng, extent, jnp.float32) * scale * level
    return jnp.minimum(jnp.maximum(entries, -reach), reach).astype(held_as)


def setup_inputs(seed: int = 0) -> dict:
    splits = jax.random.split(jax.random.key(seed), 17)
    return {
        "tokens": noise(splits[0], (GROUPS, GLEN, D), 1.0, 6.0, ((0, 8), (1, 4))),
        "prompt_lens": draw_prompt_lens(jax.random.fold_in(splits[16], 71), 0),
        "cont_lens": draw_cont_lens(jax.random.fold_in(splits[16], 71), 0),
        "gain_one": jnp.clip(1.0 + 0.1 * jax.random.normal(splits[3], (D,), jnp.float32), 0.5, 1.5).astype(jnp.bfloat16),
        "shift_one": noise(splits[4], (D,), 0.3, 4.0, ((0, 8),)),
        "w_qkv": noise(splits[5], (D, 3 * D), (D // 2) ** -0.5, 0.25, ((0, 8),)),
        "bias_qv": noise(splits[6], (2 * D,), 0.3, 4.0, ((0, 8),)),
        "w_out": noise(splits[7], (D, D), (D // 4) ** -0.5, 0.375, ((0, 8),)),
        "bias_out": noise(splits[8], (D,), 0.3, 4.0, ((0, 8),)),
        "gain_two": jnp.clip(1.0 + 0.1 * jax.random.normal(splits[9], (D,), jnp.float32), 0.5, 1.5).astype(jnp.bfloat16),
        "shift_two": noise(splits[10], (D,), 0.3, 4.0, ((0, 8),)),
        "w_fc": noise(splits[11], (D, FF), D ** -0.5, 0.1875, ((0, 8),)),
        "bias_fc": noise(splits[12], (FF,), 0.3, 4.0, ((0, 8),)),
        "w_proj": noise(splits[13], (FF, D), (FF // 4) ** -0.5, 0.1875, ((0, 8),)),
        "bias_proj": noise(splits[14], (D,), 0.3, 4.0, ((0, 8),)),
        "cotangent": noise(splits[15], (GROUPS, GLEN, D), 1.0, 6.0, ((0, 8), (1, 4))),
    }


@jax.custom_vjp
def low(v):
    return lax.optimization_barrier(v.astype(jnp.bfloat16)).astype(jnp.float32)

@jax.custom_vjp
def low_back(v):
    return v

def low_keep(v):
    return (low(v), None)

def low_pass(kept, grad):
    return (grad,)

def back_keep(v):
    return (v, None)

def back_low(kept, grad):
    return (low(grad),)
low.defvjp(low_keep, low_pass)
low_back.defvjp(back_keep, back_low)
EPS = 1e-05
GELU_C = 0.7978845608028654
NEG = -1e+30
HIGHEST = lax.Precision.HIGHEST

def layer_norm(values, gain, shift):
    center = values - lax.optimization_barrier(jnp.mean(values, axis=-1, keepdims=True))
    spread = lax.optimization_barrier(jnp.mean(center * center, axis=-1, keepdims=True))
    return center * lax.rsqrt(spread + EPS) * gain + shift

def gelu_tanh(values):
    return 0.5 * values * (1.0 + jnp.tanh(GELU_C * (values + 0.044715 * values * values * values)))

def describe(index, prompt_len, cont_len):
    in_prompt = index < PROMPT
    segment = jnp.where(in_prompt, 0, 1 + (index - PROMPT) // CONTLEN).astype(jnp.int32)
    offset = jnp.where(in_prompt, index, (index - PROMPT) % CONTLEN).astype(jnp.int32)
    slots = jnp.arange(1, CONTS + 1, dtype=jnp.int32)
    picked = lax.optimization_barrier(jnp.sum(jnp.where(segment[:, None] == slots[None, :], cont_len[None, :], 0), axis=1)).astype(jnp.int32)
    limit = jnp.where(in_prompt, prompt_len, picked)
    return (segment, offset < limit)

def mask_of(rows, cols, prompt_len, cont_len):
    seg_rows, live_rows = describe(rows, prompt_len, cont_len)
    seg_cols, live_cols = describe(cols, prompt_len, cont_len)
    causal = (seg_rows[:, None] == seg_cols[None, :]) & (cols[None, :] <= rows[:, None])
    shared = (seg_cols[None, :] == 0) & (seg_rows[:, None] > 0)
    itself = cols[None, :] == rows[:, None]
    return (causal | shared) & (live_cols[None, :] | itself)

def attend_block(query_block, key_rows, value_rows, start, prompt_len, cont_len):
    rows = start + jnp.arange(query_block.shape[0], dtype=jnp.int32)
    cols = jnp.arange(key_rows.shape[0], dtype=jnp.int32)
    allowed = mask_of(rows, cols, prompt_len, cont_len)
    scores = jnp.einsum('qhd,khd->hqk', query_block, key_rows, precision=HIGHEST) * 0.125
    scores = low_back(scores)
    scores = jnp.where(allowed[None], scores, NEG)
    top = lax.optimization_barrier(jnp.max(scores, axis=-1, keepdims=True))
    expo = jnp.exp(scores - top)
    probs = expo / lax.optimization_barrier(jnp.sum(expo, axis=-1, keepdims=True))
    return jnp.einsum('hqk,khd->qhd', low(probs), value_rows, precision=HIGHEST)

def group_layer(group_in, prompt_len, cont_len, params):
    gain_a, shift_a, qkv_mat, qv_vec, out_mat, out_vec, gain_b, shift_b, fc_mat, fc_vec, proj_mat, proj_vec = params
    first = low(layer_norm(group_in, gain_a, shift_a))
    bias_all = jnp.concatenate([qv_vec[:D], jnp.zeros((D,), jnp.float32), qv_vec[D:]])
    qkv = low(low_back(jnp.dot(first, qkv_mat, precision=HIGHEST, preferred_element_type=jnp.float32) + bias_all))
    queries = qkv[:, :D].reshape(GLEN, H, HD)
    key_rows = qkv[:, D:2 * D].reshape(GLEN, H, HD)
    value_rows = qkv[:, 2 * D:].reshape(GLEN, H, HD)
    block_rows = min(512, GLEN)
    starts = jnp.arange(GLEN // block_rows, dtype=jnp.int32) * block_rows

    def one_block(start):
        query_block = lax.dynamic_slice_in_dim(queries, start, block_rows, 0)
        return attend_block(query_block, key_rows, value_rows, start, prompt_len, cont_len)
    blocks = lax.map(jax.checkpoint(one_block), starts)
    mixed = low(low_back(blocks.reshape(GLEN, D)))
    attn = low_back(jnp.dot(mixed, out_mat, precision=HIGHEST, preferred_element_type=jnp.float32) + out_vec)
    hidden = group_in + attn
    second = low(layer_norm(hidden, gain_b, shift_b))
    pre = low_back(jnp.dot(second, fc_mat, precision=HIGHEST, preferred_element_type=jnp.float32) + fc_vec)
    act = low(gelu_tanh(pre))
    branch = low_back(jnp.dot(act, proj_mat, precision=HIGHEST, preferred_element_type=jnp.float32) + proj_vec)
    return hidden + branch

def reference(tokens, prompt_lens, cont_lens, gain_one, shift_one, w_qkv, bias_qv, w_out, bias_out, gain_two, shift_two, w_fc, bias_fc, w_proj, bias_proj, cotangent):
    params = (gain_one.astype(jnp.float32), shift_one.astype(jnp.float32), w_qkv.astype(jnp.float32), bias_qv.astype(jnp.float32), w_out.astype(jnp.float32), bias_out.astype(jnp.float32), gain_two.astype(jnp.float32), shift_two.astype(jnp.float32), w_fc.astype(jnp.float32), bias_fc.astype(jnp.float32), w_proj.astype(jnp.float32), bias_proj.astype(jnp.float32))
    inputs = tokens.astype(jnp.float32)

    def forward(layer_in, layer_params):

        def per_group(group_args):
            group_in, prompt_len, cont_len = group_args
            return jax.checkpoint(group_layer)(group_in, prompt_len, cont_len, layer_params)
        return lax.map(per_group, (layer_in, prompt_lens, cont_lens))
    result, pullback = jax.vjp(forward, inputs, params)
    grad_in, grads = pullback(cotangent.astype(jnp.float32))
    return (result.astype(jnp.bfloat16), grad_in, grads[0], grads[1], grads[2], grads[3], grads[4], grads[5], grads[6], grads[7], grads[8], grads[9], grads[10], grads[11])
```

```python
import functools

import jax
import jax.numpy as jnp
from jax import lax
from jax.experimental import pallas as pl
from jax.experimental.pallas import tpu as pltpu
from jax.sharding import PartitionSpec as P

H = 16
HD = 64
PROMPT = 1024
CONTLEN = 512
CONTS = 2

EPS = 1e-05
GELU_C = 0.7978845608028654
GELU_A = 0.044715
NEG = -1e30
BF = jnp.bfloat16
F32 = jnp.float32


def swap(values, axis, bits):
    size = lax.axis_size(axis)
    return lax.ppermute(values, axis, [(i, i ^ bits) for i in range(size)])


def xor_take(values, index, axis):
    size = values.shape[axis]
    bit = 1
    while bit < size:
        parts = [lax.slice_in_dim(values, i, i + 1, axis=axis) for i in range(size)]
        flipped = jnp.concatenate([parts[i ^ bit] for i in range(size)], axis=axis)
        values = jnp.where((index & bit) != 0, flipped, values)
        bit *= 2
    return values


def xor_blocks(values, index, count, axis):
    width = values.shape[axis] // count
    return jnp.concatenate(
        [
            lax.dynamic_slice_in_dim(values, (i ^ index) * width, width, axis=axis)
            for i in range(count)
        ],
        axis=axis,
    )


def plane_gather(values):
    size = lax.axis_size("seq")
    if size != 4:
        return [values] + [swap(values, "seq", k) for k in range(1, size)]
    half = values.shape[0] // 2
    one = swap(values, "seq", 1)
    two = swap(values, "seq", 2)
    three = jnp.concatenate(
        [swap(two[:half], "seq", 1), swap(one[half:], "seq", 2)], axis=0
    )
    return [values, one, two, three]


def plane_scatter(blocks):
    size = lax.axis_size("seq")
    if size != 4:
        total = blocks[0].astype(F32)
        for k in range(1, size):
            total = total + swap(blocks[k].astype(BF), "seq", k).astype(F32)
        return total
    half = blocks[0].shape[0] // 2
    sent_x = jnp.concatenate([blocks[1][:half], blocks[3][:half]], axis=0).astype(BF)
    sent_y = jnp.concatenate([blocks[2][half:], blocks[3][half:]], axis=0).astype(BF)
    got_x = swap(sent_x, "seq", 1).astype(F32)
    got_y = swap(sent_y, "seq", 2).astype(F32)
    next_y = (blocks[2][:half].astype(F32) + got_x[half:]).astype(BF)
    next_x = (blocks[1][half:].astype(F32) + got_y[half:]).astype(BF)
    last_y = swap(next_y, "seq", 2).astype(F32)
    last_x = swap(next_x, "seq", 1).astype(F32)
    upper = blocks[0][:half].astype(F32) + got_x[:half] + last_y
    lower = blocks[0][half:].astype(F32) + got_y[:half] + last_x
    return jnp.concatenate([upper, lower], axis=0)


def tile_rows(total, blocks):
    return min(256, total // blocks)


def rel_row(tile, rows, block_rows, me):
    per = block_rows // rows
    return pl.multiple_of(((tile // per) ^ me) * block_rows + (tile % per) * rows, rows)


def walk(tile, rows):
    prompt_tiles = PROMPT // rows
    cont_tiles = CONTLEN // rows
    in_prompt = tile < prompt_tiles
    inside = lax.rem(jnp.maximum(tile - prompt_tiles, 0), cont_tiles)
    count = jnp.where(in_prompt, tile, prompt_tiles + inside)
    return count, tile - inside - prompt_tiles


def key_limit(lens, tile, rows):
    prompt_tiles = PROMPT // rows
    cont_tiles = CONTLEN // rows
    past = jnp.maximum(tile - prompt_tiles, 0)
    cont = jnp.minimum(past // cont_tiles, CONTS - 1)
    length = lens[1]
    for i in range(1, CONTS):
        length = jnp.where(cont == i, lens[1 + i], length)
    return jnp.where(
        tile < prompt_tiles, lens[0] - tile * rows, length - lax.rem(past, cont_tiles) * rows
    )


def pair_stack(block, per_pair, scale=None):
    if scale is not None:
        block = block * scale
    if per_pair == 1:
        return block
    lane = lax.broadcasted_iota(jnp.int32, block.shape, 1) // HD
    return jnp.concatenate(
        [jnp.where(lane == h, block, jnp.zeros_like(block)) for h in range(per_pair)], axis=0
    )


def diagonal_mask(rows, per_pair, limit):
    key = lax.broadcasted_iota(jnp.int32, (rows, per_pair * rows), 0)
    query = lax.broadcasted_iota(jnp.int32, (rows, per_pair * rows), 1) % rows
    return ((key <= query) & (key < limit)) | (key == query)


def live_mask(rows, per_pair, limit):
    return lax.broadcasted_iota(jnp.int32, (rows, per_pair * rows), 0) < limit


def nt(left, right):
    return lax.dot_general(left, right, (((1,), (1,)), ((), ())), preferred_element_type=F32)


def nn(left, right):
    return lax.dot_general(left, right, (((1,), (0,)), ((), ())), preferred_element_type=F32)


def unstack(values, per_pair, rows):
    if per_pair == 1:
        return values
    return jnp.concatenate(
        [values[h * HD : (h + 1) * HD, h * rows : (h + 1) * rows] for h in range(per_pair)], axis=0
    )


def forward_kernel(rows, block_rows, per_pair, lens, q_ref, k_ref, v_ref, out_ref, norm_ref, vt_ref):
    tile = pl.program_id(1)
    me = lens[1 + CONTS]
    tiles = q_ref.shape[0] // rows

    @pl.when(tile == 0)
    def _():
        def turn(i, carry):
            at = rel_row(i, rows, block_rows, me)
            vt_ref[i] = v_ref[pl.ds(at, rows), :].T
            return carry

        lax.fori_loop(0, tiles, turn, 0)

    at = rel_row(tile, rows, block_rows, me)
    query = pair_stack(q_ref[pl.ds(at, rows), :], per_pair, jnp.asarray(0.125, BF))

    def scores(i):
        return nt(k_ref[pl.ds(rel_row(i, rows, block_rows, me), rows), :], query)

    first = jnp.where(
        diagonal_mask(rows, per_pair, key_limit(lens, tile, rows)), scores(tile), NEG
    )
    top = jnp.max(first, axis=0, keepdims=True)
    weights = jnp.exp(first - top)
    denom = jnp.sum(weights, axis=0, keepdims=True)
    total = nn(vt_ref[tile], weights.astype(BF))
    count, shift = walk(tile, rows)

    def step(i, carry):
        top, denom, total = carry
        key_tile = jnp.where(i < PROMPT // rows, i, i + shift)
        part = jnp.where(
            live_mask(rows, per_pair, key_limit(lens, key_tile, rows)), scores(key_tile), NEG
        )
        higher = jnp.maximum(top, jnp.max(part, axis=0, keepdims=True))
        scale = jnp.exp(top - higher)
        weights = jnp.exp(part - higher)
        denom = denom * scale + jnp.sum(weights, axis=0, keepdims=True)
        total = total * scale + nn(vt_ref[key_tile], weights.astype(BF))
        return higher, denom, total

    top, denom, total = lax.fori_loop(0, count, step, (top, denom, total))
    mixed = unstack(total / denom, per_pair, rows)
    out_ref[...] = mixed.T.astype(BF)
    norm_ref[0, 0] = top + jnp.log(denom)


def backward_kernel(
    rows, block_rows, per_pair, lens, q_ref, k_ref, v_ref, out_ref, grad_ref, norm_ref,
    dq_ref, dk_ref, dv_ref, kt_ref, dk_sum, dv_sum, dq_sum,
):
    tile = pl.program_id(1)
    me = lens[1 + CONTS]
    tiles = q_ref.shape[0] // rows
    width = q_ref.shape[1]

    @pl.when(tile == 0)
    def _():
        def turn(i, carry):
            at = rel_row(i, rows, block_rows, me)
            kt_ref[i] = k_ref[pl.ds(at, rows), :].T
            return carry

        lax.fori_loop(0, tiles, turn, 0)
        dk_sum[...] = jnp.zeros_like(dk_sum)
        dv_sum[...] = jnp.zeros_like(dv_sum)

    at = rel_row(tile, rows, block_rows, me)
    query = pair_stack(q_ref[pl.ds(at, rows), :], per_pair, jnp.asarray(0.125, BF))
    grad_block = grad_ref[pl.ds(at, rows), :]
    grad = pair_stack(grad_block, per_pair)
    product = (grad_block.astype(F32) * out_ref[pl.ds(at, rows), :].astype(F32)).T
    inner = jnp.concatenate(
        [
            jnp.sum(product[h * HD : (h + 1) * HD], axis=0, keepdims=True)
            for h in range(per_pair)
        ],
        axis=1,
    )
    norm = norm_ref[0, 0]

    def one(key_tile, mask):
        key_at = rel_row(key_tile, rows, block_rows, me)
        keys = pl.ds(key_at, rows)
        part = jnp.where(mask, nt(k_ref[keys, :], query), NEG)
        probs = jnp.exp(part - norm)
        slope = probs * (nt(v_ref[keys, :], grad) - inner)
        slope_low = slope.astype(BF)
        dv_sum[keys, :] += nn(probs.astype(BF), grad)
        dk_sum[keys, :] += nn(slope_low, query)
        return nn(kt_ref[key_tile], slope_low)

    dq_sum[...] = one(tile, diagonal_mask(rows, per_pair, key_limit(lens, tile, rows)))
    count, shift = walk(tile, rows)

    def step(i, carry):
        key_tile = jnp.where(i < PROMPT // rows, i, i + shift)
        dq_sum[...] += one(key_tile, live_mask(rows, per_pair, key_limit(lens, key_tile, rows)))
        return carry

    lax.fori_loop(0, count, step, 0)
    dq_ref[...] = (unstack(dq_sum[...], per_pair, rows).T * 0.125).astype(BF)

    @pl.when(tile == tiles - 1)
    def _():
        dk_ref[...] = dk_sum[...].astype(BF)
        dv_ref[...] = dv_sum[...].astype(BF)


def attention_plan(total, heads):
    blocks = lax.axis_size("seq")
    rows = tile_rows(total, blocks)
    per_pair = 2 if heads % 2 == 0 else 1
    return rows, total // blocks, per_pair, heads // per_pair, per_pair * HD


def thirds(qkv, width, pair_width):
    if pair_width % 128 == 0:
        per = width // pair_width
        return (qkv, qkv, qkv), (0, per, 2 * per)
    return tuple(qkv[:, i * width : (i + 1) * width] for i in range(3)), (0, 0, 0)


def row_block(rows, block_rows):
    per = block_rows // rows

    def index(pair, tile, lens):
        return ((tile // per) ^ lens[1 + CONTS]) * per + tile % per, pair

    return index


def attend_forward(lens, qkv, heads):
    total = qkv.shape[0]
    width = heads * HD
    rows, block_rows, per_pair, pairs, pair_width = attention_plan(total, heads)
    arrays, firsts = thirds(qkv, width, pair_width)
    tiles = total // rows

    def whole(first):
        return pl.BlockSpec((total, pair_width), lambda pair, tile, lens: (0, first + pair))

    return pl.pallas_call(
        functools.partial(forward_kernel, rows, block_rows, per_pair),
        out_shape=(
            jax.ShapeDtypeStruct((total, width), BF),
            jax.ShapeDtypeStruct((pairs, tiles, 1, per_pair * rows), F32),
        ),
        grid_spec=pltpu.PrefetchScalarGridSpec(
            num_scalar_prefetch=1,
            grid=(pairs, tiles),
            in_specs=[whole(first) for first in firsts],
            out_specs=(
                pl.BlockSpec((rows, pair_width), row_block(rows, block_rows)),
                pl.BlockSpec(
                    (1, 1, 1, per_pair * rows), lambda pair, tile, lens: (pair, tile, 0, 0)
                ),
            ),
            scratch_shapes=[pltpu.VMEM((tiles, pair_width, rows), BF)],
        ),
        name="attend_forward",
    )(lens, *arrays)


def attend_backward(lens, qkv, mixed, grad, norm, heads):
    total = qkv.shape[0]
    width = heads * HD
    rows, block_rows, per_pair, pairs, pair_width = attention_plan(total, heads)
    arrays, firsts = thirds(qkv, width, pair_width)
    tiles = total // rows

    def whole(first):
        return pl.BlockSpec((total, pair_width), lambda pair, tile, lens: (0, first + pair))

    return pl.pallas_call(
        functools.partial(backward_kernel, rows, block_rows, per_pair),
        out_shape=(jax.ShapeDtypeStruct((total, width), BF),) * 3,
        grid_spec=pltpu.PrefetchScalarGridSpec(
            num_scalar_prefetch=1,
            grid=(pairs, tiles),
            in_specs=[whole(first) for first in firsts]
            + [
                whole(0),
                whole(0),
                pl.BlockSpec(
                    (1, 1, 1, per_pair * rows), lambda pair, tile, lens: (pair, tile, 0, 0)
                ),
            ],
            out_specs=(
                pl.BlockSpec((rows, pair_width), row_block(rows, block_rows)),
                whole(0),
                whole(0),
            ),
            scratch_shapes=[
                pltpu.VMEM((tiles, pair_width, rows), BF),
                pltpu.VMEM((total, pair_width), F32),
                pltpu.VMEM((total, pair_width), F32),
                pltpu.VMEM((pair_width, per_pair * rows), F32),
            ],
        ),
        name="attend_backward",
    )(lens, *arrays, mixed, grad, norm)


def norm_stats(values):
    center = values - jnp.mean(values, axis=-1, keepdims=True)
    spread = jnp.mean(center * center, axis=-1, keepdims=True)
    scale = lax.rsqrt(spread + EPS)
    return center * scale, scale


def norm_pull(unit, scale, slope):
    return scale * (
        slope
        - jnp.mean(slope, axis=-1, keepdims=True)
        - unit * jnp.mean(slope * unit, axis=-1, keepdims=True)
    )


def gelu_both(values):
    square = values * values
    bent = jnp.tanh(GELU_C * (values + GELU_A * square * values))
    value = 0.5 * values * (1.0 + bent)
    slope = 0.5 * (1.0 + bent) + 0.5 * values * (1.0 - bent * bent) * GELU_C * (
        1.0 + 3.0 * GELU_A * square
    )
    return value, slope


def tn(left, right):
    return lax.dot_general(left, right, (((0,), (0,)), ((), ())), preferred_element_type=F32)


def pick(values, index, axis):
    return lax.dynamic_index_in_dim(values, index, axis, keepdims=False)


def by_core(core, mine, other, axis):
    return jnp.where(
        core == 0, jnp.stack([mine, other], axis=axis), jnp.stack([other, mine], axis=axis)
    )


def body_general(
    tokens,
    prompt_lens,
    cont_lens,
    gain_one,
    shift_one,
    w_qkv,
    bias_qv,
    w_out,
    bias_out,
    gain_two,
    shift_two,
    w_fc,
    bias_fc,
    w_proj,
    bias_proj,
    cotangent,
):
    ns = lax.axis_size("seq")
    nf = lax.axis_size("fsdp")
    nz = nf // 2
    me = lax.axis_index("seq")
    owner = lax.axis_index("fsdp")
    floor = owner // 2
    core = owner % 2
    toks, width = tokens.shape[1:]
    hidden_all = w_fc.shape[1]
    own = width // nf
    heads = H // ns
    local = width // ns
    hw = hidden_all // (nf * ns)
    cols = nz * hw

    token_block = tokens[0]
    branch = cotangent[0]

    token_blocks = plane_gather(token_block)
    vectors = [gain_one, shift_one, bias_qv, bias_out, gain_two, shift_two, bias_fc, bias_proj]
    packed = jnp.concatenate([v.reshape(-1, own) for v in vectors], axis=0)
    lines = packed.shape[0]
    packed_rows = -(-packed.size // (3 * local))
    packed = jnp.pad(packed.reshape(-1), (0, 16 * (-(-packed_rows // 16)) * 3 * local - packed.size))
    mine_qkv = pick(w_qkv.reshape(own, 3, ns, local), me, 2).reshape(own, 3 * local)
    sent_qkv = jnp.concatenate([mine_qkv, packed.reshape(-1, 3 * local)], axis=0)
    got_qkv = jnp.stack([sent_qkv] + [swap(sent_qkv, "fsdp", 2 * k) for k in range(1, nz)])
    got_qkv = xor_take(by_core(core, got_qkv, swap(got_qkv, "fsdp", 1), 1), floor, 0)
    qkv_mat = got_qkv[:, :, :own].reshape(width, 3 * local)
    small = got_qkv[:, :, own:].reshape(nf, -1)[:, : lines * own].reshape(nf, lines, own)
    at = 0
    full = []
    for v in vectors:
        count = v.shape[0] // own
        full.append(small[:, at : at + count].reshape(-1).astype(F32))
        at += count
    gain_a, shift_a, qv_vec, out_vec, gain_b, shift_b, fc_vec, proj_vec = full

    fc_cut = w_fc.reshape(own, nz, 2, ns, hw)
    fc_mine = pick(fc_cut, core, 2)
    fc_other = swap(pick(fc_cut, 1 - core, 2).reshape(own, -1), "fsdp", 1)
    fc_rows = by_core(core, fc_mine.reshape(own, -1), fc_other, 0).reshape(2 * own, nz, ns, hw)
    fc_rows = xor_take(xor_take(fc_rows, floor, 1), me, 2)
    proj_rows = xor_take(w_proj.reshape(ns, hw, width), me, 0)
    out_cols = xor_take(w_out.reshape(own, ns, local), me, 1)
    proj_parts = width // cols
    out_parts = max(1, cols // local)

    def share(q, k):
        fc = jnp.concatenate([fc_rows[:, j ^ k, q] for j in range(nz)], axis=1)
        proj = [proj_rows[q][:, i * cols : (i + 1) * cols] for i in range(proj_parts)]
        out = out_cols[:, q]
        if out_parts > 1:
            step = own // out_parts
            out = jnp.concatenate([out[i * step : (i + 1) * step] for i in range(out_parts)], axis=1)
        return fc, proj, out

    def message(k):
        fc, proj, out = share(0, k)
        return jnp.concatenate([fc, *proj, out.reshape(-1, cols)], axis=0)

    got = [swap(message(k), "fsdp", 2 * k) for k in range(1, nz)]
    rows_each = got[0].shape[0]
    planes = plane_gather(jnp.concatenate(got, axis=0))

    def parts_of(q, k):
        if k == 0:
            fc, proj, out = share(q, 0)
            return fc, jnp.concatenate(proj, axis=1), out_cols[:, q]
        block = planes[q][(k - 1) * rows_each : k * rows_each]
        fc = block[: 2 * own]
        proj = jnp.concatenate(
            [block[2 * own + i * hw : 2 * own + (i + 1) * hw] for i in range(proj_parts)], axis=1
        )
        out = block[2 * own + proj_parts * hw :]
        if out_parts > 1:
            out = jnp.concatenate(
                [out[:, i * local : (i + 1) * local] for i in range(out_parts)], axis=0
            )
        else:
            out = out.reshape(own, local)
        return fc, proj, out

    pieces = [[parts_of(q, k) for k in range(nz)] for q in range(ns)]
    out_half = jnp.stack(
        [jnp.stack([pieces[q][k][2] for q in range(ns)], axis=1) for k in range(nz)]
    )
    out_half = xor_take(out_half, me, 2).reshape(nz, own, width)
    out_both = by_core(core, out_half, swap(out_half, "fsdp", 1), 1)
    out_mat = xor_take(out_both, floor, 0).reshape(ns, local, width)
    out_mat = xor_take(out_mat, me, 0).reshape(width, width)
    fc_mat = jnp.concatenate(
        [jnp.concatenate([pieces[q][k][0] for k in range(nz)], axis=0) for q in range(ns)], axis=1
    )
    proj_mat = jnp.concatenate([pieces[q][k][1] for q in range(ns) for k in range(nz)], axis=0)
    fc_bias = pick(fc_vec.reshape(nz, 2, ns, hw), core, 1)
    fc_bias = xor_take(xor_take(fc_bias, floor, 0), me, 1).transpose(1, 0, 2).reshape(-1)

    all_tokens = jnp.concatenate(token_blocks, axis=0).astype(F32)
    unit_all, _ = norm_stats(all_tokens)
    first = (unit_all * gain_a + shift_a).astype(BF)
    bias_all = jnp.concatenate(
        [
            pick(qv_vec.reshape(2, ns, local)[0], me, 0),
            jnp.zeros((local,), F32),
            pick(qv_vec.reshape(2, ns, local)[1], me, 0),
        ]
    )
    qkv = (jnp.dot(first, qkv_mat, preferred_element_type=F32) + bias_all).astype(BF)
    lens = jnp.concatenate([prompt_lens, cont_lens[0], me.reshape(1)]).astype(jnp.int32)
    mixed_heads, log_norm = attend_forward(lens, qkv, heads)

    def to_tokens(values):
        return jnp.concatenate(
            [values[:toks]]
            + [swap(values[k * toks : (k + 1) * toks], "seq", k) for k in range(1, ns)],
            axis=1,
        )

    def to_heads(values):
        return jnp.concatenate(
            [values[:, :local]]
            + [swap(values[:, k * local : (k + 1) * local], "seq", k) for k in range(1, ns)],
            axis=0,
        )

    mixed = to_tokens(mixed_heads)
    hidden = token_block.astype(F32) + jnp.dot(mixed, out_mat, preferred_element_type=F32) + out_vec
    unit_two, scale_two = norm_stats(hidden)
    second = (unit_two * gain_b + shift_b).astype(BF)

    second_both = jnp.concatenate([second, swap(second, "fsdp", 1)], axis=0)
    second_both = xor_blocks(second_both, floor, nz, 1)
    branch_both = jnp.concatenate([branch, swap(branch, "fsdp", 1)], axis=0)
    pre = jnp.dot(second_both, fc_mat, preferred_element_type=F32) + fc_bias
    act_full, bend = gelu_both(pre)
    act = act_full.astype(BF)
    grad_act = nt(branch_both, proj_mat)
    grad_pre = (grad_act * bend).astype(BF)
    grad_second_both = nt(grad_pre, fc_mat)
    grad_second = grad_second_both[:toks] + swap(
        grad_second_both[toks:].astype(BF), "fsdp", 1
    ).astype(F32)
    grad_second = xor_blocks(grad_second, floor, nz, 1)
    out_sum = jnp.dot(act, proj_mat, preferred_element_type=F32)
    result = hidden + out_sum[:toks] + proj_vec
    result = result + swap(out_sum[toks:].astype(BF), "fsdp", 1).astype(F32)
    output = result.astype(BF)[None]

    grad_hidden = branch.astype(F32) + norm_pull(unit_two, scale_two, grad_second * gain_b)
    grad_attn = grad_hidden.astype(BF)
    grad_mixed = nt(grad_attn, out_mat).astype(BF)
    grad_heads = to_heads(grad_mixed)

    grad_q, grad_k, grad_v = attend_backward(lens, qkv, mixed_heads, grad_heads, log_norm, heads)
    grad_qkv = jnp.concatenate([grad_q, grad_k, grad_v], axis=1)
    grad_first_part = nt(grad_qkv, qkv_mat).astype(BF)
    grad_first = plane_scatter(
        [grad_first_part[k * toks : (k + 1) * toks] for k in range(ns)]
    )
    unit_one, scale_one = norm_stats(token_block.astype(F32))
    input_grad = (grad_hidden + norm_pull(unit_one, scale_one, grad_first * gain_a))[None]

    span = nz * hw
    grad_fc = [tn(second_both, grad_pre[:, q * span : (q + 1) * span]).astype(BF) for q in range(ns)]
    grad_proj = [tn(act[:, q * span : (q + 1) * span], branch_both).astype(BF) for q in range(ns)]
    fc_sum = plane_scatter(grad_fc)
    proj_sum = plane_scatter(grad_proj)

    def fc_for(k):
        block = fc_sum[k * 2 * own : (k + 1) * 2 * own].reshape(2 * own, nz, hw)
        return jnp.concatenate([block[:, j ^ k] for j in range(nz)], axis=1)

    def proj_for(k):
        block = proj_sum[k * hw : (k + 1) * hw]
        return jnp.concatenate(
            [block[:, i * span : (i + 1) * span] for i in range(proj_parts)], axis=0
        )

    both_sum = jnp.concatenate([fc_for(0), proj_for(0)], axis=0)
    for k in range(1, nz):
        sent = jnp.concatenate([fc_for(k), proj_for(k)], axis=0).astype(BF)
        both_sum = both_sum + swap(sent, "fsdp", 2 * k).astype(F32)
    fc_owned = both_sum[: 2 * own].reshape(2, own, span)
    fc_kept = pick(fc_owned, core, 0).astype(BF)
    fc_moved = swap(pick(fc_owned, 1 - core, 0).astype(BF), "fsdp", 1)
    final = jnp.concatenate([fc_kept, fc_moved, both_sum[2 * own :].astype(BF)], axis=0)
    finals = plane_gather(final)
    fc_kept_all = jnp.stack([v[:own].reshape(own, nz, hw) for v in finals], axis=2)
    fc_moved_all = jnp.stack([v[own : 2 * own].reshape(own, nz, hw) for v in finals], axis=2)
    grad_w_fc = by_core(core, fc_kept_all, fc_moved_all, 2)
    grad_w_fc = xor_take(xor_take(grad_w_fc, floor, 1), me, 3).reshape(own, hidden_all).astype(F32)
    grad_w_proj = jnp.stack(
        [
            jnp.concatenate(
                [v[2 * own + i * hw : 2 * own + (i + 1) * hw] for i in range(proj_parts)], axis=1
            )
            for v in finals
        ]
    )
    grad_w_proj = xor_take(grad_w_proj, me, 0).reshape(ns * hw, width).astype(F32)

    grad_out = tn(mixed, grad_attn).astype(BF).reshape(ns, local, width)
    grad_out = xor_take(grad_out, me, 0).reshape(nz, 2, own, width)
    grad_out = xor_take(grad_out, floor, 0)
    out_kept = pick(grad_out, core, 1).astype(F32) + swap(
        pick(grad_out, 1 - core, 1), "fsdp", 1
    ).astype(F32)
    out_owned = out_kept[0]
    for k in range(1, nz):
        out_owned = out_owned + swap(out_kept[k].astype(BF), "fsdp", 2 * k).astype(F32)
    bit = 1
    while bit < ns:
        out_owned = out_owned + swap(out_owned.astype(BF), "seq", bit).astype(F32)
        bit *= 2
    grad_w_out = out_owned

    grad_in = tn(first, grad_qkv).astype(BF).reshape(nz, 2, own, 3 * local)
    grad_in = xor_take(grad_in, floor, 0)
    in_kept = pick(grad_in, core, 1).astype(F32) + swap(
        pick(grad_in, 1 - core, 1), "fsdp", 1
    ).astype(F32)
    in_owned = in_kept[0]
    for k in range(1, nz):
        in_owned = in_owned + swap(in_kept[k].astype(BF), "fsdp", 2 * k).astype(F32)
    in_owned = in_owned.astype(BF)
    in_blocks = jnp.stack(
        [in_owned.reshape(own, 3, local)]
        + [swap(in_owned, "seq", k).reshape(own, 3, local) for k in range(1, ns)],
        axis=2,
    )
    grad_w_qkv = xor_take(in_blocks, me, 2).reshape(own, 3 * width).astype(F32)

    def placed(values, parts):
        slots = jnp.arange(parts)[:, None] == me
        return jnp.where(slots, values[None, :], 0.0).reshape(-1)

    part_f32 = grad_first_part.astype(F32)
    fc_bias_grad = jnp.sum(grad_pre.astype(F32), axis=0).reshape(ns, nz, hw).transpose(1, 0, 2)
    fc_bias_grad = xor_take(xor_take(fc_bias_grad, floor, 0), me, 1)
    fc_bias_grad = jnp.where(
        (jnp.arange(2) == core)[None, :, None, None], fc_bias_grad[:, None], 0.0
    ).reshape(-1)
    vector_grads = [
        jnp.sum(part_f32 * unit_all, axis=0),
        jnp.sum(part_f32, axis=0),
        placed(jnp.sum(grad_q.astype(F32), axis=0), ns),
        placed(jnp.sum(grad_v.astype(F32), axis=0), ns),
        jnp.sum(grad_attn.astype(F32), axis=0),
        jnp.sum(grad_second * unit_two, axis=0),
        jnp.sum(grad_second, axis=0),
        fc_bias_grad,
        jnp.sum(branch.astype(F32), axis=0),
    ]
    vector_sum = jnp.concatenate([v.reshape(-1, width) for v in vector_grads], axis=0)
    for axis, size in (("seq", ns), ("fsdp", nf)):
        bit = 1
        while bit < size:
            vector_sum = vector_sum + swap(vector_sum, axis, bit)
            bit *= 2
    vector_sum = vector_sum.reshape(-1)
    outs = []
    at = 0
    for v in vectors:
        count = v.shape[0]
        outs.append(lax.dynamic_slice_in_dim(vector_sum, at + owner * count, count))
        at += nf * count
    (g_gain_one, g_shift_one, g_bias_qv, g_bias_out, g_gain_two, g_shift_two, g_bias_fc, g_bias_proj) = outs

    return (
        output,
        input_grad,
        g_gain_one,
        g_shift_one,
        grad_w_qkv,
        g_bias_qv,
        grad_w_out,
        g_bias_out,
        g_gain_two,
        g_shift_two,
        grad_w_fc,
        g_bias_fc,
        grad_w_proj,
        g_bias_proj,
    )


UPPER = (0, 2, 1, 3)


def hidden_at(q, half, size):
    return half * 4 * size + (UPPER[q] if half == 0 else q) * size


def start_all(copies, sems):
    made = [
        pltpu.make_async_copy(source, target, sems.at[i]) for i, (source, target) in enumerate(copies)
    ]
    for copy in made:
        copy.start()
    return made


def aligned(value, size):
    return pl.multiple_of(value, size)


def pack_kernel(hw, place, fc_ref, proj_ref, mine_ref, other_ref, share_ref):
    me, core = place[0], place[2]
    for q in range(4):
        for z in range(4):
            target = hidden_at(q, z // 2, 2 * hw) + (z % 2) * hw
            for out_ref, which in ((mine_ref, core), (other_ref, 1 - core)):
                source = aligned(z * 8 * hw + which * 4 * hw + (me ^ q) * hw, hw)
                out_ref[:, target : target + hw] = fc_ref[:, pl.ds(source, hw)]
    share_ref[...] = proj_ref[...]


def pack(place, w_fc, w_proj):
    own, hidden_all = w_fc.shape
    hw, width = w_proj.shape[0] // 4, w_proj.shape[1]

    def whole(shape):
        return pl.BlockSpec(shape, lambda i, place: (0, 0))

    half = jax.ShapeDtypeStruct((own, hidden_all // 2), BF)
    return pl.pallas_call(
        functools.partial(pack_kernel, hw),
        out_shape=(half, half, jax.ShapeDtypeStruct((hw, width), BF)),
        grid_spec=pltpu.PrefetchScalarGridSpec(
            num_scalar_prefetch=1,
            grid=(1,),
            in_specs=[
                whole((own, hidden_all)),
                pl.BlockSpec((hw, width), lambda i, place: (place[0], 0)),
            ],
            out_specs=(whole(half.shape), whole(half.shape), whole((hw, width))),
        ),
        name="pack_shares",
    )(place, w_fc, w_proj)


def join_kernel(place, m0, m1, o0, o1, out_ref):
    core = place[2]
    own, chunk = m0.shape
    for refs, which in (((m0, m1), core), ((o0, o1), 1 - core)):
        rows = pl.ds(aligned(which * own, own), own)
        for half in range(2):
            out_ref[rows, half * chunk : (half + 1) * chunk] = refs[half][...]


def join(place, mine, other):
    own, hidden = mine.shape
    chunk = hidden // 8
    pieces = [
        pl.BlockSpec((own, chunk), lambda i, place, at=hidden_at(0, half, 1): (0, at))
        for half in range(2)
    ]
    return pl.pallas_call(
        join_kernel,
        out_shape=jax.ShapeDtypeStruct((2 * own, hidden // 4), BF),
        grid_spec=pltpu.PrefetchScalarGridSpec(
            num_scalar_prefetch=1,
            grid=(1,),
            in_specs=pieces * 2,
            out_specs=pl.BlockSpec((2 * own, hidden // 4), lambda i, place: (0, 0)),
        ),
        name="join_rows",
    )(place, mine, mine, other, other)


def project_kernel(
    place, own_ref, one_ref, two_ref, up_ref, low_ref, kept_ref, moved_ref, gain_ref, shift_ref,
    bias_ref, first_ref, unit_ref, qkv_ref, toks, mat, sems,
):
    step = pl.program_id(0)
    floor, core = place[1], place[2]
    block = own_ref.shape[0]
    half = block // 2
    own = mat.shape[0] // 8

    def copies():
        made = [
            (own_ref, toks.at[pl.ds(0, block), :]),
            (one_ref, toks.at[pl.ds(block, block), :]),
            (two_ref, toks.at[pl.ds(2 * block, block), :]),
            (up_ref, toks.at[pl.ds(3 * block, half), :]),
            (low_ref, toks.at[pl.ds(3 * block + half, half), :]),
        ]
        for k in range(4):
            for ref, which in ((kept_ref, core), (moved_ref, 1 - core)):
                row = aligned((floor ^ k) * 2 * own + which * own, own)
                made.append((ref.at[k, pl.ds(0, own), :], mat.at[pl.ds(row, own), :]))
        return made

    @pl.when(step == 0)
    def _():
        for copy in start_all(copies(), sems):
            copy.wait()

    rows = first_ref.shape[0]
    values = toks[pl.ds(aligned(step * rows, rows), rows), :].astype(F32)
    unit, _ = norm_stats(values)
    first = (unit * gain_ref[...] + shift_ref[...]).astype(BF)
    first_ref[...] = first
    unit_ref[...] = unit.astype(BF)
    qkv_ref[...] = (nn(first, mat[...]) + bias_ref[...]).astype(BF)


def project(place, blocks, kept, moved, gain, shift, bias):
    block, width = blocks[0].shape
    outs = kept.shape[2]
    total = 4 * block
    rows = 256
    raw = pl.BlockSpec(memory_space=pl.ANY)

    def line(size):
        return pl.BlockSpec((1, size), lambda i, place: (0, 0))

    def tile(size):
        return pl.BlockSpec((rows, size), lambda i, place: (i, 0))

    return pl.pallas_call(
        project_kernel,
        out_shape=(
            jax.ShapeDtypeStruct((total, width), BF),
            jax.ShapeDtypeStruct((total, width), BF),
            jax.ShapeDtypeStruct((total, outs), BF),
        ),
        grid_spec=pltpu.PrefetchScalarGridSpec(
            num_scalar_prefetch=1,
            grid=(total // rows,),
            in_specs=[raw] * 7 + [line(width), line(width), line(outs)],
            out_specs=(tile(width), tile(width), tile(outs)),
            scratch_shapes=[
                pltpu.VMEM((total, width), BF),
                pltpu.VMEM((width, outs), BF),
                pltpu.SemaphoreType.DMA((13,)),
            ],
        ),
        name="project",
    )(place, *blocks, kept, moved, gain, shift, bias)


def attn_out_kernel(
    place, m0, m1, m2, m3, kept_ref, moved_ref, token_ref, bias_ref, gain_ref, shift_ref,
    hidden_ref, second_ref, mixed_ref, mat_ref, mixed, sems,
):
    step = pl.program_id(0)
    me, floor, core = place[0], place[1], place[2]
    local = m1.shape[1]
    own = mat_ref.shape[0] // 8
    block = m1.shape[0]

    @pl.when(step == 0)
    def _():
        made = []
        for k, ref in enumerate((m0, m1, m2, m3)):
            lanes = pl.ds(aligned((me ^ k) * local, local), local)
            made.append((ref.at[pl.ds(0, block), :], mixed.at[:, lanes]))
        for k in range(4):
            for ref, which in ((kept_ref, core), (moved_ref, 1 - core)):
                row = aligned((floor ^ k) * 2 * own + which * own, own)
                made.append((ref.at[k], mat_ref.at[pl.ds(row, own), :]))
        for copy in start_all(made, sems):
            copy.wait()

    rows = hidden_ref.shape[0]
    here = mixed[pl.ds(aligned(step * rows, rows), rows), :]
    mixed_ref[...] = here
    hidden = token_ref[...].astype(F32) + nn(here, mat_ref[...]) + bias_ref[...]
    hidden_ref[...] = hidden
    unit, _ = norm_stats(hidden)
    second_ref[...] = (unit * gain_ref[...] + shift_ref[...]).astype(BF)


def attn_out(place, mixed, kept, moved, tokens, bias, gain, shift):
    block, width = tokens.shape
    rows = 256
    raw = pl.BlockSpec(memory_space=pl.ANY)
    line = pl.BlockSpec((1, width), lambda i, place: (0, 0))
    tile = pl.BlockSpec((rows, width), lambda i, place: (i, 0))
    return pl.pallas_call(
        attn_out_kernel,
        out_shape=(
            jax.ShapeDtypeStruct((block, width), F32),
            jax.ShapeDtypeStruct((block, width), BF),
            jax.ShapeDtypeStruct((block, width), BF),
            jax.ShapeDtypeStruct((width, width), BF),
        ),
        grid_spec=pltpu.PrefetchScalarGridSpec(
            num_scalar_prefetch=1,
            grid=(block // rows,),
            in_specs=[raw] * 6 + [tile, line, line, line],
            out_specs=(tile, tile, tile, pl.BlockSpec((width, width), lambda i, place: (0, 0))),
            scratch_shapes=[pltpu.VMEM((block, width), BF), pltpu.SemaphoreType.DMA((12,))],
        ),
        name="attn_out",
    )(place, *mixed, kept, moved, tokens, bias, gain, shift)


def feed_kernel(
    hw, place, second_ref, branch_ref, bias_ref, mine_ref, other_ref, a0, a1, a2, a3, proj_ref,
    b0, b1, b2, b3, act_ref, slope_ref, out_own, out_oth, back_own, back_oth, colsum_ref,
    fc, proj, sems,
):
    step = pl.program_id(0)
    me, floor, core = place[0], place[1], place[2]
    own = mine_ref.shape[0]
    chunk = 2 * hw
    steps = pl.num_programs(0)

    @pl.when(step == 0)
    def _():
        made = []
        for ref, which in ((mine_ref, core), (other_ref, 1 - core)):
            row = aligned(floor * 2 * own + which * own, own)
            made.append((ref, fc.at[pl.ds(row, own), :]))
        for q, ref in enumerate((a0, a1, a2, a3)):
            for k in range(1, 4):
                row = aligned((floor ^ k) * 2 * own, 2 * own)
                for half in range(2):
                    made.append(
                        (
                            ref.at[pl.ds((k - 1) * 2 * own, 2 * own), pl.ds(half * chunk, chunk)],
                            fc.at[pl.ds(row, 2 * own), pl.ds(hidden_at(q, half, chunk), chunk)],
                        )
                    )
        for q, ref in enumerate((b0, b1, b2, b3)):
            for k in range(4):
                z = floor ^ k
                row = jnp.where(z < 2, hidden_at(q, 0, chunk), hidden_at(q, 1, chunk)) + (z % 2) * hw
                if k == 0:
                    source = proj_ref.at[pl.ds(aligned((me ^ q) * hw, hw), hw), :]
                else:
                    source = ref.at[pl.ds((k - 1) * hw, hw), :]
                made.append((source, proj.at[pl.ds(aligned(row, hw), hw), :]))
        for copy in start_all(made, sems):
            copy.wait()

    second = second_ref[...]
    branch = branch_ref[...]
    total = None
    back = None
    span = 4 * hw
    for q in range(fc.shape[1] // span):
        here = pl.ds(q * span, span)
        pre = nn(second, fc[:, here]) + bias_ref[:, here]
        value, bend = gelu_both(pre)
        act = value.astype(BF)
        act_ref[:, here] = act
        slope_full = nt(branch, proj[here, :]) * bend
        slope = slope_full.astype(BF)
        slope_ref[:, here] = slope
        partial = jnp.sum(slope_full, axis=0, keepdims=True)

        @pl.when(step == 0)
        def _():
            colsum_ref[:, here] = partial

        @pl.when(step > 0)
        def _():
            colsum_ref[:, here] += partial

        more = nn(act, proj[here, :])
        total = more if total is None else total + more
        more = nt(slope, fc[:, here])
        back = more if back is None else back + more

    @pl.when(step < steps // 2)
    def _():
        out_oth[...] = total.astype(BF)
        back_oth[...] = back.astype(BF)

    @pl.when(step >= steps // 2)
    def _():
        out_own[...] = total
        back_own[...] = back


def feed(place, second, branch, bias, mine, other, shares, w_proj, proj_shares):
    both, width = second.shape
    hidden = mine.shape[1]
    hw = hidden // 16
    rows = 256
    steps = both // rows
    half = steps // 2
    raw = pl.BlockSpec(memory_space=pl.ANY)

    def tile(size):
        return pl.BlockSpec((rows, size), lambda i, place: (i, 0))

    line = pl.BlockSpec((1, hidden), lambda i, place: (0, 0))
    early = pl.BlockSpec((rows, width), lambda i, place: (jnp.minimum(i, half - 1), 0))
    late = pl.BlockSpec((rows, width), lambda i, place: (jnp.maximum(i - half, 0), 0))
    return pl.pallas_call(
        functools.partial(feed_kernel, hw),
        out_shape=(
            jax.ShapeDtypeStruct((both, hidden), BF),
            jax.ShapeDtypeStruct((both, hidden), BF),
            jax.ShapeDtypeStruct((both // 2, width), F32),
            jax.ShapeDtypeStruct((both // 2, width), BF),
            jax.ShapeDtypeStruct((both // 2, width), F32),
            jax.ShapeDtypeStruct((both // 2, width), BF),
            jax.ShapeDtypeStruct((1, hidden), F32),
        ),
        grid_spec=pltpu.PrefetchScalarGridSpec(
            num_scalar_prefetch=1,
            grid=(steps,),
            in_specs=[tile(width), tile(width), line] + [raw] * 11,
            out_specs=(tile(hidden), tile(hidden), late, early, late, early, line),
            scratch_shapes=[
                pltpu.VMEM((width, hidden), BF),
                pltpu.VMEM((hidden, width), BF),
                pltpu.SemaphoreType.DMA((42,)),
            ],
        ),
        name="feed",
    )(place, second, branch, bias, mine, other, *shares, w_proj, *proj_shares)


def mixed_back_kernel(
    place, own_ref, oth_ref, hidden_ref, branch_ref, gain_ref, mat_ref,
    full_ref, low_ref, g0, g1, g2, g3, sums_ref,
):
    step = pl.program_id(0)
    me = place[0]
    local = g0.shape[1]
    slope = own_ref[...] + oth_ref[...].astype(F32)
    unit, scale = norm_stats(hidden_ref[...])
    full = branch_ref[...].astype(F32) + norm_pull(unit, scale, slope * gain_ref[...])
    low = full.astype(BF)
    full_ref[...] = full
    low_ref[...] = low
    for k, ref in enumerate((g0, g1, g2, g3)):
        rows = pl.ds(aligned((me ^ k) * local, local), local)
        ref[...] = nt(low, mat_ref[rows, :]).astype(BF)
    sums = jnp.concatenate(
        [
            jnp.sum(low.astype(F32), axis=0, keepdims=True),
            jnp.sum(slope * unit, axis=0, keepdims=True),
            jnp.sum(slope, axis=0, keepdims=True),
            jnp.sum(branch_ref[...].astype(F32), axis=0, keepdims=True),
        ],
        axis=0,
    )

    @pl.when(step == 0)
    def _():
        sums_ref[...] = sums

    @pl.when(step > 0)
    def _():
        sums_ref[...] += sums


def mixed_back(place, own, oth, hidden, branch, gain, mat):
    block, width = own.shape
    local = width // 4
    rows = 256

    def tile(size):
        return pl.BlockSpec((rows, size), lambda i, place: (i, 0))

    def whole(height):
        return pl.BlockSpec((height, width), lambda i, place: (0, 0))

    return pl.pallas_call(
        mixed_back_kernel,
        out_shape=(
            jax.ShapeDtypeStruct((block, width), F32),
            jax.ShapeDtypeStruct((block, width), BF),
        )
        + (jax.ShapeDtypeStruct((block, local), BF),) * 4
        + (jax.ShapeDtypeStruct((4, width), F32),),
        grid_spec=pltpu.PrefetchScalarGridSpec(
            num_scalar_prefetch=1,
            grid=(block // rows,),
            in_specs=[tile(width)] * 4 + [whole(1), whole(width)],
            out_specs=(tile(width), tile(width)) + (tile(local),) * 4 + (whole(4),),
        ),
        name="mixed_back",
    )(place, own, oth, hidden, branch, gain, mat)


def first_back_kernel(tiles, place, grad_ref, unit_ref, mat_ref, *refs):
    step = pl.program_id(0)
    count = len(tiles)
    out_refs, sums_ref = refs[:count], refs[count]
    part = nt(grad_ref[...], mat_ref[...])
    low = part.astype(BF)
    for i in range(count):

        @pl.when(step == i)
        def _():
            out_refs[i][...] = low

    sums = jnp.concatenate(
        [
            jnp.sum(part * unit_ref[...].astype(F32), axis=0, keepdims=True),
            jnp.sum(part, axis=0, keepdims=True),
        ],
        axis=0,
    )

    @pl.when(step == 0)
    def _():
        sums_ref[...] = sums

    @pl.when(step > 0)
    def _():
        sums_ref[...] += sums


def first_back(tiles, groups, grad, unit, mat):
    total, outs = grad.shape
    width = mat.shape[0]
    rows = 256
    table = jnp.asarray(tiles, jnp.int32)
    del groups

    def at(i, place):
        return (place[i], 0)

    return pl.pallas_call(
        functools.partial(first_back_kernel, tiles),
        out_shape=tuple(jax.ShapeDtypeStruct((rows, width), BF) for _ in tiles)
        + (jax.ShapeDtypeStruct((2, width), F32),),
        grid_spec=pltpu.PrefetchScalarGridSpec(
            num_scalar_prefetch=1,
            grid=(len(tiles),),
            in_specs=[
                pl.BlockSpec((rows, outs), at),
                pl.BlockSpec((rows, width), at),
                pl.BlockSpec((width, outs), lambda i, place: (0, 0)),
            ],
            out_specs=tuple(pl.BlockSpec((rows, width), lambda i, place: (0, 0)) for _ in tiles)
            + (pl.BlockSpec((2, width), lambda i, place: (0, 0)),),
        ),
        name="first_back",
    )(table, grad, unit, mat)


def gather_sum_kernel(place, *refs):
    floor = place[1]
    fa, xa, la, fb, yb, lb, pa, xp, lpa, pb, yp, lpb, o0, o1, o2, o3, fc, proj = refs
    chunk = fc.shape[1] // 2
    hw = chunk // 2
    fc[:, :chunk] = fa[...].astype(F32) + xa[...].astype(F32) + la[...].astype(F32)
    fc[:, chunk:] = fb[...].astype(F32) + yb[...].astype(F32) + lb[...].astype(F32)
    proj[:chunk, :] = pa[...].astype(F32) + xp[...].astype(F32) + lpa[...].astype(F32)
    proj[chunk:, :] = pb[...].astype(F32) + yp[...].astype(F32) + lpb[...].astype(F32)
    rows = fc.shape[0] // 4
    for k, out in enumerate((o0, o1, o2, o3)):
        out[:rows, :] = fc[pl.ds(aligned((floor ^ k) * rows, rows), rows), :].astype(BF)
        piece = proj[pl.ds(aligned((floor ^ k) * hw, hw), hw), :].astype(BF)
        out[rows : rows + hw, :] = piece[:, : 2 * chunk]
        out[rows + hw :, :] = piece[:, 2 * chunk :]


def gather_sum(place, fc_parts, proj_parts):
    width = fc_parts[0].shape[0]
    chunk = width // 4
    fc_spec = pl.BlockSpec((width, chunk), lambda i, place: (0, 0))
    proj_spec = pl.BlockSpec((chunk, width), lambda i, place: (0, 0))
    out = jax.ShapeDtypeStruct((width // 2, 2 * chunk), BF)
    return pl.pallas_call(
        gather_sum_kernel,
        out_shape=(out,) * 4,
        grid_spec=pltpu.PrefetchScalarGridSpec(
            num_scalar_prefetch=1,
            grid=(1,),
            in_specs=[fc_spec] * 6 + [proj_spec] * 6,
            out_specs=(pl.BlockSpec(out.shape, lambda i, place: (0, 0)),) * 4,
            scratch_shapes=[pltpu.VMEM((width, 2 * chunk), F32), pltpu.VMEM((2 * chunk, width), F32)],
        ),
        name="gather_sum",
    )(place, *fc_parts, *proj_parts)


def floor_sum_kernel(place, r0, r1, r2, r3, kept_ref, sent_ref, total):
    core = place[2]
    total[...] = (
        r0[...].astype(F32) + r1[...].astype(F32) + r2[...].astype(F32) + r3[...].astype(F32)
    )
    own = sent_ref.shape[0]
    sent_ref[...] = total[pl.ds(aligned((1 - core) * own, own), own), :].astype(BF)
    kept_ref[:own, :] = total[pl.ds(aligned(core * own, own), own), :].astype(BF)
    kept_ref[own:, :] = total[2 * own :, :].astype(BF)


def floor_sum(place, parts):
    rows, cols = parts[0].shape
    own = rows // 4

    def whole(height):
        return pl.BlockSpec((height, cols), lambda i, place: (0, 0))

    return pl.pallas_call(
        floor_sum_kernel,
        out_shape=(
            jax.ShapeDtypeStruct((3 * own, cols), BF),
            jax.ShapeDtypeStruct((own, cols), BF),
        ),
        grid_spec=pltpu.PrefetchScalarGridSpec(
            num_scalar_prefetch=1,
            grid=(1,),
            in_specs=[whole(rows)] * 4,
            out_specs=(whole(3 * own), whole(own)),
            scratch_shapes=[pltpu.VMEM((rows, cols), F32)],
        ),
        name="floor_sum",
    )(place, *parts)


def spread_kernel(place, *refs):
    me, core = place[0], place[2]
    kept, moved, (fc_ref, proj_ref) = refs[:4], refs[4:8], refs[8:]
    own = moved[0].shape[0]
    hw = moved[0].shape[1] // 4
    for q in range(4):
        for ref, which in ((kept[q], core), (moved[q], 1 - core)):
            for z in range(4):
                lanes = pl.ds(aligned(z * 8 * hw + which * 4 * hw + (me ^ q) * hw, hw), hw)
                fc_ref[:, lanes] = ref[:own, z * hw : (z + 1) * hw].astype(F32)
        rows = pl.ds(aligned((me ^ q) * hw, hw), hw)
        proj_ref[rows, : 4 * hw] = kept[q][own : own + hw, :].astype(F32)
        proj_ref[rows, 4 * hw :] = kept[q][own + hw :, :].astype(F32)


def spread(place, kept, moved):
    own, cols = moved[0].shape
    hw = cols // 4

    def whole(shape):
        return pl.BlockSpec(shape, lambda i, place: (0, 0))

    fc_shape, proj_shape = (own, 32 * hw), (4 * hw, 8 * hw)
    return pl.pallas_call(
        spread_kernel,
        out_shape=(jax.ShapeDtypeStruct(fc_shape, F32), jax.ShapeDtypeStruct(proj_shape, F32)),
        grid_spec=pltpu.PrefetchScalarGridSpec(
            num_scalar_prefetch=1,
            grid=(1,),
            in_specs=[whole(kept[0].shape)] * 4 + [whole(moved[0].shape)] * 4,
            out_specs=(whole(fc_shape), whole(proj_shape)),
        ),
        name="spread",
    )(place, *kept, *moved)


def last_kernel(keep_ref, got_ref, last_ref, token_ref, hidden_ref, gain_ref, out_ref):
    slope = keep_ref[...].astype(F32) + got_ref[...].astype(F32) + last_ref[...].astype(F32)
    unit, scale = norm_stats(token_ref[...].astype(F32))
    out_ref[...] = hidden_ref[...] + norm_pull(unit, scale, slope * gain_ref[...])


def body_aligned(
    tokens,
    prompt_lens,
    cont_lens,
    gain_one,
    shift_one,
    w_qkv,
    bias_qv,
    w_out,
    bias_out,
    gain_two,
    shift_two,
    w_fc,
    bias_fc,
    w_proj,
    bias_proj,
    cotangent,
):
    ns = nz = 4
    nf = 8
    me = lax.axis_index("seq")
    owner = lax.axis_index("fsdp")
    floor = owner // 2
    core = owner % 2
    place = jnp.stack([me, floor, core]).astype(jnp.int32)
    toks, width = tokens.shape[1:]
    own = width // nf
    heads = H // ns
    local = width // ns
    hw = w_fc.shape[1] // (nf * ns)
    token_block = tokens[0]
    branch = cotangent[0]

    half = toks // 2
    tok_one = swap(token_block, "seq", 1)
    tok_two = swap(token_block, "seq", 2)
    tok_up = swap(tok_two[:half], "seq", 1)
    tok_low = swap(tok_one[half:], "seq", 2)

    vectors = [gain_one, shift_one, bias_qv, bias_out, gain_two, shift_two, bias_fc, bias_proj]
    packed = jnp.concatenate([v.reshape(-1, own) for v in vectors], axis=0)
    lines = packed.shape[0]
    packed = jnp.pad(packed.reshape(-1), (0, 16 * 3 * local - packed.size)).reshape(16, 3 * local)
    mine_qkv = pick(w_qkv.reshape(own, 3, ns, local), me, 2).reshape(own, 3 * local)
    sent_qkv = jnp.concatenate([mine_qkv, packed], axis=0)
    kept_qkv = jnp.stack([sent_qkv] + [swap(sent_qkv, "fsdp", 2 * k) for k in range(1, nz)])
    moved_qkv = swap(kept_qkv, "fsdp", 1)

    fc_mine, fc_sent, proj_share = pack(place, w_fc, w_proj)
    fc_other = swap(fc_sent, "fsdp", 1)
    fc_share = join(place, fc_mine, fc_other)
    fc_zero = jnp.concatenate([swap(fc_share, "fsdp", 2 * k) for k in range(1, nz)], axis=0)
    proj_zero = jnp.concatenate([swap(proj_share, "fsdp", 2 * k) for k in range(1, nz)], axis=0)
    kept_out = jnp.stack([w_out] + [swap(w_out, "fsdp", 2 * k) for k in range(1, nz)])
    moved_out = swap(kept_out, "fsdp", 1)
    fc_one = swap(fc_zero, "seq", 1)
    fc_two = swap(fc_zero, "seq", 2)
    fc_three = swap(fc_two, "seq", 1)
    proj_one = swap(proj_zero, "seq", 1)
    proj_two = swap(proj_zero, "seq", 2)
    proj_three = swap(proj_one, "seq", 2)
    branch_both = jnp.concatenate([swap(branch, "fsdp", 1), branch], axis=0)

    small = by_core(core, kept_qkv[:, own : own + 2], moved_qkv[:, own : own + 2], 1)
    small = xor_take(small, floor, 0).reshape(nf, -1).reshape(nf, lines, own)
    at = 0
    full = []
    for v in vectors:
        count = v.shape[0] // own
        full.append(small[:, at : at + count].reshape(1, -1).astype(F32))
        at += count
    gain_a, shift_a, qv_vec, out_vec, gain_b, shift_b, fc_vec, proj_vec = full
    qv_mine = pick(qv_vec.reshape(2, ns, local), me, 1)
    bias_all = jnp.concatenate([qv_mine[0], jnp.zeros((local,), F32), qv_mine[1]]).reshape(1, -1)
    fc_bias = xor_take(pick(fc_vec.reshape(nz, 2, ns, hw), core, 1), me, 1)
    order = [(q, 0) for q in (0, 2, 1, 3)] + [(q, 1) for q in range(4)]
    fc_bias = jnp.concatenate(
        [fc_bias[2 * part : 2 * part + 2, q].reshape(1, -1) for q, part in order], axis=1
    )

    first, unit_all, qkv = project(
        place, (token_block, tok_one, tok_two, tok_up, tok_low), kept_qkv, moved_qkv, gain_a, shift_a,
        bias_all,
    )
    lens = jnp.concatenate([prompt_lens, cont_lens[0], me.reshape(1)]).astype(jnp.int32)
    mixed_heads, log_norm = attend_forward(lens, qkv, heads)
    mixed_blocks = [mixed_heads] + [
        swap(mixed_heads[k * toks : (k + 1) * toks], "seq", k) for k in range(1, ns)
    ]
    hidden, second, mixed, out_mat = attn_out(
        place, mixed_blocks, kept_out, moved_out, token_block, out_vec, gain_b, shift_b
    )

    second_both = jnp.concatenate([swap(second, "fsdp", 1), second], axis=0)
    act, grad_pre, out_own, out_oth, back_own, back_oth, fc_bias_sum = feed(
        place, second_both, branch_both, fc_bias, fc_mine, fc_other,
        (fc_zero, fc_one, fc_two, fc_three), w_proj, (proj_zero, proj_one, proj_two, proj_three),
    )
    back_got = swap(back_oth, "fsdp", 1)
    out_got = swap(out_oth, "fsdp", 1)
    output = (hidden + out_own + proj_vec + out_got.astype(F32)).astype(BF)[None]
    grad_hidden, grad_attn, *grad_blocks, sums_two = mixed_back(
        place, back_own, back_got, hidden, branch, gain_b, out_mat
    )
    grad_heads = jnp.concatenate(
        [grad_blocks[0]] + [swap(grad_blocks[k], "seq", k) for k in range(1, ns)], axis=0
    )

    edge = 4 * hw
    fc_grads = [tn(second_both, grad_pre[:, i * edge : (i + 1) * edge]).astype(BF) for i in range(4)]
    proj_grads = [tn(act[:, i * edge : (i + 1) * edge], branch_both).astype(BF) for i in range(4)]
    chunk = 2 * hw
    fc_x = swap(fc_grads[1], "seq", 1)
    fc_y = swap(fc_grads[3], "seq", 2)
    proj_x = swap(proj_grads[1], "seq", 1)
    proj_y = swap(proj_grads[3], "seq", 2)

    def added(left, right):
        return (left.astype(F32) + right.astype(F32)).astype(BF)

    fc_last_y = swap(added(fc_grads[0][:, chunk:], fc_x[:, chunk:]), "seq", 2)
    fc_last_x = swap(added(fc_grads[2][:, chunk:], fc_y[:, chunk:]), "seq", 1)
    proj_last_y = swap(added(proj_grads[0][chunk:], proj_x[chunk:]), "seq", 2)
    proj_last_x = swap(added(proj_grads[2][chunk:], proj_y[chunk:]), "seq", 1)
    cuts = gather_sum(
        place,
        (fc_grads[0], fc_x, fc_last_y, fc_grads[2], fc_y, fc_last_x),
        (proj_grads[0], proj_x, proj_last_y, proj_grads[2], proj_y, proj_last_x),
    )
    kept, moved = floor_sum(
        place, [cuts[0]] + [swap(cuts[k], "fsdp", 2 * k) for k in range(1, nz)]
    )
    moved = swap(moved, "fsdp", 1)
    grad_w_fc, grad_w_proj = spread(
        place,
        [kept] + [swap(kept, "seq", k) for k in range(1, ns)],
        [moved] + [swap(moved, "seq", k) for k in range(1, ns)],
    )

    grad_q, grad_k, grad_v = attend_backward(lens, qkv, mixed_heads, grad_heads, log_norm, heads)
    grad_qkv = jnp.concatenate([grad_q, grad_k, grad_v], axis=1)
    qkv_mat = by_core(core, kept_qkv[:, :own], moved_qkv[:, :own], 1)
    qkv_mat = xor_take(qkv_mat, floor, 0).reshape(width, 3 * local)
    up1, up3, low2, low3, sums_early = first_back((2, 6, 5, 7), None, grad_qkv, unit_all, qkv_mat)
    got_x1, got_x3 = swap(up1, "seq", 1), swap(up3, "seq", 1)
    got_y2, got_y3 = swap(low2, "seq", 2), swap(low3, "seq", 2)
    up2, low1, up0, low0, sums_late = first_back((4, 3, 0, 1), None, grad_qkv, unit_all, qkv_mat)
    last_y = swap(added(up2, got_x3), "seq", 2)
    last_x = swap(added(low1, got_y3), "seq", 1)
    tile = pl.BlockSpec((half, width), lambda: (0, 0))

    def last(keep, got, end, rows):
        return pl.pallas_call(
            last_kernel,
            out_shape=jax.ShapeDtypeStruct((half, width), F32),
            in_specs=[tile] * 5 + [pl.BlockSpec((1, width), lambda: (0, 0))],
            out_specs=tile,
            name="last",
        )(keep, got, end, token_block[rows], grad_hidden[rows], gain_a)

    input_grad = jnp.concatenate(
        [
            last(up0, got_x1, last_y, slice(0, half)),
            last(low0, got_y2, last_x, slice(half, toks)),
        ],
        axis=0,
    )[None]

    def over_floors(grad):
        cut = grad.reshape(nz, 2, own, -1)
        total = pick(cut, core, 1).astype(F32) + swap(pick(cut, 1 - core, 1), "fsdp", 1).astype(F32)
        owned = pick(total, floor, 0)
        for k in range(1, nz):
            owned = owned + swap(pick(total, floor ^ k, 0).astype(BF), "fsdp", 2 * k).astype(F32)
        return owned

    grad_w_out = over_floors(tn(mixed, grad_attn).astype(BF))
    for bit in (1, 2):
        grad_w_out = grad_w_out + swap(grad_w_out.astype(BF), "seq", bit).astype(F32)

    in_owned = over_floors(tn(first, grad_qkv).astype(BF)).astype(BF)
    in_blocks = jnp.stack(
        [in_owned.reshape(own, 3, local)]
        + [swap(in_owned, "seq", k).reshape(own, 3, local) for k in range(1, ns)],
        axis=2,
    )
    grad_w_qkv = xor_take(in_blocks, me, 2).reshape(own, 3 * width).astype(F32)

    def placed(values):
        slots = jnp.arange(ns)[:, None] == me
        return jnp.where(slots, values[None, :], 0.0).reshape(-1)

    spots = {}
    for i, (q, part) in enumerate(order):
        spots[q, part] = fc_bias_sum[0, i * chunk : (i + 1) * chunk].reshape(2, hw)
    fc_bias_grad = jnp.stack(
        [jnp.concatenate([spots[q, 0], spots[q, 1]], axis=0) for q in range(ns)], axis=1
    )
    fc_bias_grad = xor_take(fc_bias_grad, me, 1)
    fc_bias_grad = jnp.where(
        (jnp.arange(2) == core)[None, :, None, None], fc_bias_grad[:, None], 0.0
    ).reshape(-1)
    sums_one = sums_early + sums_late
    vector_grads = [
        sums_one[0],
        sums_one[1],
        placed(jnp.sum(grad_q.astype(F32), axis=0)),
        placed(jnp.sum(grad_v.astype(F32), axis=0)),
        sums_two[0],
        sums_two[1],
        sums_two[2],
        fc_bias_grad,
        sums_two[3],
    ]
    vector_sum = jnp.concatenate([v.reshape(-1, width) for v in vector_grads], axis=0)
    for axis, size in (("seq", ns), ("fsdp", nf)):
        bit = 1
        while bit < size:
            vector_sum = vector_sum + swap(vector_sum, axis, bit)
            bit *= 2
    vector_sum = vector_sum.reshape(-1)
    outs = []
    at = 0
    for v in vectors:
        count = v.shape[0]
        outs.append(lax.dynamic_slice_in_dim(vector_sum, at + owner * count, count))
        at += nf * count
    (g_gain_one, g_shift_one, g_bias_qv, g_bias_out, g_gain_two, g_shift_two, g_bias_fc, g_bias_proj) = outs

    return (
        output,
        input_grad,
        g_gain_one,
        g_shift_one,
        grad_w_qkv,
        g_bias_qv,
        grad_w_out,
        g_bias_out,
        g_gain_two,
        g_shift_two,
        grad_w_fc,
        g_bias_fc,
        grad_w_proj,
        g_bias_proj,
    )


def body(*args):
    tokens, w_proj = args[0], args[13]
    fits = (
        lax.axis_size("seq") == 4
        and lax.axis_size("fsdp") == 8
        and tokens.shape[1:] == (512, 1024)
        and w_proj.shape == (512, 1024)
    )
    return body_aligned(*args) if fits else body_general(*args)


def solution(mesh):
    rows = P("fsdp", None)
    vec = P("fsdp")
    acts = P("fsdp", "seq", None)
    return jax.shard_map(
        body,
        mesh=mesh,
        in_specs=(
            acts, vec, rows, vec, vec, rows, vec, rows, vec, vec, vec, rows, vec, rows, vec, acts,
        ),
        out_specs=(
            acts, acts, vec, vec, rows, vec, rows, vec, vec, vec, rows, vec, rows, vec,
        ),
        check_vma=False,
    )
```

```python
import functools

import jax
import jax.numpy as jnp
from jax import lax
from jax.experimental import pallas as pl
from jax.experimental.pallas import tpu as pltpu
from jax.sharding import PartitionSpec as P

H = 16
HD = 64
PROMPT = 1024
CONTLEN = 512
CONTS = 2

EPS = 1e-05
GELU_C = 0.7978845608028654
GELU_A = 0.044715
NEG = -1e30
BF = jnp.bfloat16
F32 = jnp.float32


def swap(values, axis, bits):
    size = lax.axis_size(axis)
    return lax.ppermute(values, axis, [(i, i ^ bits) for i in range(size)])


def xor_take(values, index, axis):
    size = values.shape[axis]
    bit = 1
    while bit < size:
        parts = [lax.slice_in_dim(values, i, i + 1, axis=axis) for i in range(size)]
        flipped = jnp.concatenate([parts[i ^ bit] for i in range(size)], axis=axis)
        values = jnp.where((index & bit) != 0, flipped, values)
        bit *= 2
    return values


def xor_blocks(values, index, count, axis):
    width = values.shape[axis] // count
    return jnp.concatenate(
        [
            lax.dynamic_slice_in_dim(values, (i ^ index) * width, width, axis=axis)
            for i in range(count)
        ],
        axis=axis,
    )


def plane_gather(values):
    size = lax.axis_size("seq")
    if size != 4:
        return [values] + [swap(values, "seq", k) for k in range(1, size)]
    half = values.shape[0] // 2
    one = swap(values, "seq", 1)
    two = swap(values, "seq", 2)
    three = jnp.concatenate(
        [swap(two[:half], "seq", 1), swap(one[half:], "seq", 2)], axis=0
    )
    return [values, one, two, three]


def plane_scatter(blocks):
    size = lax.axis_size("seq")
    if size != 4:
        total = blocks[0].astype(F32)
        for k in range(1, size):
            total = total + swap(blocks[k].astype(BF), "seq", k).astype(F32)
        return total
    half = blocks[0].shape[0] // 2
    sent_x = jnp.concatenate([blocks[1][:half], blocks[3][:half]], axis=0).astype(BF)
    sent_y = jnp.concatenate([blocks[2][half:], blocks[3][half:]], axis=0).astype(BF)
    got_x = swap(sent_x, "seq", 1).astype(F32)
    got_y = swap(sent_y, "seq", 2).astype(F32)
    next_y = (blocks[2][:half].astype(F32) + got_x[half:]).astype(BF)
    next_x = (blocks[1][half:].astype(F32) + got_y[half:]).astype(BF)
    last_y = swap(next_y, "seq", 2).astype(F32)
    last_x = swap(next_x, "seq", 1).astype(F32)
    upper = blocks[0][:half].astype(F32) + got_x[:half] + last_y
    lower = blocks[0][half:].astype(F32) + got_y[:half] + last_x
    return jnp.concatenate([upper, lower], axis=0)


def after(values, *needed):
    return lax.optimization_barrier((values, needed))[0]


def cost(micros, size=0):
    return pl.CostEstimate(flops=int(micros * 1.15e6), bytes_accessed=int(size), transcendentals=0)


def tile_rows(total, blocks):
    return min(256, total // blocks)


def rel_row(tile, rows, block_rows, me):
    per = block_rows // rows
    return pl.multiple_of(((tile // per) ^ me) * block_rows + (tile % per) * rows, rows)


def walk(tile, rows):
    prompt_tiles = PROMPT // rows
    cont_tiles = CONTLEN // rows
    in_prompt = tile < prompt_tiles
    inside = lax.rem(jnp.maximum(tile - prompt_tiles, 0), cont_tiles)
    count = jnp.where(in_prompt, tile, prompt_tiles + inside)
    return count, tile - inside - prompt_tiles


def key_limit(lens, tile, rows):
    prompt_tiles = PROMPT // rows
    cont_tiles = CONTLEN // rows
    past = jnp.maximum(tile - prompt_tiles, 0)
    cont = jnp.minimum(past // cont_tiles, CONTS - 1)
    length = lens[1]
    for i in range(1, CONTS):
        length = jnp.where(cont == i, lens[1 + i], length)
    return jnp.where(
        tile < prompt_tiles, lens[0] - tile * rows, length - lax.rem(past, cont_tiles) * rows
    )


def pair_stack(block, per_pair, scale=None):
    if scale is not None:
        block = block * scale
    if per_pair == 1:
        return block
    lane = lax.broadcasted_iota(jnp.int32, block.shape, 1) // HD
    return jnp.concatenate(
        [jnp.where(lane == h, block, jnp.zeros_like(block)) for h in range(per_pair)], axis=0
    )


def diagonal_mask(rows, per_pair, limit):
    key = lax.broadcasted_iota(jnp.int32, (rows, per_pair * rows), 0)
    query = lax.broadcasted_iota(jnp.int32, (rows, per_pair * rows), 1) % rows
    return ((key <= query) & (key < limit)) | (key == query)


def live_mask(rows, per_pair, limit):
    return lax.broadcasted_iota(jnp.int32, (rows, per_pair * rows), 0) < limit


def nt(left, right):
    return lax.dot_general(left, right, (((1,), (1,)), ((), ())), preferred_element_type=F32)


def nn(left, right):
    return lax.dot_general(left, right, (((1,), (0,)), ((), ())), preferred_element_type=F32)


def unstack(values, per_pair, rows):
    if per_pair == 1:
        return values
    return jnp.concatenate(
        [values[h * HD : (h + 1) * HD, h * rows : (h + 1) * rows] for h in range(per_pair)], axis=0
    )


def forward_kernel(
    rows, block_rows, per_pair, lens, q_ref, k_ref, v_ref, out_ref, norm_ref, vt_ref, parts, total
):
    tile = pl.program_id(0)
    me = lens[1 + CONTS]
    tiles = q_ref.shape[0] // rows
    across = per_pair * rows

    @pl.when(tile == 0)
    def _():
        def turn(i, carry):
            at = rel_row(i, rows, block_rows, me)
            vt_ref[i] = v_ref[pl.ds(at, rows), :].T
            return carry

        lax.fori_loop(0, tiles, turn, 0)

    at = rel_row(tile, rows, block_rows, me)
    query = pair_stack(q_ref[pl.ds(at, rows), :], per_pair, jnp.asarray(0.125, BF)).T
    count, shift = walk(tile, rows)

    def folded(values):
        return values.reshape(rows // 8, 8, across)

    def scores(i):
        return nn(k_ref[pl.ds(rel_row(i, rows, block_rows, me), rows), :], query)

    def key_tile(i):
        return jnp.where(i < PROMPT // rows, i, i + shift)

    first = jnp.where(
        diagonal_mask(rows, per_pair, key_limit(lens, tile, rows)), scores(tile), NEG
    )

    def measure(i, top):
        here = key_tile(i)
        part = jnp.where(
            live_mask(rows, per_pair, key_limit(lens, here, rows)), scores(here), NEG
        )
        parts[i] = part
        return jnp.maximum(top, jnp.max(folded(part), axis=0))

    top = lax.fori_loop(0, count, measure, jnp.max(folded(first), axis=0))
    top = jnp.max(top, axis=0, keepdims=True)
    weights = jnp.exp(first - top)
    total[...] = nn(vt_ref[tile], weights.astype(BF))

    def gather(i, denom):
        weights = jnp.exp(parts[i] - top)
        total[...] += nn(vt_ref[key_tile(i)], weights.astype(BF))
        return denom + jnp.sum(folded(weights), axis=0)

    denom = lax.fori_loop(0, count, gather, jnp.sum(folded(weights), axis=0))
    denom = jnp.sum(denom, axis=0, keepdims=True)
    mixed = unstack(total[...] / denom, per_pair, rows)
    out_ref[...] = mixed.T.astype(BF)
    norm_ref[0] = top + jnp.log(denom)


def backward_kernel(
    rows, block_rows, per_pair, lens, q_ref, k_ref, v_ref, out_ref, grad_ref, norm_ref,
    dq_ref, dk_ref, dv_ref, kt_ref, dk_sum, dv_sum, dq_sum,
):
    tile = pl.program_id(0)
    me = lens[1 + CONTS]
    tiles = q_ref.shape[0] // rows

    @pl.when(tile == 0)
    def _():
        def turn(i, carry):
            at = rel_row(i, rows, block_rows, me)
            kt_ref[i] = k_ref[pl.ds(at, rows), :].T
            return carry

        lax.fori_loop(0, tiles, turn, 0)
        dk_sum[...] = jnp.zeros_like(dk_sum)
        dv_sum[...] = jnp.zeros_like(dv_sum)

    at = rel_row(tile, rows, block_rows, me)
    query = pair_stack(q_ref[pl.ds(at, rows), :], per_pair, jnp.asarray(0.125, BF))
    grad_block = grad_ref[pl.ds(at, rows), :]
    grad = pair_stack(grad_block, per_pair)
    query_turned = query.T
    grad_turned = grad.T
    product = (grad_block.astype(F32) * out_ref[pl.ds(at, rows), :].astype(F32)).T
    inner = jnp.concatenate(
        [
            jnp.sum(product[h * HD : (h + 1) * HD], axis=0, keepdims=True)
            for h in range(per_pair)
        ],
        axis=1,
    )
    norm = norm_ref[0]

    def one(key_tile, mask):
        key_at = rel_row(key_tile, rows, block_rows, me)
        keys = pl.ds(key_at, rows)
        part = jnp.where(mask, nn(k_ref[keys, :], query_turned), NEG)
        probs = jnp.exp(part - norm)
        slope = probs * (nn(v_ref[keys, :], grad_turned) - inner)
        slope_low = slope.astype(BF)
        dv_sum[keys, :] += nn(probs.astype(BF), grad)
        dk_sum[keys, :] += nn(slope_low, query)
        return nn(kt_ref[key_tile], slope_low)

    dq_sum[...] = one(tile, diagonal_mask(rows, per_pair, key_limit(lens, tile, rows)))
    count, shift = walk(tile, rows)

    def step(i, carry):
        key_tile = jnp.where(i < PROMPT // rows, i, i + shift)
        dq_sum[...] += one(key_tile, live_mask(rows, per_pair, key_limit(lens, key_tile, rows)))
        return carry

    lax.fori_loop(0, count, step, 0)
    dq_ref[...] = (unstack(dq_sum[...], per_pair, rows).T * 0.125).astype(BF)

    @pl.when(tile == tiles - 1)
    def _():
        dk_ref[...] = dk_sum[...].astype(BF)
        dv_ref[...] = dv_sum[...].astype(BF)


def attention_plan(total, heads):
    blocks = lax.axis_size("seq")
    rows = tile_rows(total, blocks)
    per_pair = 2 if heads % 2 == 0 else 1
    return rows, total // blocks, per_pair, heads // per_pair, per_pair * HD


def thirds(qkv, width, pair_width):
    per = width // pair_width
    if pair_width % 128 == 0:
        return (qkv, qkv, qkv), (0, per, 2 * per)
    return tuple(qkv[:, i * width : (i + 1) * width] for i in range(3)), (0, 0, 0)


def row_block(rows, block_rows):
    per = block_rows // rows

    def index(tile, lens):
        return ((tile // per) ^ lens[1 + CONTS]) * per + tile % per, 0

    return index


def attend_forward(lens, qkv, heads, between=None):
    total = qkv.shape[0]
    width = heads * HD
    rows, block_rows, per_pair, pairs, pair_width = attention_plan(total, heads)
    arrays, firsts = thirds(qkv, width, pair_width)
    tiles = total // rows
    most = (PROMPT + CONTLEN) // rows
    mixed = None
    norms = []
    for pair in range(pairs):

        def whole(first):
            return pl.BlockSpec((total, pair_width), lambda tile, lens: (0, first + pair))

        def kernel(lens, q_ref, k_ref, v_ref, *refs):
            forward_kernel(
                rows, block_rows, per_pair, lens, q_ref, k_ref, v_ref, *refs[mixed is not None :]
            )

        place_row = row_block(rows, block_rows)
        more = [] if mixed is None else [mixed]
        mixed, norm = pl.pallas_call(
            kernel,
            out_shape=(
                jax.ShapeDtypeStruct((total, width), BF),
                jax.ShapeDtypeStruct((tiles, 1, per_pair * rows), F32),
            ),
            grid_spec=pltpu.PrefetchScalarGridSpec(
                num_scalar_prefetch=1,
                grid=(tiles,),
                in_specs=[whole(first) for first in firsts]
                + [pl.BlockSpec(memory_space=pl.ANY)] * len(more),
                out_specs=(
                    pl.BlockSpec(
                        (rows, pair_width), lambda tile, lens: (place_row(tile, lens)[0], pair)
                    ),
                    pl.BlockSpec((1, 1, per_pair * rows), lambda tile, lens: (tile, 0, 0)),
                ),
                scratch_shapes=[
                    pltpu.VMEM((tiles, pair_width, rows), BF),
                    pltpu.VMEM((most, rows, per_pair * rows), F32),
                    pltpu.VMEM((pair_width, per_pair * rows), F32),
                ],
            ),
            input_output_aliases={4: 0} if more else {},
            cost_estimate=cost(15),
            name="attend_forward",
        )(lens, *arrays, *more)
        norms.append(norm)
        if between is not None and pair + 1 < pairs:
            lens, mixed, arrays = between(lens, mixed, arrays)
    return mixed, norms


def attend_backward(lens, qkv, mixed, norms, grad, heads, between=None):
    total = qkv.shape[0]
    width = heads * HD
    rows, block_rows, per_pair, pairs, pair_width = attention_plan(total, heads)
    arrays, firsts = thirds(qkv, width, pair_width)
    tiles = total // rows
    made = []
    for pair in range(pairs):

        def whole(first):
            return pl.BlockSpec((total, pair_width), lambda tile, lens: (0, first))

        made.append(
            pl.pallas_call(
                functools.partial(backward_kernel, rows, block_rows, per_pair),
                out_shape=(jax.ShapeDtypeStruct((total, pair_width), BF),) * 3,
                grid_spec=pltpu.PrefetchScalarGridSpec(
                    num_scalar_prefetch=1,
                    grid=(tiles,),
                    in_specs=[whole(first + pair) for first in firsts]
                    + [
                        whole(pair),
                        whole(pair),
                        pl.BlockSpec((1, 1, per_pair * rows), lambda tile, lens: (tile, 0, 0)),
                    ],
                    out_specs=(
                        pl.BlockSpec((rows, pair_width), row_block(rows, block_rows)),
                        whole(0),
                        whole(0),
                    ),
                    scratch_shapes=[
                        pltpu.VMEM((tiles, pair_width, rows), BF),
                        pltpu.VMEM((total, pair_width), F32),
                        pltpu.VMEM((total, pair_width), F32),
                        pltpu.VMEM((pair_width, per_pair * rows), F32),
                    ],
                ),
                cost_estimate=cost(18),
                name="attend_backward",
            )(lens, *arrays, mixed, grad, norms[pair])
        )
        if between is not None and pair + 1 < pairs:
            lens, made[-1], grad = between(lens, made[-1], grad)
    return made


def norm_stats(values):
    center = values - jnp.mean(values, axis=-1, keepdims=True)
    spread = jnp.mean(center * center, axis=-1, keepdims=True)
    scale = lax.rsqrt(spread + EPS)
    return center * scale, scale


def norm_pull(unit, scale, slope):
    return scale * (
        slope
        - jnp.mean(slope, axis=-1, keepdims=True)
        - unit * jnp.mean(slope * unit, axis=-1, keepdims=True)
    )


def gelu_both(values):
    square = values * values
    bent = jnp.tanh(GELU_C * (values + GELU_A * square * values))
    value = 0.5 * values * (1.0 + bent)
    slope = 0.5 * (1.0 + bent) + 0.5 * values * (1.0 - bent * bent) * GELU_C * (
        1.0 + 3.0 * GELU_A * square
    )
    return value, slope


def tn(left, right):
    return lax.dot_general(left, right, (((0,), (0,)), ((), ())), preferred_element_type=F32)


def pick(values, index, axis):
    return lax.dynamic_index_in_dim(values, index, axis, keepdims=False)


def by_core(core, mine, other, axis):
    return jnp.where(
        core == 0, jnp.stack([mine, other], axis=axis), jnp.stack([other, mine], axis=axis)
    )


def body_general(
    tokens,
    prompt_lens,
    cont_lens,
    gain_one,
    shift_one,
    w_qkv,
    bias_qv,
    w_out,
    bias_out,
    gain_two,
    shift_two,
    w_fc,
    bias_fc,
    w_proj,
    bias_proj,
    cotangent,
):
    ns = lax.axis_size("seq")
    nf = lax.axis_size("fsdp")
    nz = nf // 2
    me = lax.axis_index("seq")
    owner = lax.axis_index("fsdp")
    floor = owner // 2
    core = owner % 2
    toks, width = tokens.shape[1:]
    hidden_all = w_fc.shape[1]
    own = width // nf
    heads = H // ns
    local = width // ns
    hw = hidden_all // (nf * ns)
    cols = nz * hw

    token_block = tokens[0]
    branch = cotangent[0]

    token_blocks = plane_gather(token_block)
    vectors = [gain_one, shift_one, bias_qv, bias_out, gain_two, shift_two, bias_fc, bias_proj]
    packed = jnp.concatenate([v.reshape(-1, own) for v in vectors], axis=0)
    lines = packed.shape[0]
    packed_rows = -(-packed.size // (3 * local))
    packed = jnp.pad(packed.reshape(-1), (0, 16 * (-(-packed_rows // 16)) * 3 * local - packed.size))
    mine_qkv = pick(w_qkv.reshape(own, 3, ns, local), me, 2).reshape(own, 3 * local)
    sent_qkv = jnp.concatenate([mine_qkv, packed.reshape(-1, 3 * local)], axis=0)
    got_qkv = jnp.stack([sent_qkv] + [swap(sent_qkv, "fsdp", 2 * k) for k in range(1, nz)])
    got_qkv = xor_take(by_core(core, got_qkv, swap(got_qkv, "fsdp", 1), 1), floor, 0)
    qkv_mat = got_qkv[:, :, :own].reshape(width, 3 * local)
    small = got_qkv[:, :, own:].reshape(nf, -1)[:, : lines * own].reshape(nf, lines, own)
    at = 0
    full = []
    for v in vectors:
        count = v.shape[0] // own
        full.append(small[:, at : at + count].reshape(-1).astype(F32))
        at += count
    gain_a, shift_a, qv_vec, out_vec, gain_b, shift_b, fc_vec, proj_vec = full

    fc_cut = w_fc.reshape(own, nz, 2, ns, hw)
    fc_mine = pick(fc_cut, core, 2)
    fc_other = swap(pick(fc_cut, 1 - core, 2).reshape(own, -1), "fsdp", 1)
    fc_rows = by_core(core, fc_mine.reshape(own, -1), fc_other, 0).reshape(2 * own, nz, ns, hw)
    fc_rows = xor_take(xor_take(fc_rows, floor, 1), me, 2)
    proj_rows = xor_take(w_proj.reshape(ns, hw, width), me, 0)
    out_cols = xor_take(w_out.reshape(own, ns, local), me, 1)
    proj_parts = width // cols
    out_parts = max(1, cols // local)

    def share(q, k):
        fc = jnp.concatenate([fc_rows[:, j ^ k, q] for j in range(nz)], axis=1)
        proj = [proj_rows[q][:, i * cols : (i + 1) * cols] for i in range(proj_parts)]
        out = out_cols[:, q]
        if out_parts > 1:
            step = own // out_parts
            out = jnp.concatenate([out[i * step : (i + 1) * step] for i in range(out_parts)], axis=1)
        return fc, proj, out

    def message(k):
        fc, proj, out = share(0, k)
        return jnp.concatenate([fc, *proj, out.reshape(-1, cols)], axis=0)

    got = [swap(message(k), "fsdp", 2 * k) for k in range(1, nz)]
    rows_each = got[0].shape[0]
    planes = plane_gather(jnp.concatenate(got, axis=0))

    def parts_of(q, k):
        if k == 0:
            fc, proj, out = share(q, 0)
            return fc, jnp.concatenate(proj, axis=1), out_cols[:, q]
        block = planes[q][(k - 1) * rows_each : k * rows_each]
        fc = block[: 2 * own]
        proj = jnp.concatenate(
            [block[2 * own + i * hw : 2 * own + (i + 1) * hw] for i in range(proj_parts)], axis=1
        )
        out = block[2 * own + proj_parts * hw :]
        if out_parts > 1:
            out = jnp.concatenate(
                [out[:, i * local : (i + 1) * local] for i in range(out_parts)], axis=0
            )
        else:
            out = out.reshape(own, local)
        return fc, proj, out

    pieces = [[parts_of(q, k) for k in range(nz)] for q in range(ns)]
    out_half = jnp.stack(
        [jnp.stack([pieces[q][k][2] for q in range(ns)], axis=1) for k in range(nz)]
    )
    out_half = xor_take(out_half, me, 2).reshape(nz, own, width)
    out_both = by_core(core, out_half, swap(out_half, "fsdp", 1), 1)
    out_mat = xor_take(out_both, floor, 0).reshape(ns, local, width)
    out_mat = xor_take(out_mat, me, 0).reshape(width, width)
    fc_mat = jnp.concatenate(
        [jnp.concatenate([pieces[q][k][0] for k in range(nz)], axis=0) for q in range(ns)], axis=1
    )
    proj_mat = jnp.concatenate([pieces[q][k][1] for q in range(ns) for k in range(nz)], axis=0)
    fc_bias = pick(fc_vec.reshape(nz, 2, ns, hw), core, 1)
    fc_bias = xor_take(xor_take(fc_bias, floor, 0), me, 1).transpose(1, 0, 2).reshape(-1)

    all_tokens = jnp.concatenate(token_blocks, axis=0).astype(F32)
    unit_all, _ = norm_stats(all_tokens)
    first = (unit_all * gain_a + shift_a).astype(BF)
    bias_all = jnp.concatenate(
        [
            pick(qv_vec.reshape(2, ns, local)[0], me, 0),
            jnp.zeros((local,), F32),
            pick(qv_vec.reshape(2, ns, local)[1], me, 0),
        ]
    )
    qkv = (jnp.dot(first, qkv_mat, preferred_element_type=F32) + bias_all).astype(BF)
    lens = jnp.concatenate([prompt_lens, cont_lens[0], me.reshape(1)]).astype(jnp.int32)
    mixed_heads, norms = attend_forward(lens, qkv, heads)

    def to_tokens(values):
        return jnp.concatenate(
            [values[:toks]]
            + [swap(values[k * toks : (k + 1) * toks], "seq", k) for k in range(1, ns)],
            axis=1,
        )

    def to_heads(values):
        return jnp.concatenate(
            [values[:, :local]]
            + [swap(values[:, k * local : (k + 1) * local], "seq", k) for k in range(1, ns)],
            axis=0,
        )

    mixed = to_tokens(mixed_heads)
    hidden = token_block.astype(F32) + jnp.dot(mixed, out_mat, preferred_element_type=F32) + out_vec
    unit_two, scale_two = norm_stats(hidden)
    second = (unit_two * gain_b + shift_b).astype(BF)

    second_both = jnp.concatenate([second, swap(second, "fsdp", 1)], axis=0)
    second_both = xor_blocks(second_both, floor, nz, 1)
    branch_both = jnp.concatenate([branch, swap(branch, "fsdp", 1)], axis=0)
    pre = jnp.dot(second_both, fc_mat, preferred_element_type=F32) + fc_bias
    act_full, bend = gelu_both(pre)
    act = act_full.astype(BF)
    grad_act = nt(branch_both, proj_mat)
    grad_pre = (grad_act * bend).astype(BF)
    grad_second_both = nt(grad_pre, fc_mat)
    grad_second = grad_second_both[:toks] + swap(
        grad_second_both[toks:].astype(BF), "fsdp", 1
    ).astype(F32)
    grad_second = xor_blocks(grad_second, floor, nz, 1)
    out_sum = jnp.dot(act, proj_mat, preferred_element_type=F32)
    result = hidden + out_sum[:toks] + proj_vec
    result = result + swap(out_sum[toks:].astype(BF), "fsdp", 1).astype(F32)
    output = result.astype(BF)[None]

    grad_hidden = branch.astype(F32) + norm_pull(unit_two, scale_two, grad_second * gain_b)
    grad_attn = grad_hidden.astype(BF)
    grad_mixed = nt(grad_attn, out_mat).astype(BF)
    grad_heads = to_heads(grad_mixed)

    backward = attend_backward(lens, qkv, mixed_heads, norms, grad_heads, heads)
    grad_q, grad_k, grad_v = (
        jnp.concatenate([part[i] for part in backward], axis=1) for i in range(3)
    )
    grad_qkv = jnp.concatenate([grad_q, grad_k, grad_v], axis=1)
    grad_first_part = nt(grad_qkv, qkv_mat).astype(BF)
    grad_first = plane_scatter(
        [grad_first_part[k * toks : (k + 1) * toks] for k in range(ns)]
    )
    unit_one, scale_one = norm_stats(token_block.astype(F32))
    input_grad = (grad_hidden + norm_pull(unit_one, scale_one, grad_first * gain_a))[None]

    span = nz * hw
    grad_fc = [tn(second_both, grad_pre[:, q * span : (q + 1) * span]).astype(BF) for q in range(ns)]
    grad_proj = [tn(act[:, q * span : (q + 1) * span], branch_both).astype(BF) for q in range(ns)]
    fc_sum = plane_scatter(grad_fc)
    proj_sum = plane_scatter(grad_proj)

    def fc_for(k):
        block = fc_sum[k * 2 * own : (k + 1) * 2 * own].reshape(2 * own, nz, hw)
        return jnp.concatenate([block[:, j ^ k] for j in range(nz)], axis=1)

    def proj_for(k):
        block = proj_sum[k * hw : (k + 1) * hw]
        return jnp.concatenate(
            [block[:, i * span : (i + 1) * span] for i in range(proj_parts)], axis=0
        )

    both_sum = jnp.concatenate([fc_for(0), proj_for(0)], axis=0)
    for k in range(1, nz):
        sent = jnp.concatenate([fc_for(k), proj_for(k)], axis=0).astype(BF)
        both_sum = both_sum + swap(sent, "fsdp", 2 * k).astype(F32)
    fc_owned = both_sum[: 2 * own].reshape(2, own, span)
    fc_kept = pick(fc_owned, core, 0).astype(BF)
    fc_moved = swap(pick(fc_owned, 1 - core, 0).astype(BF), "fsdp", 1)
    final = jnp.concatenate([fc_kept, fc_moved, both_sum[2 * own :].astype(BF)], axis=0)
    finals = plane_gather(final)
    fc_kept_all = jnp.stack([v[:own].reshape(own, nz, hw) for v in finals], axis=2)
    fc_moved_all = jnp.stack([v[own : 2 * own].reshape(own, nz, hw) for v in finals], axis=2)
    grad_w_fc = by_core(core, fc_kept_all, fc_moved_all, 2)
    grad_w_fc = xor_take(xor_take(grad_w_fc, floor, 1), me, 3).reshape(own, hidden_all).astype(F32)
    grad_w_proj = jnp.stack(
        [
            jnp.concatenate(
                [v[2 * own + i * hw : 2 * own + (i + 1) * hw] for i in range(proj_parts)], axis=1
            )
            for v in finals
        ]
    )
    grad_w_proj = xor_take(grad_w_proj, me, 0).reshape(ns * hw, width).astype(F32)

    grad_out = tn(mixed, grad_attn).astype(BF).reshape(ns, local, width)
    grad_out = xor_take(grad_out, me, 0).reshape(nz, 2, own, width)
    grad_out = xor_take(grad_out, floor, 0)
    out_kept = pick(grad_out, core, 1).astype(F32) + swap(
        pick(grad_out, 1 - core, 1), "fsdp", 1
    ).astype(F32)
    out_owned = out_kept[0]
    for k in range(1, nz):
        out_owned = out_owned + swap(out_kept[k].astype(BF), "fsdp", 2 * k).astype(F32)
    bit = 1
    while bit < ns:
        out_owned = out_owned + swap(out_owned.astype(BF), "seq", bit).astype(F32)
        bit *= 2
    grad_w_out = out_owned

    grad_in = tn(first, grad_qkv).astype(BF).reshape(nz, 2, own, 3 * local)
    grad_in = xor_take(grad_in, floor, 0)
    in_kept = pick(grad_in, core, 1).astype(F32) + swap(
        pick(grad_in, 1 - core, 1), "fsdp", 1
    ).astype(F32)
    in_owned = in_kept[0]
    for k in range(1, nz):
        in_owned = in_owned + swap(in_kept[k].astype(BF), "fsdp", 2 * k).astype(F32)
    in_owned = in_owned.astype(BF)
    in_blocks = jnp.stack(
        [in_owned.reshape(own, 3, local)]
        + [swap(in_owned, "seq", k).reshape(own, 3, local) for k in range(1, ns)],
        axis=2,
    )
    grad_w_qkv = xor_take(in_blocks, me, 2).reshape(own, 3 * width).astype(F32)

    def placed(values, parts):
        slots = jnp.arange(parts)[:, None] == me
        return jnp.where(slots, values[None, :], 0.0).reshape(-1)

    part_f32 = grad_first_part.astype(F32)
    fc_bias_grad = jnp.sum(grad_pre.astype(F32), axis=0).reshape(ns, nz, hw).transpose(1, 0, 2)
    fc_bias_grad = xor_take(xor_take(fc_bias_grad, floor, 0), me, 1)
    fc_bias_grad = jnp.where(
        (jnp.arange(2) == core)[None, :, None, None], fc_bias_grad[:, None], 0.0
    ).reshape(-1)
    vector_grads = [
        jnp.sum(part_f32 * unit_all, axis=0),
        jnp.sum(part_f32, axis=0),
        placed(jnp.sum(grad_q.astype(F32), axis=0), ns),
        placed(jnp.sum(grad_v.astype(F32), axis=0), ns),
        jnp.sum(grad_attn.astype(F32), axis=0),
        jnp.sum(grad_second * unit_two, axis=0),
        jnp.sum(grad_second, axis=0),
        fc_bias_grad,
        jnp.sum(branch.astype(F32), axis=0),
    ]
    vector_sum = jnp.concatenate([v.reshape(-1, width) for v in vector_grads], axis=0)
    for axis, size in (("seq", ns), ("fsdp", nf)):
        bit = 1
        while bit < size:
            vector_sum = vector_sum + swap(vector_sum, axis, bit)
            bit *= 2
    vector_sum = vector_sum.reshape(-1)
    outs = []
    at = 0
    for v in vectors:
        count = v.shape[0]
        outs.append(lax.dynamic_slice_in_dim(vector_sum, at + owner * count, count))
        at += nf * count
    (g_gain_one, g_shift_one, g_bias_qv, g_bias_out, g_gain_two, g_shift_two, g_bias_fc, g_bias_proj) = outs

    return (
        output,
        input_grad,
        g_gain_one,
        g_shift_one,
        grad_w_qkv,
        g_bias_qv,
        grad_w_out,
        g_bias_out,
        g_gain_two,
        g_shift_two,
        grad_w_fc,
        g_bias_fc,
        grad_w_proj,
        g_bias_proj,
    )


UPPER = (0, 2, 1, 3)


def hidden_at(q, half, size):
    return half * 4 * size + (UPPER[q] if half == 0 else q) * size


def start_all(copies, sems):
    made = [
        pltpu.make_async_copy(source, target, sems.at[i]) for i, (source, target) in enumerate(copies)
    ]
    for copy in made:
        copy.start()
    return made


def aligned(value, size):
    return pl.multiple_of(value, size)


def pack_kernel(hw, place, fc_ref, proj_ref, out_mat_ref, mine_ref, other_ref, share_ref):
    me, core = place[0], place[2]
    for q in range(4):
        for z in range(4):
            target = hidden_at(q, z // 2, 2 * hw) + (z % 2) * hw
            for out_ref, which in ((mine_ref, core), (other_ref, 1 - core)):
                source = aligned(z * 8 * hw + which * 4 * hw + (me ^ q) * hw, hw)
                out_ref[:, target : target + hw] = fc_ref[:, pl.ds(source, hw)]
    share_ref[...] = proj_ref[...]
    other_ref[:, 16 * hw :] = out_mat_ref[...]


def pack(place, w_fc, w_proj, w_out):
    own, hidden_all = w_fc.shape
    hw, width = w_proj.shape[0] // 4, w_proj.shape[1]

    def whole(shape):
        return pl.BlockSpec(shape, lambda i, place: (0, 0))

    half = jax.ShapeDtypeStruct((own, hidden_all // 2), BF)
    more = jax.ShapeDtypeStruct((own, hidden_all // 2 + width), BF)
    return pl.pallas_call(
        functools.partial(pack_kernel, hw),
        out_shape=(half, more, jax.ShapeDtypeStruct((hw, width), BF)),
        grid_spec=pltpu.PrefetchScalarGridSpec(
            num_scalar_prefetch=1,
            grid=(1,),
            in_specs=[
                whole((own, hidden_all)),
                pl.BlockSpec((hw, width), lambda i, place: (place[0], 0)),
                whole(w_out.shape),
            ],
            out_specs=(whole(half.shape), whole(more.shape), whole((hw, width))),
        ),
        cost_estimate=cost(3),
        name="pack_shares",
    )(place, w_fc, w_proj, w_out)


def join_kernel(place, m0, m1, o0, o1, mine_out, l0, l1, out_ref):
    core = place[2]
    own, chunk = m0.shape
    part = mine_out.shape[0]
    for refs, which in (((m0, m1), core), ((o0, o1), 1 - core)):
        rows = pl.ds(aligned(which * own, own), own)
        for half in range(2):
            out_ref[rows, half * chunk : (half + 1) * chunk] = refs[half][...]
    wide = 2 * chunk
    for parts, which in (
        ((mine_out[:, :wide], mine_out[:, wide:]), core),
        ((l0[...], l1[...]), 1 - core),
    ):
        for half in range(2):
            rows = pl.ds(aligned(2 * own + which * 2 * part + half * part, part), part)
            out_ref[rows, :] = parts[half]


def join(place, mine, other, w_out):
    own, hidden = mine.shape
    chunk = hidden // 8
    part = own // 4
    rows = 2 * own + 4 * part
    pieces = [
        pl.BlockSpec((own, chunk), lambda i, place, at=hidden_at(0, half, 1): (0, at))
        for half in range(2)
    ]
    quarters = [
        pl.BlockSpec((part, 2 * chunk), lambda i, place, at=4 + half: (place[0], at))
        for half in range(2)
    ]
    return pl.pallas_call(
        join_kernel,
        out_shape=jax.ShapeDtypeStruct((rows, 2 * chunk), BF),
        grid_spec=pltpu.PrefetchScalarGridSpec(
            num_scalar_prefetch=1,
            grid=(1,),
            in_specs=pieces * 2
            + [pl.BlockSpec((part, w_out.shape[1]), lambda i, place: (place[0], 0))]
            + quarters,
            out_specs=pl.BlockSpec((rows, 2 * chunk), lambda i, place: (0, 0)),
        ),
        cost_estimate=cost(2),
        name="join_rows",
    )(place, mine, mine, other, other, w_out, other, other)


def joined_kernel(*refs):
    at = 0
    for ref in refs[:-1]:
        refs[-1][at : at + ref.shape[0], :] = ref[...]
        at += ref.shape[0]


def joined(parts):
    rows = sum(part.shape[0] for part in parts)
    return pl.pallas_call(
        joined_kernel,
        out_shape=jax.ShapeDtypeStruct((rows, parts[0].shape[1]), parts[0].dtype),
        cost_estimate=cost(1),
        name="joined",
    )(*parts)


def project_kernel(
    place, own_ref, one_ref, two_ref, up_ref, low_ref, kept_ref, moved_ref, gain_ref, shift_ref,
    bias_ref, first_ref, unit_ref, qkv_ref, turned_ref, toks, mat, sems,
):
    step = pl.program_id(0)
    floor, core = place[1], place[2]
    block = own_ref.shape[0]
    half = block // 2
    own = mat.shape[0] // 8

    def copies():
        made = [
            (own_ref, toks.at[pl.ds(0, block), :]),
            (one_ref, toks.at[pl.ds(block, block), :]),
            (two_ref, toks.at[pl.ds(2 * block, block), :]),
            (up_ref, toks.at[pl.ds(3 * block, half), :]),
            (low_ref, toks.at[pl.ds(3 * block + half, half), :]),
        ]
        for k in range(4):
            for ref, which in ((kept_ref, core), (moved_ref, 1 - core)):
                row = aligned((floor ^ k) * 2 * own + which * own, own)
                made.append((ref.at[k, pl.ds(0, own), :], mat.at[pl.ds(row, own), :]))
        return made

    @pl.when(step == 0)
    def _():
        for copy in start_all(copies(), sems):
            copy.wait()

    rows = first_ref.shape[0]
    values = toks[pl.ds(aligned(step * rows, rows), rows), :].astype(F32)
    unit, _ = norm_stats(values)
    first = (unit * gain_ref[...] + shift_ref[...]).astype(BF)
    first_ref[...] = first
    unit_ref[...] = unit.astype(BF)
    qkv_ref[...] = (nn(first, mat[...]) + bias_ref[...]).astype(BF)

    @pl.when(step == pl.num_programs(0) - 1)
    def _():
        turned_ref[...] = mat[...].T


def project(place, blocks, kept, moved, gain, shift, bias):
    block, width = blocks[0].shape
    outs = kept.shape[2]
    total = 4 * block
    rows = 256
    raw = pl.BlockSpec(memory_space=pl.ANY)

    def line(size):
        return pl.BlockSpec((1, size), lambda i, place: (0, 0))

    def tile(size):
        return pl.BlockSpec((rows, size), lambda i, place: (i, 0))

    return pl.pallas_call(
        project_kernel,
        out_shape=(
            jax.ShapeDtypeStruct((total, width), BF),
            jax.ShapeDtypeStruct((total, width), BF),
            jax.ShapeDtypeStruct((total, outs), BF),
            jax.ShapeDtypeStruct((outs, width), BF),
        ),
        grid_spec=pltpu.PrefetchScalarGridSpec(
            num_scalar_prefetch=1,
            grid=(total // rows,),
            in_specs=[raw] * 7 + [line(width), line(width), line(outs)],
            out_specs=(
                tile(width),
                tile(width),
                tile(outs),
                pl.BlockSpec((outs, width), lambda i, place: (0, 0)),
            ),
            scratch_shapes=[
                pltpu.VMEM((total, width), BF),
                pltpu.VMEM((width, outs), BF),
                pltpu.SemaphoreType.DMA((13,)),
            ],
        ),
        cost_estimate=cost(12),
        name="project",
    )(place, *blocks, kept, moved, gain, shift, bias)


def attn_out_kernel(part, place, *refs):
    mixed_refs, (mine_ref, other_ref), shares = refs[:4], refs[4:6], refs[6:10]
    token_ref, bias_ref, gain_ref, shift_ref = refs[10:14]
    hidden_ref, second_ref, mixed_ref, mat_ref, mixed, sems = refs[14:]
    step = pl.program_id(0)
    me, floor, core = place[0], place[1], place[2]
    local = mixed_refs[0].shape[1]
    own, width = mine_ref.shape
    block = mixed.shape[0]
    wide = width // 2
    rows_each = 2 * own + 4 * part

    @pl.when(step == 0)
    def _():
        made = []
        for k, ref in enumerate(mixed_refs):
            lanes = pl.ds(aligned((me ^ k) * local, local), local)
            made.append((ref.at[pl.ds(0, block), :], mixed.at[:, lanes]))
        for source, which in (
            (mine_ref, core),
            (other_ref.at[:, pl.ds(other_ref.shape[1] - width, width)], 1 - core),
        ):
            row = aligned(floor * 2 * own + which * own, own)
            made.append((source, mat_ref.at[pl.ds(row, own), :]))
        for q in range(4):
            for k in range(1, 4):
                for which in range(2):
                    row = aligned((floor ^ k) * 2 * own + which * own + (me ^ q) * part, part)
                    for half in range(2):
                        at = (k - 1) * rows_each + 2 * own + which * 2 * part + half * part
                        made.append(
                            (
                                shares[q].at[pl.ds(at, part), :],
                                mat_ref.at[pl.ds(row, part), pl.ds(half * wide, wide)],
                            )
                        )
        for copy in start_all(made, sems):
            copy.wait()

    rows = hidden_ref.shape[0]
    here = mixed[pl.ds(aligned(step * rows, rows), rows), :]
    mixed_ref[...] = here
    hidden = token_ref[...].astype(F32) + nn(here, mat_ref[...]) + bias_ref[...]
    hidden_ref[...] = hidden
    unit, _ = norm_stats(hidden)
    second_ref[...] = (unit * gain_ref[...] + shift_ref[...]).astype(BF)


def attn_out(place, mixed, mine, other, shares, tokens, bias, gain, shift):
    block, width = tokens.shape
    rows = 256
    raw = pl.BlockSpec(memory_space=pl.ANY)
    line = pl.BlockSpec((1, width), lambda i, place: (0, 0))
    tile = pl.BlockSpec((rows, width), lambda i, place: (i, 0))
    return pl.pallas_call(
        functools.partial(attn_out_kernel, mine.shape[0] // 4),
        out_shape=(
            jax.ShapeDtypeStruct((block, width), F32),
            jax.ShapeDtypeStruct((block, width), BF),
            jax.ShapeDtypeStruct((block, width), BF),
            jax.ShapeDtypeStruct((width, width), BF),
        ),
        grid_spec=pltpu.PrefetchScalarGridSpec(
            num_scalar_prefetch=1,
            grid=(block // rows,),
            in_specs=[raw] * 10 + [tile, line, line, line],
            out_specs=(tile, tile, tile, pl.BlockSpec((width, width), lambda i, place: (0, 0))),
            scratch_shapes=[pltpu.VMEM((block, width), BF), pltpu.SemaphoreType.DMA((54,))],
        ),
        cost_estimate=cost(7),
        name="attn_out",
    )(place, *mixed, mine, other, *shares, tokens, bias, gain, shift)


def feed_kernel(
    hw, place, second_ref, branch_ref, bias_a, bias_b, mine_ref, other_ref, a0, a1, a2, a3, proj_ref,
    b0, b1, b2, b3, act_a, act_b, slope_a, slope_b, out_own, out_oth, back_own, back_oth, sum_a, sum_b,
    fc, proj, fc_turned, proj_turned, total, back, sems,
):
    step = pl.program_id(0)
    me, floor, core = place[0], place[1], place[2]
    own = mine_ref.shape[0]
    chunk = 2 * hw
    rows_each = a0.shape[0] // 3

    def copies(q):
        made = []
        for ref, which in ((mine_ref, core), (other_ref, 1 - core)):
            row = aligned(floor * 2 * own + which * own, own)
            for half in range(2):
                made.append(
                    (
                        ref.at[:, pl.ds(hidden_at(q, half, chunk), chunk)],
                        fc.at[q, pl.ds(row, own), pl.ds(half * chunk, chunk)],
                    )
                )
        for k in range(1, 4):
            row = aligned((floor ^ k) * 2 * own, 2 * own)
            source = (a0, a1, a2, a3)[q].at[pl.ds((k - 1) * rows_each, 2 * own), :]
            made.append((source, fc.at[q, pl.ds(row, 2 * own), :]))
        for k in range(4):
            if k == 0:
                source = proj_ref.at[pl.ds(aligned((me ^ q) * hw, hw), hw), :]
            else:
                source = (b0, b1, b2, b3)[q].at[pl.ds((k - 1) * hw, hw), :]
            made.append((source, proj.at[q, pl.ds(aligned((floor ^ k) * hw, hw), hw), :]))
        return [
            pltpu.make_async_copy(source, target, sems.at[q, i])
            for i, (source, target) in enumerate(made)
        ]

    @pl.when(step == 0)
    def _():
        for q in range(4):
            for copy in copies(q):
                copy.start()

    for q in range(4):

        @pl.when(step == q)
        def _():
            for copy in copies(q):
                copy.wait()

    fc_turned[...] = fc[step].T
    proj_turned[...] = proj[step].T
    bias = jnp.concatenate([bias_a[...], bias_b[...]], axis=1)
    both = second_ref.shape[0]
    rows = both // 2
    partial = None
    for start in range(0, both, rows):
        here = slice(start, start + rows)
        pre = nn(second_ref[here, :], fc[step]) + bias
        value, bend = gelu_both(pre)
        act = value.astype(BF)
        act_a[here, :] = act[:, :chunk]
        act_b[here, :] = act[:, chunk:]
        slope_full = nn(branch_ref[here, :], proj_turned[...]) * bend
        slope = slope_full.astype(BF)
        slope_a[here, :] = slope[:, :chunk]
        slope_b[here, :] = slope[:, chunk:]
        more = jnp.sum(slope_full, axis=0, keepdims=True)
        partial = more if partial is None else partial + more
        out_part = nn(act, proj[step])
        back_part = nn(slope, fc_turned[...])

        @pl.when(step == 0)
        def _():
            total[here, :] = out_part
            back[here, :] = back_part

        @pl.when(step > 0)
        def _():
            total[here, :] += out_part
            back[here, :] += back_part

    sum_a[...] = partial[:, :chunk]
    sum_b[...] = partial[:, chunk:]

    @pl.when(step == 3)
    def _():
        half = both // 2
        out_oth[...] = total[:half].astype(BF)
        back_oth[...] = back[:half].astype(BF)
        out_own[...] = total[half:]
        back_own[...] = back[half:]


def feed(place, second, branch, bias, mine, other, shares, w_proj, proj_shares):
    both, width = second.shape
    hidden = mine.shape[1]
    hw = hidden // 16
    chunk = 2 * hw
    raw = pl.BlockSpec(memory_space=pl.ANY)

    def whole(height):
        return pl.BlockSpec((height, width), lambda i, place: (0, 0))

    def upper(height):
        return pl.BlockSpec((height, chunk), lambda i, place: (0, (i % 2) * 2 + i // 2))

    def lower(height, first=0):
        return pl.BlockSpec((height, chunk), lambda i, place: (0, first + i))

    half = jax.ShapeDtypeStruct((both, hidden // 2), BF)
    line = jax.ShapeDtypeStruct((1, hidden // 2), F32)
    return pl.pallas_call(
        functools.partial(feed_kernel, hw),
        out_shape=(
            half,
            half,
            half,
            half,
            jax.ShapeDtypeStruct((both // 2, width), F32),
            jax.ShapeDtypeStruct((both // 2, width), BF),
            jax.ShapeDtypeStruct((both // 2, width), F32),
            jax.ShapeDtypeStruct((both // 2, width), BF),
            line,
            line,
        ),
        grid_spec=pltpu.PrefetchScalarGridSpec(
            num_scalar_prefetch=1,
            grid=(4,),
            in_specs=[whole(both), whole(both), upper(1), lower(1, 4)] + [raw] * 11,
            out_specs=(upper(both), lower(both), upper(both), lower(both))
            + (whole(both // 2),) * 4
            + (upper(1), lower(1)),
            scratch_shapes=[
                pltpu.VMEM((4, width, 2 * chunk), BF),
                pltpu.VMEM((4, 2 * chunk, width), BF),
                pltpu.VMEM((2 * chunk, width), BF),
                pltpu.VMEM((width, 2 * chunk), BF),
                pltpu.VMEM((both, width), F32),
                pltpu.VMEM((both, width), F32),
                pltpu.SemaphoreType.DMA((4, 11)),
            ],
        ),
        cost_estimate=cost(35),
        name="feed",
    )(place, second, branch, bias, bias, mine, other, *shares, w_proj, *proj_shares)


def mixed_back_kernel(
    place, own_ref, oth_ref, hidden_ref, branch_ref, gain_ref, mat_ref,
    full_ref, low_ref, g0, g1, g2, g3, sums_ref,
):
    step = pl.program_id(0)
    me = place[0]
    local = g0.shape[1]
    slope = own_ref[...] + oth_ref[...].astype(F32)
    unit, scale = norm_stats(hidden_ref[...])
    full = branch_ref[...].astype(F32) + norm_pull(unit, scale, slope * gain_ref[...])
    low = full.astype(BF)
    full_ref[...] = full
    low_ref[...] = low
    for k, ref in enumerate((g0, g1, g2, g3)):
        rows = pl.ds(aligned((me ^ k) * local, local), local)
        ref[...] = nt(low, mat_ref[rows, :]).astype(BF)
    sums = jnp.concatenate(
        [
            jnp.sum(low.astype(F32), axis=0, keepdims=True),
            jnp.sum(slope * unit, axis=0, keepdims=True),
            jnp.sum(slope, axis=0, keepdims=True),
            jnp.sum(branch_ref[...].astype(F32), axis=0, keepdims=True),
        ],
        axis=0,
    )

    @pl.when(step == 0)
    def _():
        sums_ref[...] = sums

    @pl.when(step > 0)
    def _():
        sums_ref[...] += sums


def mixed_back(place, own, oth, hidden, branch, gain, mat):
    block, width = own.shape
    local = width // 4
    rows = block

    def tile(size):
        return pl.BlockSpec((rows, size), lambda i, place: (i, 0))

    def whole(height):
        return pl.BlockSpec((height, width), lambda i, place: (0, 0))

    return pl.pallas_call(
        mixed_back_kernel,
        out_shape=(
            jax.ShapeDtypeStruct((block, width), F32),
            jax.ShapeDtypeStruct((block, width), BF),
        )
        + (jax.ShapeDtypeStruct((block, local), BF),) * 4
        + (jax.ShapeDtypeStruct((4, width), F32),),
        grid_spec=pltpu.PrefetchScalarGridSpec(
            num_scalar_prefetch=1,
            grid=(block // rows,),
            in_specs=[tile(width)] * 4 + [whole(1), whole(width)],
            out_specs=(tile(width), tile(width)) + (tile(local),) * 4 + (whole(4),),
        ),
        cost_estimate=cost(7),
        name="mixed_back",
    )(place, own, oth, hidden, branch, gain, mat)


def first_back_kernel(tiles, place, grad_ref, unit_ref, mat_ref, *refs):
    step = pl.program_id(0)
    count = len(tiles) // 2
    out_refs, sums_ref = refs[:count], refs[count]
    part = nn(grad_ref[...], mat_ref[...])
    low = part.astype(BF)
    for i in range(count):

        @pl.when(step // 2 == i)
        def _():
            out_refs[i][...] = low

    sums = jnp.concatenate(
        [
            jnp.sum(part * unit_ref[...].astype(F32), axis=0, keepdims=True),
            jnp.sum(part, axis=0, keepdims=True),
        ],
        axis=0,
    )

    @pl.when(step == 0)
    def _():
        sums_ref[...] = sums

    @pl.when(step > 0)
    def _():
        sums_ref[...] += sums


def first_back(tiles, grad, unit, mat):
    total, outs = grad.shape
    width = mat.shape[1]
    rows = 256
    table = jnp.asarray(tiles, jnp.int32)

    def at(i, place):
        return (place[i], 0)

    return pl.pallas_call(
        functools.partial(first_back_kernel, tiles),
        out_shape=tuple(jax.ShapeDtypeStruct((2 * rows, width), BF) for _ in tiles[::2])
        + (jax.ShapeDtypeStruct((2, width), F32),),
        grid_spec=pltpu.PrefetchScalarGridSpec(
            num_scalar_prefetch=1,
            grid=(len(tiles),),
            in_specs=[
                pl.BlockSpec((rows, outs), at),
                pl.BlockSpec((rows, width), at),
                pl.BlockSpec((outs, width), lambda i, place: (0, 0)),
            ],
            out_specs=tuple(
                pl.BlockSpec((rows, width), lambda i, place, g=g: (jnp.clip(i - 2 * g, 0, 1), 0))
                for g in range(len(tiles) // 2)
            )
            + (pl.BlockSpec((2, width), lambda i, place: (0, 0)),),
        ),
        cost_estimate=cost(5),
        name="first_back",
    )(table, grad, unit, mat)


def gather_fc_kernel(place, fa, xa, la, fb, yb, lb, o0, o1, o2, o3, fc):
    floor = place[1]
    chunk = fc.shape[1] // 2
    fc[:, :chunk] = fa[...].astype(F32) + xa[...].astype(F32) + la[...].astype(F32)
    fc[:, chunk:] = fb[...].astype(F32) + yb[...].astype(F32) + lb[...].astype(F32)
    rows = fc.shape[0] // 4
    for k, out in enumerate((o0, o1, o2, o3)):
        out[...] = fc[pl.ds(aligned((floor ^ k) * rows, rows), rows), :].astype(BF)


def gather_proj_kernel(place, pa, xp, lpa, pb, yp, lpb, o0, o1, o2, o3, proj):
    floor = place[1]
    chunk = proj.shape[0] // 2
    proj[:chunk, :] = pa[...].astype(F32) + xp[...].astype(F32) + lpa[...].astype(F32)
    proj[chunk:, :] = pb[...].astype(F32) + yp[...].astype(F32) + lpb[...].astype(F32)
    rows = proj.shape[0] // 4
    for k, out in enumerate((o0, o1, o2, o3)):
        out[...] = proj[pl.ds(aligned((floor ^ k) * rows, rows), rows), :].astype(BF)


def gather_sum(place, kernel, parts, shape, block):
    out = jax.ShapeDtypeStruct((shape[0] // 4, shape[1]), BF)
    return pl.pallas_call(
        kernel,
        out_shape=(out,) * 4,
        grid_spec=pltpu.PrefetchScalarGridSpec(
            num_scalar_prefetch=1,
            grid=(1,),
            in_specs=[pl.BlockSpec(block, lambda i, place: (0, 0))] * 6,
            out_specs=(pl.BlockSpec(out.shape, lambda i, place: (0, 0)),) * 4,
            scratch_shapes=[pltpu.VMEM(shape, F32)],
        ),
        cost_estimate=cost(3),
        name="gather_sum",
    )(place, *parts)


def spread_fc_kernel(place, *refs):
    me, core = place[0], place[2]
    finals, fc_ref = refs[:4], refs[4]
    own = fc_ref.shape[0]
    hw = finals[0].shape[1] // 4
    for q in range(4):
        for part, which in ((0, core), (1, 1 - core)):
            for z in range(4):
                lanes = pl.ds(aligned(z * 8 * hw + which * 4 * hw + (me ^ q) * hw, hw), hw)
                block = finals[q][part * own : (part + 1) * own, z * hw : (z + 1) * hw]
                fc_ref[:, lanes] = block.astype(F32)


def spread_proj_kernel(place, *refs):
    me = place[0]
    finals, proj_ref = refs[:4], refs[4]
    hw = finals[0].shape[0]
    for q in range(4):
        proj_ref[pl.ds(aligned((me ^ q) * hw, hw), hw), :] = finals[q][...].astype(F32)


def spread(place, kernel, finals, shape):
    def whole(shape):
        return pl.BlockSpec(shape, lambda i, place: (0, 0))

    return pl.pallas_call(
        kernel,
        out_shape=jax.ShapeDtypeStruct(shape, F32),
        grid_spec=pltpu.PrefetchScalarGridSpec(
            num_scalar_prefetch=1,
            grid=(1,),
            in_specs=[whole(finals[0].shape)] * 4,
            out_specs=whole(shape),
        ),
        cost_estimate=cost(2),
        name="spread",
    )(place, *finals)


def last_kernel(keep_ref, got_ref, last_ref, token_ref, hidden_ref, gain_ref, out_ref):
    slope = keep_ref[...].astype(F32) + got_ref[...].astype(F32) + last_ref[...].astype(F32)
    unit, scale = norm_stats(token_ref[...].astype(F32))
    out_ref[...] = hidden_ref[...] + norm_pull(unit, scale, slope * gain_ref[...])


def body_aligned(
    tokens,
    prompt_lens,
    cont_lens,
    gain_one,
    shift_one,
    w_qkv,
    bias_qv,
    w_out,
    bias_out,
    gain_two,
    shift_two,
    w_fc,
    bias_fc,
    w_proj,
    bias_proj,
    cotangent,
):
    ns = nz = 4
    nf = 8
    me = lax.axis_index("seq")
    owner = lax.axis_index("fsdp")
    floor = owner // 2
    core = owner % 2
    place = jnp.stack([me, floor, core]).astype(jnp.int32)
    toks, width = tokens.shape[1:]
    own = width // nf
    heads = H // ns
    local = width // ns
    hw = w_fc.shape[1] // (nf * ns)
    token_block = tokens[0]
    branch = cotangent[0]

    half = toks // 2
    vectors = [gain_one, shift_one, bias_qv, bias_out, gain_two, shift_two, bias_fc, bias_proj]
    packed = jnp.concatenate([v.reshape(-1, own) for v in vectors], axis=0)
    lines = packed.shape[0]
    packed = jnp.pad(packed.reshape(-1), (0, 16 * 3 * local - packed.size)).reshape(16, 3 * local)
    mine_qkv = pick(w_qkv.reshape(own, 3, ns, local), me, 2).reshape(own, 3 * local)
    sent_qkv = jnp.concatenate([mine_qkv, packed], axis=0)
    tok_one = swap(token_block, "seq", 1)
    tok_two = swap(token_block, "seq", 2)
    got_qkv = [swap(sent_qkv, "fsdp", 2 * k) for k in range(1, nz)]
    fc_mine, fc_sent, proj_share = pack(place, w_fc, w_proj, w_out)
    fc_other = swap(fc_sent, "fsdp", 1)
    fc_share = join(place, fc_mine, fc_other, w_out)

    tok_one, tok_two, got_qkv, fc_share, proj_share = lax.optimization_barrier(
        (tok_one, tok_two, got_qkv, fc_share, proj_share)
    )
    tok_up = swap(tok_two[:half], "seq", 1)
    tok_low = swap(tok_one[half:], "seq", 2)
    kept_qkv = jnp.stack([sent_qkv, *got_qkv])
    moved_qkv = swap(kept_qkv, "fsdp", 1)
    moved_qkv, fc_share = lax.optimization_barrier((moved_qkv, fc_share))
    fc_got = [swap(fc_share, "fsdp", 2 * k) for k in range(1, nz)]

    small = by_core(core, kept_qkv[:, own : own + 2], moved_qkv[:, own : own + 2], 1)
    small = xor_take(small, floor, 0).reshape(nf, -1).reshape(nf, lines, own)
    at = 0
    full = []
    for v in vectors:
        count = v.shape[0] // own
        full.append(small[:, at : at + count].reshape(1, -1).astype(F32))
        at += count
    gain_a, shift_a, qv_vec, out_vec, gain_b, shift_b, fc_vec, proj_vec = full
    qv_mine = pick(qv_vec.reshape(2, ns, local), me, 1)
    bias_all = jnp.concatenate([qv_mine[0], jnp.zeros((local,), F32), qv_mine[1]]).reshape(1, -1)
    fc_bias = xor_take(pick(fc_vec.reshape(nz, 2, ns, hw), core, 1), me, 1)
    order = [(q, 0) for q in (0, 2, 1, 3)] + [(q, 1) for q in range(4)]
    fc_bias = jnp.concatenate(
        [fc_bias[2 * part : 2 * part + 2, q].reshape(1, -1) for q, part in order], axis=1
    )

    first, unit_all, qkv, qkv_turned = project(
        place, (token_block, tok_one, tok_two, tok_up, tok_low), kept_qkv, moved_qkv, gain_a, shift_a,
        bias_all,
    )
    lens = jnp.concatenate([prompt_lens, cont_lens[0], me.reshape(1)]).astype(jnp.int32)

    qkv, fc_got, proj_share = lax.optimization_barrier((qkv, fc_got, proj_share))
    fc_zero = joined(fc_got)
    fc_one = swap(fc_zero, "seq", 1)
    fc_two = swap(fc_zero, "seq", 2)
    proj_got = [swap(proj_share, "fsdp", 2 * k) for k in range(1, nz)]
    ends = {}

    def between(lens, mixed, arrays):
        (mixed, arrays, one, two, got) = lax.optimization_barrier(
            (mixed, arrays, fc_one, fc_two, proj_got)
        )
        cut = one.shape[0] // 2
        ends["fc"] = (one, two, swap(two[:cut], "seq", 1), swap(one[cut:], "seq", 2))
        zero = joined(got)
        ends["proj"] = (zero, swap(zero, "seq", 1), swap(zero, "seq", 2))
        return lens, mixed, arrays

    mixed_heads, norms = attend_forward(lens, qkv, heads, between)
    fc_one, fc_two, fc_up, fc_low = ends["fc"]
    proj_zero, proj_one, proj_two = ends["proj"]

    mixed_heads, fc_up, fc_low, proj_one, proj_two = lax.optimization_barrier(
        (mixed_heads, fc_up, fc_low, proj_one, proj_two)
    )
    mixed_blocks = [mixed_heads] + [
        swap(mixed_heads[k * toks : (k + 1) * toks], "seq", k) for k in range(1, ns)
    ]
    fc_three = joined([fc_up, fc_low])
    shares = (fc_zero, fc_one, fc_two, fc_three)
    cut = proj_one.shape[0] // 2
    proj_three = joined([swap(proj_two[:cut], "seq", 1), swap(proj_one[cut:], "seq", 2)])
    hidden, second, mixed, out_mat = attn_out(
        place, mixed_blocks, w_out, fc_other, shares, token_block, out_vec, gain_b, shift_b
    )

    second, branch_sent = lax.optimization_barrier((second, branch))
    second_both = jnp.concatenate([swap(second, "fsdp", 1), second], axis=0)
    branch_both = jnp.concatenate([swap(branch_sent, "fsdp", 1), branch], axis=0)
    *hiddens, out_own, out_oth, back_own, back_oth, sum_upper, sum_lower = feed(
        place, second_both, branch_both, fc_bias, fc_mine, fc_other,
        shares, w_proj, (proj_zero, proj_one, proj_two, proj_three),
    )
    back_got = swap(back_oth, "fsdp", 1)
    out_got = swap(out_oth, "fsdp", 1)
    grad_hidden, grad_attn, *grad_blocks, sums_two = mixed_back(
        place, back_own, back_got, hidden, branch, gain_b, out_mat
    )

    def added(left, right):
        return (left.astype(F32) + right.astype(F32)).astype(BF)

    def halves(values, index):
        pair = values.reshape(2, values.shape[0] // 2, values.shape[1])
        return pick(pair, index, 0).astype(F32), pick(pair, 1 - index, 0).astype(BF)

    def core_halves(grad):
        cut = grad.reshape(nz, 2, own, -1)
        mine, sent = pick(cut, core, 1), pick(cut, 1 - core, 1)
        return mine.reshape(nz * own, -1), sent.reshape(nz * own, -1)

    edge = 4 * hw
    chunk = 2 * hw
    head_got = [swap(grad_blocks[k], "seq", k) for k in range(1, ns)]
    hiddens, branch_late = after((hiddens, branch_both), grad_blocks)
    acts, slopes = (
        [v[:, i * edge : (i + 1) * edge] for v in pair for i in range(2)]
        for pair in (hiddens[:2], hiddens[2:])
    )
    proj_grads = [None] * 4
    for i in (1, 3, 0, 2):
        proj_grads[i] = tn(acts[i], branch_late).astype(BF)

    proj_grads, slopes, second_late, mixed_late, attn_late, head_got, out_got = after(
        (proj_grads, slopes, second_both, mixed, grad_attn, head_got, out_got)
    )
    proj_x = swap(proj_grads[1], "seq", 1)
    proj_y = swap(proj_grads[3], "seq", 2)
    wo_mine, wo_sent = core_halves(tn(mixed_late, attn_late).astype(BF))
    wo_got = swap(wo_sent, "fsdp", 1)
    fc_grads = [None] * 4
    for i in (1, 3, 0, 2):
        fc_grads[i] = tn(second_late, slopes[i]).astype(BF)
    output = (hidden + out_own + proj_vec + out_got.astype(F32)).astype(BF)

    grad_heads = jnp.concatenate([grad_blocks[0], *head_got], axis=0)
    grad_heads, fc_grads, wo_got, output = after((grad_heads, fc_grads, wo_got, output))
    fc_x = swap(fc_grads[1], "seq", 1)
    fc_y = swap(fc_grads[3], "seq", 2)
    wo_keep, wo_sent = halves(wo_mine.astype(F32) + wo_got.astype(F32), floor // 2)
    wo_far = swap(wo_sent, "fsdp", 4)
    back = {}

    def between_back(lens, parts, grad):
        parts, grad, x, y, far = after((parts, grad, proj_x, proj_y, wo_far))
        back["proj"] = (
            x,
            y,
            swap(added(proj_grads[2][chunk:], y[chunk:]), "seq", 1),
            swap(added(proj_grads[0][chunk:], x[chunk:]), "seq", 2),
        )
        keep, sent = halves(wo_keep + far.astype(F32), floor % 2)
        back["out"] = keep, swap(sent, "fsdp", 2)
        return lens, parts, grad

    backward = attend_backward(lens, qkv, mixed_heads, norms, grad_heads, heads, between_back)
    proj_x, proj_y, proj_last_x, proj_last_y = back["proj"]
    wo_keep, wo_near = back["out"]

    backward, fc_x, fc_y, proj_x, proj_y, proj_last_x, proj_last_y, wo_near = after(
        (backward, fc_x, fc_y, proj_x, proj_y, proj_last_x, proj_last_y, wo_near)
    )
    fc_far = [added(fc_grads[0][:, chunk:], fc_x[:, chunk:]), added(fc_grads[2][:, chunk:], fc_y[:, chunk:])]
    fc_last_y = swap(fc_far[0], "seq", 2)
    fc_last_x = swap(fc_far[1], "seq", 1)
    cuts = gather_sum(
        place, gather_proj_kernel,
        (proj_grads[0], proj_x, proj_last_y, proj_grads[2], proj_y, proj_last_x),
        (4 * hw, width), (chunk, width),
    )
    cuts_proj = [swap(cuts[k], "fsdp", 2 * k) for k in range(1, nz)]
    grad_proj_kept = cuts[0]
    backward = after(backward, fc_far, cuts)
    grad_qkv = jnp.concatenate([part[i] for i in range(3) for part in backward], axis=1)
    sent_x, sent_y, sums_early = first_back((2, 6, 5, 7), grad_qkv, unit_all, qkv_turned)
    first_late, qkv_late = after((first, grad_qkv), sent_x)
    wi_mine, wi_sent = core_halves(tn(first_late, qkv_late).astype(BF))

    sent_x, sent_y, grad_qkv, fc_last_x, fc_last_y, wi_sent = after(
        (sent_x, sent_y, grad_qkv, fc_last_x, fc_last_y, wi_sent)
    )
    got_x = swap(sent_x, "seq", 1)
    got_y = swap(sent_y, "seq", 2)
    cuts = gather_sum(
        place, gather_fc_kernel,
        (fc_grads[0], fc_x, fc_last_y, fc_grads[2], fc_y, fc_last_x),
        (width, 4 * hw), (width, chunk),
    )
    far_late, kept_late, sums_late = first_back((4, 3, 0, 1), grad_qkv, unit_all, qkv_turned)

    cuts_proj, cuts, far_late, wi_sent = after((cuts_proj, cuts, far_late, wi_sent))
    wi_got = swap(wi_sent, "fsdp", 1)
    proj_owned = grad_proj_kept.astype(F32)
    for part in cuts_proj:
        proj_owned = proj_owned + part.astype(F32)
    proj_owned = proj_owned.astype(BF)
    cuts, wi_got = after((cuts, wi_got))
    cuts_fc = [swap(cuts[k], "fsdp", 2 * k) for k in range(1, nz)]
    fc_kept = cuts[0]

    got_x, got_y, wi_got = after((got_x, got_y, wi_got))
    last_y = swap(added(far_late[:half], got_x[half:]), "seq", 2)
    last_x = swap(added(far_late[half:], got_y[half:]), "seq", 1)
    wi_keep, wi_sent = halves(wi_mine.astype(F32) + wi_got.astype(F32), floor // 2)

    last_x, last_y, proj_owned, wo_near = after((last_x, last_y, proj_owned, wo_near))
    proj_finals = [proj_owned] + [swap(proj_owned, "seq", k) for k in range(1, ns)]

    def last(at, end, got):
        block = pl.BlockSpec((half, width), lambda i: (at, 0))
        first_block = pl.BlockSpec((half, width), lambda i: (0, 0))
        return pl.pallas_call(
            last_kernel,
            out_shape=jax.ShapeDtypeStruct((half, width), F32),
            grid=(1,),
            in_specs=[block, first_block, first_block, block, block]
            + [pl.BlockSpec((1, width), lambda i: (0, 0))],
            out_specs=first_block,
            cost_estimate=cost(3),
            name="last",
        )(kept_late, got, end, token_block, grad_hidden, gain_a)

    input_grad = jnp.concatenate([last(0, last_y, got_x), last(1, last_x, got_y)], axis=0)[None]

    cuts_fc, wi_sent, last_x = after((cuts_fc, wi_sent, last_x))
    wi_far = swap(wi_sent, "fsdp", 4)
    fc_owned = fc_kept.astype(F32)
    for part in cuts_fc:
        fc_owned = fc_owned + part.astype(F32)
    fc_mine, fc_sent = halves(fc_owned, core)
    fc_final = jnp.concatenate([fc_mine.astype(BF), swap(fc_sent, "fsdp", 1)], axis=0)
    fc_finals = [fc_final] + [swap(fc_final, "seq", k) for k in range(1, ns)]
    grad_w_out = wo_keep + wo_near.astype(F32)
    for bit in (1, 2):
        grad_w_out = grad_w_out + swap(grad_w_out.astype(BF), "seq", bit).astype(F32)
    grad_w_proj = spread(place, spread_proj_kernel, proj_finals, (4 * hw, width))
    wi_keep, wi_sent = halves(wi_keep + wi_far.astype(F32), floor % 2)
    wi_owned = (wi_keep + swap(wi_sent, "fsdp", 2).astype(F32)).astype(BF)
    wi_blocks = jnp.stack(
        [wi_owned.reshape(own, 3, local)]
        + [swap(wi_owned, "seq", k).reshape(own, 3, local) for k in range(1, ns)],
        axis=2,
    )
    grad_w_qkv = xor_take(wi_blocks, me, 2).reshape(own, 3 * width).astype(F32)
    grad_w_fc = spread(place, spread_fc_kernel, fc_finals, (own, 32 * hw))
    output = output[None]

    def placed(values):
        slots = jnp.arange(ns)[:, None] == me
        return jnp.where(slots, values[None, :], 0.0).reshape(-1)

    spots = {}
    for i, (q, part) in enumerate(order):
        here = (sum_upper, sum_lower)[part][0, (i % 4) * chunk : (i % 4 + 1) * chunk]
        spots[q, part] = here.reshape(2, hw)
    fc_bias_grad = jnp.stack(
        [jnp.concatenate([spots[q, 0], spots[q, 1]], axis=0) for q in range(ns)], axis=1
    )
    fc_bias_grad = xor_take(fc_bias_grad, me, 1)
    fc_bias_grad = jnp.where(
        (jnp.arange(2) == core)[None, :, None, None], fc_bias_grad[:, None], 0.0
    ).reshape(-1)
    sums_one = sums_early + sums_late
    qkv_sum = jnp.sum(grad_qkv.astype(F32), axis=0)
    vector_grads = [
        sums_one[0],
        sums_one[1],
        placed(qkv_sum[:local]),
        placed(qkv_sum[2 * local :]),
        sums_two[0],
        sums_two[1],
        sums_two[2],
        fc_bias_grad,
        sums_two[3],
    ]
    vector_sum = jnp.concatenate([v.reshape(-1, width) for v in vector_grads], axis=0)
    vector_sum = after(vector_sum, cuts_fc)
    for axis, size in (("seq", ns), ("fsdp", nf)):
        bit = 1
        while bit < size:
            vector_sum = vector_sum + swap(vector_sum, axis, bit)
            bit *= 2
    vector_sum = vector_sum.reshape(-1)
    outs = []
    at = 0
    for v in vectors:
        count = v.shape[0]
        outs.append(lax.dynamic_slice_in_dim(vector_sum, at + owner * count, count))
        at += nf * count
    (g_gain_one, g_shift_one, g_bias_qv, g_bias_out, g_gain_two, g_shift_two, g_bias_fc, g_bias_proj) = outs

    return (
        output,
        input_grad,
        g_gain_one,
        g_shift_one,
        grad_w_qkv,
        g_bias_qv,
        grad_w_out,
        g_bias_out,
        g_gain_two,
        g_shift_two,
        grad_w_fc,
        g_bias_fc,
        grad_w_proj,
        g_bias_proj,
    )


def body(*args):
    tokens, w_proj = args[0], args[13]
    fits = (
        lax.axis_size("seq") == 4
        and lax.axis_size("fsdp") == 8
        and tokens.shape[1:] == (512, 1024)
        and w_proj.shape == (512, 1024)
    )
    return body_aligned(*args) if fits else body_general(*args)


def solution(mesh):
    rows = P("fsdp", None)
    vec = P("fsdp")
    acts = P("fsdp", "seq", None)
    return jax.shard_map(
        body,
        mesh=mesh,
        in_specs=(
            acts, vec, rows, vec, vec, rows, vec, rows, vec, vec, vec, rows, vec, rows, vec, acts,
        ),
        out_specs=(
            acts, acts, vec, vec, rows, vec, rows, vec, vec, vec, rows, vec, rows, vec,
        ),
        check_vma=False,
    )
```

```python
import functools

import jax
import jax.numpy as jnp
from jax import lax
from jax.experimental import pallas as pl
from jax.experimental.pallas import tpu as pltpu
from jax.sharding import PartitionSpec as P

H = 16
HD = 64
PROMPT = 1024
CONTLEN = 512
CONTS = 2

EPS = 1e-05
GELU_C = 0.7978845608028654
GELU_A = 0.044715
NEG = -1e30
BF = jnp.bfloat16
F32 = jnp.float32


def swap(values, axis, bits):
    size = lax.axis_size(axis)
    return lax.ppermute(values, axis, [(i, i ^ bits) for i in range(size)])


def xor_take(values, index, axis):
    size = values.shape[axis]
    bit = 1
    while bit < size:
        parts = [lax.slice_in_dim(values, i, i + 1, axis=axis) for i in range(size)]
        flipped = jnp.concatenate([parts[i ^ bit] for i in range(size)], axis=axis)
        values = jnp.where((index & bit) != 0, flipped, values)
        bit *= 2
    return values


def xor_blocks(values, index, count, axis):
    width = values.shape[axis] // count
    return jnp.concatenate(
        [
            lax.dynamic_slice_in_dim(values, (i ^ index) * width, width, axis=axis)
            for i in range(count)
        ],
        axis=axis,
    )


def plane_gather(values):
    size = lax.axis_size("seq")
    if size != 4:
        return [values] + [swap(values, "seq", k) for k in range(1, size)]
    half = values.shape[0] // 2
    one = swap(values, "seq", 1)
    two = swap(values, "seq", 2)
    three = jnp.concatenate(
        [swap(two[:half], "seq", 1), swap(one[half:], "seq", 2)], axis=0
    )
    return [values, one, two, three]


def plane_scatter(blocks):
    size = lax.axis_size("seq")
    if size != 4:
        total = blocks[0].astype(F32)
        for k in range(1, size):
            total = total + swap(blocks[k].astype(BF), "seq", k).astype(F32)
        return total
    half = blocks[0].shape[0] // 2
    sent_x = jnp.concatenate([blocks[1][:half], blocks[3][:half]], axis=0).astype(BF)
    sent_y = jnp.concatenate([blocks[2][half:], blocks[3][half:]], axis=0).astype(BF)
    got_x = swap(sent_x, "seq", 1).astype(F32)
    got_y = swap(sent_y, "seq", 2).astype(F32)
    next_y = (blocks[2][:half].astype(F32) + got_x[half:]).astype(BF)
    next_x = (blocks[1][half:].astype(F32) + got_y[half:]).astype(BF)
    last_y = swap(next_y, "seq", 2).astype(F32)
    last_x = swap(next_x, "seq", 1).astype(F32)
    upper = blocks[0][:half].astype(F32) + got_x[:half] + last_y
    lower = blocks[0][half:].astype(F32) + got_y[:half] + last_x
    return jnp.concatenate([upper, lower], axis=0)


def after(values, *needed):
    return lax.optimization_barrier((values, needed))[0]


def cost(micros, size=0):
    return pl.CostEstimate(flops=int(micros * 1.15e6), bytes_accessed=int(size), transcendentals=0)


def tile_rows(total, blocks):
    return min(512, total // blocks)


def rel_row(tile, rows, block_rows, me):
    per = block_rows // rows
    return pl.multiple_of(((tile // per) ^ me) * block_rows + (tile % per) * rows, rows)


def walk(tile, rows):
    prompt_tiles = PROMPT // rows
    cont_tiles = CONTLEN // rows
    in_prompt = tile < prompt_tiles
    inside = lax.rem(jnp.maximum(tile - prompt_tiles, 0), cont_tiles)
    count = jnp.where(in_prompt, tile, prompt_tiles + inside)
    return count, tile - inside - prompt_tiles


def key_limit(lens, tile, rows):
    prompt_tiles = PROMPT // rows
    cont_tiles = CONTLEN // rows
    past = jnp.maximum(tile - prompt_tiles, 0)
    cont = jnp.minimum(past // cont_tiles, CONTS - 1)
    length = lens[1]
    for i in range(1, CONTS):
        length = jnp.where(cont == i, lens[1 + i], length)
    return jnp.where(
        tile < prompt_tiles, lens[0] - tile * rows, length - lax.rem(past, cont_tiles) * rows
    )


def pair_stack(block, per_pair, scale=None):
    if scale is not None:
        block = block * scale
    if per_pair == 1:
        return block
    lane = lax.broadcasted_iota(jnp.int32, block.shape, 1) // HD
    return jnp.concatenate(
        [jnp.where(lane == h, block, jnp.zeros_like(block)) for h in range(per_pair)], axis=0
    )


def diagonal_mask(rows, per_pair, limit):
    key = lax.broadcasted_iota(jnp.int32, (rows, per_pair * rows), 0)
    query = lax.broadcasted_iota(jnp.int32, (rows, per_pair * rows), 1) % rows
    return ((key <= query) & (key < limit)) | (key == query)


def live_mask(rows, per_pair, limit):
    return lax.broadcasted_iota(jnp.int32, (rows, per_pair * rows), 0) < limit


def nt(left, right):
    return lax.dot_general(left, right, (((1,), (1,)), ((), ())), preferred_element_type=F32)


def nn(left, right):
    return lax.dot_general(left, right, (((1,), (0,)), ((), ())), preferred_element_type=F32)


def unstack(values, per_pair, rows):
    if per_pair == 1:
        return values
    return jnp.concatenate(
        [values[h * HD : (h + 1) * HD, h * rows : (h + 1) * rows] for h in range(per_pair)], axis=0
    )


def forward_kernel(
    rows, block_rows, per_pair, lens, q_ref, k_ref, v_ref, out_ref, norm_ref, vt_ref, parts, total
):
    tile = pl.program_id(0)
    me = lens[1 + CONTS]
    tiles = q_ref.shape[0] // rows
    across = per_pair * rows

    @pl.when(tile == 0)
    def _():
        def turn(i, carry):
            at = rel_row(i, rows, block_rows, me)
            vt_ref[i] = v_ref[pl.ds(at, rows), :].T
            return carry

        lax.fori_loop(0, tiles, turn, 0)

    at = rel_row(tile, rows, block_rows, me)
    query = pair_stack(q_ref[pl.ds(at, rows), :], per_pair, jnp.asarray(0.125, BF)).T
    count, shift = walk(tile, rows)

    def folded(values):
        return values.reshape(rows // 8, 8, across)

    def scores(i):
        return nn(k_ref[pl.ds(rel_row(i, rows, block_rows, me), rows), :], query)

    def key_tile(i):
        return jnp.where(i < PROMPT // rows, i, i + shift)

    first = jnp.where(
        diagonal_mask(rows, per_pair, key_limit(lens, tile, rows)), scores(tile), NEG
    )

    def measure(i, top):
        here = key_tile(i)
        part = jnp.where(
            live_mask(rows, per_pair, key_limit(lens, here, rows)), scores(here), NEG
        )
        parts[i] = part
        return jnp.maximum(top, jnp.max(folded(part), axis=0))

    top = lax.fori_loop(0, count, measure, jnp.max(folded(first), axis=0))
    top = jnp.max(top, axis=0, keepdims=True)
    weights = jnp.exp(first - top)
    total[...] = nn(vt_ref[tile], weights.astype(BF))

    def gather(i, denom):
        weights = jnp.exp(parts[i] - top)
        total[...] += nn(vt_ref[key_tile(i)], weights.astype(BF))
        return denom + jnp.sum(folded(weights), axis=0)

    denom = lax.fori_loop(0, count, gather, jnp.sum(folded(weights), axis=0))
    denom = jnp.sum(denom, axis=0, keepdims=True)
    mixed = unstack(total[...] / denom, per_pair, rows)
    out_ref[...] = mixed.T.astype(BF)
    norm_ref[0] = top + jnp.log(denom)


def backward_kernel(
    rows, block_rows, per_pair, lens, q_ref, k_ref, v_ref, out_ref, grad_ref, norm_ref,
    dq_ref, dk_ref, dv_ref, kt_ref, dk_sum, dv_sum, dq_sum,
):
    tile = pl.program_id(0)
    me = lens[1 + CONTS]
    tiles = q_ref.shape[0] // rows

    @pl.when(tile == 0)
    def _():
        def turn(i, carry):
            at = rel_row(i, rows, block_rows, me)
            kt_ref[i] = k_ref[pl.ds(at, rows), :].T
            return carry

        lax.fori_loop(0, tiles, turn, 0)
        dk_sum[...] = jnp.zeros_like(dk_sum)
        dv_sum[...] = jnp.zeros_like(dv_sum)

    at = rel_row(tile, rows, block_rows, me)
    query = pair_stack(q_ref[pl.ds(at, rows), :], per_pair, jnp.asarray(0.125, BF))
    grad_block = grad_ref[pl.ds(at, rows), :]
    grad = pair_stack(grad_block, per_pair)
    query_turned = query.T
    grad_turned = grad.T
    product = (grad_block.astype(F32) * out_ref[pl.ds(at, rows), :].astype(F32)).T
    inner = jnp.concatenate(
        [
            jnp.sum(product[h * HD : (h + 1) * HD], axis=0, keepdims=True)
            for h in range(per_pair)
        ],
        axis=1,
    )
    norm = norm_ref[0]

    def one(key_tile, mask):
        key_at = rel_row(key_tile, rows, block_rows, me)
        keys = pl.ds(key_at, rows)
        part = jnp.where(mask, nn(k_ref[keys, :], query_turned), NEG)
        probs = jnp.exp(part - norm)
        slope = probs * (nn(v_ref[keys, :], grad_turned) - inner)
        slope_low = slope.astype(BF)
        dv_sum[keys, :] += nn(probs.astype(BF), grad)
        dk_sum[keys, :] += nn(slope_low, query)
        return nn(kt_ref[key_tile], slope_low)

    dq_sum[...] = one(tile, diagonal_mask(rows, per_pair, key_limit(lens, tile, rows)))
    count, shift = walk(tile, rows)

    def step(i, carry):
        key_tile = jnp.where(i < PROMPT // rows, i, i + shift)
        dq_sum[...] += one(key_tile, live_mask(rows, per_pair, key_limit(lens, key_tile, rows)))
        return carry

    lax.fori_loop(0, count, step, 0)
    dq_ref[...] = (unstack(dq_sum[...], per_pair, rows).T * 0.125).astype(BF)

    @pl.when(tile == tiles - 1)
    def _():
        dk_ref[...] = dk_sum[...].astype(BF)
        dv_ref[...] = dv_sum[...].astype(BF)


def attention_plan(total, heads):
    blocks = lax.axis_size("seq")
    rows = tile_rows(total, blocks)
    per_pair = 2 if heads % 2 == 0 else 1
    return rows, total // blocks, per_pair, heads // per_pair, per_pair * HD


def thirds(qkv, width, pair_width):
    per = width // pair_width
    if pair_width % 128 == 0:
        return (qkv, qkv, qkv), (0, per, 2 * per)
    return tuple(qkv[:, i * width : (i + 1) * width] for i in range(3)), (0, 0, 0)


def row_block(rows, block_rows):
    per = block_rows // rows

    def index(tile, lens):
        return ((tile // per) ^ lens[1 + CONTS]) * per + tile % per, 0

    return index


def attend_forward(lens, qkv, heads, between=None):
    total = qkv.shape[0]
    width = heads * HD
    rows, block_rows, per_pair, pairs, pair_width = attention_plan(total, heads)
    arrays, firsts = thirds(qkv, width, pair_width)
    tiles = total // rows
    most = (PROMPT + CONTLEN) // rows
    mixed = None
    norms = []
    for pair in range(pairs):

        def whole(first):
            return pl.BlockSpec((total, pair_width), lambda tile, lens: (0, first + pair))

        def kernel(lens, q_ref, k_ref, v_ref, *refs):
            forward_kernel(
                rows, block_rows, per_pair, lens, q_ref, k_ref, v_ref, *refs[mixed is not None :]
            )

        place_row = row_block(rows, block_rows)
        more = [] if mixed is None else [mixed]
        mixed, norm = pl.pallas_call(
            kernel,
            out_shape=(
                jax.ShapeDtypeStruct((total, width), BF),
                jax.ShapeDtypeStruct((tiles, 1, per_pair * rows), F32),
            ),
            grid_spec=pltpu.PrefetchScalarGridSpec(
                num_scalar_prefetch=1,
                grid=(tiles,),
                in_specs=[whole(first) for first in firsts]
                + [pl.BlockSpec(memory_space=pl.ANY)] * len(more),
                out_specs=(
                    pl.BlockSpec(
                        (rows, pair_width), lambda tile, lens: (place_row(tile, lens)[0], pair)
                    ),
                    pl.BlockSpec((1, 1, per_pair * rows), lambda tile, lens: (tile, 0, 0)),
                ),
                scratch_shapes=[
                    pltpu.VMEM((tiles, pair_width, rows), BF),
                    pltpu.VMEM((most, rows, per_pair * rows), F32),
                    pltpu.VMEM((pair_width, per_pair * rows), F32),
                ],
            ),
            input_output_aliases={4: 0} if more else {},
            cost_estimate=cost(15),
            name="attend_forward",
        )(lens, *arrays, *more)
        norms.append(norm)
        if between is not None and pair + 1 < pairs:
            lens, mixed, arrays = between(lens, mixed, arrays)
    return mixed, norms


def attend_backward(lens, qkv, mixed, norms, grad, heads, between=None):
    total = qkv.shape[0]
    width = heads * HD
    rows, block_rows, per_pair, pairs, pair_width = attention_plan(total, heads)
    arrays, firsts = thirds(qkv, width, pair_width)
    tiles = total // rows
    made = []
    for pair in range(pairs):

        def whole(first):
            return pl.BlockSpec((total, pair_width), lambda tile, lens: (0, first))

        made.append(
            pl.pallas_call(
                functools.partial(backward_kernel, rows, block_rows, per_pair),
                out_shape=(jax.ShapeDtypeStruct((total, pair_width), BF),) * 3,
                grid_spec=pltpu.PrefetchScalarGridSpec(
                    num_scalar_prefetch=1,
                    grid=(tiles,),
                    in_specs=[whole(first + pair) for first in firsts]
                    + [
                        whole(pair),
                        whole(pair),
                        pl.BlockSpec((1, 1, per_pair * rows), lambda tile, lens: (tile, 0, 0)),
                    ],
                    out_specs=(
                        pl.BlockSpec((rows, pair_width), row_block(rows, block_rows)),
                        whole(0),
                        whole(0),
                    ),
                    scratch_shapes=[
                        pltpu.VMEM((tiles, pair_width, rows), BF),
                        pltpu.VMEM((total, pair_width), F32),
                        pltpu.VMEM((total, pair_width), F32),
                        pltpu.VMEM((pair_width, per_pair * rows), F32),
                    ],
                ),
                cost_estimate=cost(18),
                name="attend_backward",
            )(lens, *arrays, mixed, grad, norms[pair])
        )
        if between is not None and pair + 1 < pairs:
            lens, made[-1], grad = between(lens, made[-1], grad)
    return made


def norm_stats(values):
    center = values - jnp.mean(values, axis=-1, keepdims=True)
    spread = jnp.mean(center * center, axis=-1, keepdims=True)
    scale = lax.rsqrt(spread + EPS)
    return center * scale, scale


def norm_pull(unit, scale, slope):
    return scale * (
        slope
        - jnp.mean(slope, axis=-1, keepdims=True)
        - unit * jnp.mean(slope * unit, axis=-1, keepdims=True)
    )


def gelu_both(values):
    square = values * values
    bent = jnp.tanh(GELU_C * (values + GELU_A * square * values))
    value = 0.5 * values * (1.0 + bent)
    slope = 0.5 * (1.0 + bent) + 0.5 * values * (1.0 - bent * bent) * GELU_C * (
        1.0 + 3.0 * GELU_A * square
    )
    return value, slope


def tn(left, right):
    return lax.dot_general(left, right, (((0,), (0,)), ((), ())), preferred_element_type=F32)


def pick(values, index, axis):
    return lax.dynamic_index_in_dim(values, index, axis, keepdims=False)


def by_core(core, mine, other, axis):
    return jnp.where(
        core == 0, jnp.stack([mine, other], axis=axis), jnp.stack([other, mine], axis=axis)
    )


def body_general(
    tokens,
    prompt_lens,
    cont_lens,
    gain_one,
    shift_one,
    w_qkv,
    bias_qv,
    w_out,
    bias_out,
    gain_two,
    shift_two,
    w_fc,
    bias_fc,
    w_proj,
    bias_proj,
    cotangent,
):
    ns = lax.axis_size("seq")
    nf = lax.axis_size("fsdp")
    nz = nf // 2
    me = lax.axis_index("seq")
    owner = lax.axis_index("fsdp")
    floor = owner // 2
    core = owner % 2
    toks, width = tokens.shape[1:]
    hidden_all = w_fc.shape[1]
    own = width // nf
    heads = H // ns
    local = width // ns
    hw = hidden_all // (nf * ns)
    cols = nz * hw

    token_block = tokens[0]
    branch = cotangent[0]

    token_blocks = plane_gather(token_block)
    vectors = [gain_one, shift_one, bias_qv, bias_out, gain_two, shift_two, bias_fc, bias_proj]
    packed = jnp.concatenate([v.reshape(-1, own) for v in vectors], axis=0)
    lines = packed.shape[0]
    packed_rows = -(-packed.size // (3 * local))
    packed = jnp.pad(packed.reshape(-1), (0, 16 * (-(-packed_rows // 16)) * 3 * local - packed.size))
    mine_qkv = pick(w_qkv.reshape(own, 3, ns, local), me, 2).reshape(own, 3 * local)
    sent_qkv = jnp.concatenate([mine_qkv, packed.reshape(-1, 3 * local)], axis=0)
    got_qkv = jnp.stack([sent_qkv] + [swap(sent_qkv, "fsdp", 2 * k) for k in range(1, nz)])
    got_qkv = xor_take(by_core(core, got_qkv, swap(got_qkv, "fsdp", 1), 1), floor, 0)
    qkv_mat = got_qkv[:, :, :own].reshape(width, 3 * local)
    small = got_qkv[:, :, own:].reshape(nf, -1)[:, : lines * own].reshape(nf, lines, own)
    at = 0
    full = []
    for v in vectors:
        count = v.shape[0] // own
        full.append(small[:, at : at + count].reshape(-1).astype(F32))
        at += count
    gain_a, shift_a, qv_vec, out_vec, gain_b, shift_b, fc_vec, proj_vec = full

    fc_cut = w_fc.reshape(own, nz, 2, ns, hw)
    fc_mine = pick(fc_cut, core, 2)
    fc_other = swap(pick(fc_cut, 1 - core, 2).reshape(own, -1), "fsdp", 1)
    fc_rows = by_core(core, fc_mine.reshape(own, -1), fc_other, 0).reshape(2 * own, nz, ns, hw)
    fc_rows = xor_take(xor_take(fc_rows, floor, 1), me, 2)
    proj_rows = xor_take(w_proj.reshape(ns, hw, width), me, 0)
    out_cols = xor_take(w_out.reshape(own, ns, local), me, 1)
    proj_parts = width // cols
    out_parts = max(1, cols // local)

    def share(q, k):
        fc = jnp.concatenate([fc_rows[:, j ^ k, q] for j in range(nz)], axis=1)
        proj = [proj_rows[q][:, i * cols : (i + 1) * cols] for i in range(proj_parts)]
        out = out_cols[:, q]
        if out_parts > 1:
            step = own // out_parts
            out = jnp.concatenate([out[i * step : (i + 1) * step] for i in range(out_parts)], axis=1)
        return fc, proj, out

    def message(k):
        fc, proj, out = share(0, k)
        return jnp.concatenate([fc, *proj, out.reshape(-1, cols)], axis=0)

    got = [swap(message(k), "fsdp", 2 * k) for k in range(1, nz)]
    rows_each = got[0].shape[0]
    planes = plane_gather(jnp.concatenate(got, axis=0))

    def parts_of(q, k):
        if k == 0:
            fc, proj, out = share(q, 0)
            return fc, jnp.concatenate(proj, axis=1), out_cols[:, q]
        block = planes[q][(k - 1) * rows_each : k * rows_each]
        fc = block[: 2 * own]
        proj = jnp.concatenate(
            [block[2 * own + i * hw : 2 * own + (i + 1) * hw] for i in range(proj_parts)], axis=1
        )
        out = block[2 * own + proj_parts * hw :]
        if out_parts > 1:
            out = jnp.concatenate(
                [out[:, i * local : (i + 1) * local] for i in range(out_parts)], axis=0
            )
        else:
            out = out.reshape(own, local)
        return fc, proj, out

    pieces = [[parts_of(q, k) for k in range(nz)] for q in range(ns)]
    out_half = jnp.stack(
        [jnp.stack([pieces[q][k][2] for q in range(ns)], axis=1) for k in range(nz)]
    )
    out_half = xor_take(out_half, me, 2).reshape(nz, own, width)
    out_both = by_core(core, out_half, swap(out_half, "fsdp", 1), 1)
    out_mat = xor_take(out_both, floor, 0).reshape(ns, local, width)
    out_mat = xor_take(out_mat, me, 0).reshape(width, width)
    fc_mat = jnp.concatenate(
        [jnp.concatenate([pieces[q][k][0] for k in range(nz)], axis=0) for q in range(ns)], axis=1
    )
    proj_mat = jnp.concatenate([pieces[q][k][1] for q in range(ns) for k in range(nz)], axis=0)
    fc_bias = pick(fc_vec.reshape(nz, 2, ns, hw), core, 1)
    fc_bias = xor_take(xor_take(fc_bias, floor, 0), me, 1).transpose(1, 0, 2).reshape(-1)

    all_tokens = jnp.concatenate(token_blocks, axis=0).astype(F32)
    unit_all, _ = norm_stats(all_tokens)
    first = (unit_all * gain_a + shift_a).astype(BF)
    bias_all = jnp.concatenate(
        [
            pick(qv_vec.reshape(2, ns, local)[0], me, 0),
            jnp.zeros((local,), F32),
            pick(qv_vec.reshape(2, ns, local)[1], me, 0),
        ]
    )
    qkv = (jnp.dot(first, qkv_mat, preferred_element_type=F32) + bias_all).astype(BF)
    lens = jnp.concatenate([prompt_lens, cont_lens[0], me.reshape(1)]).astype(jnp.int32)
    mixed_heads, norms = attend_forward(lens, qkv, heads)

    def to_tokens(values):
        return jnp.concatenate(
            [values[:toks]]
            + [swap(values[k * toks : (k + 1) * toks], "seq", k) for k in range(1, ns)],
            axis=1,
        )

    def to_heads(values):
        return jnp.concatenate(
            [values[:, :local]]
            + [swap(values[:, k * local : (k + 1) * local], "seq", k) for k in range(1, ns)],
            axis=0,
        )

    mixed = to_tokens(mixed_heads)
    hidden = token_block.astype(F32) + jnp.dot(mixed, out_mat, preferred_element_type=F32) + out_vec
    unit_two, scale_two = norm_stats(hidden)
    second = (unit_two * gain_b + shift_b).astype(BF)

    second_both = jnp.concatenate([second, swap(second, "fsdp", 1)], axis=0)
    second_both = xor_blocks(second_both, floor, nz, 1)
    branch_both = jnp.concatenate([branch, swap(branch, "fsdp", 1)], axis=0)
    pre = jnp.dot(second_both, fc_mat, preferred_element_type=F32) + fc_bias
    act_full, bend = gelu_both(pre)
    act = act_full.astype(BF)
    grad_act = nt(branch_both, proj_mat)
    grad_pre = (grad_act * bend).astype(BF)
    grad_second_both = nt(grad_pre, fc_mat)
    grad_second = grad_second_both[:toks] + swap(
        grad_second_both[toks:].astype(BF), "fsdp", 1
    ).astype(F32)
    grad_second = xor_blocks(grad_second, floor, nz, 1)
    out_sum = jnp.dot(act, proj_mat, preferred_element_type=F32)
    result = hidden + out_sum[:toks] + proj_vec
    result = result + swap(out_sum[toks:].astype(BF), "fsdp", 1).astype(F32)
    output = result.astype(BF)[None]

    grad_hidden = branch.astype(F32) + norm_pull(unit_two, scale_two, grad_second * gain_b)
    grad_attn = grad_hidden.astype(BF)
    grad_mixed = nt(grad_attn, out_mat).astype(BF)
    grad_heads = to_heads(grad_mixed)

    backward = attend_backward(lens, qkv, mixed_heads, norms, grad_heads, heads)
    grad_q, grad_k, grad_v = (
        jnp.concatenate([part[i] for part in backward], axis=1) for i in range(3)
    )
    grad_qkv = jnp.concatenate([grad_q, grad_k, grad_v], axis=1)
    grad_first_part = nt(grad_qkv, qkv_mat).astype(BF)
    grad_first = plane_scatter(
        [grad_first_part[k * toks : (k + 1) * toks] for k in range(ns)]
    )
    unit_one, scale_one = norm_stats(token_block.astype(F32))
    input_grad = (grad_hidden + norm_pull(unit_one, scale_one, grad_first * gain_a))[None]

    span = nz * hw
    grad_fc = [tn(second_both, grad_pre[:, q * span : (q + 1) * span]).astype(BF) for q in range(ns)]
    grad_proj = [tn(act[:, q * span : (q + 1) * span], branch_both).astype(BF) for q in range(ns)]
    fc_sum = plane_scatter(grad_fc)
    proj_sum = plane_scatter(grad_proj)

    def fc_for(k):
        block = fc_sum[k * 2 * own : (k + 1) * 2 * own].reshape(2 * own, nz, hw)
        return jnp.concatenate([block[:, j ^ k] for j in range(nz)], axis=1)

    def proj_for(k):
        block = proj_sum[k * hw : (k + 1) * hw]
        return jnp.concatenate(
            [block[:, i * span : (i + 1) * span] for i in range(proj_parts)], axis=0
        )

    both_sum = jnp.concatenate([fc_for(0), proj_for(0)], axis=0)
    for k in range(1, nz):
        sent = jnp.concatenate([fc_for(k), proj_for(k)], axis=0).astype(BF)
        both_sum = both_sum + swap(sent, "fsdp", 2 * k).astype(F32)
    fc_owned = both_sum[: 2 * own].reshape(2, own, span)
    fc_kept = pick(fc_owned, core, 0).astype(BF)
    fc_moved = swap(pick(fc_owned, 1 - core, 0).astype(BF), "fsdp", 1)
    final = jnp.concatenate([fc_kept, fc_moved, both_sum[2 * own :].astype(BF)], axis=0)
    finals = plane_gather(final)
    fc_kept_all = jnp.stack([v[:own].reshape(own, nz, hw) for v in finals], axis=2)
    fc_moved_all = jnp.stack([v[own : 2 * own].reshape(own, nz, hw) for v in finals], axis=2)
    grad_w_fc = by_core(core, fc_kept_all, fc_moved_all, 2)
    grad_w_fc = xor_take(xor_take(grad_w_fc, floor, 1), me, 3).reshape(own, hidden_all).astype(F32)
    grad_w_proj = jnp.stack(
        [
            jnp.concatenate(
                [v[2 * own + i * hw : 2 * own + (i + 1) * hw] for i in range(proj_parts)], axis=1
            )
            for v in finals
        ]
    )
    grad_w_proj = xor_take(grad_w_proj, me, 0).reshape(ns * hw, width).astype(F32)

    grad_out = tn(mixed, grad_attn).astype(BF).reshape(ns, local, width)
    grad_out = xor_take(grad_out, me, 0).reshape(nz, 2, own, width)
    grad_out = xor_take(grad_out, floor, 0)
    out_kept = pick(grad_out, core, 1).astype(F32) + swap(
        pick(grad_out, 1 - core, 1), "fsdp", 1
    ).astype(F32)
    out_owned = out_kept[0]
    for k in range(1, nz):
        out_owned = out_owned + swap(out_kept[k].astype(BF), "fsdp", 2 * k).astype(F32)
    bit = 1
    while bit < ns:
        out_owned = out_owned + swap(out_owned.astype(BF), "seq", bit).astype(F32)
        bit *= 2
    grad_w_out = out_owned

    grad_in = tn(first, grad_qkv).astype(BF).reshape(nz, 2, own, 3 * local)
    grad_in = xor_take(grad_in, floor, 0)
    in_kept = pick(grad_in, core, 1).astype(F32) + swap(
        pick(grad_in, 1 - core, 1), "fsdp", 1
    ).astype(F32)
    in_owned = in_kept[0]
    for k in range(1, nz):
        in_owned = in_owned + swap(in_kept[k].astype(BF), "fsdp", 2 * k).astype(F32)
    in_owned = in_owned.astype(BF)
    in_blocks = jnp.stack(
        [in_owned.reshape(own, 3, local)]
        + [swap(in_owned, "seq", k).reshape(own, 3, local) for k in range(1, ns)],
        axis=2,
    )
    grad_w_qkv = xor_take(in_blocks, me, 2).reshape(own, 3 * width).astype(F32)

    def placed(values, parts):
        slots = jnp.arange(parts)[:, None] == me
        return jnp.where(slots, values[None, :], 0.0).reshape(-1)

    part_f32 = grad_first_part.astype(F32)
    fc_bias_grad = jnp.sum(grad_pre.astype(F32), axis=0).reshape(ns, nz, hw).transpose(1, 0, 2)
    fc_bias_grad = xor_take(xor_take(fc_bias_grad, floor, 0), me, 1)
    fc_bias_grad = jnp.where(
        (jnp.arange(2) == core)[None, :, None, None], fc_bias_grad[:, None], 0.0
    ).reshape(-1)
    vector_grads = [
        jnp.sum(part_f32 * unit_all, axis=0),
        jnp.sum(part_f32, axis=0),
        placed(jnp.sum(grad_q.astype(F32), axis=0), ns),
        placed(jnp.sum(grad_v.astype(F32), axis=0), ns),
        jnp.sum(grad_attn.astype(F32), axis=0),
        jnp.sum(grad_second * unit_two, axis=0),
        jnp.sum(grad_second, axis=0),
        fc_bias_grad,
        jnp.sum(branch.astype(F32), axis=0),
    ]
    vector_sum = jnp.concatenate([v.reshape(-1, width) for v in vector_grads], axis=0)
    for axis, size in (("seq", ns), ("fsdp", nf)):
        bit = 1
        while bit < size:
            vector_sum = vector_sum + swap(vector_sum, axis, bit)
            bit *= 2
    vector_sum = vector_sum.reshape(-1)
    outs = []
    at = 0
    for v in vectors:
        count = v.shape[0]
        outs.append(lax.dynamic_slice_in_dim(vector_sum, at + owner * count, count))
        at += nf * count
    (g_gain_one, g_shift_one, g_bias_qv, g_bias_out, g_gain_two, g_shift_two, g_bias_fc, g_bias_proj) = outs

    return (
        output,
        input_grad,
        g_gain_one,
        g_shift_one,
        grad_w_qkv,
        g_bias_qv,
        grad_w_out,
        g_bias_out,
        g_gain_two,
        g_shift_two,
        grad_w_fc,
        g_bias_fc,
        grad_w_proj,
        g_bias_proj,
    )


UPPER = (0, 2, 1, 3)


def hidden_at(q, half, size):
    return half * 4 * size + (UPPER[q] if half == 0 else q) * size


def start_all(copies, sems):
    made = [
        pltpu.make_async_copy(source, target, sems.at[i]) for i, (source, target) in enumerate(copies)
    ]
    for copy in made:
        copy.start()
    return made


def aligned(value, size):
    return pl.multiple_of(value, size)


def pack_kernel(hw, place, fc_ref, proj_ref, out_mat_ref, mine_ref, other_ref, share_ref):
    me, core = place[0], place[2]
    for q in range(4):
        for z in range(4):
            target = hidden_at(q, z // 2, 2 * hw) + (z % 2) * hw
            for out_ref, which in ((mine_ref, core), (other_ref, 1 - core)):
                source = aligned(z * 8 * hw + which * 4 * hw + (me ^ q) * hw, hw)
                out_ref[:, target : target + hw] = fc_ref[:, pl.ds(source, hw)]
    share_ref[...] = proj_ref[...]
    other_ref[:, 16 * hw :] = out_mat_ref[...]


def pack(place, w_fc, w_proj, w_out):
    own, hidden_all = w_fc.shape
    hw, width = w_proj.shape[0] // 4, w_proj.shape[1]

    def whole(shape):
        return pl.BlockSpec(shape, lambda i, place: (0, 0))

    half = jax.ShapeDtypeStruct((own, hidden_all // 2), BF)
    more = jax.ShapeDtypeStruct((own, hidden_all // 2 + width), BF)
    return pl.pallas_call(
        functools.partial(pack_kernel, hw),
        out_shape=(half, more, jax.ShapeDtypeStruct((hw, width), BF)),
        grid_spec=pltpu.PrefetchScalarGridSpec(
            num_scalar_prefetch=1,
            grid=(1,),
            in_specs=[
                whole((own, hidden_all)),
                pl.BlockSpec((hw, width), lambda i, place: (place[0], 0)),
                whole(w_out.shape),
            ],
            out_specs=(whole(half.shape), whole(more.shape), whole((hw, width))),
        ),
        cost_estimate=cost(3),
        name="pack_shares",
    )(place, w_fc, w_proj, w_out)


def join_kernel(place, m0, m1, o0, o1, mine_out, l0, l1, out_ref):
    core = place[2]
    own, chunk = m0.shape
    part = mine_out.shape[0]
    for refs, which in (((m0, m1), core), ((o0, o1), 1 - core)):
        rows = pl.ds(aligned(which * own, own), own)
        for half in range(2):
            out_ref[rows, half * chunk : (half + 1) * chunk] = refs[half][...]
    wide = 2 * chunk
    for parts, which in (
        ((mine_out[:, :wide], mine_out[:, wide:]), core),
        ((l0[...], l1[...]), 1 - core),
    ):
        for half in range(2):
            rows = pl.ds(aligned(2 * own + which * 2 * part + half * part, part), part)
            out_ref[rows, :] = parts[half]


def join(place, mine, other, w_out):
    own, hidden = mine.shape
    chunk = hidden // 8
    part = own // 4
    rows = 2 * own + 4 * part
    pieces = [
        pl.BlockSpec((own, chunk), lambda i, place, at=hidden_at(0, half, 1): (0, at))
        for half in range(2)
    ]
    quarters = [
        pl.BlockSpec((part, 2 * chunk), lambda i, place, at=4 + half: (place[0], at))
        for half in range(2)
    ]
    return pl.pallas_call(
        join_kernel,
        out_shape=jax.ShapeDtypeStruct((rows, 2 * chunk), BF),
        grid_spec=pltpu.PrefetchScalarGridSpec(
            num_scalar_prefetch=1,
            grid=(1,),
            in_specs=pieces * 2
            + [pl.BlockSpec((part, w_out.shape[1]), lambda i, place: (place[0], 0))]
            + quarters,
            out_specs=pl.BlockSpec((rows, 2 * chunk), lambda i, place: (0, 0)),
        ),
        cost_estimate=cost(2),
        name="join_rows",
    )(place, mine, mine, other, other, w_out, other, other)


def joined_kernel(*refs):
    at = 0
    for ref in refs[:-1]:
        refs[-1][at : at + ref.shape[0], :] = ref[...]
        at += ref.shape[0]


def joined(parts):
    rows = sum(part.shape[0] for part in parts)
    return pl.pallas_call(
        joined_kernel,
        out_shape=jax.ShapeDtypeStruct((rows, parts[0].shape[1]), parts[0].dtype),
        cost_estimate=cost(1),
        name="joined",
    )(*parts)


def project_kernel(
    place, own_ref, one_ref, two_ref, up_ref, low_ref, kept_ref, moved_ref, gain_ref, shift_ref,
    bias_ref, first_ref, unit_ref, qkv_ref, turned_ref, toks, mat, sems,
):
    step = pl.program_id(0)
    floor, core = place[1], place[2]
    block = own_ref.shape[0]
    half = block // 2
    own = mat.shape[0] // 8

    def copies():
        made = [
            (own_ref, toks.at[pl.ds(0, block), :]),
            (one_ref, toks.at[pl.ds(block, block), :]),
            (two_ref, toks.at[pl.ds(2 * block, block), :]),
            (up_ref, toks.at[pl.ds(3 * block, half), :]),
            (low_ref, toks.at[pl.ds(3 * block + half, half), :]),
        ]
        for k in range(4):
            for ref, which in ((kept_ref, core), (moved_ref, 1 - core)):
                row = aligned((floor ^ k) * 2 * own + which * own, own)
                made.append((ref.at[k, pl.ds(0, own), :], mat.at[pl.ds(row, own), :]))
        return made

    @pl.when(step == 0)
    def _():
        for copy in start_all(copies(), sems):
            copy.wait()

    rows = first_ref.shape[0]
    values = toks[pl.ds(aligned(step * rows, rows), rows), :].astype(F32)
    unit, _ = norm_stats(values)
    first = (unit * gain_ref[...] + shift_ref[...]).astype(BF)
    first_ref[...] = first
    unit_ref[...] = unit.astype(BF)
    qkv_ref[...] = (nn(first, mat[...]) + bias_ref[...]).astype(BF)

    @pl.when(step == pl.num_programs(0) - 1)
    def _():
        turned_ref[...] = mat[...].T


def project(place, blocks, kept, moved, gain, shift, bias):
    block, width = blocks[0].shape
    outs = kept.shape[2]
    total = 4 * block
    rows = 256
    raw = pl.BlockSpec(memory_space=pl.ANY)

    def line(size):
        return pl.BlockSpec((1, size), lambda i, place: (0, 0))

    def tile(size):
        return pl.BlockSpec((rows, size), lambda i, place: (i, 0))

    return pl.pallas_call(
        project_kernel,
        out_shape=(
            jax.ShapeDtypeStruct((total, width), BF),
            jax.ShapeDtypeStruct((total, width), BF),
            jax.ShapeDtypeStruct((total, outs), BF),
            jax.ShapeDtypeStruct((outs, width), BF),
        ),
        grid_spec=pltpu.PrefetchScalarGridSpec(
            num_scalar_prefetch=1,
            grid=(total // rows,),
            in_specs=[raw] * 7 + [line(width), line(width), line(outs)],
            out_specs=(
                tile(width),
                tile(width),
                tile(outs),
                pl.BlockSpec((outs, width), lambda i, place: (0, 0)),
            ),
            scratch_shapes=[
                pltpu.VMEM((total, width), BF),
                pltpu.VMEM((width, outs), BF),
                pltpu.SemaphoreType.DMA((13,)),
            ],
        ),
        cost_estimate=cost(12),
        name="project",
    )(place, *blocks, kept, moved, gain, shift, bias)


def attn_out_kernel(part, place, *refs):
    mixed_refs, (mine_ref, other_ref), shares = refs[:4], refs[4:6], refs[6:10]
    token_ref, bias_ref, gain_ref, shift_ref = refs[10:14]
    hidden_ref, second_ref, mixed_ref, mat_ref, mixed, sems = refs[14:]
    step = pl.program_id(0)
    me, floor, core = place[0], place[1], place[2]
    local = mixed_refs[0].shape[1]
    own, width = mine_ref.shape
    block = mixed.shape[0]
    wide = width // 2
    rows_each = 2 * own + 4 * part

    @pl.when(step == 0)
    def _():
        made = []
        for k, ref in enumerate(mixed_refs):
            lanes = pl.ds(aligned((me ^ k) * local, local), local)
            made.append((ref.at[pl.ds(0, block), :], mixed.at[:, lanes]))
        for source, which in (
            (mine_ref, core),
            (other_ref.at[:, pl.ds(other_ref.shape[1] - width, width)], 1 - core),
        ):
            row = aligned(floor * 2 * own + which * own, own)
            made.append((source, mat_ref.at[pl.ds(row, own), :]))
        for q in range(4):
            for k in range(1, 4):
                for which in range(2):
                    row = aligned((floor ^ k) * 2 * own + which * own + (me ^ q) * part, part)
                    for half in range(2):
                        at = (k - 1) * rows_each + 2 * own + which * 2 * part + half * part
                        made.append(
                            (
                                shares[q].at[pl.ds(at, part), :],
                                mat_ref.at[pl.ds(row, part), pl.ds(half * wide, wide)],
                            )
                        )
        for copy in start_all(made, sems):
            copy.wait()

    rows = hidden_ref.shape[0]
    here = mixed[pl.ds(aligned(step * rows, rows), rows), :]
    mixed_ref[...] = here
    hidden = token_ref[...].astype(F32) + nn(here, mat_ref[...]) + bias_ref[...]
    hidden_ref[...] = hidden
    unit, _ = norm_stats(hidden)
    second_ref[...] = (unit * gain_ref[...] + shift_ref[...]).astype(BF)


def attn_out(place, mixed, mine, other, shares, tokens, bias, gain, shift):
    block, width = tokens.shape
    rows = 256
    raw = pl.BlockSpec(memory_space=pl.ANY)
    line = pl.BlockSpec((1, width), lambda i, place: (0, 0))
    tile = pl.BlockSpec((rows, width), lambda i, place: (i, 0))
    return pl.pallas_call(
        functools.partial(attn_out_kernel, mine.shape[0] // 4),
        out_shape=(
            jax.ShapeDtypeStruct((block, width), F32),
            jax.ShapeDtypeStruct((block, width), BF),
            jax.ShapeDtypeStruct((block, width), BF),
            jax.ShapeDtypeStruct((width, width), BF),
        ),
        grid_spec=pltpu.PrefetchScalarGridSpec(
            num_scalar_prefetch=1,
            grid=(block // rows,),
            in_specs=[raw] * 10 + [tile, line, line, line],
            out_specs=(tile, tile, tile, pl.BlockSpec((width, width), lambda i, place: (0, 0))),
            scratch_shapes=[pltpu.VMEM((block, width), BF), pltpu.SemaphoreType.DMA((54,))],
        ),
        cost_estimate=cost(7),
        name="attn_out",
    )(place, *mixed, mine, other, *shares, tokens, bias, gain, shift)


def feed_kernel(
    hw, place, second_oth, second_own, branch_oth, branch_own, bias_a, bias_b, mine_ref, other_ref,
    a0, a1, a2, a3, proj_ref, b0, b1, b2, b_up, b_low, act_a, act_b, slope_a, slope_b, out_own, out_oth, back_own, back_oth, sum_a, sum_b,
    fc, proj, fc_turned, proj_turned, total, back, sems,
):
    step = pl.program_id(0)
    me, floor, core = place[0], place[1], place[2]
    own = mine_ref.shape[0]
    chunk = 2 * hw
    rows_each = a0.shape[0] // 3

    def copies(q):
        made = []
        for ref, which in ((mine_ref, core), (other_ref, 1 - core)):
            row = aligned(floor * 2 * own + which * own, own)
            for half in range(2):
                made.append(
                    (
                        ref.at[:, pl.ds(hidden_at(q, half, chunk), chunk)],
                        fc.at[q, pl.ds(row, own), pl.ds(half * chunk, chunk)],
                    )
                )
        for k in range(1, 4):
            row = aligned((floor ^ k) * 2 * own, 2 * own)
            source = (a0, a1, a2, a3)[q].at[pl.ds((k - 1) * rows_each, 2 * own), :]
            made.append((source, fc.at[q, pl.ds(row, 2 * own), :]))
        cut = hw // 2
        for k in range(4):
            row = aligned((floor ^ k) * hw, hw)
            if k == 0:
                made.append((proj_ref.at[pl.ds(aligned((me ^ q) * hw, hw), hw), :], proj.at[q, pl.ds(row, hw), :]))
            elif q < 3:
                source = (b0, b1, b2)[q].at[pl.ds((k - 1) * hw, hw), :]
                made.append((source, proj.at[q, pl.ds(row, hw), :]))
            else:
                for i in range(2):
                    at = (k - 1) * hw + i * cut
                    source = (b_up if at < 3 * cut else b_low).at[pl.ds(at % (3 * cut), cut), :]
                    made.append((source, proj.at[q, pl.ds(aligned(row + i * cut, cut), cut), :]))
        return [
            pltpu.make_async_copy(source, target, sems.at[q, i])
            for i, (source, target) in enumerate(made)
        ]

    @pl.when(step == 0)
    def _():
        for q in range(4):
            for copy in copies(q):
                copy.start()

    for q in range(4):

        @pl.when(step == q)
        def _():
            for copy in copies(q):
                copy.wait()

    fc_turned[...] = fc[step].T
    proj_turned[...] = proj[step].T
    bias = jnp.concatenate([bias_a[...], bias_b[...]], axis=1)
    rows = second_own.shape[0]
    both = 2 * rows
    partial = None
    for start, second_ref, branch_ref in ((0, second_oth, branch_oth), (rows, second_own, branch_own)):
        here = slice(start, start + rows)
        pre = nn(second_ref[...], fc[step]) + bias
        value, bend = gelu_both(pre)
        act = value.astype(BF)
        act_a[here, :] = act[:, :chunk]
        act_b[here, :] = act[:, chunk:]
        slope_full = nn(branch_ref[...], proj_turned[...]) * bend
        slope = slope_full.astype(BF)
        slope_a[here, :] = slope[:, :chunk]
        slope_b[here, :] = slope[:, chunk:]
        more = jnp.sum(slope_full, axis=0, keepdims=True)
        partial = more if partial is None else partial + more
        out_part = nn(act, proj[step])
        back_part = nn(slope, fc_turned[...])

        @pl.when(step == 0)
        def _():
            total[here, :] = out_part
            back[here, :] = back_part

        @pl.when(step > 0)
        def _():
            total[here, :] += out_part
            back[here, :] += back_part

    sum_a[...] = partial[:, :chunk]
    sum_b[...] = partial[:, chunk:]

    @pl.when(step == 3)
    def _():
        half = both // 2
        out_oth[...] = total[:half].astype(BF)
        back_oth[...] = back[:half].astype(BF)
        out_own[...] = total[half:]
        back_own[...] = back[half:]


def feed(place, second, branch, bias, mine, other, shares, w_proj, proj_shares):
    both, width = 2 * second[0].shape[0], second[0].shape[1]
    hidden = mine.shape[1]
    hw = hidden // 16
    chunk = 2 * hw
    raw = pl.BlockSpec(memory_space=pl.ANY)

    def whole(height):
        return pl.BlockSpec((height, width), lambda i, place: (0, 0))

    def upper(height):
        return pl.BlockSpec((height, chunk), lambda i, place: (0, (i % 2) * 2 + i // 2))

    def lower(height, first=0):
        return pl.BlockSpec((height, chunk), lambda i, place: (0, first + i))

    half = jax.ShapeDtypeStruct((both, hidden // 2), BF)
    line = jax.ShapeDtypeStruct((1, hidden // 2), F32)
    return pl.pallas_call(
        functools.partial(feed_kernel, hw),
        out_shape=(
            half,
            half,
            half,
            half,
            jax.ShapeDtypeStruct((both // 2, width), F32),
            jax.ShapeDtypeStruct((both // 2, width), BF),
            jax.ShapeDtypeStruct((both // 2, width), F32),
            jax.ShapeDtypeStruct((both // 2, width), BF),
            line,
            line,
        ),
        grid_spec=pltpu.PrefetchScalarGridSpec(
            num_scalar_prefetch=1,
            grid=(4,),
            in_specs=[whole(both // 2)] * 4 + [upper(1), lower(1, 4)] + [raw] * 12,
            out_specs=(upper(both), lower(both), upper(both), lower(both))
            + (whole(both // 2),) * 4
            + (upper(1), lower(1)),
            scratch_shapes=[
                pltpu.VMEM((4, width, 2 * chunk), BF),
                pltpu.VMEM((4, 2 * chunk, width), BF),
                pltpu.VMEM((2 * chunk, width), BF),
                pltpu.VMEM((width, 2 * chunk), BF),
                pltpu.VMEM((both, width), F32),
                pltpu.VMEM((both, width), F32),
                pltpu.SemaphoreType.DMA((4, 14)),
            ],
        ),
        cost_estimate=cost(35),
        name="feed",
    )(place, *second, *branch, bias, bias, mine, other, *shares, w_proj, *proj_shares)


def mixed_back_kernel(
    place, own_ref, oth_ref, hidden_ref, branch_ref, gain_ref, mat_ref,
    full_ref, low_ref, g0, g1, g2, g3, sums_ref,
):
    step = pl.program_id(0)
    me = place[0]
    local = g0.shape[1]
    slope = own_ref[...] + oth_ref[...].astype(F32)
    unit, scale = norm_stats(hidden_ref[...])
    full = branch_ref[...].astype(F32) + norm_pull(unit, scale, slope * gain_ref[...])
    low = full.astype(BF)
    full_ref[...] = full
    low_ref[...] = low
    for k, ref in enumerate((g0, g1, g2, g3)):
        rows = pl.ds(aligned((me ^ k) * local, local), local)
        ref[...] = nt(low, mat_ref[rows, :]).astype(BF)
    sums = jnp.concatenate(
        [
            jnp.sum(low.astype(F32), axis=0, keepdims=True),
            jnp.sum(slope * unit, axis=0, keepdims=True),
            jnp.sum(slope, axis=0, keepdims=True),
            jnp.sum(branch_ref[...].astype(F32), axis=0, keepdims=True),
        ],
        axis=0,
    )

    @pl.when(step == 0)
    def _():
        sums_ref[...] = sums

    @pl.when(step > 0)
    def _():
        sums_ref[...] += sums


def mixed_back(place, own, oth, hidden, branch, gain, mat):
    block, width = own.shape
    local = width // 4
    rows = block

    def tile(size):
        return pl.BlockSpec((rows, size), lambda i, place: (i, 0))

    def whole(height):
        return pl.BlockSpec((height, width), lambda i, place: (0, 0))

    return pl.pallas_call(
        mixed_back_kernel,
        out_shape=(
            jax.ShapeDtypeStruct((block, width), F32),
            jax.ShapeDtypeStruct((block, width), BF),
        )
        + (jax.ShapeDtypeStruct((block, local), BF),) * 4
        + (jax.ShapeDtypeStruct((4, width), F32),),
        grid_spec=pltpu.PrefetchScalarGridSpec(
            num_scalar_prefetch=1,
            grid=(block // rows,),
            in_specs=[tile(width)] * 4 + [whole(1), whole(width)],
            out_specs=(tile(width), tile(width)) + (tile(local),) * 4 + (whole(4),),
        ),
        cost_estimate=cost(7),
        name="mixed_back",
    )(place, own, oth, hidden, branch, gain, mat)


def first_back_kernel(tiles, parts, place, *refs):
    step = pl.program_id(0)
    count = len(tiles) // 2
    grad_refs, (unit_ref, mat_ref), refs = refs[:parts], refs[parts : parts + 2], refs[parts + 2 :]
    out_refs, sums_ref = refs[:count], refs[count]
    part = nn(jnp.concatenate([ref[...] for ref in grad_refs], axis=1), mat_ref[...])
    low = part.astype(BF)
    for i in range(count):

        @pl.when(step // 2 == i)
        def _():
            out_refs[i][...] = low

    sums = jnp.concatenate(
        [
            jnp.sum(part * unit_ref[...].astype(F32), axis=0, keepdims=True),
            jnp.sum(part, axis=0, keepdims=True),
        ],
        axis=0,
    )

    @pl.when(step == 0)
    def _():
        sums_ref[...] = sums

    @pl.when(step > 0)
    def _():
        sums_ref[...] += sums


def first_back(tiles, grads, unit, mat):
    outs, width = mat.shape
    rows = 256
    table = jnp.asarray(tiles, jnp.int32)

    def at(i, place):
        return (place[i], 0)

    return pl.pallas_call(
        functools.partial(first_back_kernel, tiles, len(grads)),
        out_shape=tuple(jax.ShapeDtypeStruct((2 * rows, width), BF) for _ in tiles[::2])
        + (jax.ShapeDtypeStruct((2, width), F32),),
        grid_spec=pltpu.PrefetchScalarGridSpec(
            num_scalar_prefetch=1,
            grid=(len(tiles),),
            in_specs=[pl.BlockSpec((rows, grad.shape[1]), at) for grad in grads]
            + [
                pl.BlockSpec((rows, width), at),
                pl.BlockSpec((outs, width), lambda i, place: (0, 0)),
            ],
            out_specs=tuple(
                pl.BlockSpec((rows, width), lambda i, place, g=g: (jnp.clip(i - 2 * g, 0, 1), 0))
                for g in range(len(tiles) // 2)
            )
            + (pl.BlockSpec((2, width), lambda i, place: (0, 0)),),
        ),
        cost_estimate=cost(5),
        name="first_back",
    )(table, *grads, unit, mat)


def gather_fc_kernel(place, fa, xa, la, fb, yb, lb, o0, o1, o2, o3, fc):
    floor = place[1]
    chunk = fc.shape[1] // 2
    fc[:, :chunk] = fa[...].astype(F32) + xa[...].astype(F32) + la[...].astype(F32)
    fc[:, chunk:] = fb[...].astype(F32) + yb[...].astype(F32) + lb[...].astype(F32)
    rows = fc.shape[0] // 4
    for k, out in enumerate((o0, o1, o2, o3)):
        out[...] = fc[pl.ds(aligned((floor ^ k) * rows, rows), rows), :].astype(BF)


def gather_proj_kernel(place, pa, xp, lpa, pb, yp, lpb, o0, o1, o2, o3, proj):
    floor = place[1]
    chunk = proj.shape[0] // 2
    proj[:chunk, :] = pa[...].astype(F32) + xp[...].astype(F32) + lpa[...].astype(F32)
    proj[chunk:, :] = pb[...].astype(F32) + yp[...].astype(F32) + lpb[...].astype(F32)
    rows = proj.shape[0] // 4
    for k, out in enumerate((o0, o1, o2, o3)):
        out[...] = proj[pl.ds(aligned((floor ^ k) * rows, rows), rows), :].astype(BF)


def gather_sum(place, kernel, parts, shape, block):
    out = jax.ShapeDtypeStruct((shape[0] // 4, shape[1]), BF)
    return pl.pallas_call(
        kernel,
        out_shape=(out,) * 4,
        grid_spec=pltpu.PrefetchScalarGridSpec(
            num_scalar_prefetch=1,
            grid=(1,),
            in_specs=[pl.BlockSpec(block, lambda i, place: (0, 0))] * 6,
            out_specs=(pl.BlockSpec(out.shape, lambda i, place: (0, 0)),) * 4,
            scratch_shapes=[pltpu.VMEM(shape, F32)],
        ),
        cost_estimate=cost(3),
        name="gather_sum",
    )(place, *parts)


def spread_fc_kernel(place, *refs):
    me, core = place[0], place[2]
    finals, fc_ref = refs[:4], refs[4]
    own = fc_ref.shape[0]
    hw = finals[0].shape[1] // 4
    for q in range(4):
        for part, which in ((0, core), (1, 1 - core)):
            for z in range(4):
                lanes = pl.ds(aligned(z * 8 * hw + which * 4 * hw + (me ^ q) * hw, hw), hw)
                block = finals[q][part * own : (part + 1) * own, z * hw : (z + 1) * hw]
                fc_ref[:, lanes] = block.astype(F32)


def spread_proj_kernel(place, *refs):
    me = place[0]
    finals, proj_ref = refs[:4], refs[4]
    hw = finals[0].shape[0]
    for q in range(4):
        proj_ref[pl.ds(aligned((me ^ q) * hw, hw), hw), :] = finals[q][...].astype(F32)


def spread(place, kernel, finals, shape):
    def whole(shape):
        return pl.BlockSpec(shape, lambda i, place: (0, 0))

    return pl.pallas_call(
        kernel,
        out_shape=jax.ShapeDtypeStruct(shape, F32),
        grid_spec=pltpu.PrefetchScalarGridSpec(
            num_scalar_prefetch=1,
            grid=(1,),
            in_specs=[whole(finals[0].shape)] * 4,
            out_specs=whole(shape),
        ),
        cost_estimate=cost(2),
        name="spread",
    )(place, *finals)


def last_kernel(
    keep_ref, got_x, got_y, last_y, last_x, token_ref, hidden_ref, gain_ref, out_ref
):
    def finish(got, last):
        slope = keep_ref[...].astype(F32) + got[...].astype(F32) + last[...].astype(F32)
        unit, scale = norm_stats(token_ref[...].astype(F32))
        out_ref[...] = hidden_ref[...] + norm_pull(unit, scale, slope * gain_ref[...])

    @pl.when(pl.program_id(0) == 0)
    def _():
        finish(got_x, last_y)

    @pl.when(pl.program_id(0) == 1)
    def _():
        finish(got_y, last_x)


def body_aligned(
    tokens,
    prompt_lens,
    cont_lens,
    gain_one,
    shift_one,
    w_qkv,
    bias_qv,
    w_out,
    bias_out,
    gain_two,
    shift_two,
    w_fc,
    bias_fc,
    w_proj,
    bias_proj,
    cotangent,
):
    ns = nz = 4
    nf = 8
    me = lax.axis_index("seq")
    owner = lax.axis_index("fsdp")
    floor = owner // 2
    core = owner % 2
    place = jnp.stack([me, floor, core]).astype(jnp.int32)
    toks, width = tokens.shape[1:]
    own = width // nf
    heads = H // ns
    local = width // ns
    hw = w_fc.shape[1] // (nf * ns)
    token_block = tokens[0]
    branch = cotangent[0]

    half = toks // 2
    vectors = [gain_one, shift_one, bias_qv, bias_out, gain_two, shift_two, bias_fc, bias_proj]
    packed = jnp.concatenate([v.reshape(-1, own) for v in vectors], axis=0)
    lines = packed.shape[0]
    packed = jnp.pad(packed.reshape(-1), (0, 16 * 3 * local - packed.size)).reshape(16, 3 * local)
    mine_qkv = pick(w_qkv.reshape(own, 3, ns, local), me, 2).reshape(own, 3 * local)
    sent_qkv = jnp.concatenate([mine_qkv, packed], axis=0)
    tok_one = swap(token_block, "seq", 1)
    tok_two = swap(token_block, "seq", 2)
    got_qkv = [swap(sent_qkv, "fsdp", 2 * k) for k in range(1, nz)]
    fc_mine, fc_sent, proj_share = pack(place, after(w_fc, sent_qkv), w_proj, w_out)
    fc_other = swap(fc_sent, "fsdp", 1)
    fc_share = join(place, fc_mine, fc_other, w_out)

    tok_one, tok_two, got_qkv, fc_share, proj_share = lax.optimization_barrier(
        (tok_one, tok_two, got_qkv, fc_share, proj_share)
    )
    tok_up = swap(tok_two[:half], "seq", 1)
    tok_low = swap(tok_one[half:], "seq", 2)
    kept_qkv = jnp.stack([sent_qkv, *got_qkv])
    moved_qkv = swap(kept_qkv, "fsdp", 1)
    moved_qkv, fc_share = lax.optimization_barrier((moved_qkv, fc_share))
    fc_got = [swap(fc_share, "fsdp", 2 * k) for k in range(1, nz)]

    small = by_core(core, kept_qkv[:, own : own + 2], moved_qkv[:, own : own + 2], 1)
    small = xor_take(small, floor, 0).reshape(nf, -1).reshape(nf, lines, own)
    at = 0
    full = []
    for v in vectors:
        count = v.shape[0] // own
        full.append(small[:, at : at + count].reshape(1, -1).astype(F32))
        at += count
    gain_a, shift_a, qv_vec, out_vec, gain_b, shift_b, fc_vec, proj_vec = full
    qv_mine = pick(qv_vec.reshape(2, ns, local), me, 1)
    bias_all = jnp.concatenate([qv_mine[0], jnp.zeros((local,), F32), qv_mine[1]]).reshape(1, -1)
    fc_bias = xor_take(pick(fc_vec.reshape(nz, 2, ns, hw), core, 1), me, 1)
    order = [(q, 0) for q in (0, 2, 1, 3)] + [(q, 1) for q in range(4)]
    fc_bias = jnp.concatenate(
        [fc_bias[2 * part : 2 * part + 2, q].reshape(1, -1) for q, part in order], axis=1
    )

    first, unit_all, qkv, qkv_turned = project(
        place, (token_block, tok_one, tok_two, tok_up, tok_low), kept_qkv, moved_qkv, gain_a, shift_a,
        bias_all,
    )
    lens = jnp.concatenate([prompt_lens, cont_lens[0], me.reshape(1)]).astype(jnp.int32)

    qkv, fc_got, proj_share = lax.optimization_barrier((qkv, fc_got, proj_share))
    fc_zero = joined(fc_got)
    fc_one = swap(fc_zero, "seq", 1)
    fc_two = swap(fc_zero, "seq", 2)
    proj_got = [swap(proj_share, "fsdp", 2 * k) for k in range(1, nz)]
    ends = {}

    def between(lens, mixed, arrays):
        (mixed, arrays, one, two, got, ends["branch"]) = lax.optimization_barrier(
            (mixed, arrays, fc_one, fc_two, proj_got, branch)
        )
        ends["branch_got"] = swap(ends["branch"], "fsdp", 1)
        cut = one.shape[0] // 2
        ends["fc"] = (one, two, swap(two[:cut], "seq", 1), swap(one[cut:], "seq", 2))
        zero = joined(got)
        ends["proj"] = (zero, swap(zero, "seq", 1), swap(zero, "seq", 2))
        return lens, mixed, arrays

    mixed_heads, norms = attend_forward(lens, qkv, heads, between)
    fc_one, fc_two, fc_up, fc_low = ends["fc"]
    proj_zero, proj_one, proj_two = ends["proj"]

    mixed_heads, fc_up, fc_low, proj_one, proj_two, branch_got = lax.optimization_barrier(
        (mixed_heads, fc_up, fc_low, proj_one, proj_two, ends["branch_got"])
    )
    branch_both = jnp.concatenate([branch_got, branch], axis=0)
    mixed_blocks = [mixed_heads] + [
        swap(mixed_heads[k * toks : (k + 1) * toks], "seq", k) for k in range(1, ns)
    ]
    fc_three = joined([fc_up, fc_low])
    shares = (fc_zero, fc_one, fc_two, fc_three)
    cut = proj_one.shape[0] // 2
    proj_three = swap(proj_two[:cut], "seq", 1), swap(proj_one[cut:], "seq", 2)
    mixed_blocks, branch_both = lax.optimization_barrier((mixed_blocks, branch_both))
    hidden, second, mixed, out_mat = attn_out(
        place, mixed_blocks, w_out, fc_other, shares, token_block, out_vec, gain_b, shift_b
    )

    second_got = swap(second, "fsdp", 1)
    *hiddens, out_own, out_oth, back_own, back_oth, sum_upper, sum_lower = feed(
        place, (second_got, second), (branch_got, branch), fc_bias, fc_mine, fc_other,
        shares, w_proj, (proj_zero, proj_one, proj_two, *proj_three),
    )
    back_got = swap(back_oth, "fsdp", 1)
    out_got = swap(out_oth, "fsdp", 1)
    grad_hidden, grad_attn, *grad_blocks, sums_two = mixed_back(
        place, back_own, back_got, hidden, branch, gain_b, out_mat
    )

    def added(left, right):
        return (left.astype(F32) + right.astype(F32)).astype(BF)

    def halves(values, index):
        pair = values.reshape(2, values.shape[0] // 2, values.shape[1])
        return pick(pair, index, 0).astype(F32), pick(pair, 1 - index, 0).astype(BF)

    def core_halves(grad):
        cut = grad.reshape(nz, 2, own, -1)
        mine, sent = pick(cut, core, 1), pick(cut, 1 - core, 1)
        return mine.reshape(nz * own, -1), sent.reshape(nz * own, -1)

    edge = 4 * hw
    chunk = 2 * hw
    head_got = [swap(grad_blocks[k], "seq", k) for k in range(1, ns)]
    hiddens, branch_late, second_late, second_got, mixed_late, attn_late = after(
        (hiddens, branch_both, second, second_got, mixed, grad_attn), grad_blocks
    )
    acts, slopes = (
        [v[:, i * edge : (i + 1) * edge] for v in pair for i in range(2)]
        for pair in (hiddens[:2], hiddens[2:])
    )
    wo_mine, wo_sent = core_halves(tn(mixed_late, attn_late).astype(BF))
    second_both = jnp.concatenate([second_got, second_late], axis=0)

    head_x = head_got[0]
    acts, slopes, second_both, branch_late, wo_sent, head_x, out_got = after(
        (acts, slopes, second_both, branch_late, wo_sent, head_x, out_got)
    )
    proj_grads = [tn(v, branch_late).astype(BF) if i % 2 else None for i, v in enumerate(acts)]
    proj_x = swap(proj_grads[1], "seq", 1)
    proj_y = swap(proj_grads[3], "seq", 2)
    wo_got = swap(wo_sent, "fsdp", 1)
    fc_grads = [None] * 4
    for i in (1, 3, 0, 2):
        fc_grads[i] = tn(second_both, slopes[i]).astype(BF)
    for i in (0, 2):
        proj_grads[i] = tn(acts[i], branch_late).astype(BF)
    output = (hidden + out_own + proj_vec + out_got.astype(F32)).astype(BF)

    grad_heads = jnp.concatenate([grad_blocks[0], head_x, *head_got[1:]], axis=0)
    grad_heads, fc_grads, proj_keep, wo_got, output = after(
        (grad_heads, fc_grads, proj_grads[::2], wo_got, output)
    )
    fc_x = swap(fc_grads[1], "seq", 1)
    fc_y = swap(fc_grads[3], "seq", 2)
    wo_keep, wo_sent = halves(wo_mine.astype(F32) + wo_got.astype(F32), floor // 2)
    wo_far = swap(wo_sent, "fsdp", 4)
    back = {}

    def between_back(lens, parts, grad):
        parts, grad, x, y, far = after((parts, grad, proj_x, proj_y, wo_far))
        back["proj"] = (
            x,
            y,
            swap(added(proj_keep[1][chunk:], y[chunk:]), "seq", 1),
            swap(added(proj_keep[0][chunk:], x[chunk:]), "seq", 2),
        )
        keep, sent = halves(wo_keep + far.astype(F32), floor % 2)
        back["out"] = keep, swap(sent, "fsdp", 2)
        return lens, parts, grad

    backward = attend_backward(lens, qkv, mixed_heads, norms, grad_heads, heads, between_back)
    proj_x, proj_y, proj_last_x, proj_last_y = back["proj"]
    wo_keep, wo_near = back["out"]

    backward, fc_x, fc_y, proj_x, proj_y, proj_last_x, proj_last_y, wo_near = after(
        (backward, fc_x, fc_y, proj_x, proj_y, proj_last_x, proj_last_y, wo_near)
    )
    fc_far = [added(fc_grads[0][:, chunk:], fc_x[:, chunk:]), added(fc_grads[2][:, chunk:], fc_y[:, chunk:])]
    fc_last_y = swap(fc_far[0], "seq", 2)
    fc_last_x = swap(fc_far[1], "seq", 1)
    wo_sum = wo_keep + wo_near.astype(F32)
    wo_got = swap(wo_sum.astype(BF), "seq", 1)
    backward = after(backward, fc_far)
    parts = [part[i] for i in range(3) for part in backward]
    sent_x, sent_y, sums_early = first_back((2, 6, 5, 7), parts, unit_all, qkv_turned)

    sent_x, sent_y, parts, fc_last_x, fc_last_y, proj_x, proj_y = after(
        (sent_x, sent_y, parts, fc_last_x, fc_last_y, proj_x, proj_y)
    )
    proj_keep, wo_got = after((proj_keep, wo_got))
    got_x = swap(sent_x, "seq", 1)
    got_y = swap(sent_y, "seq", 2)
    cuts = gather_sum(
        place, gather_proj_kernel,
        (proj_keep[0], proj_x, proj_last_y, proj_keep[1], proj_y, proj_last_x),
        (4 * hw, width), (chunk, width),
    )
    cuts_proj = [swap(cuts[k], "fsdp", 2 * k) for k in range(1, nz)]
    grad_proj_kept = cuts[0]
    fc_grads = after(fc_grads, cuts)
    cuts = gather_sum(
        place, gather_fc_kernel,
        (fc_grads[0], fc_x, fc_last_y, fc_grads[2], fc_y, fc_last_x),
        (width, 4 * hw), (width, chunk),
    )

    parts = after(parts, cuts)
    far_late, kept_late, sums_late = first_back((4, 3, 0, 1), parts, unit_all, qkv_turned)
    cuts_proj, cuts, far_late = after((cuts_proj, cuts, far_late))
    cuts_fc = [swap(cuts[k], "fsdp", 2 * k) for k in range(1, nz)]
    fc_kept = cuts[0]

    got_x, got_y, far_late, parts = after((got_x, got_y, far_late, parts))
    far_y = added(far_late[:half], got_x[half:])
    far_x = added(far_late[half:], got_y[half:])
    last_y = swap(far_y, "seq", 2)
    last_x = swap(far_x, "seq", 1)
    parts, first_late, cuts_proj = after((parts, first, cuts_proj), far_x, far_y)
    grad_qkv = jnp.concatenate(parts, axis=1)
    wi_grad = tn(first_late, grad_qkv).astype(BF)
    proj_owned = grad_proj_kept.astype(F32)
    for part in cuts_proj:
        proj_owned = proj_owned + part.astype(F32)
    proj_owned = proj_owned.astype(BF)

    def placed(values):
        slots = jnp.arange(ns)[:, None] == me
        return jnp.where(slots, values[None, :], 0.0).reshape(-1)

    spots = {}
    for i, (q, part) in enumerate(order):
        here = (sum_upper, sum_lower)[part][0, (i % 4) * chunk : (i % 4 + 1) * chunk]
        spots[q, part] = here.reshape(2, hw)
    fc_bias_grad = jnp.stack(
        [jnp.concatenate([spots[q, 0], spots[q, 1]], axis=0) for q in range(ns)], axis=1
    )
    fc_bias_grad = xor_take(fc_bias_grad, me, 1)
    fc_bias_grad = jnp.where(
        (jnp.arange(2) == core)[None, :, None, None], fc_bias_grad[:, None], 0.0
    ).reshape(-1)
    sums_one = sums_early + sums_late
    qkv_sum = jnp.sum(grad_qkv.astype(F32), axis=0)
    vector_grads = [
        sums_one[0],
        sums_one[1],
        jnp.concatenate([placed(qkv_sum[:local]), placed(qkv_sum[2 * local :])]),
        sums_two[0],
        sums_two[1],
        sums_two[2],
        fc_bias_grad,
        sums_two[3],
    ]
    by_owner = jnp.concatenate([v.reshape(nf, -1) for v in vector_grads], axis=1)
    by_owner = by_owner.reshape(nz, 2, -1, 3 * local)
    lines = by_owner.shape[2]
    tall = own + 16
    by_owner = jnp.pad(by_owner, ((0, 0), (0, 0), (0, 16 - lines), (0, 0)))
    wi_cut = jnp.concatenate([wi_grad.reshape(nz, 2, own, 3 * local), by_owner.astype(BF)], axis=2)
    wi_mine = pick(wi_cut, core, 1).reshape(nz * tall, 3 * local)
    wi_sent = pick(wi_cut, 1 - core, 1).reshape(nz * tall, 3 * local)
    last_x, last_y, cuts_fc, wi_sent, proj_owned, wo_sum, wo_got = after(
        (last_x, last_y, cuts_fc, wi_sent, proj_owned, wo_sum, wo_got)
    )
    wi_got = swap(wi_sent, "fsdp", 1)
    fc_owned = fc_kept.astype(F32)
    for part in cuts_fc:
        fc_owned = fc_owned + part.astype(F32)
    fc_mine, fc_sent = halves(fc_owned, core)
    fc_got = swap(fc_sent, "fsdp", 1)
    wo_sum = wo_sum + wo_got.astype(F32)
    wo_got = swap(wo_sum.astype(BF), "seq", 2)

    wi_got, fc_got = after((wi_got, fc_got))
    wi_keep, wi_sent = halves(wi_mine.astype(F32) + wi_got.astype(F32), floor // 2)
    wi_far = swap(wi_sent, "fsdp", 4)
    fc_final = jnp.concatenate([fc_mine.astype(BF), fc_got], axis=0)
    fc_finals = [fc_final] + [swap(fc_final, "seq", k) for k in range(1, ns)]
    last_x, last_y, kept_late = after((last_x, last_y, kept_late), fc_final, wi_sent)
    ends_at = pl.BlockSpec((half, width), lambda i: (i, 0))
    one_end = pl.BlockSpec((half, width), lambda i: (0, 0))
    input_grad = pl.pallas_call(
        last_kernel,
        out_shape=jax.ShapeDtypeStruct((toks, width), F32),
        grid=(2,),
        in_specs=[ends_at] + [one_end] * 4 + [ends_at] * 2 + [pl.BlockSpec((1, width), lambda i: (0, 0))],
        out_specs=ends_at,
        cost_estimate=cost(5),
        name="last",
    )(kept_late, got_x, got_y, last_y, last_x, token_block, grad_hidden, gain_a)

    fc_finals, input_grad, wo_got, proj_owned = after((fc_finals, input_grad, wo_got, proj_owned))
    input_grad = input_grad[None]
    proj_finals = [proj_owned] + [swap(proj_owned, "seq", k) for k in range(1, ns)]
    grad_w_out = wo_sum + wo_got.astype(F32)
    grad_w_fc = spread(place, spread_fc_kernel, fc_finals, (own, 32 * hw))

    wi_far, grad_w_fc = after((wi_far, grad_w_fc))
    wi_keep, wi_sent = halves(wi_keep + wi_far.astype(F32), floor % 2)
    wi_near = swap(wi_sent, "fsdp", 2)

    wi_near, proj_finals = after((wi_near, proj_finals))
    wi_owned = wi_keep + wi_near.astype(F32)
    wi_low = wi_owned.astype(BF)
    wi_finals = [wi_low] + [swap(wi_low, "seq", k) for k in range(1, ns)]
    grad_w_proj = spread(place, spread_proj_kernel, proj_finals, (4 * hw, width))
    wi_blocks = jnp.stack([v[:own].reshape(own, 3, local) for v in wi_finals], axis=2)
    grad_w_qkv = xor_take(wi_blocks, me, 2).reshape(own, 3 * width).astype(F32)
    output = output[None]
    vector_sum = wi_owned[own : own + lines]
    for v in wi_finals[1:]:
        vector_sum = vector_sum + v[own : own + lines].astype(F32)
    vector_sum = vector_sum.reshape(-1)
    outs = []
    at = 0
    for v in vectors:
        count = v.shape[0]
        outs.append(vector_sum[at : at + count])
        at += count
    (g_gain_one, g_shift_one, g_bias_qv, g_bias_out, g_gain_two, g_shift_two, g_bias_fc, g_bias_proj) = outs

    return (
        output,
        input_grad,
        g_gain_one,
        g_shift_one,
        grad_w_qkv,
        g_bias_qv,
        grad_w_out,
        g_bias_out,
        g_gain_two,
        g_shift_two,
        grad_w_fc,
        g_bias_fc,
        grad_w_proj,
        g_bias_proj,
    )


def body(*args):
    tokens, w_proj = args[0], args[13]
    fits = (
        lax.axis_size("seq") == 4
        and lax.axis_size("fsdp") == 8
        and tokens.shape[1:] == (512, 1024)
        and w_proj.shape == (512, 1024)
    )
    return body_aligned(*args) if fits else body_general(*args)


def solution(mesh):
    rows = P("fsdp", None)
    vec = P("fsdp")
    acts = P("fsdp", "seq", None)
    return jax.shard_map(
        body,
        mesh=mesh,
        in_specs=(
            acts, vec, rows, vec, vec, rows, vec, rows, vec, vec, vec, rows, vec, rows, vec, acts,
        ),
        out_specs=(
            acts, acts, vec, vec, rows, vec, rows, vec, vec, vec, rows, vec, rows, vec,
        ),
        check_vma=False,
    )
```

```python
import functools

import jax
import jax.numpy as jnp
from jax import lax
from jax.experimental import pallas as pl
from jax.experimental.pallas import tpu as pltpu
from jax.sharding import PartitionSpec as P

H = 16
HD = 64
PROMPT = 1024
CONTLEN = 512
CONTS = 2

EPS = 1e-05
GELU_C = 0.7978845608028654
GELU_A = 0.044715
NEG = -1e30
BF = jnp.bfloat16
F32 = jnp.float32


def swap(values, axis, bits):
    size = lax.axis_size(axis)
    return lax.ppermute(values, axis, [(i, i ^ bits) for i in range(size)])


def xor_take(values, index, axis):
    size = values.shape[axis]
    bit = 1
    while bit < size:
        parts = [lax.slice_in_dim(values, i, i + 1, axis=axis) for i in range(size)]
        flipped = jnp.concatenate([parts[i ^ bit] for i in range(size)], axis=axis)
        values = jnp.where((index & bit) != 0, flipped, values)
        bit *= 2
    return values


def xor_blocks(values, index, count, axis):
    width = values.shape[axis] // count
    return jnp.concatenate(
        [
            lax.dynamic_slice_in_dim(values, (i ^ index) * width, width, axis=axis)
            for i in range(count)
        ],
        axis=axis,
    )


def plane_gather(values):
    size = lax.axis_size("seq")
    if size != 4:
        return [values] + [swap(values, "seq", k) for k in range(1, size)]
    half = values.shape[0] // 2
    one = swap(values, "seq", 1)
    two = swap(values, "seq", 2)
    three = jnp.concatenate(
        [swap(two[:half], "seq", 1), swap(one[half:], "seq", 2)], axis=0
    )
    return [values, one, two, three]


def plane_scatter(blocks):
    size = lax.axis_size("seq")
    if size != 4:
        total = blocks[0].astype(F32)
        for k in range(1, size):
            total = total + swap(blocks[k].astype(BF), "seq", k).astype(F32)
        return total
    half = blocks[0].shape[0] // 2
    sent_x = jnp.concatenate([blocks[1][:half], blocks[3][:half]], axis=0).astype(BF)
    sent_y = jnp.concatenate([blocks[2][half:], blocks[3][half:]], axis=0).astype(BF)
    got_x = swap(sent_x, "seq", 1).astype(F32)
    got_y = swap(sent_y, "seq", 2).astype(F32)
    next_y = (blocks[2][:half].astype(F32) + got_x[half:]).astype(BF)
    next_x = (blocks[1][half:].astype(F32) + got_y[half:]).astype(BF)
    last_y = swap(next_y, "seq", 2).astype(F32)
    last_x = swap(next_x, "seq", 1).astype(F32)
    upper = blocks[0][:half].astype(F32) + got_x[:half] + last_y
    lower = blocks[0][half:].astype(F32) + got_y[:half] + last_x
    return jnp.concatenate([upper, lower], axis=0)


def after(values, *needed):
    return lax.optimization_barrier((values, needed))[0]


def cost(micros, size=0):
    return pl.CostEstimate(flops=int(micros * 1.15e6), bytes_accessed=int(size), transcendentals=0)


def tile_rows(total, blocks):
    return min(512, total // blocks)


def rel_row(tile, rows, block_rows, me):
    per = block_rows // rows
    return pl.multiple_of(((tile // per) ^ me) * block_rows + (tile % per) * rows, rows)


def walk(tile, rows):
    prompt_tiles = PROMPT // rows
    cont_tiles = CONTLEN // rows
    in_prompt = tile < prompt_tiles
    inside = lax.rem(jnp.maximum(tile - prompt_tiles, 0), cont_tiles)
    count = jnp.where(in_prompt, tile, prompt_tiles + inside)
    return count, tile - inside - prompt_tiles


def key_limit(lens, tile, rows):
    prompt_tiles = PROMPT // rows
    cont_tiles = CONTLEN // rows
    past = jnp.maximum(tile - prompt_tiles, 0)
    cont = jnp.minimum(past // cont_tiles, CONTS - 1)
    length = lens[1]
    for i in range(1, CONTS):
        length = jnp.where(cont == i, lens[1 + i], length)
    return jnp.where(
        tile < prompt_tiles, lens[0] - tile * rows, length - lax.rem(past, cont_tiles) * rows
    )


def pair_stack(block, per_pair, scale=None):
    if scale is not None:
        block = block * scale
    if per_pair == 1:
        return block
    lane = lax.broadcasted_iota(jnp.int32, block.shape, 1) // HD
    return jnp.concatenate(
        [jnp.where(lane == h, block, jnp.zeros_like(block)) for h in range(per_pair)], axis=0
    )


def diagonal_mask(rows, per_pair, limit):
    key = lax.broadcasted_iota(jnp.int32, (rows, per_pair * rows), 0)
    query = lax.broadcasted_iota(jnp.int32, (rows, per_pair * rows), 1) % rows
    return ((key <= query) & (key < limit)) | (key == query)


def live_mask(rows, per_pair, limit):
    return lax.broadcasted_iota(jnp.int32, (rows, per_pair * rows), 0) < limit


def nt(left, right):
    return lax.dot_general(left, right, (((1,), (1,)), ((), ())), preferred_element_type=F32)


def nn(left, right):
    return lax.dot_general(left, right, (((1,), (0,)), ((), ())), preferred_element_type=F32)


def unstack(values, per_pair, rows):
    if per_pair == 1:
        return values
    return jnp.concatenate(
        [values[h * HD : (h + 1) * HD, h * rows : (h + 1) * rows] for h in range(per_pair)], axis=0
    )


def forward_kernel(
    rows, block_rows, per_pair, lens, q_ref, k_ref, v_ref, out_ref, norm_ref, vt_ref, parts, total
):
    tile = pl.program_id(0)
    me = lens[1 + CONTS]
    tiles = q_ref.shape[0] // rows
    across = per_pair * rows

    @pl.when(tile == 0)
    def _():
        def turn(i, carry):
            at = rel_row(i, rows, block_rows, me)
            vt_ref[i] = v_ref[pl.ds(at, rows), :].T
            return carry

        lax.fori_loop(0, tiles, turn, 0)

    at = rel_row(tile, rows, block_rows, me)
    query = pair_stack(q_ref[pl.ds(at, rows), :], per_pair, jnp.asarray(0.125, BF)).T
    count, shift = walk(tile, rows)

    def folded(values):
        return values.reshape(rows // 8, 8, across)

    def scores(i):
        return nn(k_ref[pl.ds(rel_row(i, rows, block_rows, me), rows), :], query)

    def key_tile(i):
        return jnp.where(i < PROMPT // rows, i, i + shift)

    first = jnp.where(
        diagonal_mask(rows, per_pair, key_limit(lens, tile, rows)), scores(tile), NEG
    )

    def measure(i, top):
        here = key_tile(i)
        part = jnp.where(
            live_mask(rows, per_pair, key_limit(lens, here, rows)), scores(here), NEG
        )
        parts[i] = part
        return jnp.maximum(top, jnp.max(folded(part), axis=0))

    top = lax.fori_loop(0, count, measure, jnp.max(folded(first), axis=0))
    top = jnp.max(top, axis=0, keepdims=True)
    weights = jnp.exp(first - top)
    total[...] = nn(vt_ref[tile], weights.astype(BF))

    def gather(i, denom):
        weights = jnp.exp(parts[i] - top)
        total[...] += nn(vt_ref[key_tile(i)], weights.astype(BF))
        return denom + jnp.sum(folded(weights), axis=0)

    denom = lax.fori_loop(0, count, gather, jnp.sum(folded(weights), axis=0))
    denom = jnp.sum(denom, axis=0, keepdims=True)
    mixed = unstack(total[...] / denom, per_pair, rows)
    out_ref[...] = mixed.T.astype(BF)
    norm_ref[0] = top + jnp.log(denom)


def backward_kernel(
    rows, block_rows, per_pair, lens, q_ref, k_ref, v_ref, out_ref, grad_ref, norm_ref,
    dq_ref, dk_ref, dv_ref, kt_ref, dk_sum, dv_sum, dq_sum,
):
    tile = pl.program_id(0)
    me = lens[1 + CONTS]
    tiles = q_ref.shape[0] // rows

    @pl.when(tile == 0)
    def _():
        def turn(i, carry):
            at = rel_row(i, rows, block_rows, me)
            kt_ref[i] = k_ref[pl.ds(at, rows), :].T
            return carry

        lax.fori_loop(0, tiles, turn, 0)
        dk_sum[...] = jnp.zeros_like(dk_sum)
        dv_sum[...] = jnp.zeros_like(dv_sum)

    at = rel_row(tile, rows, block_rows, me)
    query = pair_stack(q_ref[pl.ds(at, rows), :], per_pair, jnp.asarray(0.125, BF))
    grad_block = grad_ref[pl.ds(at, rows), :]
    grad = pair_stack(grad_block, per_pair)
    query_turned = query.T
    grad_turned = grad.T
    product = (grad_block.astype(F32) * out_ref[pl.ds(at, rows), :].astype(F32)).T
    inner = jnp.concatenate(
        [
            jnp.sum(product[h * HD : (h + 1) * HD], axis=0, keepdims=True)
            for h in range(per_pair)
        ],
        axis=1,
    )
    norm = norm_ref[0]

    def one(key_tile, mask):
        key_at = rel_row(key_tile, rows, block_rows, me)
        keys = pl.ds(key_at, rows)
        part = jnp.where(mask, nn(k_ref[keys, :], query_turned), NEG)
        probs = jnp.exp(part - norm)
        slope = probs * (nn(v_ref[keys, :], grad_turned) - inner)
        slope_low = slope.astype(BF)
        dv_sum[keys, :] += nn(probs.astype(BF), grad)
        dk_sum[keys, :] += nn(slope_low, query)
        return nn(kt_ref[key_tile], slope_low)

    dq_sum[...] = one(tile, diagonal_mask(rows, per_pair, key_limit(lens, tile, rows)))
    count, shift = walk(tile, rows)

    def step(i, carry):
        key_tile = jnp.where(i < PROMPT // rows, i, i + shift)
        dq_sum[...] += one(key_tile, live_mask(rows, per_pair, key_limit(lens, key_tile, rows)))
        return carry

    lax.fori_loop(0, count, step, 0)
    dq_ref[...] = (unstack(dq_sum[...], per_pair, rows).T * 0.125).astype(BF)

    @pl.when(tile == tiles - 1)
    def _():
        dk_ref[...] = dk_sum[...].astype(BF)
        dv_ref[...] = dv_sum[...].astype(BF)


def attention_plan(total, heads):
    blocks = lax.axis_size("seq")
    rows = tile_rows(total, blocks)
    per_pair = 2 if heads % 2 == 0 else 1
    return rows, total // blocks, per_pair, heads // per_pair, per_pair * HD


def thirds(qkv, width, pair_width):
    per = width // pair_width
    if pair_width % 128 == 0:
        return (qkv, qkv, qkv), (0, per, 2 * per)
    return tuple(qkv[:, i * width : (i + 1) * width] for i in range(3)), (0, 0, 0)


def row_block(rows, block_rows):
    per = block_rows // rows

    def index(tile, lens):
        return ((tile // per) ^ lens[1 + CONTS]) * per + tile % per, 0

    return index


def attend_forward(lens, qkv, heads, between=None):
    total = qkv.shape[0]
    width = heads * HD
    rows, block_rows, per_pair, pairs, pair_width = attention_plan(total, heads)
    arrays, firsts = thirds(qkv, width, pair_width)
    tiles = total // rows
    most = (PROMPT + CONTLEN) // rows
    mixed = None
    norms = []
    for pair in range(pairs):

        def whole(first):
            return pl.BlockSpec((total, pair_width), lambda tile, lens: (0, first + pair))

        def kernel(lens, q_ref, k_ref, v_ref, *refs):
            forward_kernel(
                rows, block_rows, per_pair, lens, q_ref, k_ref, v_ref, *refs[mixed is not None :]
            )

        place_row = row_block(rows, block_rows)
        more = [] if mixed is None else [mixed]
        mixed, norm = pl.pallas_call(
            kernel,
            out_shape=(
                jax.ShapeDtypeStruct((total, width), BF),
                jax.ShapeDtypeStruct((tiles, 1, per_pair * rows), F32),
            ),
            grid_spec=pltpu.PrefetchScalarGridSpec(
                num_scalar_prefetch=1,
                grid=(tiles,),
                in_specs=[whole(first) for first in firsts]
                + [pl.BlockSpec(memory_space=pl.ANY)] * len(more),
                out_specs=(
                    pl.BlockSpec(
                        (rows, pair_width), lambda tile, lens: (place_row(tile, lens)[0], pair)
                    ),
                    pl.BlockSpec((1, 1, per_pair * rows), lambda tile, lens: (tile, 0, 0)),
                ),
                scratch_shapes=[
                    pltpu.VMEM((tiles, pair_width, rows), BF),
                    pltpu.VMEM((most, rows, per_pair * rows), F32),
                    pltpu.VMEM((pair_width, per_pair * rows), F32),
                ],
            ),
            input_output_aliases={4: 0} if more else {},
            cost_estimate=cost(15),
            name="attend_forward",
        )(lens, *arrays, *more)
        norms.append(norm)
        if between is not None and pair + 1 < pairs:
            lens, mixed, arrays = between(lens, mixed, arrays)
    return mixed, norms


def attend_backward(lens, qkv, mixed, norms, grad, heads, between=None):
    total = qkv.shape[0]
    width = heads * HD
    rows, block_rows, per_pair, pairs, pair_width = attention_plan(total, heads)
    arrays, firsts = thirds(qkv, width, pair_width)
    tiles = total // rows
    made = []
    for pair in range(pairs):

        def whole(first):
            return pl.BlockSpec((total, pair_width), lambda tile, lens: (0, first))

        made.append(
            pl.pallas_call(
                functools.partial(backward_kernel, rows, block_rows, per_pair),
                out_shape=(jax.ShapeDtypeStruct((total, pair_width), BF),) * 3,
                grid_spec=pltpu.PrefetchScalarGridSpec(
                    num_scalar_prefetch=1,
                    grid=(tiles,),
                    in_specs=[whole(first + pair) for first in firsts]
                    + [
                        whole(pair),
                        whole(pair),
                        pl.BlockSpec((1, 1, per_pair * rows), lambda tile, lens: (tile, 0, 0)),
                    ],
                    out_specs=(
                        pl.BlockSpec((rows, pair_width), row_block(rows, block_rows)),
                        whole(0),
                        whole(0),
                    ),
                    scratch_shapes=[
                        pltpu.VMEM((tiles, pair_width, rows), BF),
                        pltpu.VMEM((total, pair_width), F32),
                        pltpu.VMEM((total, pair_width), F32),
                        pltpu.VMEM((pair_width, per_pair * rows), F32),
                    ],
                ),
                cost_estimate=cost(18),
                name="attend_backward",
            )(lens, *arrays, mixed, grad, norms[pair])
        )
        if between is not None and pair + 1 < pairs:
            lens, made[-1], grad = between(lens, made[-1], grad)
    return made


def norm_stats(values):
    center = values - jnp.mean(values, axis=-1, keepdims=True)
    spread = jnp.mean(center * center, axis=-1, keepdims=True)
    scale = lax.rsqrt(spread + EPS)
    return center * scale, scale


def norm_pull(unit, scale, slope):
    return scale * (
        slope
        - jnp.mean(slope, axis=-1, keepdims=True)
        - unit * jnp.mean(slope * unit, axis=-1, keepdims=True)
    )


def gelu_both(values):
    square = values * values
    bent = jnp.tanh(GELU_C * (values + GELU_A * square * values))
    value = 0.5 * values * (1.0 + bent)
    slope = 0.5 * (1.0 + bent) + 0.5 * values * (1.0 - bent * bent) * GELU_C * (
        1.0 + 3.0 * GELU_A * square
    )
    return value, slope


def tn(left, right):
    return lax.dot_general(left, right, (((0,), (0,)), ((), ())), preferred_element_type=F32)


def pick(values, index, axis):
    return lax.dynamic_index_in_dim(values, index, axis, keepdims=False)


def by_core(core, mine, other, axis):
    return jnp.where(
        core == 0, jnp.stack([mine, other], axis=axis), jnp.stack([other, mine], axis=axis)
    )


def body_general(
    tokens,
    prompt_lens,
    cont_lens,
    gain_one,
    shift_one,
    w_qkv,
    bias_qv,
    w_out,
    bias_out,
    gain_two,
    shift_two,
    w_fc,
    bias_fc,
    w_proj,
    bias_proj,
    cotangent,
):
    ns = lax.axis_size("seq")
    nf = lax.axis_size("fsdp")
    nz = nf // 2
    me = lax.axis_index("seq")
    owner = lax.axis_index("fsdp")
    floor = owner // 2
    core = owner % 2
    toks, width = tokens.shape[1:]
    hidden_all = w_fc.shape[1]
    own = width // nf
    heads = H // ns
    local = width // ns
    hw = hidden_all // (nf * ns)
    cols = nz * hw

    token_block = tokens[0]
    branch = cotangent[0]

    token_blocks = plane_gather(token_block)
    vectors = [gain_one, shift_one, bias_qv, bias_out, gain_two, shift_two, bias_fc, bias_proj]
    packed = jnp.concatenate([v.reshape(-1, own) for v in vectors], axis=0)
    lines = packed.shape[0]
    packed_rows = -(-packed.size // (3 * local))
    packed = jnp.pad(packed.reshape(-1), (0, 16 * (-(-packed_rows // 16)) * 3 * local - packed.size))
    mine_qkv = pick(w_qkv.reshape(own, 3, ns, local), me, 2).reshape(own, 3 * local)
    sent_qkv = jnp.concatenate([mine_qkv, packed.reshape(-1, 3 * local)], axis=0)
    got_qkv = jnp.stack([sent_qkv] + [swap(sent_qkv, "fsdp", 2 * k) for k in range(1, nz)])
    got_qkv = xor_take(by_core(core, got_qkv, swap(got_qkv, "fsdp", 1), 1), floor, 0)
    qkv_mat = got_qkv[:, :, :own].reshape(width, 3 * local)
    small = got_qkv[:, :, own:].reshape(nf, -1)[:, : lines * own].reshape(nf, lines, own)
    at = 0
    full = []
    for v in vectors:
        count = v.shape[0] // own
        full.append(small[:, at : at + count].reshape(-1).astype(F32))
        at += count
    gain_a, shift_a, qv_vec, out_vec, gain_b, shift_b, fc_vec, proj_vec = full

    fc_cut = w_fc.reshape(own, nz, 2, ns, hw)
    fc_mine = pick(fc_cut, core, 2)
    fc_other = swap(pick(fc_cut, 1 - core, 2).reshape(own, -1), "fsdp", 1)
    fc_rows = by_core(core, fc_mine.reshape(own, -1), fc_other, 0).reshape(2 * own, nz, ns, hw)
    fc_rows = xor_take(xor_take(fc_rows, floor, 1), me, 2)
    proj_rows = xor_take(w_proj.reshape(ns, hw, width), me, 0)
    out_cols = xor_take(w_out.reshape(own, ns, local), me, 1)
    proj_parts = width // cols
    out_parts = max(1, cols // local)

    def share(q, k):
        fc = jnp.concatenate([fc_rows[:, j ^ k, q] for j in range(nz)], axis=1)
        proj = [proj_rows[q][:, i * cols : (i + 1) * cols] for i in range(proj_parts)]
        out = out_cols[:, q]
        if out_parts > 1:
            step = own // out_parts
            out = jnp.concatenate([out[i * step : (i + 1) * step] for i in range(out_parts)], axis=1)
        return fc, proj, out

    def message(k):
        fc, proj, out = share(0, k)
        return jnp.concatenate([fc, *proj, out.reshape(-1, cols)], axis=0)

    got = [swap(message(k), "fsdp", 2 * k) for k in range(1, nz)]
    rows_each = got[0].shape[0]
    planes = plane_gather(jnp.concatenate(got, axis=0))

    def parts_of(q, k):
        if k == 0:
            fc, proj, out = share(q, 0)
            return fc, jnp.concatenate(proj, axis=1), out_cols[:, q]
        block = planes[q][(k - 1) * rows_each : k * rows_each]
        fc = block[: 2 * own]
        proj = jnp.concatenate(
            [block[2 * own + i * hw : 2 * own + (i + 1) * hw] for i in range(proj_parts)], axis=1
        )
        out = block[2 * own + proj_parts * hw :]
        if out_parts > 1:
            out = jnp.concatenate(
                [out[:, i * local : (i + 1) * local] for i in range(out_parts)], axis=0
            )
        else:
            out = out.reshape(own, local)
        return fc, proj, out

    pieces = [[parts_of(q, k) for k in range(nz)] for q in range(ns)]
    out_half = jnp.stack(
        [jnp.stack([pieces[q][k][2] for q in range(ns)], axis=1) for k in range(nz)]
    )
    out_half = xor_take(out_half, me, 2).reshape(nz, own, width)
    out_both = by_core(core, out_half, swap(out_half, "fsdp", 1), 1)
    out_mat = xor_take(out_both, floor, 0).reshape(ns, local, width)
    out_mat = xor_take(out_mat, me, 0).reshape(width, width)
    fc_mat = jnp.concatenate(
        [jnp.concatenate([pieces[q][k][0] for k in range(nz)], axis=0) for q in range(ns)], axis=1
    )
    proj_mat = jnp.concatenate([pieces[q][k][1] for q in range(ns) for k in range(nz)], axis=0)
    fc_bias = pick(fc_vec.reshape(nz, 2, ns, hw), core, 1)
    fc_bias = xor_take(xor_take(fc_bias, floor, 0), me, 1).transpose(1, 0, 2).reshape(-1)

    all_tokens = jnp.concatenate(token_blocks, axis=0).astype(F32)
    unit_all, _ = norm_stats(all_tokens)
    first = (unit_all * gain_a + shift_a).astype(BF)
    bias_all = jnp.concatenate(
        [
            pick(qv_vec.reshape(2, ns, local)[0], me, 0),
            jnp.zeros((local,), F32),
            pick(qv_vec.reshape(2, ns, local)[1], me, 0),
        ]
    )
    qkv = (jnp.dot(first, qkv_mat, preferred_element_type=F32) + bias_all).astype(BF)
    lens = jnp.concatenate([prompt_lens, cont_lens[0], me.reshape(1)]).astype(jnp.int32)
    mixed_heads, norms = attend_forward(lens, qkv, heads)

    def to_tokens(values):
        return jnp.concatenate(
            [values[:toks]]
            + [swap(values[k * toks : (k + 1) * toks], "seq", k) for k in range(1, ns)],
            axis=1,
        )

    def to_heads(values):
        return jnp.concatenate(
            [values[:, :local]]
            + [swap(values[:, k * local : (k + 1) * local], "seq", k) for k in range(1, ns)],
            axis=0,
        )

    mixed = to_tokens(mixed_heads)
    hidden = token_block.astype(F32) + jnp.dot(mixed, out_mat, preferred_element_type=F32) + out_vec
    unit_two, scale_two = norm_stats(hidden)
    second = (unit_two * gain_b + shift_b).astype(BF)

    second_both = jnp.concatenate([second, swap(second, "fsdp", 1)], axis=0)
    second_both = xor_blocks(second_both, floor, nz, 1)
    branch_both = jnp.concatenate([branch, swap(branch, "fsdp", 1)], axis=0)
    pre = jnp.dot(second_both, fc_mat, preferred_element_type=F32) + fc_bias
    act_full, bend = gelu_both(pre)
    act = act_full.astype(BF)
    grad_act = nt(branch_both, proj_mat)
    grad_pre = (grad_act * bend).astype(BF)
    grad_second_both = nt(grad_pre, fc_mat)
    grad_second = grad_second_both[:toks] + swap(
        grad_second_both[toks:].astype(BF), "fsdp", 1
    ).astype(F32)
    grad_second = xor_blocks(grad_second, floor, nz, 1)
    out_sum = jnp.dot(act, proj_mat, preferred_element_type=F32)
    result = hidden + out_sum[:toks] + proj_vec
    result = result + swap(out_sum[toks:].astype(BF), "fsdp", 1).astype(F32)
    output = result.astype(BF)[None]

    grad_hidden = branch.astype(F32) + norm_pull(unit_two, scale_two, grad_second * gain_b)
    grad_attn = grad_hidden.astype(BF)
    grad_mixed = nt(grad_attn, out_mat).astype(BF)
    grad_heads = to_heads(grad_mixed)

    backward = attend_backward(lens, qkv, mixed_heads, norms, grad_heads, heads)
    grad_q, grad_k, grad_v = (
        jnp.concatenate([part[i] for part in backward], axis=1) for i in range(3)
    )
    grad_qkv = jnp.concatenate([grad_q, grad_k, grad_v], axis=1)
    grad_first_part = nt(grad_qkv, qkv_mat).astype(BF)
    grad_first = plane_scatter(
        [grad_first_part[k * toks : (k + 1) * toks] for k in range(ns)]
    )
    unit_one, scale_one = norm_stats(token_block.astype(F32))
    input_grad = (grad_hidden + norm_pull(unit_one, scale_one, grad_first * gain_a))[None]

    span = nz * hw
    grad_fc = [tn(second_both, grad_pre[:, q * span : (q + 1) * span]).astype(BF) for q in range(ns)]
    grad_proj = [tn(act[:, q * span : (q + 1) * span], branch_both).astype(BF) for q in range(ns)]
    fc_sum = plane_scatter(grad_fc)
    proj_sum = plane_scatter(grad_proj)

    def fc_for(k):
        block = fc_sum[k * 2 * own : (k + 1) * 2 * own].reshape(2 * own, nz, hw)
        return jnp.concatenate([block[:, j ^ k] for j in range(nz)], axis=1)

    def proj_for(k):
        block = proj_sum[k * hw : (k + 1) * hw]
        return jnp.concatenate(
            [block[:, i * span : (i + 1) * span] for i in range(proj_parts)], axis=0
        )

    both_sum = jnp.concatenate([fc_for(0), proj_for(0)], axis=0)
    for k in range(1, nz):
        sent = jnp.concatenate([fc_for(k), proj_for(k)], axis=0).astype(BF)
        both_sum = both_sum + swap(sent, "fsdp", 2 * k).astype(F32)
    fc_owned = both_sum[: 2 * own].reshape(2, own, span)
    fc_kept = pick(fc_owned, core, 0).astype(BF)
    fc_moved = swap(pick(fc_owned, 1 - core, 0).astype(BF), "fsdp", 1)
    final = jnp.concatenate([fc_kept, fc_moved, both_sum[2 * own :].astype(BF)], axis=0)
    finals = plane_gather(final)
    fc_kept_all = jnp.stack([v[:own].reshape(own, nz, hw) for v in finals], axis=2)
    fc_moved_all = jnp.stack([v[own : 2 * own].reshape(own, nz, hw) for v in finals], axis=2)
    grad_w_fc = by_core(core, fc_kept_all, fc_moved_all, 2)
    grad_w_fc = xor_take(xor_take(grad_w_fc, floor, 1), me, 3).reshape(own, hidden_all).astype(F32)
    grad_w_proj = jnp.stack(
        [
            jnp.concatenate(
                [v[2 * own + i * hw : 2 * own + (i + 1) * hw] for i in range(proj_parts)], axis=1
            )
            for v in finals
        ]
    )
    grad_w_proj = xor_take(grad_w_proj, me, 0).reshape(ns * hw, width).astype(F32)

    grad_out = tn(mixed, grad_attn).astype(BF).reshape(ns, local, width)
    grad_out = xor_take(grad_out, me, 0).reshape(nz, 2, own, width)
    grad_out = xor_take(grad_out, floor, 0)
    out_kept = pick(grad_out, core, 1).astype(F32) + swap(
        pick(grad_out, 1 - core, 1), "fsdp", 1
    ).astype(F32)
    out_owned = out_kept[0]
    for k in range(1, nz):
        out_owned = out_owned + swap(out_kept[k].astype(BF), "fsdp", 2 * k).astype(F32)
    bit = 1
    while bit < ns:
        out_owned = out_owned + swap(out_owned.astype(BF), "seq", bit).astype(F32)
        bit *= 2
    grad_w_out = out_owned

    grad_in = tn(first, grad_qkv).astype(BF).reshape(nz, 2, own, 3 * local)
    grad_in = xor_take(grad_in, floor, 0)
    in_kept = pick(grad_in, core, 1).astype(F32) + swap(
        pick(grad_in, 1 - core, 1), "fsdp", 1
    ).astype(F32)
    in_owned = in_kept[0]
    for k in range(1, nz):
        in_owned = in_owned + swap(in_kept[k].astype(BF), "fsdp", 2 * k).astype(F32)
    in_owned = in_owned.astype(BF)
    in_blocks = jnp.stack(
        [in_owned.reshape(own, 3, local)]
        + [swap(in_owned, "seq", k).reshape(own, 3, local) for k in range(1, ns)],
        axis=2,
    )
    grad_w_qkv = xor_take(in_blocks, me, 2).reshape(own, 3 * width).astype(F32)

    def placed(values, parts):
        slots = jnp.arange(parts)[:, None] == me
        return jnp.where(slots, values[None, :], 0.0).reshape(-1)

    part_f32 = grad_first_part.astype(F32)
    fc_bias_grad = jnp.sum(grad_pre.astype(F32), axis=0).reshape(ns, nz, hw).transpose(1, 0, 2)
    fc_bias_grad = xor_take(xor_take(fc_bias_grad, floor, 0), me, 1)
    fc_bias_grad = jnp.where(
        (jnp.arange(2) == core)[None, :, None, None], fc_bias_grad[:, None], 0.0
    ).reshape(-1)
    vector_grads = [
        jnp.sum(part_f32 * unit_all, axis=0),
        jnp.sum(part_f32, axis=0),
        placed(jnp.sum(grad_q.astype(F32), axis=0), ns),
        placed(jnp.sum(grad_v.astype(F32), axis=0), ns),
        jnp.sum(grad_attn.astype(F32), axis=0),
        jnp.sum(grad_second * unit_two, axis=0),
        jnp.sum(grad_second, axis=0),
        fc_bias_grad,
        jnp.sum(branch.astype(F32), axis=0),
    ]
    vector_sum = jnp.concatenate([v.reshape(-1, width) for v in vector_grads], axis=0)
    for axis, size in (("seq", ns), ("fsdp", nf)):
        bit = 1
        while bit < size:
            vector_sum = vector_sum + swap(vector_sum, axis, bit)
            bit *= 2
    vector_sum = vector_sum.reshape(-1)
    outs = []
    at = 0
    for v in vectors:
        count = v.shape[0]
        outs.append(lax.dynamic_slice_in_dim(vector_sum, at + owner * count, count))
        at += nf * count
    (g_gain_one, g_shift_one, g_bias_qv, g_bias_out, g_gain_two, g_shift_two, g_bias_fc, g_bias_proj) = outs

    return (
        output,
        input_grad,
        g_gain_one,
        g_shift_one,
        grad_w_qkv,
        g_bias_qv,
        grad_w_out,
        g_bias_out,
        g_gain_two,
        g_shift_two,
        grad_w_fc,
        g_bias_fc,
        grad_w_proj,
        g_bias_proj,
    )


UPPER = (0, 2, 1, 3)


def hidden_at(q, half, size):
    return half * 4 * size + (UPPER[q] if half == 0 else q) * size


def start_all(copies, sems):
    made = [
        pltpu.make_async_copy(source, target, sems.at[i]) for i, (source, target) in enumerate(copies)
    ]
    for copy in made:
        copy.start()
    return made


def aligned(value, size):
    return pl.multiple_of(value, size)


def pack_kernel(hw, place, fc_ref, proj_ref, out_mat_ref, mine_ref, other_ref, share_ref):
    me, core = place[0], place[2]
    for q in range(4):
        for z in range(4):
            target = hidden_at(q, z // 2, 2 * hw) + (z % 2) * hw
            for out_ref, which in ((mine_ref, core), (other_ref, 1 - core)):
                source = aligned(z * 8 * hw + which * 4 * hw + (me ^ q) * hw, hw)
                out_ref[:, target : target + hw] = fc_ref[:, pl.ds(source, hw)]
    share_ref[...] = proj_ref[...]
    other_ref[:, 16 * hw :] = out_mat_ref[...]


def pack(place, w_fc, w_proj, w_out):
    own, hidden_all = w_fc.shape
    hw, width = w_proj.shape[0] // 4, w_proj.shape[1]

    def whole(shape):
        return pl.BlockSpec(shape, lambda i, place: (0, 0))

    half = jax.ShapeDtypeStruct((own, hidden_all // 2), BF)
    more = jax.ShapeDtypeStruct((own, hidden_all // 2 + width), BF)
    return pl.pallas_call(
        functools.partial(pack_kernel, hw),
        out_shape=(half, more, jax.ShapeDtypeStruct((hw, width), BF)),
        grid_spec=pltpu.PrefetchScalarGridSpec(
            num_scalar_prefetch=1,
            grid=(1,),
            in_specs=[
                whole((own, hidden_all)),
                pl.BlockSpec((hw, width), lambda i, place: (place[0], 0)),
                whole(w_out.shape),
            ],
            out_specs=(whole(half.shape), whole(more.shape), whole((hw, width))),
        ),
        cost_estimate=cost(3),
        name="pack_shares",
    )(place, w_fc, w_proj, w_out)


def join_kernel(place, m0, m1, o0, o1, mine_out, l0, l1, out_ref):
    core = place[2]
    own, chunk = m0.shape
    part = mine_out.shape[0]
    for refs, which in (((m0, m1), core), ((o0, o1), 1 - core)):
        rows = pl.ds(aligned(which * own, own), own)
        for half in range(2):
            out_ref[rows, half * chunk : (half + 1) * chunk] = refs[half][...]
    wide = 2 * chunk
    for parts, which in (
        ((mine_out[:, :wide], mine_out[:, wide:]), core),
        ((l0[...], l1[...]), 1 - core),
    ):
        for half in range(2):
            rows = pl.ds(aligned(2 * own + which * 2 * part + half * part, part), part)
            out_ref[rows, :] = parts[half]


def join(place, mine, other, w_out):
    own, hidden = mine.shape
    chunk = hidden // 8
    part = own // 4
    rows = 2 * own + 4 * part
    pieces = [
        pl.BlockSpec((own, chunk), lambda i, place, at=hidden_at(0, half, 1): (0, at))
        for half in range(2)
    ]
    quarters = [
        pl.BlockSpec((part, 2 * chunk), lambda i, place, at=4 + half: (place[0], at))
        for half in range(2)
    ]
    return pl.pallas_call(
        join_kernel,
        out_shape=jax.ShapeDtypeStruct((rows, 2 * chunk), BF),
        grid_spec=pltpu.PrefetchScalarGridSpec(
            num_scalar_prefetch=1,
            grid=(1,),
            in_specs=pieces * 2
            + [pl.BlockSpec((part, w_out.shape[1]), lambda i, place: (place[0], 0))]
            + quarters,
            out_specs=pl.BlockSpec((rows, 2 * chunk), lambda i, place: (0, 0)),
        ),
        cost_estimate=cost(2),
        name="join_rows",
    )(place, mine, mine, other, other, w_out, other, other)


def joined_kernel(*refs):
    at = 0
    for ref in refs[:-1]:
        refs[-1][at : at + ref.shape[0], :] = ref[...]
        at += ref.shape[0]


def joined(parts):
    rows = sum(part.shape[0] for part in parts)
    return pl.pallas_call(
        joined_kernel,
        out_shape=jax.ShapeDtypeStruct((rows, parts[0].shape[1]), parts[0].dtype),
        cost_estimate=cost(1),
        name="joined",
    )(*parts)


def project_kernel(
    place, own_ref, one_ref, two_ref, up_ref, low_ref, kept_ref, moved_ref, gain_ref, shift_ref,
    bias_ref, first_ref, unit_ref, qkv_ref, turned_ref, toks, mat, sems,
):
    step = pl.program_id(0)
    floor, core = place[1], place[2]
    block = own_ref.shape[0]
    half = block // 2
    own = mat.shape[0] // 8

    def copies():
        made = [
            (own_ref, toks.at[pl.ds(0, block), :]),
            (one_ref, toks.at[pl.ds(block, block), :]),
            (two_ref, toks.at[pl.ds(2 * block, block), :]),
            (up_ref, toks.at[pl.ds(3 * block, half), :]),
            (low_ref, toks.at[pl.ds(3 * block + half, half), :]),
        ]
        for k in range(4):
            for ref, which in ((kept_ref, core), (moved_ref, 1 - core)):
                row = aligned((floor ^ k) * 2 * own + which * own, own)
                made.append((ref.at[k, pl.ds(0, own), :], mat.at[pl.ds(row, own), :]))
        return made

    @pl.when(step == 0)
    def _():
        for copy in start_all(copies(), sems):
            copy.wait()

    rows = first_ref.shape[0]
    values = toks[pl.ds(aligned(step * rows, rows), rows), :].astype(F32)
    unit, _ = norm_stats(values)
    first = (unit * gain_ref[...] + shift_ref[...]).astype(BF)
    first_ref[...] = first
    unit_ref[...] = unit.astype(BF)
    qkv_ref[...] = (nn(first, mat[...]) + bias_ref[...]).astype(BF)

    @pl.when(step == pl.num_programs(0) - 1)
    def _():
        turned_ref[...] = mat[...].T


def project(place, blocks, kept, moved, gain, shift, bias):
    block, width = blocks[0].shape
    outs = kept.shape[2]
    total = 4 * block
    rows = 256
    raw = pl.BlockSpec(memory_space=pl.ANY)

    def line(size):
        return pl.BlockSpec((1, size), lambda i, place: (0, 0))

    def tile(size):
        return pl.BlockSpec((rows, size), lambda i, place: (i, 0))

    return pl.pallas_call(
        project_kernel,
        out_shape=(
            jax.ShapeDtypeStruct((total, width), BF),
            jax.ShapeDtypeStruct((total, width), BF),
            jax.ShapeDtypeStruct((total, outs), BF),
            jax.ShapeDtypeStruct((outs, width), BF),
        ),
        grid_spec=pltpu.PrefetchScalarGridSpec(
            num_scalar_prefetch=1,
            grid=(total // rows,),
            in_specs=[raw] * 7 + [line(width), line(width), line(outs)],
            out_specs=(
                tile(width),
                tile(width),
                tile(outs),
                pl.BlockSpec((outs, width), lambda i, place: (0, 0)),
            ),
            scratch_shapes=[
                pltpu.VMEM((total, width), BF),
                pltpu.VMEM((width, outs), BF),
                pltpu.SemaphoreType.DMA((13,)),
            ],
        ),
        cost_estimate=cost(12),
        name="project",
    )(place, *blocks, kept, moved, gain, shift, bias)


def out_mat_kernel(part, place, *refs):
    (mine_ref, other_ref), shares, (mat_ref, sems) = refs[:2], refs[2:6], refs[6:]
    me, floor, core = place[0], place[1], place[2]
    own, width = mine_ref.shape
    wide = width // 2
    rows_each = 2 * own + 4 * part
    made = []
    for source, which in (
        (mine_ref, core),
        (other_ref.at[:, pl.ds(other_ref.shape[1] - width, width)], 1 - core),
    ):
        row = aligned(floor * 2 * own + which * own, own)
        made.append((source, mat_ref.at[pl.ds(row, own), :]))
    for q in range(4):
        for k in range(1, 4):
            for which in range(2):
                row = aligned((floor ^ k) * 2 * own + which * own + (me ^ q) * part, part)
                for half in range(2):
                    at = (k - 1) * rows_each + 2 * own + which * 2 * part + half * part
                    made.append(
                        (
                            shares[q].at[pl.ds(at, part), :],
                            mat_ref.at[pl.ds(row, part), pl.ds(half * wide, wide)],
                        )
                    )
    for copy in start_all(made, sems):
        copy.wait()


def out_matrix(place, mine, other, shares):
    width = mine.shape[1]
    return pl.pallas_call(
        functools.partial(out_mat_kernel, mine.shape[0] // 4),
        out_shape=jax.ShapeDtypeStruct((width, width), BF),
        grid_spec=pltpu.PrefetchScalarGridSpec(
            num_scalar_prefetch=1,
            grid=(1,),
            in_specs=[pl.BlockSpec(memory_space=pl.ANY)] * 6,
            out_specs=pl.BlockSpec((width, width), lambda i, place: (0, 0)),
            scratch_shapes=[pltpu.SemaphoreType.DMA((50,))],
        ),
        cost_estimate=cost(3),
        name="out_matrix",
    )(place, mine, other, *shares)


def attn_out_kernel(place, *refs):
    mixed_refs, (mat_ref, token_ref, bias_ref, gain_ref, shift_ref) = refs[:4], refs[4:9]
    hidden_ref, second_ref, mixed_ref, mixed, sems = refs[9:]
    step = pl.program_id(0)
    me = place[0]
    local = mixed_refs[0].shape[1]
    block = mixed.shape[0]

    @pl.when(step == 0)
    def _():
        made = []
        for k, ref in enumerate(mixed_refs):
            lanes = pl.ds(aligned((me ^ k) * local, local), local)
            made.append((ref.at[pl.ds(0, block), :], mixed.at[:, lanes]))
        for copy in start_all(made, sems):
            copy.wait()

    rows = hidden_ref.shape[0]
    here = mixed[pl.ds(aligned(step * rows, rows), rows), :]
    mixed_ref[...] = here
    hidden = token_ref[...].astype(F32) + nn(here, mat_ref[...]) + bias_ref[...]
    hidden_ref[...] = hidden
    unit, _ = norm_stats(hidden)
    second_ref[...] = (unit * gain_ref[...] + shift_ref[...]).astype(BF)


def attn_out(place, mixed, mat, tokens, bias, gain, shift):
    block, width = tokens.shape
    rows = 256
    raw = pl.BlockSpec(memory_space=pl.ANY)
    line = pl.BlockSpec((1, width), lambda i, place: (0, 0))
    tile = pl.BlockSpec((rows, width), lambda i, place: (i, 0))
    return pl.pallas_call(
        attn_out_kernel,
        out_shape=(
            jax.ShapeDtypeStruct((block, width), F32),
            jax.ShapeDtypeStruct((block, width), BF),
            jax.ShapeDtypeStruct((block, width), BF),
        ),
        grid_spec=pltpu.PrefetchScalarGridSpec(
            num_scalar_prefetch=1,
            grid=(block // rows,),
            in_specs=[raw] * 4
            + [pl.BlockSpec((width, width), lambda i, place: (0, 0)), tile, line, line, line],
            out_specs=(tile, tile, tile),
            scratch_shapes=[pltpu.VMEM((block, width), BF), pltpu.SemaphoreType.DMA((4,))],
        ),
        cost_estimate=cost(5),
        name="attn_out",
    )(place, *mixed, mat, tokens, bias, gain, shift)


def feed_kernel(
    hw, place, second_oth, second_own, branch_oth, branch_own, bias_a, bias_b, mine_ref, other_ref,
    a0, a1, a2, a3, proj_ref, b0, b1, b2, b_up, b_low, act_a, act_b, slope_a, slope_b, out_own, out_oth, back_own, back_oth, sum_a, sum_b,
    fc, proj, fc_turned, proj_turned, total, back, sems,
):
    step = pl.program_id(0)
    me, floor, core = place[0], place[1], place[2]
    own = mine_ref.shape[0]
    chunk = 2 * hw
    rows_each = a0.shape[0] // 3

    def copies(q):
        made = []
        for ref, which in ((mine_ref, core), (other_ref, 1 - core)):
            row = aligned(floor * 2 * own + which * own, own)
            for half in range(2):
                made.append(
                    (
                        ref.at[:, pl.ds(hidden_at(q, half, chunk), chunk)],
                        fc.at[q, pl.ds(row, own), pl.ds(half * chunk, chunk)],
                    )
                )
        for k in range(1, 4):
            row = aligned((floor ^ k) * 2 * own, 2 * own)
            source = (a0, a1, a2, a3)[q].at[pl.ds((k - 1) * rows_each, 2 * own), :]
            made.append((source, fc.at[q, pl.ds(row, 2 * own), :]))
        cut = hw // 2
        for k in range(4):
            row = aligned((floor ^ k) * hw, hw)
            if k == 0:
                made.append((proj_ref.at[pl.ds(aligned((me ^ q) * hw, hw), hw), :], proj.at[q, pl.ds(row, hw), :]))
            elif q < 3:
                source = (b0, b1, b2)[q].at[pl.ds((k - 1) * hw, hw), :]
                made.append((source, proj.at[q, pl.ds(row, hw), :]))
            else:
                for i in range(2):
                    at = (k - 1) * hw + i * cut
                    source = (b_up if at < 3 * cut else b_low).at[pl.ds(at % (3 * cut), cut), :]
                    made.append((source, proj.at[q, pl.ds(aligned(row + i * cut, cut), cut), :]))
        return [
            pltpu.make_async_copy(source, target, sems.at[q, i])
            for i, (source, target) in enumerate(made)
        ]

    @pl.when(step == 0)
    def _():
        for q in range(4):
            for copy in copies(q):
                copy.start()

    for q in range(4):

        @pl.when(step == q)
        def _():
            for copy in copies(q):
                copy.wait()

    fc_turned[...] = fc[step].T
    proj_turned[...] = proj[step].T
    bias = jnp.concatenate([bias_a[...], bias_b[...]], axis=1)
    rows = second_own.shape[0]
    both = 2 * rows
    partial = None
    for start, second_ref, branch_ref in ((0, second_oth, branch_oth), (rows, second_own, branch_own)):
        here = slice(start, start + rows)
        pre = nn(second_ref[...], fc[step]) + bias
        value, bend = gelu_both(pre)
        act = value.astype(BF)
        act_a[here, :] = act[:, :chunk]
        act_b[here, :] = act[:, chunk:]
        slope_full = nn(branch_ref[...], proj_turned[...]) * bend
        slope = slope_full.astype(BF)
        slope_a[here, :] = slope[:, :chunk]
        slope_b[here, :] = slope[:, chunk:]
        more = jnp.sum(slope_full, axis=0, keepdims=True)
        partial = more if partial is None else partial + more
        out_part = nn(act, proj[step])
        back_part = nn(slope, fc_turned[...])

        @pl.when(step == 0)
        def _():
            total[here, :] = out_part
            back[here, :] = back_part

        @pl.when(step > 0)
        def _():
            total[here, :] += out_part
            back[here, :] += back_part

    sum_a[...] = partial[:, :chunk]
    sum_b[...] = partial[:, chunk:]

    @pl.when(step == 3)
    def _():
        half = both // 2
        out_oth[...] = total[:half].astype(BF)
        back_oth[...] = back[:half].astype(BF)
        out_own[...] = total[half:]
        back_own[...] = back[half:]


def feed(place, second, branch, bias, mine, other, shares, w_proj, proj_shares):
    both, width = 2 * second[0].shape[0], second[0].shape[1]
    hidden = mine.shape[1]
    hw = hidden // 16
    chunk = 2 * hw
    raw = pl.BlockSpec(memory_space=pl.ANY)

    def whole(height):
        return pl.BlockSpec((height, width), lambda i, place: (0, 0))

    def upper(height):
        return pl.BlockSpec((height, chunk), lambda i, place: (0, (i % 2) * 2 + i // 2))

    def lower(height, first=0):
        return pl.BlockSpec((height, chunk), lambda i, place: (0, first + i))

    half = jax.ShapeDtypeStruct((both, hidden // 2), BF)
    line = jax.ShapeDtypeStruct((1, hidden // 2), F32)
    return pl.pallas_call(
        functools.partial(feed_kernel, hw),
        out_shape=(
            half,
            half,
            half,
            half,
            jax.ShapeDtypeStruct((both // 2, width), F32),
            jax.ShapeDtypeStruct((both // 2, width), BF),
            jax.ShapeDtypeStruct((both // 2, width), F32),
            jax.ShapeDtypeStruct((both // 2, width), BF),
            line,
            line,
        ),
        grid_spec=pltpu.PrefetchScalarGridSpec(
            num_scalar_prefetch=1,
            grid=(4,),
            in_specs=[whole(both // 2)] * 4 + [upper(1), lower(1, 4)] + [raw] * 12,
            out_specs=(upper(both), lower(both), upper(both), lower(both))
            + (whole(both // 2),) * 4
            + (upper(1), lower(1)),
            scratch_shapes=[
                pltpu.VMEM((4, width, 2 * chunk), BF),
                pltpu.VMEM((4, 2 * chunk, width), BF),
                pltpu.VMEM((2 * chunk, width), BF),
                pltpu.VMEM((width, 2 * chunk), BF),
                pltpu.VMEM((both, width), F32),
                pltpu.VMEM((both, width), F32),
                pltpu.SemaphoreType.DMA((4, 14)),
            ],
        ),
        cost_estimate=cost(35),
        name="feed",
    )(place, *second, *branch, bias, bias, mine, other, *shares, w_proj, *proj_shares)


def mixed_back_kernel(
    place, own_ref, oth_ref, hidden_ref, branch_ref, gain_ref, mat_ref,
    full_ref, low_ref, g0, g1, g2, g3, sums_ref,
):
    step = pl.program_id(0)
    me = place[0]
    local = g0.shape[1]
    slope = own_ref[...] + oth_ref[...].astype(F32)
    unit, scale = norm_stats(hidden_ref[...])
    full = branch_ref[...].astype(F32) + norm_pull(unit, scale, slope * gain_ref[...])
    low = full.astype(BF)
    full_ref[...] = full
    low_ref[...] = low
    for k, ref in enumerate((g0, g1, g2, g3)):
        rows = pl.ds(aligned((me ^ k) * local, local), local)
        ref[...] = nt(low, mat_ref[rows, :]).astype(BF)
    sums = jnp.concatenate(
        [
            jnp.sum(low.astype(F32), axis=0, keepdims=True),
            jnp.sum(slope * unit, axis=0, keepdims=True),
            jnp.sum(slope, axis=0, keepdims=True),
            jnp.sum(branch_ref[...].astype(F32), axis=0, keepdims=True),
        ],
        axis=0,
    )

    @pl.when(step == 0)
    def _():
        sums_ref[...] = sums

    @pl.when(step > 0)
    def _():
        sums_ref[...] += sums


def mixed_back(place, own, oth, hidden, branch, gain, mat):
    block, width = own.shape
    local = width // 4
    rows = block

    def tile(size):
        return pl.BlockSpec((rows, size), lambda i, place: (i, 0))

    def whole(height):
        return pl.BlockSpec((height, width), lambda i, place: (0, 0))

    return pl.pallas_call(
        mixed_back_kernel,
        out_shape=(
            jax.ShapeDtypeStruct((block, width), F32),
            jax.ShapeDtypeStruct((block, width), BF),
        )
        + (jax.ShapeDtypeStruct((block, local), BF),) * 4
        + (jax.ShapeDtypeStruct((4, width), F32),),
        grid_spec=pltpu.PrefetchScalarGridSpec(
            num_scalar_prefetch=1,
            grid=(block // rows,),
            in_specs=[tile(width)] * 4 + [whole(1), whole(width)],
            out_specs=(tile(width), tile(width)) + (tile(local),) * 4 + (whole(4),),
        ),
        cost_estimate=cost(7),
        name="mixed_back",
    )(place, own, oth, hidden, branch, gain, mat)


def first_back_kernel(tiles, parts, place, *refs):
    step = pl.program_id(0)
    count = len(tiles) // 2
    grad_refs, (unit_ref, mat_ref), refs = refs[:parts], refs[parts : parts + 2], refs[parts + 2 :]
    out_refs, sums_ref = refs[:count], refs[count]
    part = nn(jnp.concatenate([ref[...] for ref in grad_refs], axis=1), mat_ref[...])
    low = part.astype(BF)
    for i in range(count):

        @pl.when(step // 2 == i)
        def _():
            out_refs[i][...] = low

    sums = jnp.concatenate(
        [
            jnp.sum(part * unit_ref[...].astype(F32), axis=0, keepdims=True),
            jnp.sum(part, axis=0, keepdims=True),
        ],
        axis=0,
    )

    @pl.when(step == 0)
    def _():
        sums_ref[...] = sums

    @pl.when(step > 0)
    def _():
        sums_ref[...] += sums


def first_back(tiles, grads, unit, mat):
    outs, width = mat.shape
    rows = 256
    table = jnp.asarray(tiles, jnp.int32)

    def at(i, place):
        return (place[i], 0)

    return pl.pallas_call(
        functools.partial(first_back_kernel, tiles, len(grads)),
        out_shape=tuple(jax.ShapeDtypeStruct((2 * rows, width), BF) for _ in tiles[::2])
        + (jax.ShapeDtypeStruct((2, width), F32),),
        grid_spec=pltpu.PrefetchScalarGridSpec(
            num_scalar_prefetch=1,
            grid=(len(tiles),),
            in_specs=[pl.BlockSpec((rows, grad.shape[1]), at) for grad in grads]
            + [
                pl.BlockSpec((rows, width), at),
                pl.BlockSpec((outs, width), lambda i, place: (0, 0)),
            ],
            out_specs=tuple(
                pl.BlockSpec((rows, width), lambda i, place, g=g: (jnp.clip(i - 2 * g, 0, 1), 0))
                for g in range(len(tiles) // 2)
            )
            + (pl.BlockSpec((2, width), lambda i, place: (0, 0)),),
        ),
        cost_estimate=cost(5),
        name="first_back",
    )(table, *grads, unit, mat)


def gather_fc_kernel(place, fa, xa, la, fb, yb, lb, o0, o1, o2, o3, fc):
    floor = place[1]
    chunk = fc.shape[1] // 2
    fc[:, :chunk] = fa[...].astype(F32) + xa[...].astype(F32) + la[...].astype(F32)
    fc[:, chunk:] = fb[...].astype(F32) + yb[...].astype(F32) + lb[...].astype(F32)
    rows = fc.shape[0] // 4
    for k, out in enumerate((o0, o1, o2, o3)):
        out[...] = fc[pl.ds(aligned((floor ^ k) * rows, rows), rows), :].astype(BF)


def gather_proj_kernel(place, pa, xp, lpa, pb, yp, lpb, o0, o1, o2, o3, proj):
    floor = place[1]
    chunk = proj.shape[0] // 2
    proj[:chunk, :] = pa[...].astype(F32) + xp[...].astype(F32) + lpa[...].astype(F32)
    proj[chunk:, :] = pb[...].astype(F32) + yp[...].astype(F32) + lpb[...].astype(F32)
    rows = proj.shape[0] // 4
    for k, out in enumerate((o0, o1, o2, o3)):
        out[...] = proj[pl.ds(aligned((floor ^ k) * rows, rows), rows), :].astype(BF)


def gather_sum(place, kernel, parts, shape, block):
    out = jax.ShapeDtypeStruct((shape[0] // 4, shape[1]), BF)
    return pl.pallas_call(
        kernel,
        out_shape=(out,) * 4,
        grid_spec=pltpu.PrefetchScalarGridSpec(
            num_scalar_prefetch=1,
            grid=(1,),
            in_specs=[pl.BlockSpec(block, lambda i, place: (0, 0))] * 6,
            out_specs=(pl.BlockSpec(out.shape, lambda i, place: (0, 0)),) * 4,
            scratch_shapes=[pltpu.VMEM(shape, F32)],
        ),
        cost_estimate=cost(3),
        name="gather_sum",
    )(place, *parts)


def spread_fc_kernel(place, *refs):
    me, core = place[0], place[2]
    finals, fc_ref = refs[:4], refs[4]
    own = fc_ref.shape[0]
    hw = finals[0].shape[1] // 4
    for q in range(4):
        for part, which in ((0, core), (1, 1 - core)):
            for z in range(4):
                lanes = pl.ds(aligned(z * 8 * hw + which * 4 * hw + (me ^ q) * hw, hw), hw)
                block = finals[q][part * own : (part + 1) * own, z * hw : (z + 1) * hw]
                fc_ref[:, lanes] = block.astype(F32)


def spread_proj_kernel(place, *refs):
    me = place[0]
    finals, proj_ref = refs[:4], refs[4]
    hw = finals[0].shape[0]
    for q in range(4):
        proj_ref[pl.ds(aligned((me ^ q) * hw, hw), hw), :] = finals[q][...].astype(F32)


def spread(place, kernel, finals, shape):
    def whole(shape):
        return pl.BlockSpec(shape, lambda i, place: (0, 0))

    return pl.pallas_call(
        kernel,
        out_shape=jax.ShapeDtypeStruct(shape, F32),
        grid_spec=pltpu.PrefetchScalarGridSpec(
            num_scalar_prefetch=1,
            grid=(1,),
            in_specs=[whole(finals[0].shape)] * 4,
            out_specs=whole(shape),
        ),
        cost_estimate=cost(2),
        name="spread",
    )(place, *finals)


def last_kernel(
    keep_ref, got_x, got_y, last_y, last_x, token_ref, hidden_ref, gain_ref, out_ref
):
    def finish(got, last):
        slope = keep_ref[...].astype(F32) + got[...].astype(F32) + last[...].astype(F32)
        unit, scale = norm_stats(token_ref[...].astype(F32))
        out_ref[...] = hidden_ref[...] + norm_pull(unit, scale, slope * gain_ref[...])

    @pl.when(pl.program_id(0) == 0)
    def _():
        finish(got_x, last_y)

    @pl.when(pl.program_id(0) == 1)
    def _():
        finish(got_y, last_x)


def body_aligned(
    tokens,
    prompt_lens,
    cont_lens,
    gain_one,
    shift_one,
    w_qkv,
    bias_qv,
    w_out,
    bias_out,
    gain_two,
    shift_two,
    w_fc,
    bias_fc,
    w_proj,
    bias_proj,
    cotangent,
):
    ns = nz = 4
    nf = 8
    me = lax.axis_index("seq")
    owner = lax.axis_index("fsdp")
    floor = owner // 2
    core = owner % 2
    place = jnp.stack([me, floor, core]).astype(jnp.int32)
    toks, width = tokens.shape[1:]
    own = width // nf
    heads = H // ns
    local = width // ns
    hw = w_fc.shape[1] // (nf * ns)
    token_block = tokens[0]
    branch = cotangent[0]

    half = toks // 2
    vectors = [gain_one, shift_one, bias_qv, bias_out, gain_two, shift_two, bias_fc, bias_proj]
    packed = jnp.concatenate([v.reshape(-1, own) for v in vectors], axis=0)
    lines = packed.shape[0]
    packed = jnp.pad(packed.reshape(-1), (0, 16 * 3 * local - packed.size)).reshape(16, 3 * local)
    mine_qkv = pick(w_qkv.reshape(own, 3, ns, local), me, 2).reshape(own, 3 * local)
    sent_qkv = jnp.concatenate([mine_qkv, packed], axis=0)
    tok_one = swap(token_block, "seq", 1)
    tok_two = swap(token_block, "seq", 2)
    got_qkv = [swap(sent_qkv, "fsdp", 2 * k) for k in range(1, nz)]
    fc_mine, fc_sent, proj_share = pack(place, after(w_fc, sent_qkv), w_proj, w_out)
    fc_other = swap(fc_sent, "fsdp", 1)
    fc_share = join(place, fc_mine, fc_other, w_out)

    tok_one, tok_two, got_qkv, fc_share, proj_share = lax.optimization_barrier(
        (tok_one, tok_two, got_qkv, fc_share, proj_share)
    )
    tok_up = swap(tok_two[:half], "seq", 1)
    tok_low = swap(tok_one[half:], "seq", 2)
    kept_qkv = jnp.stack([sent_qkv, *got_qkv])
    moved_qkv = swap(kept_qkv, "fsdp", 1)
    moved_qkv, fc_share = lax.optimization_barrier((moved_qkv, fc_share))
    fc_got = [swap(fc_share, "fsdp", 2 * k) for k in range(1, nz)]

    small = by_core(core, kept_qkv[:, own : own + 2], moved_qkv[:, own : own + 2], 1)
    small = xor_take(small, floor, 0).reshape(nf, -1).reshape(nf, lines, own)
    at = 0
    full = []
    for v in vectors:
        count = v.shape[0] // own
        full.append(small[:, at : at + count].reshape(1, -1).astype(F32))
        at += count
    gain_a, shift_a, qv_vec, out_vec, gain_b, shift_b, fc_vec, proj_vec = full
    qv_mine = pick(qv_vec.reshape(2, ns, local), me, 1)
    bias_all = jnp.concatenate([qv_mine[0], jnp.zeros((local,), F32), qv_mine[1]]).reshape(1, -1)
    fc_bias = xor_take(pick(fc_vec.reshape(nz, 2, ns, hw), core, 1), me, 1)
    order = [(q, 0) for q in (0, 2, 1, 3)] + [(q, 1) for q in range(4)]
    fc_bias = jnp.concatenate(
        [fc_bias[2 * part : 2 * part + 2, q].reshape(1, -1) for q, part in order], axis=1
    )

    first, unit_all, qkv, qkv_turned = project(
        place, (token_block, tok_one, tok_two, tok_up, tok_low), kept_qkv, moved_qkv, gain_a, shift_a,
        bias_all,
    )
    lens = jnp.concatenate([prompt_lens, cont_lens[0], me.reshape(1)]).astype(jnp.int32)

    qkv, fc_got, proj_share = lax.optimization_barrier((qkv, fc_got, proj_share))
    fc_zero = joined(fc_got)
    fc_one = swap(fc_zero, "seq", 1)
    fc_two = swap(fc_zero, "seq", 2)
    proj_got = [swap(proj_share, "fsdp", 2 * k) for k in range(1, nz)]
    ends = {}

    def between(lens, mixed, arrays):
        (mixed, arrays, one, two, got, ends["branch"]) = lax.optimization_barrier(
            (mixed, arrays, fc_one, fc_two, proj_got, branch)
        )
        ends["branch_got"] = swap(ends["branch"], "fsdp", 1)
        cut = one.shape[0] // 2
        ends["fc"] = (one, two, swap(two[:cut], "seq", 1), swap(one[cut:], "seq", 2))
        ends["proj"] = joined(got)
        return lens, mixed, arrays

    mixed_heads, norms = attend_forward(lens, qkv, heads, between)
    fc_one, fc_two, fc_up, fc_low = ends["fc"]
    proj_zero = ends["proj"]

    mixed_heads, fc_up, fc_low, proj_zero, branch_got = lax.optimization_barrier(
        (mixed_heads, fc_up, fc_low, proj_zero, ends["branch_got"])
    )
    branch_both = jnp.concatenate([branch_got, branch], axis=0)
    mixed_blocks = [mixed_heads] + [
        swap(mixed_heads[k * toks : (k + 1) * toks], "seq", k) for k in range(1, ns)
    ]
    fc_three = joined([fc_up, fc_low])
    shares = (fc_zero, fc_one, fc_two, fc_three)
    proj_one = swap(proj_zero, "seq", 1)
    proj_two = swap(proj_zero, "seq", 2)
    cut = proj_one.shape[0] // 2
    proj_three = swap(proj_two[:cut], "seq", 1), swap(proj_one[cut:], "seq", 2)
    out_mat = out_matrix(place, w_out, fc_other, shares)
    mixed_blocks, branch_both, out_mat = lax.optimization_barrier((mixed_blocks, branch_both, out_mat))
    hidden, second, mixed = attn_out(
        place, mixed_blocks, out_mat, token_block, out_vec, gain_b, shift_b
    )

    second_got = swap(second, "fsdp", 1)
    *hiddens, out_own, out_oth, back_own, back_oth, sum_upper, sum_lower = feed(
        place, (second_got, second), (branch_got, branch), fc_bias, fc_mine, fc_other,
        shares, w_proj, (proj_zero, proj_one, proj_two, *proj_three),
    )
    back_got = swap(back_oth, "fsdp", 1)
    out_got = swap(out_oth, "fsdp", 1)
    grad_hidden, grad_attn, *grad_blocks, sums_two = mixed_back(
        place, back_own, back_got, hidden, branch, gain_b, out_mat
    )

    def added(left, right):
        return (left.astype(F32) + right.astype(F32)).astype(BF)

    def halves(values, index):
        pair = values.reshape(2, values.shape[0] // 2, values.shape[1])
        return pick(pair, index, 0).astype(F32), pick(pair, 1 - index, 0).astype(BF)

    def core_halves(grad):
        cut = grad.reshape(nz, 2, own, -1)
        mine, sent = pick(cut, core, 1), pick(cut, 1 - core, 1)
        return mine.reshape(nz * own, -1), sent.reshape(nz * own, -1)

    edge = 4 * hw
    chunk = 2 * hw
    head_got = [swap(grad_blocks[k], "seq", k) for k in range(1, ns)]
    hiddens, branch_late, second_late, second_got, mixed_late, attn_late = after(
        (hiddens, branch_both, second, second_got, mixed, grad_attn), grad_blocks
    )
    acts, slopes = (
        [v[:, i * edge : (i + 1) * edge] for v in pair for i in range(2)]
        for pair in (hiddens[:2], hiddens[2:])
    )
    wo_mine, wo_sent = core_halves(tn(mixed_late, attn_late).astype(BF))
    second_both = jnp.concatenate([second_got, second_late], axis=0)

    head_x = head_got[0]
    acts, slopes, second_both, branch_late, wo_sent, head_x, out_got = after(
        (acts, slopes, second_both, branch_late, wo_sent, head_x, out_got)
    )
    proj_grads = [tn(v, branch_late).astype(BF) if i % 2 else None for i, v in enumerate(acts)]
    proj_x = swap(proj_grads[1], "seq", 1)
    proj_y = swap(proj_grads[3], "seq", 2)
    wo_got = swap(wo_sent, "fsdp", 1)
    fc_grads = [None] * 4
    for i in (1, 3, 0, 2):
        fc_grads[i] = tn(second_both, slopes[i]).astype(BF)
    for i in (0, 2):
        proj_grads[i] = tn(acts[i], branch_late).astype(BF)
    output = (hidden + out_own + proj_vec + out_got.astype(F32)).astype(BF)

    grad_heads = jnp.concatenate([grad_blocks[0], head_x, *head_got[1:]], axis=0)
    grad_heads, fc_grads, proj_keep, wo_got, output = after(
        (grad_heads, fc_grads, proj_grads[::2], wo_got, output)
    )
    fc_x = swap(fc_grads[1], "seq", 1)
    fc_y = swap(fc_grads[3], "seq", 2)
    wo_keep, wo_sent = halves(wo_mine.astype(F32) + wo_got.astype(F32), floor // 2)
    wo_far = swap(wo_sent, "fsdp", 4)
    back = {}

    def between_back(lens, parts, grad):
        parts, grad, x, y, far = after((parts, grad, proj_x, proj_y, wo_far))
        back["proj"] = (
            x,
            y,
            swap(added(proj_keep[1][chunk:], y[chunk:]), "seq", 1),
            swap(added(proj_keep[0][chunk:], x[chunk:]), "seq", 2),
        )
        keep, sent = halves(wo_keep + far.astype(F32), floor % 2)
        back["out"] = keep, swap(sent, "fsdp", 2)
        return lens, parts, grad

    backward = attend_backward(lens, qkv, mixed_heads, norms, grad_heads, heads, between_back)
    proj_x, proj_y, proj_last_x, proj_last_y = back["proj"]
    wo_keep, wo_near = back["out"]

    backward, fc_x, fc_y, proj_x, proj_y, proj_last_x, proj_last_y, wo_near = after(
        (backward, fc_x, fc_y, proj_x, proj_y, proj_last_x, proj_last_y, wo_near)
    )
    fc_far = [added(fc_grads[0][:, chunk:], fc_x[:, chunk:]), added(fc_grads[2][:, chunk:], fc_y[:, chunk:])]
    fc_last_y = swap(fc_far[0], "seq", 2)
    fc_last_x = swap(fc_far[1], "seq", 1)
    wo_sum = wo_keep + wo_near.astype(F32)
    wo_got = swap(wo_sum.astype(BF), "seq", 1)
    backward = after(backward, fc_far)
    parts = [part[i] for i in range(3) for part in backward]
    sent_x, sent_y, sums_early = first_back((2, 6, 5, 7), parts, unit_all, qkv_turned)

    sent_x, sent_y, parts, fc_last_x, fc_last_y, proj_x, proj_y = after(
        (sent_x, sent_y, parts, fc_last_x, fc_last_y, proj_x, proj_y)
    )
    got_x = swap(sent_x, "seq", 1)
    got_y = swap(sent_y, "seq", 2)
    cuts = gather_sum(
        place, gather_proj_kernel,
        (proj_keep[0], proj_x, proj_last_y, proj_keep[1], proj_y, proj_last_x),
        (4 * hw, width), (chunk, width),
    )
    cuts, wo_got = after((cuts, wo_got))
    cuts_proj = [swap(cuts[k], "fsdp", 2 * k) for k in range(1, nz)]
    grad_proj_kept = cuts[0]
    fc_grads = after(fc_grads, cuts)
    cuts = gather_sum(
        place, gather_fc_kernel,
        (fc_grads[0], fc_x, fc_last_y, fc_grads[2], fc_y, fc_last_x),
        (width, 4 * hw), (width, chunk),
    )

    parts = after(parts, cuts)
    far_late, kept_late, sums_late = first_back((4, 3, 0, 1), parts, unit_all, qkv_turned)
    cuts_proj, cuts, far_late = after((cuts_proj, cuts, far_late))
    cuts_fc = [swap(cuts[k], "fsdp", 2 * k) for k in range(1, nz)]
    fc_kept = cuts[0]

    got_x, got_y, far_late, parts = after((got_x, got_y, far_late, parts))
    far_y = added(far_late[:half], got_x[half:])
    far_x = added(far_late[half:], got_y[half:])
    last_y = swap(far_y, "seq", 2)
    last_x = swap(far_x, "seq", 1)
    parts, first_late, cuts_proj = after((parts, first, cuts_proj), far_x, far_y)
    grad_qkv = jnp.concatenate(parts, axis=1)
    wi_grad = tn(first_late, grad_qkv).astype(BF)
    proj_owned = grad_proj_kept.astype(F32)
    for part in cuts_proj:
        proj_owned = proj_owned + part.astype(F32)
    proj_owned = proj_owned.astype(BF)
    wo_sum = wo_sum + wo_got.astype(F32)
    wo_sent = wo_sum.astype(BF)

    def placed(values):
        slots = jnp.arange(ns)[:, None] == me
        return jnp.where(slots, values[None, :], 0.0).reshape(-1)

    spots = {}
    for i, (q, part) in enumerate(order):
        here = (sum_upper, sum_lower)[part][0, (i % 4) * chunk : (i % 4 + 1) * chunk]
        spots[q, part] = here.reshape(2, hw)
    fc_bias_grad = jnp.stack(
        [jnp.concatenate([spots[q, 0], spots[q, 1]], axis=0) for q in range(ns)], axis=1
    )
    fc_bias_grad = xor_take(fc_bias_grad, me, 1)
    fc_bias_grad = jnp.where(
        (jnp.arange(2) == core)[None, :, None, None], fc_bias_grad[:, None], 0.0
    ).reshape(-1)
    sums_one = sums_early + sums_late
    qkv_sum = jnp.sum(grad_qkv.astype(F32), axis=0)
    vector_grads = [
        sums_one[0],
        sums_one[1],
        jnp.concatenate([placed(qkv_sum[:local]), placed(qkv_sum[2 * local :])]),
        sums_two[0],
        sums_two[1],
        sums_two[2],
        fc_bias_grad,
        sums_two[3],
    ]
    by_owner = jnp.concatenate([v.reshape(nf, -1) for v in vector_grads], axis=1)
    by_owner = by_owner.reshape(nz, 2, -1, 3 * local)
    lines = by_owner.shape[2]
    tall = own + 16
    by_owner = jnp.pad(by_owner, ((0, 0), (0, 0), (0, 16 - lines), (0, 0)))
    wi_cut = jnp.concatenate([wi_grad.reshape(nz, 2, own, 3 * local), by_owner.astype(BF)], axis=2)
    wi_mine = pick(wi_cut, core, 1).reshape(nz * tall, 3 * local)
    wi_sent = pick(wi_cut, 1 - core, 1).reshape(nz * tall, 3 * local)
    last_x, last_y, cuts_fc, wi_sent, proj_owned, wo_sum, wo_sent = after(
        (last_x, last_y, cuts_fc, wi_sent, proj_owned, wo_sum, wo_sent)
    )
    wo_got = swap(wo_sent, "seq", 2)
    wi_got = swap(wi_sent, "fsdp", 1)
    fc_owned = fc_kept.astype(F32)
    for part in cuts_fc:
        fc_owned = fc_owned + part.astype(F32)
    fc_mine, fc_sent = halves(fc_owned, core)
    fc_got = swap(fc_sent, "fsdp", 1)

    wi_got, fc_got, wo_got = after((wi_got, fc_got, wo_got))
    wi_keep, wi_sent = halves(wi_mine.astype(F32) + wi_got.astype(F32), floor // 2)
    wi_far = swap(wi_sent, "fsdp", 4)
    fc_final = jnp.concatenate([fc_mine.astype(BF), fc_got], axis=0)
    fc_finals = [fc_final] + [swap(fc_final, "seq", k) for k in range(1, ns)]
    last_x, last_y, kept_late = after((last_x, last_y, kept_late), fc_final, wi_sent)
    ends_at = pl.BlockSpec((half, width), lambda i: (i, 0))
    one_end = pl.BlockSpec((half, width), lambda i: (0, 0))
    input_grad = pl.pallas_call(
        last_kernel,
        out_shape=jax.ShapeDtypeStruct((toks, width), F32),
        grid=(2,),
        in_specs=[ends_at] + [one_end] * 4 + [ends_at] * 2 + [pl.BlockSpec((1, width), lambda i: (0, 0))],
        out_specs=ends_at,
        cost_estimate=cost(5),
        name="last",
    )(kept_late, got_x, got_y, last_y, last_x, token_block, grad_hidden, gain_a)

    fc_finals, input_grad, proj_owned, wi_far = after((fc_finals, input_grad, proj_owned, wi_far))
    input_grad = input_grad[None]
    proj_finals = [proj_owned] + [swap(proj_owned, "seq", k) for k in range(1, ns)]
    grad_w_out = wo_sum + wo_got.astype(F32)
    grad_w_fc = spread(place, spread_fc_kernel, fc_finals, (own, 32 * hw))

    wi_keep, wi_sent = halves(wi_keep + wi_far.astype(F32), floor % 2)
    wi_near = swap(wi_sent, "fsdp", 2)

    wi_near, grad_w_fc = after((wi_near, grad_w_fc))
    wi_owned = wi_keep + wi_near.astype(F32)
    wi_low = wi_owned.astype(BF)
    wi_finals = [wi_low] + [swap(wi_low, "seq", k) for k in range(1, ns)]
    grad_w_proj = spread(place, spread_proj_kernel, proj_finals, (4 * hw, width))
    wi_blocks = jnp.stack([v[:own].reshape(own, 3, local) for v in wi_finals], axis=2)
    grad_w_qkv = xor_take(wi_blocks, me, 2).reshape(own, 3 * width).astype(F32)
    output = output[None]
    vector_sum = wi_owned[own : own + lines]
    for v in wi_finals[1:]:
        vector_sum = vector_sum + v[own : own + lines].astype(F32)
    vector_sum = vector_sum.reshape(-1)
    outs = []
    at = 0
    for v in vectors:
        count = v.shape[0]
        outs.append(vector_sum[at : at + count])
        at += count
    (g_gain_one, g_shift_one, g_bias_qv, g_bias_out, g_gain_two, g_shift_two, g_bias_fc, g_bias_proj) = outs

    return (
        output,
        input_grad,
        g_gain_one,
        g_shift_one,
        grad_w_qkv,
        g_bias_qv,
        grad_w_out,
        g_bias_out,
        g_gain_two,
        g_shift_two,
        grad_w_fc,
        g_bias_fc,
        grad_w_proj,
        g_bias_proj,
    )


def body(*args):
    tokens, w_proj = args[0], args[13]
    fits = (
        lax.axis_size("seq") == 4
        and lax.axis_size("fsdp") == 8
        and tokens.shape[1:] == (512, 1024)
        and w_proj.shape == (512, 1024)
    )
    return body_aligned(*args) if fits else body_general(*args)


def solution(mesh):
    rows = P("fsdp", None)
    vec = P("fsdp")
    acts = P("fsdp", "seq", None)
    return jax.shard_map(
        body,
        mesh=mesh,
        in_specs=(
            acts, vec, rows, vec, vec, rows, vec, rows, vec, vec, vec, rows, vec, rows, vec, acts,
        ),
        out_specs=(
            acts, acts, vec, vec, rows, vec, rows, vec, vec, vec, rows, vec, rows, vec,
        ),
        check_vma=False,
    )
```

```python
import functools

import jax
import jax.numpy as jnp
from jax import lax
from jax.experimental import pallas as pl
from jax.experimental.pallas import tpu as pltpu
from jax.sharding import PartitionSpec as P

H = 16
HD = 64
PROMPT = 1024
CONTLEN = 512
CONTS = 2

EPS = 1e-05
GELU_C = 0.7978845608028654
GELU_A = 0.044715
NEG = -1e30
BF = jnp.bfloat16
F32 = jnp.float32


def swap(values, axis, bits):
    size = lax.axis_size(axis)
    return lax.ppermute(values, axis, [(i, i ^ bits) for i in range(size)])


def xor_take(values, index, axis):
    size = values.shape[axis]
    bit = 1
    while bit < size:
        parts = [lax.slice_in_dim(values, i, i + 1, axis=axis) for i in range(size)]
        flipped = jnp.concatenate([parts[i ^ bit] for i in range(size)], axis=axis)
        values = jnp.where((index & bit) != 0, flipped, values)
        bit *= 2
    return values


def xor_blocks(values, index, count, axis):
    width = values.shape[axis] // count
    return jnp.concatenate(
        [
            lax.dynamic_slice_in_dim(values, (i ^ index) * width, width, axis=axis)
            for i in range(count)
        ],
        axis=axis,
    )


def plane_gather(values):
    size = lax.axis_size("seq")
    if size != 4:
        return [values] + [swap(values, "seq", k) for k in range(1, size)]
    half = values.shape[0] // 2
    one = swap(values, "seq", 1)
    two = swap(values, "seq", 2)
    three = jnp.concatenate(
        [swap(two[:half], "seq", 1), swap(one[half:], "seq", 2)], axis=0
    )
    return [values, one, two, three]


def plane_scatter(blocks):
    size = lax.axis_size("seq")
    if size != 4:
        total = blocks[0].astype(F32)
        for k in range(1, size):
            total = total + swap(blocks[k].astype(BF), "seq", k).astype(F32)
        return total
    half = blocks[0].shape[0] // 2
    sent_x = jnp.concatenate([blocks[1][:half], blocks[3][:half]], axis=0).astype(BF)
    sent_y = jnp.concatenate([blocks[2][half:], blocks[3][half:]], axis=0).astype(BF)
    got_x = swap(sent_x, "seq", 1).astype(F32)
    got_y = swap(sent_y, "seq", 2).astype(F32)
    next_y = (blocks[2][:half].astype(F32) + got_x[half:]).astype(BF)
    next_x = (blocks[1][half:].astype(F32) + got_y[half:]).astype(BF)
    last_y = swap(next_y, "seq", 2).astype(F32)
    last_x = swap(next_x, "seq", 1).astype(F32)
    upper = blocks[0][:half].astype(F32) + got_x[:half] + last_y
    lower = blocks[0][half:].astype(F32) + got_y[:half] + last_x
    return jnp.concatenate([upper, lower], axis=0)


def after(values, *needed):
    return lax.optimization_barrier((values, needed))[0]


def cost(micros, size=0):
    return pl.CostEstimate(flops=int(micros * 1.15e6), bytes_accessed=int(size), transcendentals=0)


def tile_rows(total, blocks):
    return min(512, total // blocks)


def rel_row(tile, rows, block_rows, me):
    per = block_rows // rows
    return pl.multiple_of(((tile // per) ^ me) * block_rows + (tile % per) * rows, rows)


def walk(tile, rows):
    prompt_tiles = PROMPT // rows
    cont_tiles = CONTLEN // rows
    in_prompt = tile < prompt_tiles
    inside = lax.rem(jnp.maximum(tile - prompt_tiles, 0), cont_tiles)
    count = jnp.where(in_prompt, tile, prompt_tiles + inside)
    return count, tile - inside - prompt_tiles


def key_limit(lens, tile, rows):
    prompt_tiles = PROMPT // rows
    cont_tiles = CONTLEN // rows
    past = jnp.maximum(tile - prompt_tiles, 0)
    cont = jnp.minimum(past // cont_tiles, CONTS - 1)
    length = lens[1]
    for i in range(1, CONTS):
        length = jnp.where(cont == i, lens[1 + i], length)
    return jnp.where(
        tile < prompt_tiles, lens[0] - tile * rows, length - lax.rem(past, cont_tiles) * rows
    )


def pair_stack(block, per_pair, scale=None):
    if scale is not None:
        block = block * scale
    if per_pair == 1:
        return block
    lane = lax.broadcasted_iota(jnp.int32, block.shape, 1) // HD
    return jnp.concatenate(
        [jnp.where(lane == h, block, jnp.zeros_like(block)) for h in range(per_pair)], axis=0
    )


def diagonal_mask(rows, per_pair, limit):
    key = lax.broadcasted_iota(jnp.int32, (rows, per_pair * rows), 0)
    query = lax.broadcasted_iota(jnp.int32, (rows, per_pair * rows), 1) % rows
    return ((key <= query) & (key < limit)) | (key == query)


def live_mask(rows, per_pair, limit):
    return lax.broadcasted_iota(jnp.int32, (rows, per_pair * rows), 0) < limit


def nt(left, right):
    return lax.dot_general(left, right, (((1,), (1,)), ((), ())), preferred_element_type=F32)


def nn(left, right):
    return lax.dot_general(left, right, (((1,), (0,)), ((), ())), preferred_element_type=F32)


def unstack(values, per_pair, rows):
    if per_pair == 1:
        return values
    return jnp.concatenate(
        [values[h * HD : (h + 1) * HD, h * rows : (h + 1) * rows] for h in range(per_pair)], axis=0
    )


def forward_kernel(
    rows, block_rows, per_pair, lens, q_ref, k_ref, v_ref, out_ref, norm_ref, vt_ref, parts, total
):
    tile = pl.program_id(0)
    me = lens[1 + CONTS]
    tiles = q_ref.shape[0] // rows
    across = per_pair * rows

    @pl.when(tile == 0)
    def _():
        def turn(i, carry):
            at = rel_row(i, rows, block_rows, me)
            vt_ref[i] = v_ref[pl.ds(at, rows), :].T
            return carry

        lax.fori_loop(0, tiles, turn, 0)

    at = rel_row(tile, rows, block_rows, me)
    query = pair_stack(q_ref[pl.ds(at, rows), :], per_pair, jnp.asarray(0.125, BF)).T
    count, shift = walk(tile, rows)

    def folded(values):
        return values.reshape(rows // 8, 8, across)

    def scores(i):
        return nn(k_ref[pl.ds(rel_row(i, rows, block_rows, me), rows), :], query)

    def key_tile(i):
        return jnp.where(i < PROMPT // rows, i, i + shift)

    first = jnp.where(
        diagonal_mask(rows, per_pair, key_limit(lens, tile, rows)), scores(tile), NEG
    )

    def measure(i, top):
        here = key_tile(i)
        part = jnp.where(
            live_mask(rows, per_pair, key_limit(lens, here, rows)), scores(here), NEG
        )
        parts[i] = part
        return jnp.maximum(top, jnp.max(folded(part), axis=0))

    top = lax.fori_loop(0, count, measure, jnp.max(folded(first), axis=0))
    top = jnp.max(top, axis=0, keepdims=True)
    weights = jnp.exp(first - top)
    total[...] = nn(vt_ref[tile], weights.astype(BF))

    def gather(i, denom):
        weights = jnp.exp(parts[i] - top)
        total[...] += nn(vt_ref[key_tile(i)], weights.astype(BF))
        return denom + jnp.sum(folded(weights), axis=0)

    denom = lax.fori_loop(0, count, gather, jnp.sum(folded(weights), axis=0))
    denom = jnp.sum(denom, axis=0, keepdims=True)
    mixed = unstack(total[...] / denom, per_pair, rows)
    out_ref[...] = mixed.T.astype(BF)
    norm_ref[0] = top + jnp.log(denom)


def backward_kernel(
    rows, block_rows, per_pair, lens, q_ref, k_ref, v_ref, out_ref, grad_ref, norm_ref,
    dq_ref, dk_ref, dv_ref, kt_ref, dk_sum, dv_sum, dq_sum,
):
    tile = pl.program_id(0)
    me = lens[1 + CONTS]
    tiles = q_ref.shape[0] // rows

    @pl.when(tile == 0)
    def _():
        def turn(i, carry):
            at = rel_row(i, rows, block_rows, me)
            kt_ref[i] = k_ref[pl.ds(at, rows), :].T
            return carry

        lax.fori_loop(0, tiles, turn, 0)
        dk_sum[...] = jnp.zeros_like(dk_sum)
        dv_sum[...] = jnp.zeros_like(dv_sum)

    at = rel_row(tile, rows, block_rows, me)
    query = pair_stack(q_ref[pl.ds(at, rows), :], per_pair, jnp.asarray(0.125, BF))
    grad_block = grad_ref[pl.ds(at, rows), :]
    grad = pair_stack(grad_block, per_pair)
    query_turned = query.T
    grad_turned = grad.T
    product = (grad_block.astype(F32) * out_ref[pl.ds(at, rows), :].astype(F32)).T
    inner = jnp.concatenate(
        [
            jnp.sum(product[h * HD : (h + 1) * HD], axis=0, keepdims=True)
            for h in range(per_pair)
        ],
        axis=1,
    )
    norm = norm_ref[0]

    def one(key_tile, mask):
        key_at = rel_row(key_tile, rows, block_rows, me)
        keys = pl.ds(key_at, rows)
        part = jnp.where(mask, nn(k_ref[keys, :], query_turned), NEG)
        probs = jnp.exp(part - norm)
        slope = probs * (nn(v_ref[keys, :], grad_turned) - inner)
        slope_low = slope.astype(BF)
        dv_sum[keys, :] += nn(probs.astype(BF), grad)
        dk_sum[keys, :] += nn(slope_low, query)
        return nn(kt_ref[key_tile], slope_low)

    dq_sum[...] = one(tile, diagonal_mask(rows, per_pair, key_limit(lens, tile, rows)))
    count, shift = walk(tile, rows)

    def step(i, carry):
        key_tile = jnp.where(i < PROMPT // rows, i, i + shift)
        dq_sum[...] += one(key_tile, live_mask(rows, per_pair, key_limit(lens, key_tile, rows)))
        return carry

    lax.fori_loop(0, count, step, 0)
    dq_ref[...] = (unstack(dq_sum[...], per_pair, rows).T * 0.125).astype(BF)

    @pl.when(tile == tiles - 1)
    def _():
        dk_ref[...] = dk_sum[...].astype(BF)
        dv_ref[...] = dv_sum[...].astype(BF)


def attention_plan(total, heads):
    blocks = lax.axis_size("seq")
    rows = tile_rows(total, blocks)
    per_pair = 2 if heads % 2 == 0 else 1
    return rows, total // blocks, per_pair, heads // per_pair, per_pair * HD


def thirds(qkv, width, pair_width):
    per = width // pair_width
    if pair_width % 128 == 0:
        return (qkv, qkv, qkv), (0, per, 2 * per)
    return tuple(qkv[:, i * width : (i + 1) * width] for i in range(3)), (0, 0, 0)


def row_block(rows, block_rows):
    per = block_rows // rows

    def index(tile, lens):
        return ((tile // per) ^ lens[1 + CONTS]) * per + tile % per, 0

    return index


def attend_forward(lens, qkv, heads, between=None):
    total = qkv.shape[0]
    width = heads * HD
    rows, block_rows, per_pair, pairs, pair_width = attention_plan(total, heads)
    arrays, firsts = thirds(qkv, width, pair_width)
    tiles = total // rows
    most = (PROMPT + CONTLEN) // rows
    mixed = None
    norms = []
    for pair in range(pairs):

        def whole(first):
            return pl.BlockSpec((total, pair_width), lambda tile, lens: (0, first + pair))

        def kernel(lens, q_ref, k_ref, v_ref, *refs):
            forward_kernel(
                rows, block_rows, per_pair, lens, q_ref, k_ref, v_ref, *refs[mixed is not None :]
            )

        place_row = row_block(rows, block_rows)
        more = [] if mixed is None else [mixed]
        mixed, norm = pl.pallas_call(
            kernel,
            out_shape=(
                jax.ShapeDtypeStruct((total, width), BF),
                jax.ShapeDtypeStruct((tiles, 1, per_pair * rows), F32),
            ),
            grid_spec=pltpu.PrefetchScalarGridSpec(
                num_scalar_prefetch=1,
                grid=(tiles,),
                in_specs=[whole(first) for first in firsts]
                + [pl.BlockSpec(memory_space=pl.ANY)] * len(more),
                out_specs=(
                    pl.BlockSpec(
                        (rows, pair_width), lambda tile, lens: (place_row(tile, lens)[0], pair)
                    ),
                    pl.BlockSpec((1, 1, per_pair * rows), lambda tile, lens: (tile, 0, 0)),
                ),
                scratch_shapes=[
                    pltpu.VMEM((tiles, pair_width, rows), BF),
                    pltpu.VMEM((most, rows, per_pair * rows), F32),
                    pltpu.VMEM((pair_width, per_pair * rows), F32),
                ],
            ),
            input_output_aliases={4: 0} if more else {},
            cost_estimate=cost(15),
            name="attend_forward",
        )(lens, *arrays, *more)
        norms.append(norm)
        if between is not None and pair + 1 < pairs:
            lens, mixed, arrays = between(lens, mixed, arrays)
    return mixed, norms


def attend_backward(lens, qkv, mixed, norms, grad, heads, between=None):
    total = qkv.shape[0]
    width = heads * HD
    rows, block_rows, per_pair, pairs, pair_width = attention_plan(total, heads)
    arrays, firsts = thirds(qkv, width, pair_width)
    tiles = total // rows
    made = []
    for pair in range(pairs):

        def whole(first):
            return pl.BlockSpec((total, pair_width), lambda tile, lens: (0, first))

        made.append(
            pl.pallas_call(
                functools.partial(backward_kernel, rows, block_rows, per_pair),
                out_shape=(jax.ShapeDtypeStruct((total, pair_width), BF),) * 3,
                grid_spec=pltpu.PrefetchScalarGridSpec(
                    num_scalar_prefetch=1,
                    grid=(tiles,),
                    in_specs=[whole(first + pair) for first in firsts]
                    + [
                        whole(pair),
                        whole(pair),
                        pl.BlockSpec((1, 1, per_pair * rows), lambda tile, lens: (tile, 0, 0)),
                    ],
                    out_specs=(
                        pl.BlockSpec((rows, pair_width), row_block(rows, block_rows)),
                        whole(0),
                        whole(0),
                    ),
                    scratch_shapes=[
                        pltpu.VMEM((tiles, pair_width, rows), BF),
                        pltpu.VMEM((total, pair_width), F32),
                        pltpu.VMEM((total, pair_width), F32),
                        pltpu.VMEM((pair_width, per_pair * rows), F32),
                    ],
                ),
                cost_estimate=cost(18),
                name="attend_backward",
            )(lens, *arrays, mixed, grad, norms[pair])
        )
        if between is not None and pair + 1 < pairs:
            lens, made[-1], grad = between(lens, made[-1], grad)
    return made


def norm_stats(values):
    center = values - jnp.mean(values, axis=-1, keepdims=True)
    spread = jnp.mean(center * center, axis=-1, keepdims=True)
    scale = lax.rsqrt(spread + EPS)
    return center * scale, scale


def norm_pull(unit, scale, slope):
    return scale * (
        slope
        - jnp.mean(slope, axis=-1, keepdims=True)
        - unit * jnp.mean(slope * unit, axis=-1, keepdims=True)
    )


def gelu_both(values):
    square = values * values
    bent = jnp.tanh(GELU_C * (values + GELU_A * square * values))
    value = 0.5 * values * (1.0 + bent)
    slope = 0.5 * (1.0 + bent) + 0.5 * values * (1.0 - bent * bent) * GELU_C * (
        1.0 + 3.0 * GELU_A * square
    )
    return value, slope


def tn(left, right):
    return lax.dot_general(left, right, (((0,), (0,)), ((), ())), preferred_element_type=F32)


def pick(values, index, axis):
    return lax.dynamic_index_in_dim(values, index, axis, keepdims=False)


def by_core(core, mine, other, axis):
    return jnp.where(
        core == 0, jnp.stack([mine, other], axis=axis), jnp.stack([other, mine], axis=axis)
    )


def body_general(
    tokens,
    prompt_lens,
    cont_lens,
    gain_one,
    shift_one,
    w_qkv,
    bias_qv,
    w_out,
    bias_out,
    gain_two,
    shift_two,
    w_fc,
    bias_fc,
    w_proj,
    bias_proj,
    cotangent,
):
    ns = lax.axis_size("seq")
    nf = lax.axis_size("fsdp")
    nz = nf // 2
    me = lax.axis_index("seq")
    owner = lax.axis_index("fsdp")
    floor = owner // 2
    core = owner % 2
    toks, width = tokens.shape[1:]
    hidden_all = w_fc.shape[1]
    own = width // nf
    heads = H // ns
    local = width // ns
    hw = hidden_all // (nf * ns)
    cols = nz * hw

    token_block = tokens[0]
    branch = cotangent[0]

    token_blocks = plane_gather(token_block)
    vectors = [gain_one, shift_one, bias_qv, bias_out, gain_two, shift_two, bias_fc, bias_proj]
    packed = jnp.concatenate([v.reshape(-1, own) for v in vectors], axis=0)
    lines = packed.shape[0]
    packed_rows = -(-packed.size // (3 * local))
    packed = jnp.pad(packed.reshape(-1), (0, 16 * (-(-packed_rows // 16)) * 3 * local - packed.size))
    mine_qkv = pick(w_qkv.reshape(own, 3, ns, local), me, 2).reshape(own, 3 * local)
    sent_qkv = jnp.concatenate([mine_qkv, packed.reshape(-1, 3 * local)], axis=0)
    got_qkv = jnp.stack([sent_qkv] + [swap(sent_qkv, "fsdp", 2 * k) for k in range(1, nz)])
    got_qkv = xor_take(by_core(core, got_qkv, swap(got_qkv, "fsdp", 1), 1), floor, 0)
    qkv_mat = got_qkv[:, :, :own].reshape(width, 3 * local)
    small = got_qkv[:, :, own:].reshape(nf, -1)[:, : lines * own].reshape(nf, lines, own)
    at = 0
    full = []
    for v in vectors:
        count = v.shape[0] // own
        full.append(small[:, at : at + count].reshape(-1).astype(F32))
        at += count
    gain_a, shift_a, qv_vec, out_vec, gain_b, shift_b, fc_vec, proj_vec = full

    fc_cut = w_fc.reshape(own, nz, 2, ns, hw)
    fc_mine = pick(fc_cut, core, 2)
    fc_other = swap(pick(fc_cut, 1 - core, 2).reshape(own, -1), "fsdp", 1)
    fc_rows = by_core(core, fc_mine.reshape(own, -1), fc_other, 0).reshape(2 * own, nz, ns, hw)
    fc_rows = xor_take(xor_take(fc_rows, floor, 1), me, 2)
    proj_rows = xor_take(w_proj.reshape(ns, hw, width), me, 0)
    out_cols = xor_take(w_out.reshape(own, ns, local), me, 1)
    proj_parts = width // cols
    out_parts = max(1, cols // local)

    def share(q, k):
        fc = jnp.concatenate([fc_rows[:, j ^ k, q] for j in range(nz)], axis=1)
        proj = [proj_rows[q][:, i * cols : (i + 1) * cols] for i in range(proj_parts)]
        out = out_cols[:, q]
        if out_parts > 1:
            step = own // out_parts
            out = jnp.concatenate([out[i * step : (i + 1) * step] for i in range(out_parts)], axis=1)
        return fc, proj, out

    def message(k):
        fc, proj, out = share(0, k)
        return jnp.concatenate([fc, *proj, out.reshape(-1, cols)], axis=0)

    got = [swap(message(k), "fsdp", 2 * k) for k in range(1, nz)]
    rows_each = got[0].shape[0]
    planes = plane_gather(jnp.concatenate(got, axis=0))

    def parts_of(q, k):
        if k == 0:
            fc, proj, out = share(q, 0)
            return fc, jnp.concatenate(proj, axis=1), out_cols[:, q]
        block = planes[q][(k - 1) * rows_each : k * rows_each]
        fc = block[: 2 * own]
        proj = jnp.concatenate(
            [block[2 * own + i * hw : 2 * own + (i + 1) * hw] for i in range(proj_parts)], axis=1
        )
        out = block[2 * own + proj_parts * hw :]
        if out_parts > 1:
            out = jnp.concatenate(
                [out[:, i * local : (i + 1) * local] for i in range(out_parts)], axis=0
            )
        else:
            out = out.reshape(own, local)
        return fc, proj, out

    pieces = [[parts_of(q, k) for k in range(nz)] for q in range(ns)]
    out_half = jnp.stack(
        [jnp.stack([pieces[q][k][2] for q in range(ns)], axis=1) for k in range(nz)]
    )
    out_half = xor_take(out_half, me, 2).reshape(nz, own, width)
    out_both = by_core(core, out_half, swap(out_half, "fsdp", 1), 1)
    out_mat = xor_take(out_both, floor, 0).reshape(ns, local, width)
    out_mat = xor_take(out_mat, me, 0).reshape(width, width)
    fc_mat = jnp.concatenate(
        [jnp.concatenate([pieces[q][k][0] for k in range(nz)], axis=0) for q in range(ns)], axis=1
    )
    proj_mat = jnp.concatenate([pieces[q][k][1] for q in range(ns) for k in range(nz)], axis=0)
    fc_bias = pick(fc_vec.reshape(nz, 2, ns, hw), core, 1)
    fc_bias = xor_take(xor_take(fc_bias, floor, 0), me, 1).transpose(1, 0, 2).reshape(-1)

    all_tokens = jnp.concatenate(token_blocks, axis=0).astype(F32)
    unit_all, _ = norm_stats(all_tokens)
    first = (unit_all * gain_a + shift_a).astype(BF)
    bias_all = jnp.concatenate(
        [
            pick(qv_vec.reshape(2, ns, local)[0], me, 0),
            jnp.zeros((local,), F32),
            pick(qv_vec.reshape(2, ns, local)[1], me, 0),
        ]
    )
    qkv = (jnp.dot(first, qkv_mat, preferred_element_type=F32) + bias_all).astype(BF)
    lens = jnp.concatenate([prompt_lens, cont_lens[0], me.reshape(1)]).astype(jnp.int32)
    mixed_heads, norms = attend_forward(lens, qkv, heads)

    def to_tokens(values):
        return jnp.concatenate(
            [values[:toks]]
            + [swap(values[k * toks : (k + 1) * toks], "seq", k) for k in range(1, ns)],
            axis=1,
        )

    def to_heads(values):
        return jnp.concatenate(
            [values[:, :local]]
            + [swap(values[:, k * local : (k + 1) * local], "seq", k) for k in range(1, ns)],
            axis=0,
        )

    mixed = to_tokens(mixed_heads)
    hidden = token_block.astype(F32) + jnp.dot(mixed, out_mat, preferred_element_type=F32) + out_vec
    unit_two, scale_two = norm_stats(hidden)
    second = (unit_two * gain_b + shift_b).astype(BF)

    second_both = jnp.concatenate([second, swap(second, "fsdp", 1)], axis=0)
    second_both = xor_blocks(second_both, floor, nz, 1)
    branch_both = jnp.concatenate([branch, swap(branch, "fsdp", 1)], axis=0)
    pre = jnp.dot(second_both, fc_mat, preferred_element_type=F32) + fc_bias
    act_full, bend = gelu_both(pre)
    act = act_full.astype(BF)
    grad_act = nt(branch_both, proj_mat)
    grad_pre = (grad_act * bend).astype(BF)
    grad_second_both = nt(grad_pre, fc_mat)
    grad_second = grad_second_both[:toks] + swap(
        grad_second_both[toks:].astype(BF), "fsdp", 1
    ).astype(F32)
    grad_second = xor_blocks(grad_second, floor, nz, 1)
    out_sum = jnp.dot(act, proj_mat, preferred_element_type=F32)
    result = hidden + out_sum[:toks] + proj_vec
    result = result + swap(out_sum[toks:].astype(BF), "fsdp", 1).astype(F32)
    output = result.astype(BF)[None]

    grad_hidden = branch.astype(F32) + norm_pull(unit_two, scale_two, grad_second * gain_b)
    grad_attn = grad_hidden.astype(BF)
    grad_mixed = nt(grad_attn, out_mat).astype(BF)
    grad_heads = to_heads(grad_mixed)

    backward = attend_backward(lens, qkv, mixed_heads, norms, grad_heads, heads)
    grad_q, grad_k, grad_v = (
        jnp.concatenate([part[i] for part in backward], axis=1) for i in range(3)
    )
    grad_qkv = jnp.concatenate([grad_q, grad_k, grad_v], axis=1)
    grad_first_part = nt(grad_qkv, qkv_mat).astype(BF)
    grad_first = plane_scatter(
        [grad_first_part[k * toks : (k + 1) * toks] for k in range(ns)]
    )
    unit_one, scale_one = norm_stats(token_block.astype(F32))
    input_grad = (grad_hidden + norm_pull(unit_one, scale_one, grad_first * gain_a))[None]

    span = nz * hw
    grad_fc = [tn(second_both, grad_pre[:, q * span : (q + 1) * span]).astype(BF) for q in range(ns)]
    grad_proj = [tn(act[:, q * span : (q + 1) * span], branch_both).astype(BF) for q in range(ns)]
    fc_sum = plane_scatter(grad_fc)
    proj_sum = plane_scatter(grad_proj)

    def fc_for(k):
        block = fc_sum[k * 2 * own : (k + 1) * 2 * own].reshape(2 * own, nz, hw)
        return jnp.concatenate([block[:, j ^ k] for j in range(nz)], axis=1)

    def proj_for(k):
        block = proj_sum[k * hw : (k + 1) * hw]
        return jnp.concatenate(
            [block[:, i * span : (i + 1) * span] for i in range(proj_parts)], axis=0
        )

    both_sum = jnp.concatenate([fc_for(0), proj_for(0)], axis=0)
    for k in range(1, nz):
        sent = jnp.concatenate([fc_for(k), proj_for(k)], axis=0).astype(BF)
        both_sum = both_sum + swap(sent, "fsdp", 2 * k).astype(F32)
    fc_owned = both_sum[: 2 * own].reshape(2, own, span)
    fc_kept = pick(fc_owned, core, 0).astype(BF)
    fc_moved = swap(pick(fc_owned, 1 - core, 0).astype(BF), "fsdp", 1)
    final = jnp.concatenate([fc_kept, fc_moved, both_sum[2 * own :].astype(BF)], axis=0)
    finals = plane_gather(final)
    fc_kept_all = jnp.stack([v[:own].reshape(own, nz, hw) for v in finals], axis=2)
    fc_moved_all = jnp.stack([v[own : 2 * own].reshape(own, nz, hw) for v in finals], axis=2)
    grad_w_fc = by_core(core, fc_kept_all, fc_moved_all, 2)
    grad_w_fc = xor_take(xor_take(grad_w_fc, floor, 1), me, 3).reshape(own, hidden_all).astype(F32)
    grad_w_proj = jnp.stack(
        [
            jnp.concatenate(
                [v[2 * own + i * hw : 2 * own + (i + 1) * hw] for i in range(proj_parts)], axis=1
            )
            for v in finals
        ]
    )
    grad_w_proj = xor_take(grad_w_proj, me, 0).reshape(ns * hw, width).astype(F32)

    grad_out = tn(mixed, grad_attn).astype(BF).reshape(ns, local, width)
    grad_out = xor_take(grad_out, me, 0).reshape(nz, 2, own, width)
    grad_out = xor_take(grad_out, floor, 0)
    out_kept = pick(grad_out, core, 1).astype(F32) + swap(
        pick(grad_out, 1 - core, 1), "fsdp", 1
    ).astype(F32)
    out_owned = out_kept[0]
    for k in range(1, nz):
        out_owned = out_owned + swap(out_kept[k].astype(BF), "fsdp", 2 * k).astype(F32)
    bit = 1
    while bit < ns:
        out_owned = out_owned + swap(out_owned.astype(BF), "seq", bit).astype(F32)
        bit *= 2
    grad_w_out = out_owned

    grad_in = tn(first, grad_qkv).astype(BF).reshape(nz, 2, own, 3 * local)
    grad_in = xor_take(grad_in, floor, 0)
    in_kept = pick(grad_in, core, 1).astype(F32) + swap(
        pick(grad_in, 1 - core, 1), "fsdp", 1
    ).astype(F32)
    in_owned = in_kept[0]
    for k in range(1, nz):
        in_owned = in_owned + swap(in_kept[k].astype(BF), "fsdp", 2 * k).astype(F32)
    in_owned = in_owned.astype(BF)
    in_blocks = jnp.stack(
        [in_owned.reshape(own, 3, local)]
        + [swap(in_owned, "seq", k).reshape(own, 3, local) for k in range(1, ns)],
        axis=2,
    )
    grad_w_qkv = xor_take(in_blocks, me, 2).reshape(own, 3 * width).astype(F32)

    def placed(values, parts):
        slots = jnp.arange(parts)[:, None] == me
        return jnp.where(slots, values[None, :], 0.0).reshape(-1)

    part_f32 = grad_first_part.astype(F32)
    fc_bias_grad = jnp.sum(grad_pre.astype(F32), axis=0).reshape(ns, nz, hw).transpose(1, 0, 2)
    fc_bias_grad = xor_take(xor_take(fc_bias_grad, floor, 0), me, 1)
    fc_bias_grad = jnp.where(
        (jnp.arange(2) == core)[None, :, None, None], fc_bias_grad[:, None], 0.0
    ).reshape(-1)
    vector_grads = [
        jnp.sum(part_f32 * unit_all, axis=0),
        jnp.sum(part_f32, axis=0),
        placed(jnp.sum(grad_q.astype(F32), axis=0), ns),
        placed(jnp.sum(grad_v.astype(F32), axis=0), ns),
        jnp.sum(grad_attn.astype(F32), axis=0),
        jnp.sum(grad_second * unit_two, axis=0),
        jnp.sum(grad_second, axis=0),
        fc_bias_grad,
        jnp.sum(branch.astype(F32), axis=0),
    ]
    vector_sum = jnp.concatenate([v.reshape(-1, width) for v in vector_grads], axis=0)
    for axis, size in (("seq", ns), ("fsdp", nf)):
        bit = 1
        while bit < size:
            vector_sum = vector_sum + swap(vector_sum, axis, bit)
            bit *= 2
    vector_sum = vector_sum.reshape(-1)
    outs = []
    at = 0
    for v in vectors:
        count = v.shape[0]
        outs.append(lax.dynamic_slice_in_dim(vector_sum, at + owner * count, count))
        at += nf * count
    (g_gain_one, g_shift_one, g_bias_qv, g_bias_out, g_gain_two, g_shift_two, g_bias_fc, g_bias_proj) = outs

    return (
        output,
        input_grad,
        g_gain_one,
        g_shift_one,
        grad_w_qkv,
        g_bias_qv,
        grad_w_out,
        g_bias_out,
        g_gain_two,
        g_shift_two,
        grad_w_fc,
        g_bias_fc,
        grad_w_proj,
        g_bias_proj,
    )


UPPER = (0, 2, 1, 3)


def hidden_at(q, half, size):
    return half * 4 * size + (UPPER[q] if half == 0 else q) * size


def start_all(copies, sems):
    made = [
        pltpu.make_async_copy(source, target, sems.at[i]) for i, (source, target) in enumerate(copies)
    ]
    for copy in made:
        copy.start()
    return made


def aligned(value, size):
    return pl.multiple_of(value, size)


def pack_kernel(hw, place, fc_ref, proj_ref, out_mat_ref, mine_ref, other_ref, share_ref):
    me, core = place[0], place[2]
    for q in range(4):
        for z in range(4):
            target = hidden_at(q, z // 2, 2 * hw) + (z % 2) * hw
            for out_ref, which in ((mine_ref, core), (other_ref, 1 - core)):
                source = aligned(z * 8 * hw + which * 4 * hw + (me ^ q) * hw, hw)
                out_ref[:, target : target + hw] = fc_ref[:, pl.ds(source, hw)]
    share_ref[...] = proj_ref[...]
    other_ref[:, 16 * hw :] = out_mat_ref[...]


def pack(place, w_fc, w_proj, w_out):
    own, hidden_all = w_fc.shape
    hw, width = w_proj.shape[0] // 4, w_proj.shape[1]

    def whole(shape):
        return pl.BlockSpec(shape, lambda i, place: (0, 0))

    half = jax.ShapeDtypeStruct((own, hidden_all // 2), BF)
    more = jax.ShapeDtypeStruct((own, hidden_all // 2 + width), BF)
    return pl.pallas_call(
        functools.partial(pack_kernel, hw),
        out_shape=(half, more, jax.ShapeDtypeStruct((hw, width), BF)),
        grid_spec=pltpu.PrefetchScalarGridSpec(
            num_scalar_prefetch=1,
            grid=(1,),
            in_specs=[
                whole((own, hidden_all)),
                pl.BlockSpec((hw, width), lambda i, place: (place[0], 0)),
                whole(w_out.shape),
            ],
            out_specs=(whole(half.shape), whole(more.shape), whole((hw, width))),
        ),
        cost_estimate=cost(3),
        name="pack_shares",
    )(place, w_fc, w_proj, w_out)


def join_kernel(place, m0, m1, o0, o1, mine_out, l0, l1, out_ref):
    core = place[2]
    own, chunk = m0.shape
    part = mine_out.shape[0]
    for refs, which in (((m0, m1), core), ((o0, o1), 1 - core)):
        rows = pl.ds(aligned(which * own, own), own)
        for half in range(2):
            out_ref[rows, half * chunk : (half + 1) * chunk] = refs[half][...]
    wide = 2 * chunk
    for parts, which in (
        ((mine_out[:, :wide], mine_out[:, wide:]), core),
        ((l0[...], l1[...]), 1 - core),
    ):
        for half in range(2):
            rows = pl.ds(aligned(2 * own + which * 2 * part + half * part, part), part)
            out_ref[rows, :] = parts[half]


def join(place, mine, other, w_out):
    own, hidden = mine.shape
    chunk = hidden // 8
    part = own // 4
    rows = 2 * own + 4 * part
    pieces = [
        pl.BlockSpec((own, chunk), lambda i, place, at=hidden_at(0, half, 1): (0, at))
        for half in range(2)
    ]
    quarters = [
        pl.BlockSpec((part, 2 * chunk), lambda i, place, at=4 + half: (place[0], at))
        for half in range(2)
    ]
    return pl.pallas_call(
        join_kernel,
        out_shape=jax.ShapeDtypeStruct((rows, 2 * chunk), BF),
        grid_spec=pltpu.PrefetchScalarGridSpec(
            num_scalar_prefetch=1,
            grid=(1,),
            in_specs=pieces * 2
            + [pl.BlockSpec((part, w_out.shape[1]), lambda i, place: (place[0], 0))]
            + quarters,
            out_specs=pl.BlockSpec((rows, 2 * chunk), lambda i, place: (0, 0)),
        ),
        cost_estimate=cost(2),
        name="join_rows",
    )(place, mine, mine, other, other, w_out, other, other)


def joined_kernel(*refs):
    at = 0
    for ref in refs[:-1]:
        refs[-1][at : at + ref.shape[0], :] = ref[...]
        at += ref.shape[0]


def joined(parts):
    rows = sum(part.shape[0] for part in parts)
    return pl.pallas_call(
        joined_kernel,
        out_shape=jax.ShapeDtypeStruct((rows, parts[0].shape[1]), parts[0].dtype),
        cost_estimate=cost(1),
        name="joined",
    )(*parts)


def project_kernel(
    place, own_ref, one_ref, two_ref, up_ref, low_ref, kept_ref, moved_ref, gain_ref, shift_ref,
    bias_ref, first_ref, unit_ref, qkv_ref, turned_ref, toks, mat, sems,
):
    step = pl.program_id(0)
    floor, core = place[1], place[2]
    block = own_ref.shape[0]
    half = block // 2
    own = mat.shape[0] // 8

    def copies():
        made = [
            (own_ref, toks.at[pl.ds(0, block), :]),
            (one_ref, toks.at[pl.ds(block, block), :]),
            (two_ref, toks.at[pl.ds(2 * block, block), :]),
            (up_ref, toks.at[pl.ds(3 * block, half), :]),
            (low_ref, toks.at[pl.ds(3 * block + half, half), :]),
        ]
        for k in range(4):
            for ref, which in ((kept_ref, core), (moved_ref, 1 - core)):
                row = aligned((floor ^ k) * 2 * own + which * own, own)
                made.append((ref.at[k, pl.ds(0, own), :], mat.at[pl.ds(row, own), :]))
        return made

    @pl.when(step == 0)
    def _():
        for copy in start_all(copies(), sems):
            copy.wait()

    rows = first_ref.shape[0]
    values = toks[pl.ds(aligned(step * rows, rows), rows), :].astype(F32)
    unit, _ = norm_stats(values)
    first = (unit * gain_ref[...] + shift_ref[...]).astype(BF)
    first_ref[...] = first
    unit_ref[...] = unit.astype(BF)
    qkv_ref[...] = (nn(first, mat[...]) + bias_ref[...]).astype(BF)

    @pl.when(step == pl.num_programs(0) - 1)
    def _():
        turned_ref[...] = mat[...].T


def project(place, blocks, kept, moved, gain, shift, bias):
    block, width = blocks[0].shape
    outs = kept.shape[2]
    total = 4 * block
    rows = 256
    raw = pl.BlockSpec(memory_space=pl.ANY)

    def line(size):
        return pl.BlockSpec((1, size), lambda i, place: (0, 0))

    def tile(size):
        return pl.BlockSpec((rows, size), lambda i, place: (i, 0))

    return pl.pallas_call(
        project_kernel,
        out_shape=(
            jax.ShapeDtypeStruct((total, width), BF),
            jax.ShapeDtypeStruct((total, width), BF),
            jax.ShapeDtypeStruct((total, outs), BF),
            jax.ShapeDtypeStruct((outs, width), BF),
        ),
        grid_spec=pltpu.PrefetchScalarGridSpec(
            num_scalar_prefetch=1,
            grid=(total // rows,),
            in_specs=[raw] * 7 + [line(width), line(width), line(outs)],
            out_specs=(
                tile(width),
                tile(width),
                tile(outs),
                pl.BlockSpec((outs, width), lambda i, place: (0, 0)),
            ),
            scratch_shapes=[
                pltpu.VMEM((total, width), BF),
                pltpu.VMEM((width, outs), BF),
                pltpu.SemaphoreType.DMA((13,)),
            ],
        ),
        cost_estimate=cost(12),
        name="project",
    )(place, *blocks, kept, moved, gain, shift, bias)


def out_mat_kernel(part, place, *refs):
    (mine_ref, other_ref), shares, (mat_ref, sems) = refs[:2], refs[2:6], refs[6:]
    me, floor, core = place[0], place[1], place[2]
    own, width = mine_ref.shape
    wide = width // 2
    rows_each = 2 * own + 4 * part
    made = []
    for source, which in (
        (mine_ref, core),
        (other_ref.at[:, pl.ds(other_ref.shape[1] - width, width)], 1 - core),
    ):
        row = aligned(floor * 2 * own + which * own, own)
        made.append((source, mat_ref.at[pl.ds(row, own), :]))
    for q in range(4):
        for k in range(1, 4):
            for which in range(2):
                row = aligned((floor ^ k) * 2 * own + which * own + (me ^ q) * part, part)
                for half in range(2):
                    at = (k - 1) * rows_each + 2 * own + which * 2 * part + half * part
                    made.append(
                        (
                            shares[q].at[pl.ds(at, part), :],
                            mat_ref.at[pl.ds(row, part), pl.ds(half * wide, wide)],
                        )
                    )
    for copy in start_all(made, sems):
        copy.wait()


def out_matrix(place, mine, other, shares):
    width = mine.shape[1]
    return pl.pallas_call(
        functools.partial(out_mat_kernel, mine.shape[0] // 4),
        out_shape=jax.ShapeDtypeStruct((width, width), BF),
        grid_spec=pltpu.PrefetchScalarGridSpec(
            num_scalar_prefetch=1,
            grid=(1,),
            in_specs=[pl.BlockSpec(memory_space=pl.ANY)] * 6,
            out_specs=pl.BlockSpec((width, width), lambda i, place: (0, 0)),
            scratch_shapes=[pltpu.SemaphoreType.DMA((50,))],
        ),
        cost_estimate=cost(3),
        name="out_matrix",
    )(place, mine, other, *shares)


def attn_out_kernel(place, *refs):
    mixed_refs, (mat_ref, token_ref, bias_ref, gain_ref, shift_ref) = refs[:4], refs[4:9]
    hidden_ref, second_ref, mixed_ref, mixed, sems = refs[9:]
    step = pl.program_id(0)
    me = place[0]
    local = mixed_refs[0].shape[1]
    block = mixed.shape[0]

    @pl.when(step == 0)
    def _():
        made = []
        for k, ref in enumerate(mixed_refs):
            lanes = pl.ds(aligned((me ^ k) * local, local), local)
            made.append((ref.at[pl.ds(0, block), :], mixed.at[:, lanes]))
        for copy in start_all(made, sems):
            copy.wait()

    rows = hidden_ref.shape[0]
    here = mixed[pl.ds(aligned(step * rows, rows), rows), :]
    mixed_ref[...] = here
    hidden = token_ref[...].astype(F32) + nn(here, mat_ref[...]) + bias_ref[...]
    hidden_ref[...] = hidden
    unit, _ = norm_stats(hidden)
    second_ref[...] = (unit * gain_ref[...] + shift_ref[...]).astype(BF)


def attn_out(place, mixed, mat, tokens, bias, gain, shift):
    block, width = tokens.shape
    rows = 256
    raw = pl.BlockSpec(memory_space=pl.ANY)
    line = pl.BlockSpec((1, width), lambda i, place: (0, 0))
    tile = pl.BlockSpec((rows, width), lambda i, place: (i, 0))
    return pl.pallas_call(
        attn_out_kernel,
        out_shape=(
            jax.ShapeDtypeStruct((block, width), F32),
            jax.ShapeDtypeStruct((block, width), BF),
            jax.ShapeDtypeStruct((block, width), BF),
        ),
        grid_spec=pltpu.PrefetchScalarGridSpec(
            num_scalar_prefetch=1,
            grid=(block // rows,),
            in_specs=[raw] * 4
            + [pl.BlockSpec((width, width), lambda i, place: (0, 0)), tile, line, line, line],
            out_specs=(tile, tile, tile),
            scratch_shapes=[pltpu.VMEM((block, width), BF), pltpu.SemaphoreType.DMA((4,))],
        ),
        cost_estimate=cost(5),
        name="attn_out",
    )(place, *mixed, mat, tokens, bias, gain, shift)


def feed_kernel(
    hw, place, second_oth, second_own, branch_oth, branch_own, bias_a, bias_b, mine_ref, other_ref,
    a0, a1, a2, a3, proj_ref, b0, b1, b2, b_up, b_low, act_a, act_b, slope_a, slope_b, out_own, out_oth, back_own, back_oth, sum_a, sum_b,
    fc, proj, fc_turned, proj_turned, total, back, sems,
):
    step = pl.program_id(0)
    me, floor, core = place[0], place[1], place[2]
    own = mine_ref.shape[0]
    chunk = 2 * hw
    rows_each = a0.shape[0] // 3

    def copies(q):
        made = []
        for ref, which in ((mine_ref, core), (other_ref, 1 - core)):
            row = aligned(floor * 2 * own + which * own, own)
            for half in range(2):
                made.append(
                    (
                        ref.at[:, pl.ds(hidden_at(q, half, chunk), chunk)],
                        fc.at[q, pl.ds(row, own), pl.ds(half * chunk, chunk)],
                    )
                )
        for k in range(1, 4):
            row = aligned((floor ^ k) * 2 * own, 2 * own)
            source = (a0, a1, a2, a3)[q].at[pl.ds((k - 1) * rows_each, 2 * own), :]
            made.append((source, fc.at[q, pl.ds(row, 2 * own), :]))
        cut = hw // 2
        for k in range(4):
            row = aligned((floor ^ k) * hw, hw)
            if k == 0:
                made.append((proj_ref.at[pl.ds(aligned((me ^ q) * hw, hw), hw), :], proj.at[q, pl.ds(row, hw), :]))
            elif q < 3:
                source = (b0, b1, b2)[q].at[pl.ds((k - 1) * hw, hw), :]
                made.append((source, proj.at[q, pl.ds(row, hw), :]))
            else:
                for i in range(2):
                    at = (k - 1) * hw + i * cut
                    source = (b_up if at < 3 * cut else b_low).at[pl.ds(at % (3 * cut), cut), :]
                    made.append((source, proj.at[q, pl.ds(aligned(row + i * cut, cut), cut), :]))
        return [
            pltpu.make_async_copy(source, target, sems.at[q, i])
            for i, (source, target) in enumerate(made)
        ]

    @pl.when(step == 0)
    def _():
        for q in range(4):
            for copy in copies(q):
                copy.start()

    for q in range(4):

        @pl.when(step == q)
        def _():
            for copy in copies(q):
                copy.wait()

    fc_turned[...] = fc[step].T
    proj_turned[...] = proj[step].T
    bias = jnp.concatenate([bias_a[...], bias_b[...]], axis=1)
    rows = second_own.shape[0]
    both = 2 * rows
    partial = None
    for start, second_ref, branch_ref in ((0, second_oth, branch_oth), (rows, second_own, branch_own)):
        here = slice(start, start + rows)
        pre = nn(second_ref[...], fc[step]) + bias
        value, bend = gelu_both(pre)
        act = value.astype(BF)
        act_a[here, :] = act[:, :chunk]
        act_b[here, :] = act[:, chunk:]
        slope_full = nn(branch_ref[...], proj_turned[...]) * bend
        slope = slope_full.astype(BF)
        slope_a[here, :] = slope[:, :chunk]
        slope_b[here, :] = slope[:, chunk:]
        more = jnp.sum(slope_full, axis=0, keepdims=True)
        partial = more if partial is None else partial + more
        out_part = nn(act, proj[step])
        back_part = nn(slope, fc_turned[...])

        @pl.when(step == 0)
        def _():
            total[here, :] = out_part
            back[here, :] = back_part

        @pl.when(step > 0)
        def _():
            total[here, :] += out_part
            back[here, :] += back_part

    sum_a[...] = partial[:, :chunk]
    sum_b[...] = partial[:, chunk:]

    @pl.when(step == 3)
    def _():
        half = both // 2
        out_oth[...] = total[:half].astype(BF)
        back_oth[...] = back[:half].astype(BF)
        out_own[...] = total[half:]
        back_own[...] = back[half:]


def feed(place, second, branch, bias, mine, other, shares, w_proj, proj_shares):
    both, width = 2 * second[0].shape[0], second[0].shape[1]
    hidden = mine.shape[1]
    hw = hidden // 16
    chunk = 2 * hw
    raw = pl.BlockSpec(memory_space=pl.ANY)

    def whole(height):
        return pl.BlockSpec((height, width), lambda i, place: (0, 0))

    def upper(height):
        return pl.BlockSpec((height, chunk), lambda i, place: (0, (i % 2) * 2 + i // 2))

    def lower(height, first=0):
        return pl.BlockSpec((height, chunk), lambda i, place: (0, first + i))

    half = jax.ShapeDtypeStruct((both, hidden // 2), BF)
    line = jax.ShapeDtypeStruct((1, hidden // 2), F32)
    return pl.pallas_call(
        functools.partial(feed_kernel, hw),
        out_shape=(
            half,
            half,
            half,
            half,
            jax.ShapeDtypeStruct((both // 2, width), F32),
            jax.ShapeDtypeStruct((both // 2, width), BF),
            jax.ShapeDtypeStruct((both // 2, width), F32),
            jax.ShapeDtypeStruct((both // 2, width), BF),
            line,
            line,
        ),
        grid_spec=pltpu.PrefetchScalarGridSpec(
            num_scalar_prefetch=1,
            grid=(4,),
            in_specs=[whole(both // 2)] * 4 + [upper(1), lower(1, 4)] + [raw] * 12,
            out_specs=(upper(both), lower(both), upper(both), lower(both))
            + (whole(both // 2),) * 4
            + (upper(1), lower(1)),
            scratch_shapes=[
                pltpu.VMEM((4, width, 2 * chunk), BF),
                pltpu.VMEM((4, 2 * chunk, width), BF),
                pltpu.VMEM((2 * chunk, width), BF),
                pltpu.VMEM((width, 2 * chunk), BF),
                pltpu.VMEM((both, width), F32),
                pltpu.VMEM((both, width), F32),
                pltpu.SemaphoreType.DMA((4, 14)),
            ],
        ),
        cost_estimate=cost(35),
        name="feed",
    )(place, *second, *branch, bias, bias, mine, other, *shares, w_proj, *proj_shares)


def mixed_back_kernel(
    place, own_ref, oth_ref, hidden_ref, branch_ref, gain_ref, mat_ref,
    full_ref, low_ref, g0, g1, g2, g3, sums_ref,
):
    step = pl.program_id(0)
    me = place[0]
    local = g0.shape[1]
    slope = own_ref[...] + oth_ref[...].astype(F32)
    unit, scale = norm_stats(hidden_ref[...])
    full = branch_ref[...].astype(F32) + norm_pull(unit, scale, slope * gain_ref[...])
    low = full.astype(BF)
    full_ref[...] = full
    low_ref[...] = low
    for k, ref in enumerate((g0, g1, g2, g3)):
        rows = pl.ds(aligned((me ^ k) * local, local), local)
        ref[...] = nt(low, mat_ref[rows, :]).astype(BF)
    sums = jnp.concatenate(
        [
            jnp.sum(low.astype(F32), axis=0, keepdims=True),
            jnp.sum(slope * unit, axis=0, keepdims=True),
            jnp.sum(slope, axis=0, keepdims=True),
            jnp.sum(branch_ref[...].astype(F32), axis=0, keepdims=True),
        ],
        axis=0,
    )

    @pl.when(step == 0)
    def _():
        sums_ref[...] = sums

    @pl.when(step > 0)
    def _():
        sums_ref[...] += sums


def mixed_back(place, own, oth, hidden, branch, gain, mat):
    block, width = own.shape
    local = width // 4
    rows = block

    def tile(size):
        return pl.BlockSpec((rows, size), lambda i, place: (i, 0))

    def whole(height):
        return pl.BlockSpec((height, width), lambda i, place: (0, 0))

    return pl.pallas_call(
        mixed_back_kernel,
        out_shape=(
            jax.ShapeDtypeStruct((block, width), F32),
            jax.ShapeDtypeStruct((block, width), BF),
        )
        + (jax.ShapeDtypeStruct((block, local), BF),) * 4
        + (jax.ShapeDtypeStruct((4, width), F32),),
        grid_spec=pltpu.PrefetchScalarGridSpec(
            num_scalar_prefetch=1,
            grid=(block // rows,),
            in_specs=[tile(width)] * 4 + [whole(1), whole(width)],
            out_specs=(tile(width), tile(width)) + (tile(local),) * 4 + (whole(4),),
        ),
        cost_estimate=cost(7),
        name="mixed_back",
    )(place, own, oth, hidden, branch, gain, mat)


def first_back_kernel(tiles, parts, place, *refs):
    step = pl.program_id(0)
    count = len(tiles) // 2
    grad_refs, (unit_ref, mat_ref), refs = refs[:parts], refs[parts : parts + 2], refs[parts + 2 :]
    out_refs, sums_ref = refs[:count], refs[count]
    part = nn(jnp.concatenate([ref[...] for ref in grad_refs], axis=1), mat_ref[...])
    low = part.astype(BF)
    for i in range(count):

        @pl.when(step // 2 == i)
        def _():
            out_refs[i][...] = low

    sums = jnp.concatenate(
        [
            jnp.sum(part * unit_ref[...].astype(F32), axis=0, keepdims=True),
            jnp.sum(part, axis=0, keepdims=True),
        ],
        axis=0,
    )

    @pl.when(step == 0)
    def _():
        sums_ref[...] = sums

    @pl.when(step > 0)
    def _():
        sums_ref[...] += sums


def first_back(tiles, grads, unit, mat):
    outs, width = mat.shape
    rows = 256
    table = jnp.asarray(tiles, jnp.int32)

    def at(i, place):
        return (place[i], 0)

    return pl.pallas_call(
        functools.partial(first_back_kernel, tiles, len(grads)),
        out_shape=tuple(jax.ShapeDtypeStruct((2 * rows, width), BF) for _ in tiles[::2])
        + (jax.ShapeDtypeStruct((2, width), F32),),
        grid_spec=pltpu.PrefetchScalarGridSpec(
            num_scalar_prefetch=1,
            grid=(len(tiles),),
            in_specs=[pl.BlockSpec((rows, grad.shape[1]), at) for grad in grads]
            + [
                pl.BlockSpec((rows, width), at),
                pl.BlockSpec((outs, width), lambda i, place: (0, 0)),
            ],
            out_specs=tuple(
                pl.BlockSpec((rows, width), lambda i, place, g=g: (jnp.clip(i - 2 * g, 0, 1), 0))
                for g in range(len(tiles) // 2)
            )
            + (pl.BlockSpec((2, width), lambda i, place: (0, 0)),),
        ),
        cost_estimate=cost(5),
        name="first_back",
    )(table, *grads, unit, mat)


def gather_fc_kernel(place, fa, xa, la, fb, yb, lb, o0, o1, o2, o3, fc):
    floor = place[1]
    chunk = fc.shape[1] // 2
    fc[:, :chunk] = fa[...].astype(F32) + xa[...].astype(F32) + la[...].astype(F32)
    fc[:, chunk:] = fb[...].astype(F32) + yb[...].astype(F32) + lb[...].astype(F32)
    rows = fc.shape[0] // 4
    for k, out in enumerate((o0, o1, o2, o3)):
        out[...] = fc[pl.ds(aligned((floor ^ k) * rows, rows), rows), :].astype(BF)


def gather_proj_kernel(place, pa, xp, lpa, pb, yp, lpb, o0, o1, o2, o3, proj):
    floor = place[1]
    chunk = proj.shape[0] // 2
    proj[:chunk, :] = pa[...].astype(F32) + xp[...].astype(F32) + lpa[...].astype(F32)
    proj[chunk:, :] = pb[...].astype(F32) + yp[...].astype(F32) + lpb[...].astype(F32)
    rows = proj.shape[0] // 4
    for k, out in enumerate((o0, o1, o2, o3)):
        out[...] = proj[pl.ds(aligned((floor ^ k) * rows, rows), rows), :].astype(BF)


def gather_sum(place, kernel, parts, shape, block):
    out = jax.ShapeDtypeStruct((shape[0] // 4, shape[1]), BF)
    return pl.pallas_call(
        kernel,
        out_shape=(out,) * 4,
        grid_spec=pltpu.PrefetchScalarGridSpec(
            num_scalar_prefetch=1,
            grid=(1,),
            in_specs=[pl.BlockSpec(block, lambda i, place: (0, 0))] * 6,
            out_specs=(pl.BlockSpec(out.shape, lambda i, place: (0, 0)),) * 4,
            scratch_shapes=[pltpu.VMEM(shape, F32)],
        ),
        cost_estimate=cost(3),
        name="gather_sum",
    )(place, *parts)


def spread_fc_kernel(place, *refs):
    me, core = place[0], place[2]
    finals, fc_ref = refs[:4], refs[4]
    own = fc_ref.shape[0]
    hw = finals[0].shape[1] // 4
    for q in range(4):
        for part, which in ((0, core), (1, 1 - core)):
            for z in range(4):
                lanes = pl.ds(aligned(z * 8 * hw + which * 4 * hw + (me ^ q) * hw, hw), hw)
                block = finals[q][part * own : (part + 1) * own, z * hw : (z + 1) * hw]
                fc_ref[:, lanes] = block.astype(F32)


def spread_proj_kernel(place, *refs):
    me = place[0]
    finals, proj_ref = refs[:4], refs[4]
    hw = finals[0].shape[0]
    for q in range(4):
        proj_ref[pl.ds(aligned((me ^ q) * hw, hw), hw), :] = finals[q][...].astype(F32)


def spread(place, kernel, finals, shape):
    def whole(shape):
        return pl.BlockSpec(shape, lambda i, place: (0, 0))

    return pl.pallas_call(
        kernel,
        out_shape=jax.ShapeDtypeStruct(shape, F32),
        grid_spec=pltpu.PrefetchScalarGridSpec(
            num_scalar_prefetch=1,
            grid=(1,),
            in_specs=[whole(finals[0].shape)] * 4,
            out_specs=whole(shape),
        ),
        cost_estimate=cost(2),
        name="spread",
    )(place, *finals)


def last_kernel(
    keep_ref, got_x, got_y, last_y, last_x, token_ref, hidden_ref, gain_ref, out_ref
):
    def finish(got, last):
        slope = keep_ref[...].astype(F32) + got[...].astype(F32) + last[...].astype(F32)
        unit, scale = norm_stats(token_ref[...].astype(F32))
        out_ref[...] = hidden_ref[...] + norm_pull(unit, scale, slope * gain_ref[...])

    @pl.when(pl.program_id(0) == 0)
    def _():
        finish(got_x, last_y)

    @pl.when(pl.program_id(0) == 1)
    def _():
        finish(got_y, last_x)


def body_aligned(
    tokens,
    prompt_lens,
    cont_lens,
    gain_one,
    shift_one,
    w_qkv,
    bias_qv,
    w_out,
    bias_out,
    gain_two,
    shift_two,
    w_fc,
    bias_fc,
    w_proj,
    bias_proj,
    cotangent,
):
    ns = nz = 4
    nf = 8
    me = lax.axis_index("seq")
    owner = lax.axis_index("fsdp")
    floor = owner // 2
    core = owner % 2
    place = jnp.stack([me, floor, core]).astype(jnp.int32)
    toks, width = tokens.shape[1:]
    own = width // nf
    heads = H // ns
    local = width // ns
    hw = w_fc.shape[1] // (nf * ns)
    token_block = tokens[0]
    branch = cotangent[0]

    half = toks // 2
    vectors = [gain_one, shift_one, bias_qv, bias_out, gain_two, shift_two, bias_fc, bias_proj]
    packed = jnp.concatenate([v.reshape(-1, own) for v in vectors], axis=0)
    lines = packed.shape[0]
    packed = jnp.pad(packed.reshape(-1), (0, 16 * 3 * local - packed.size)).reshape(16, 3 * local)
    mine_qkv = pick(w_qkv.reshape(own, 3, ns, local), me, 2).reshape(own, 3 * local)
    sent_qkv = jnp.concatenate([mine_qkv, packed], axis=0)
    tok_one = swap(token_block, "seq", 1)
    tok_two = swap(token_block, "seq", 2)
    got_qkv = [swap(sent_qkv, "fsdp", 2 * k) for k in range(1, nz)]
    fc_mine, fc_sent, proj_share = pack(place, after(w_fc, sent_qkv), w_proj, w_out)
    fc_other = swap(fc_sent, "fsdp", 1)
    fc_share = join(place, fc_mine, fc_other, w_out)

    tok_one, tok_two, got_qkv, fc_share, proj_share = lax.optimization_barrier(
        (tok_one, tok_two, got_qkv, fc_share, proj_share)
    )
    tok_up = swap(tok_two[:half], "seq", 1)
    tok_low = swap(tok_one[half:], "seq", 2)
    kept_qkv = jnp.stack([sent_qkv, *got_qkv])
    moved_qkv = swap(kept_qkv, "fsdp", 1)
    moved_qkv, fc_share = lax.optimization_barrier((moved_qkv, fc_share))
    fc_got = [swap(fc_share, "fsdp", 2 * k) for k in range(1, nz)]

    small = by_core(core, kept_qkv[:, own : own + 2], moved_qkv[:, own : own + 2], 1)
    small = xor_take(small, floor, 0).reshape(nf, -1).reshape(nf, lines, own)
    at = 0
    full = []
    for v in vectors:
        count = v.shape[0] // own
        full.append(small[:, at : at + count].reshape(1, -1).astype(F32))
        at += count
    gain_a, shift_a, qv_vec, out_vec, gain_b, shift_b, fc_vec, proj_vec = full
    qv_mine = pick(qv_vec.reshape(2, ns, local), me, 1)
    bias_all = jnp.concatenate([qv_mine[0], jnp.zeros((local,), F32), qv_mine[1]]).reshape(1, -1)
    fc_bias = xor_take(pick(fc_vec.reshape(nz, 2, ns, hw), core, 1), me, 1)
    order = [(q, 0) for q in (0, 2, 1, 3)] + [(q, 1) for q in range(4)]
    fc_bias = jnp.concatenate(
        [fc_bias[2 * part : 2 * part + 2, q].reshape(1, -1) for q, part in order], axis=1
    )

    first, unit_all, qkv, qkv_turned = project(
        place, (token_block, tok_one, tok_two, tok_up, tok_low), kept_qkv, moved_qkv, gain_a, shift_a,
        bias_all,
    )
    lens = jnp.concatenate([prompt_lens, cont_lens[0], me.reshape(1)]).astype(jnp.int32)

    qkv, fc_got, proj_share = lax.optimization_barrier((qkv, fc_got, proj_share))
    fc_zero = joined(fc_got)
    fc_one = swap(fc_zero, "seq", 1)
    fc_two = swap(fc_zero, "seq", 2)
    proj_got = [swap(proj_share, "fsdp", 2 * k) for k in range(1, nz)]
    ends = {}

    def between(lens, mixed, arrays):
        (mixed, arrays, one, two, got, ends["branch"]) = lax.optimization_barrier(
            (mixed, arrays, fc_one, fc_two, proj_got, branch)
        )
        ends["branch_got"] = swap(ends["branch"], "fsdp", 1)
        cut = one.shape[0] // 2
        ends["fc"] = (one, two, swap(two[:cut], "seq", 1), swap(one[cut:], "seq", 2))
        ends["proj"] = joined(got)
        return lens, mixed, arrays

    mixed_heads, norms = attend_forward(lens, qkv, heads, between)
    fc_one, fc_two, fc_up, fc_low = ends["fc"]
    proj_zero = ends["proj"]

    mixed_heads, fc_up, fc_low, proj_zero, branch_got = lax.optimization_barrier(
        (mixed_heads, fc_up, fc_low, proj_zero, ends["branch_got"])
    )
    branch_both = jnp.concatenate([branch_got, branch], axis=0)
    mixed_blocks = [mixed_heads] + [
        swap(mixed_heads[k * toks : (k + 1) * toks], "seq", k) for k in range(1, ns)
    ]
    fc_three = joined([fc_up, fc_low])
    shares = (fc_zero, fc_one, fc_two, fc_three)
    proj_one = swap(proj_zero, "seq", 1)
    proj_two = swap(proj_zero, "seq", 2)
    cut = proj_one.shape[0] // 2
    proj_three = swap(proj_two[:cut], "seq", 1), swap(proj_one[cut:], "seq", 2)
    out_mat = out_matrix(place, w_out, fc_other, shares)
    mixed_blocks, branch_both, out_mat = lax.optimization_barrier((mixed_blocks, branch_both, out_mat))
    hidden, second, mixed = attn_out(
        place, mixed_blocks, out_mat, token_block, out_vec, gain_b, shift_b
    )

    second_got = swap(second, "fsdp", 1)
    *hiddens, out_own, out_oth, back_own, back_oth, sum_upper, sum_lower = feed(
        place, (second_got, second), (branch_got, branch), fc_bias, fc_mine, fc_other,
        shares, w_proj, (proj_zero, proj_one, proj_two, *proj_three),
    )
    back_got = swap(back_oth, "fsdp", 1)
    out_got = swap(out_oth, "fsdp", 1)
    grad_hidden, grad_attn, *grad_blocks, sums_two = mixed_back(
        place, back_own, back_got, hidden, branch, gain_b, out_mat
    )

    def added(left, right):
        return (left.astype(F32) + right.astype(F32)).astype(BF)

    def halves(values, index):
        pair = values.reshape(2, values.shape[0] // 2, values.shape[1])
        return pick(pair, index, 0).astype(F32), pick(pair, 1 - index, 0).astype(BF)

    def core_halves(grad):
        cut = grad.reshape(nz, 2, own, -1)
        mine, sent = pick(cut, core, 1), pick(cut, 1 - core, 1)
        return mine.reshape(nz * own, -1), sent.reshape(nz * own, -1)

    edge = 4 * hw
    chunk = 2 * hw
    head_got = [swap(grad_blocks[k], "seq", k) for k in range(1, ns)]
    hiddens, branch_late, second_late, second_got, mixed_late, attn_late = after(
        (hiddens, branch_both, second, second_got, mixed, grad_attn), grad_blocks
    )
    acts, slopes = (
        [v[:, i * edge : (i + 1) * edge] for v in pair for i in range(2)]
        for pair in (hiddens[:2], hiddens[2:])
    )
    wo_mine, wo_sent = core_halves(tn(mixed_late, attn_late).astype(BF))
    second_both = jnp.concatenate([second_got, second_late], axis=0)

    head_x = head_got[0]
    acts, slopes, second_both, branch_late, wo_sent, head_x, out_got = after(
        (acts, slopes, second_both, branch_late, wo_sent, head_x, out_got)
    )
    proj_grads = [tn(v, branch_late).astype(BF) if i % 2 else None for i, v in enumerate(acts)]
    proj_x = swap(proj_grads[1], "seq", 1)
    proj_y = swap(proj_grads[3], "seq", 2)
    wo_got = swap(wo_sent, "fsdp", 1)
    fc_grads = [None] * 4
    for i in (1, 3, 0, 2):
        fc_grads[i] = tn(second_both, slopes[i]).astype(BF)
    for i in (0, 2):
        proj_grads[i] = tn(acts[i], branch_late).astype(BF)
    output = (hidden + out_own + proj_vec + out_got.astype(F32)).astype(BF)

    grad_heads = jnp.concatenate([grad_blocks[0], head_x, *head_got[1:]], axis=0)
    grad_heads, fc_grads, proj_keep, wo_got, output = after(
        (grad_heads, fc_grads, proj_grads[::2], wo_got, output)
    )
    fc_x = swap(fc_grads[1], "seq", 1)
    fc_y = swap(fc_grads[3], "seq", 2)
    wo_keep, wo_sent = halves(wo_mine.astype(F32) + wo_got.astype(F32), floor // 2)
    wo_far = swap(wo_sent, "fsdp", 4)
    back = {}

    def between_back(lens, parts, grad):
        parts, grad, x, y, far = after((parts, grad, proj_x, proj_y, wo_far))
        back["proj"] = (
            x,
            y,
            swap(added(proj_keep[1][chunk:], y[chunk:]), "seq", 1),
            swap(added(proj_keep[0][chunk:], x[chunk:]), "seq", 2),
        )
        keep, sent = halves(wo_keep + far.astype(F32), floor % 2)
        back["out"] = keep, swap(sent, "fsdp", 2)
        return lens, parts, grad

    backward = attend_backward(lens, qkv, mixed_heads, norms, grad_heads, heads, between_back)
    proj_x, proj_y, proj_last_x, proj_last_y = back["proj"]
    wo_keep, wo_near = back["out"]

    backward, fc_x, fc_y, proj_x, proj_y, proj_last_x, proj_last_y, wo_near = after(
        (backward, fc_x, fc_y, proj_x, proj_y, proj_last_x, proj_last_y, wo_near)
    )
    fc_far = [added(fc_grads[0][:, chunk:], fc_x[:, chunk:]), added(fc_grads[2][:, chunk:], fc_y[:, chunk:])]
    fc_last_y = swap(fc_far[0], "seq", 2)
    fc_last_x = swap(fc_far[1], "seq", 1)
    wo_sum = wo_keep + wo_near.astype(F32)
    wo_got = swap(wo_sum.astype(BF), "seq", 1)
    backward = after(backward, fc_far)
    parts = [part[i] for i in range(3) for part in backward]
    sent_x, sent_y, sums_early = first_back((2, 6, 5, 7), parts, unit_all, qkv_turned)

    sent_x, sent_y, parts, fc_last_x, fc_last_y, proj_x, proj_y = after(
        (sent_x, sent_y, parts, fc_last_x, fc_last_y, proj_x, proj_y)
    )
    got_x = swap(sent_x, "seq", 1)
    got_y = swap(sent_y, "seq", 2)
    cuts = gather_sum(
        place, gather_proj_kernel,
        (proj_keep[0], proj_x, proj_last_y, proj_keep[1], proj_y, proj_last_x),
        (4 * hw, width), (chunk, width),
    )
    cuts, wo_got = after((cuts, wo_got))
    cuts_proj = [swap(cuts[k], "fsdp", 2 * k) for k in range(1, nz)]
    grad_proj_kept = cuts[0]
    fc_grads = after(fc_grads, cuts)
    cuts = gather_sum(
        place, gather_fc_kernel,
        (fc_grads[0], fc_x, fc_last_y, fc_grads[2], fc_y, fc_last_x),
        (width, 4 * hw), (width, chunk),
    )

    parts = after(parts, cuts)
    far_late, kept_late, sums_late = first_back((4, 3, 0, 1), parts, unit_all, qkv_turned)
    cuts_proj, cuts, far_late = after((cuts_proj, cuts, far_late))
    cuts_fc = [swap(cuts[k], "fsdp", 2 * k) for k in range(1, nz)]
    fc_kept = cuts[0]

    got_x, got_y, far_late, parts = after((got_x, got_y, far_late, parts))
    far_y = added(far_late[:half], got_x[half:])
    far_x = added(far_late[half:], got_y[half:])
    last_y = swap(far_y, "seq", 2)
    last_x = swap(far_x, "seq", 1)
    parts, first_late, cuts_proj = after((parts, first, cuts_proj), far_x, far_y)
    grad_qkv = jnp.concatenate(parts, axis=1)
    wi_grad = tn(first_late, grad_qkv).astype(BF)
    proj_owned = grad_proj_kept.astype(F32)
    for part in cuts_proj:
        proj_owned = proj_owned + part.astype(F32)
    proj_owned = proj_owned.astype(BF)

    def placed(values):
        slots = jnp.arange(ns)[:, None] == me
        return jnp.where(slots, values[None, :], 0.0).reshape(-1)

    spots = {}
    for i, (q, part) in enumerate(order):
        here = (sum_upper, sum_lower)[part][0, (i % 4) * chunk : (i % 4 + 1) * chunk]
        spots[q, part] = here.reshape(2, hw)
    fc_bias_grad = jnp.stack(
        [jnp.concatenate([spots[q, 0], spots[q, 1]], axis=0) for q in range(ns)], axis=1
    )
    fc_bias_grad = xor_take(fc_bias_grad, me, 1)
    fc_bias_grad = jnp.where(
        (jnp.arange(2) == core)[None, :, None, None], fc_bias_grad[:, None], 0.0
    ).reshape(-1)
    sums_one = sums_early + sums_late
    qkv_sum = jnp.sum(grad_qkv.astype(F32), axis=0)
    vector_grads = [
        sums_one[0],
        sums_one[1],
        jnp.concatenate([placed(qkv_sum[:local]), placed(qkv_sum[2 * local :])]),
        sums_two[0],
        sums_two[1],
        sums_two[2],
        fc_bias_grad,
        sums_two[3],
    ]
    by_owner = jnp.concatenate([v.reshape(nf, -1) for v in vector_grads], axis=1)
    by_owner = by_owner.reshape(nz, 2, -1, 3 * local)
    lines = by_owner.shape[2]
    tall = own + 16
    by_owner = jnp.pad(by_owner, ((0, 0), (0, 0), (0, 16 - lines), (0, 0)))
    wi_cut = jnp.concatenate([wi_grad.reshape(nz, 2, own, 3 * local), by_owner.astype(BF)], axis=2)
    wi_mine = pick(wi_cut, core, 1).reshape(nz * tall, 3 * local)
    wi_sent = pick(wi_cut, 1 - core, 1).reshape(nz * tall, 3 * local)
    last_x, last_y, cuts_fc, wi_sent, proj_owned, wo_sum, wo_got = after(
        (last_x, last_y, cuts_fc, wi_sent, proj_owned, wo_sum, wo_got)
    )
    wi_got = swap(wi_sent, "fsdp", 1)
    fc_owned = fc_kept.astype(F32)
    for part in cuts_fc:
        fc_owned = fc_owned + part.astype(F32)
    fc_mine, fc_sent = halves(fc_owned, core)
    fc_got = swap(fc_sent, "fsdp", 1)
    wo_sum = wo_sum + wo_got.astype(F32)

    wi_got, fc_got = after((wi_got, fc_got))
    wi_keep, wi_sent = halves(wi_mine.astype(F32) + wi_got.astype(F32), floor // 2)
    wi_far = swap(wi_sent, "fsdp", 4)
    fc_final = jnp.concatenate([fc_mine.astype(BF), fc_got], axis=0)
    fc_finals = [fc_final] + [swap(fc_final, "seq", k) for k in range(1, ns)]
    last_x, last_y, kept_late = after((last_x, last_y, kept_late), fc_final, wi_sent)
    ends_at = pl.BlockSpec((half, width), lambda i: (i, 0))
    one_end = pl.BlockSpec((half, width), lambda i: (0, 0))
    input_grad = pl.pallas_call(
        last_kernel,
        out_shape=jax.ShapeDtypeStruct((toks, width), F32),
        grid=(2,),
        in_specs=[ends_at] + [one_end] * 4 + [ends_at] * 2 + [pl.BlockSpec((1, width), lambda i: (0, 0))],
        out_specs=ends_at,
        cost_estimate=cost(5),
        name="last",
    )(kept_late, got_x, got_y, last_y, last_x, token_block, grad_hidden, gain_a)

    fc_finals, input_grad, wo_sum, proj_owned = after((fc_finals, input_grad, wo_sum, proj_owned))
    input_grad = input_grad[None]
    proj_finals = [proj_owned] + [swap(proj_owned, "seq", k) for k in range(1, ns)]
    wo_got = swap(wo_sum.astype(BF), "seq", 2)
    grad_w_fc = spread(place, spread_fc_kernel, fc_finals, (own, 32 * hw))

    wi_far, grad_w_fc = after((wi_far, grad_w_fc))
    wi_keep, wi_sent = halves(wi_keep + wi_far.astype(F32), floor % 2)
    wi_near = swap(wi_sent, "fsdp", 2)

    wi_near, proj_finals = after((wi_near, proj_finals))
    wi_owned = wi_keep + wi_near.astype(F32)
    wi_low = wi_owned.astype(BF)
    wi_finals = [wi_low] + [swap(wi_low, "seq", k) for k in range(1, ns)]
    grad_w_proj = spread(place, spread_proj_kernel, proj_finals, (4 * hw, width))
    wo_got, grad_w_proj = after((wo_got, grad_w_proj))
    grad_w_out = wo_sum + wo_got.astype(F32)
    wi_blocks = jnp.stack([v[:own].reshape(own, 3, local) for v in wi_finals], axis=2)
    grad_w_qkv = xor_take(wi_blocks, me, 2).reshape(own, 3 * width).astype(F32)
    output = output[None]
    vector_sum = wi_owned[own : own + lines]
    for v in wi_finals[1:]:
        vector_sum = vector_sum + v[own : own + lines].astype(F32)
    vector_sum = vector_sum.reshape(-1)
    outs = []
    at = 0
    for v in vectors:
        count = v.shape[0]
        outs.append(vector_sum[at : at + count])
        at += count
    (g_gain_one, g_shift_one, g_bias_qv, g_bias_out, g_gain_two, g_shift_two, g_bias_fc, g_bias_proj) = outs

    return (
        output,
        input_grad,
        g_gain_one,
        g_shift_one,
        grad_w_qkv,
        g_bias_qv,
        grad_w_out,
        g_bias_out,
        g_gain_two,
        g_shift_two,
        grad_w_fc,
        g_bias_fc,
        grad_w_proj,
        g_bias_proj,
    )


def body(*args):
    tokens, w_proj = args[0], args[13]
    fits = (
        lax.axis_size("seq") == 4
        and lax.axis_size("fsdp") == 8
        and tokens.shape[1:] == (512, 1024)
        and w_proj.shape == (512, 1024)
    )
    return body_aligned(*args) if fits else body_general(*args)


def solution(mesh):
    rows = P("fsdp", None)
    vec = P("fsdp")
    acts = P("fsdp", "seq", None)
    return jax.shard_map(
        body,
        mesh=mesh,
        in_specs=(
            acts, vec, rows, vec, vec, rows, vec, rows, vec, vec, vec, rows, vec, rows, vec, acts,
        ),
        out_specs=(
            acts, acts, vec, vec, rows, vec, rows, vec, vec, vec, rows, vec, rows, vec,
        ),
        check_vma=False,
    )
```

```python
import functools

import jax
import jax.numpy as jnp
from jax import lax
from jax.experimental import pallas as pl
from jax.experimental.pallas import tpu as pltpu
from jax.sharding import PartitionSpec as P

H = 16
HD = 64
PROMPT = 1024
CONTLEN = 512
CONTS = 2

EPS = 1e-05
GELU_C = 0.7978845608028654
GELU_A = 0.044715
NEG = -1e30
BF = jnp.bfloat16
F32 = jnp.float32


def swap(values, axis, bits):
    size = lax.axis_size(axis)
    return lax.ppermute(values, axis, [(i, i ^ bits) for i in range(size)])


def xor_take(values, index, axis):
    size = values.shape[axis]
    bit = 1
    while bit < size:
        parts = [lax.slice_in_dim(values, i, i + 1, axis=axis) for i in range(size)]
        flipped = jnp.concatenate([parts[i ^ bit] for i in range(size)], axis=axis)
        values = jnp.where((index & bit) != 0, flipped, values)
        bit *= 2
    return values


def xor_blocks(values, index, count, axis):
    width = values.shape[axis] // count
    return jnp.concatenate(
        [
            lax.dynamic_slice_in_dim(values, (i ^ index) * width, width, axis=axis)
            for i in range(count)
        ],
        axis=axis,
    )


def plane_gather(values):
    size = lax.axis_size("seq")
    if size != 4:
        return [values] + [swap(values, "seq", k) for k in range(1, size)]
    half = values.shape[0] // 2
    one = swap(values, "seq", 1)
    two = swap(values, "seq", 2)
    three = jnp.concatenate(
        [swap(two[:half], "seq", 1), swap(one[half:], "seq", 2)], axis=0
    )
    return [values, one, two, three]


def plane_scatter(blocks):
    size = lax.axis_size("seq")
    if size != 4:
        total = blocks[0].astype(F32)
        for k in range(1, size):
            total = total + swap(blocks[k].astype(BF), "seq", k).astype(F32)
        return total
    half = blocks[0].shape[0] // 2
    sent_x = jnp.concatenate([blocks[1][:half], blocks[3][:half]], axis=0).astype(BF)
    sent_y = jnp.concatenate([blocks[2][half:], blocks[3][half:]], axis=0).astype(BF)
    got_x = swap(sent_x, "seq", 1).astype(F32)
    got_y = swap(sent_y, "seq", 2).astype(F32)
    next_y = (blocks[2][:half].astype(F32) + got_x[half:]).astype(BF)
    next_x = (blocks[1][half:].astype(F32) + got_y[half:]).astype(BF)
    last_y = swap(next_y, "seq", 2).astype(F32)
    last_x = swap(next_x, "seq", 1).astype(F32)
    upper = blocks[0][:half].astype(F32) + got_x[:half] + last_y
    lower = blocks[0][half:].astype(F32) + got_y[:half] + last_x
    return jnp.concatenate([upper, lower], axis=0)


def after(values, *needed):
    return lax.optimization_barrier((values, needed))[0]


def cost(micros, size=0):
    return pl.CostEstimate(flops=int(micros * 1.15e6), bytes_accessed=int(size), transcendentals=0)


def tile_rows(total, blocks):
    return min(512, total // blocks)


def rel_row(tile, rows, block_rows, me):
    per = block_rows // rows
    return pl.multiple_of(((tile // per) ^ me) * block_rows + (tile % per) * rows, rows)


def walk(tile, rows):
    prompt_tiles = PROMPT // rows
    cont_tiles = CONTLEN // rows
    in_prompt = tile < prompt_tiles
    inside = lax.rem(jnp.maximum(tile - prompt_tiles, 0), cont_tiles)
    count = jnp.where(in_prompt, tile, prompt_tiles + inside)
    return count, tile - inside - prompt_tiles


def key_limit(lens, tile, rows):
    prompt_tiles = PROMPT // rows
    cont_tiles = CONTLEN // rows
    past = jnp.maximum(tile - prompt_tiles, 0)
    cont = jnp.minimum(past // cont_tiles, CONTS - 1)
    length = lens[1]
    for i in range(1, CONTS):
        length = jnp.where(cont == i, lens[1 + i], length)
    return jnp.where(
        tile < prompt_tiles, lens[0] - tile * rows, length - lax.rem(past, cont_tiles) * rows
    )


def pair_stack(block, per_pair, scale=None):
    if scale is not None:
        block = block * scale
    if per_pair == 1:
        return block
    lane = lax.broadcasted_iota(jnp.int32, block.shape, 1) // HD
    return jnp.concatenate(
        [jnp.where(lane == h, block, jnp.zeros_like(block)) for h in range(per_pair)], axis=0
    )


def diagonal_mask(rows, per_pair, limit):
    key = lax.broadcasted_iota(jnp.int32, (rows, per_pair * rows), 0)
    query = lax.broadcasted_iota(jnp.int32, (rows, per_pair * rows), 1) % rows
    return ((key <= query) & (key < limit)) | (key == query)


def live_mask(rows, per_pair, limit):
    return lax.broadcasted_iota(jnp.int32, (rows, per_pair * rows), 0) < limit


def nt(left, right):
    return lax.dot_general(left, right, (((1,), (1,)), ((), ())), preferred_element_type=F32)


def nn(left, right):
    return lax.dot_general(left, right, (((1,), (0,)), ((), ())), preferred_element_type=F32)


def unstack(values, per_pair, rows):
    if per_pair == 1:
        return values
    return jnp.concatenate(
        [values[h * HD : (h + 1) * HD, h * rows : (h + 1) * rows] for h in range(per_pair)], axis=0
    )


def forward_kernel(
    rows, block_rows, per_pair, lens, q_ref, k_ref, v_ref, out_ref, norm_ref, vt_ref, parts, total
):
    tile = pl.program_id(0)
    me = lens[1 + CONTS]
    tiles = q_ref.shape[0] // rows
    across = per_pair * rows

    @pl.when(tile == 0)
    def _():
        def turn(i, carry):
            at = rel_row(i, rows, block_rows, me)
            vt_ref[i] = v_ref[pl.ds(at, rows), :].T
            return carry

        lax.fori_loop(0, tiles, turn, 0)

    at = rel_row(tile, rows, block_rows, me)
    query = pair_stack(q_ref[pl.ds(at, rows), :], per_pair, jnp.asarray(0.125, BF)).T
    count, shift = walk(tile, rows)

    def folded(values):
        return values.reshape(rows // 8, 8, across)

    def scores(i):
        return nn(k_ref[pl.ds(rel_row(i, rows, block_rows, me), rows), :], query)

    def key_tile(i):
        return jnp.where(i < PROMPT // rows, i, i + shift)

    first = jnp.where(
        diagonal_mask(rows, per_pair, key_limit(lens, tile, rows)), scores(tile), NEG
    )

    def measure(i, top):
        here = key_tile(i)
        part = jnp.where(
            live_mask(rows, per_pair, key_limit(lens, here, rows)), scores(here), NEG
        )
        parts[i] = part
        return jnp.maximum(top, jnp.max(folded(part), axis=0))

    top = lax.fori_loop(0, count, measure, jnp.max(folded(first), axis=0))
    top = jnp.max(top, axis=0, keepdims=True)
    weights = jnp.exp(first - top)
    total[...] = nn(vt_ref[tile], weights.astype(BF))

    def gather(i, denom):
        weights = jnp.exp(parts[i] - top)
        total[...] += nn(vt_ref[key_tile(i)], weights.astype(BF))
        return denom + jnp.sum(folded(weights), axis=0)

    denom = lax.fori_loop(0, count, gather, jnp.sum(folded(weights), axis=0))
    denom = jnp.sum(denom, axis=0, keepdims=True)
    mixed = unstack(total[...] / denom, per_pair, rows)
    out_ref[...] = mixed.T.astype(BF)
    norm_ref[0] = top + jnp.log(denom)


def backward_kernel(
    rows, block_rows, per_pair, lens, q_ref, k_ref, v_ref, out_ref, grad_ref, norm_ref,
    dq_ref, dk_ref, dv_ref, kt_ref, dk_sum, dv_sum, dq_sum,
):
    tile = pl.program_id(0)
    me = lens[1 + CONTS]
    tiles = q_ref.shape[0] // rows

    @pl.when(tile == 0)
    def _():
        def turn(i, carry):
            at = rel_row(i, rows, block_rows, me)
            kt_ref[i] = k_ref[pl.ds(at, rows), :].T
            return carry

        lax.fori_loop(0, tiles, turn, 0)
        dk_sum[...] = jnp.zeros_like(dk_sum)
        dv_sum[...] = jnp.zeros_like(dv_sum)

    at = rel_row(tile, rows, block_rows, me)
    query = pair_stack(q_ref[pl.ds(at, rows), :], per_pair, jnp.asarray(0.125, BF))
    grad_block = grad_ref[pl.ds(at, rows), :]
    grad = pair_stack(grad_block, per_pair)
    query_turned = query.T
    grad_turned = grad.T
    product = (grad_block.astype(F32) * out_ref[pl.ds(at, rows), :].astype(F32)).T
    inner = jnp.concatenate(
        [
            jnp.sum(product[h * HD : (h + 1) * HD], axis=0, keepdims=True)
            for h in range(per_pair)
        ],
        axis=1,
    )
    norm = norm_ref[0]

    def one(key_tile, mask):
        key_at = rel_row(key_tile, rows, block_rows, me)
        keys = pl.ds(key_at, rows)
        part = jnp.where(mask, nn(k_ref[keys, :], query_turned), NEG)
        probs = jnp.exp(part - norm)
        slope = probs * (nn(v_ref[keys, :], grad_turned) - inner)
        slope_low = slope.astype(BF)
        dv_sum[keys, :] += nn(probs.astype(BF), grad)
        dk_sum[keys, :] += nn(slope_low, query)
        return nn(kt_ref[key_tile], slope_low)

    dq_sum[...] = one(tile, diagonal_mask(rows, per_pair, key_limit(lens, tile, rows)))
    count, shift = walk(tile, rows)

    def step(i, carry):
        key_tile = jnp.where(i < PROMPT // rows, i, i + shift)
        dq_sum[...] += one(key_tile, live_mask(rows, per_pair, key_limit(lens, key_tile, rows)))
        return carry

    lax.fori_loop(0, count, step, 0)
    dq_ref[...] = (unstack(dq_sum[...], per_pair, rows).T * 0.125).astype(BF)

    @pl.when(tile == tiles - 1)
    def _():
        dk_ref[...] = dk_sum[...].astype(BF)
        dv_ref[...] = dv_sum[...].astype(BF)


def attention_plan(total, heads):
    blocks = lax.axis_size("seq")
    rows = tile_rows(total, blocks)
    per_pair = 2 if heads % 2 == 0 else 1
    return rows, total // blocks, per_pair, heads // per_pair, per_pair * HD


def thirds(qkv, width, pair_width):
    per = width // pair_width
    if pair_width % 128 == 0:
        return (qkv, qkv, qkv), (0, per, 2 * per)
    return tuple(qkv[:, i * width : (i + 1) * width] for i in range(3)), (0, 0, 0)


def row_block(rows, block_rows):
    per = block_rows // rows

    def index(tile, lens):
        return ((tile // per) ^ lens[1 + CONTS]) * per + tile % per, 0

    return index


def attend_forward(lens, qkv, heads, between=None):
    total = qkv.shape[0]
    width = heads * HD
    rows, block_rows, per_pair, pairs, pair_width = attention_plan(total, heads)
    arrays, firsts = thirds(qkv, width, pair_width)
    tiles = total // rows
    most = (PROMPT + CONTLEN) // rows
    mixed = None
    norms = []
    for pair in range(pairs):

        def whole(first):
            return pl.BlockSpec((total, pair_width), lambda tile, lens: (0, first + pair))

        def kernel(lens, q_ref, k_ref, v_ref, *refs):
            forward_kernel(
                rows, block_rows, per_pair, lens, q_ref, k_ref, v_ref, *refs[mixed is not None :]
            )

        place_row = row_block(rows, block_rows)
        more = [] if mixed is None else [mixed]
        mixed, norm = pl.pallas_call(
            kernel,
            out_shape=(
                jax.ShapeDtypeStruct((total, width), BF),
                jax.ShapeDtypeStruct((tiles, 1, per_pair * rows), F32),
            ),
            grid_spec=pltpu.PrefetchScalarGridSpec(
                num_scalar_prefetch=1,
                grid=(tiles,),
                in_specs=[whole(first) for first in firsts]
                + [pl.BlockSpec(memory_space=pl.ANY)] * len(more),
                out_specs=(
                    pl.BlockSpec(
                        (rows, pair_width), lambda tile, lens: (place_row(tile, lens)[0], pair)
                    ),
                    pl.BlockSpec((1, 1, per_pair * rows), lambda tile, lens: (tile, 0, 0)),
                ),
                scratch_shapes=[
                    pltpu.VMEM((tiles, pair_width, rows), BF),
                    pltpu.VMEM((most, rows, per_pair * rows), F32),
                    pltpu.VMEM((pair_width, per_pair * rows), F32),
                ],
            ),
            input_output_aliases={4: 0} if more else {},
            cost_estimate=cost(15),
            name="attend_forward",
        )(lens, *arrays, *more)
        norms.append(norm)
        if between is not None and pair + 1 < pairs:
            lens, mixed, arrays = between(lens, mixed, arrays)
    return mixed, norms


def attend_backward(lens, qkv, mixed, norms, grad, heads, between=None):
    total = qkv.shape[0]
    width = heads * HD
    rows, block_rows, per_pair, pairs, pair_width = attention_plan(total, heads)
    arrays, firsts = thirds(qkv, width, pair_width)
    tiles = total // rows
    made = []
    for pair in range(pairs):

        def whole(first):
            return pl.BlockSpec((total, pair_width), lambda tile, lens: (0, first))

        made.append(
            pl.pallas_call(
                functools.partial(backward_kernel, rows, block_rows, per_pair),
                out_shape=(jax.ShapeDtypeStruct((total, pair_width), BF),) * 3,
                grid_spec=pltpu.PrefetchScalarGridSpec(
                    num_scalar_prefetch=1,
                    grid=(tiles,),
                    in_specs=[whole(first + pair) for first in firsts]
                    + [
                        whole(pair),
                        whole(pair),
                        pl.BlockSpec((1, 1, per_pair * rows), lambda tile, lens: (tile, 0, 0)),
                    ],
                    out_specs=(
                        pl.BlockSpec((rows, pair_width), row_block(rows, block_rows)),
                        whole(0),
                        whole(0),
                    ),
                    scratch_shapes=[
                        pltpu.VMEM((tiles, pair_width, rows), BF),
                        pltpu.VMEM((total, pair_width), F32),
                        pltpu.VMEM((total, pair_width), F32),
                        pltpu.VMEM((pair_width, per_pair * rows), F32),
                    ],
                ),
                cost_estimate=cost(18),
                name="attend_backward",
            )(lens, *arrays, mixed, grad, norms[pair])
        )
        if between is not None and pair + 1 < pairs:
            lens, made[-1], grad = between(lens, made[-1], grad)
    return made


def norm_stats(values):
    center = values - jnp.mean(values, axis=-1, keepdims=True)
    spread = jnp.mean(center * center, axis=-1, keepdims=True)
    scale = lax.rsqrt(spread + EPS)
    return center * scale, scale


def norm_pull(unit, scale, slope):
    return scale * (
        slope
        - jnp.mean(slope, axis=-1, keepdims=True)
        - unit * jnp.mean(slope * unit, axis=-1, keepdims=True)
    )


def gelu_both(values):
    square = values * values
    bent = jnp.tanh(GELU_C * (values + GELU_A * square * values))
    value = 0.5 * values * (1.0 + bent)
    slope = 0.5 * (1.0 + bent) + 0.5 * values * (1.0 - bent * bent) * GELU_C * (
        1.0 + 3.0 * GELU_A * square
    )
    return value, slope


def tn(left, right):
    return lax.dot_general(left, right, (((0,), (0,)), ((), ())), preferred_element_type=F32)


def pick(values, index, axis):
    return lax.dynamic_index_in_dim(values, index, axis, keepdims=False)


def by_core(core, mine, other, axis):
    return jnp.where(
        core == 0, jnp.stack([mine, other], axis=axis), jnp.stack([other, mine], axis=axis)
    )


def body_general(
    tokens,
    prompt_lens,
    cont_lens,
    gain_one,
    shift_one,
    w_qkv,
    bias_qv,
    w_out,
    bias_out,
    gain_two,
    shift_two,
    w_fc,
    bias_fc,
    w_proj,
    bias_proj,
    cotangent,
):
    ns = lax.axis_size("seq")
    nf = lax.axis_size("fsdp")
    nz = nf // 2
    me = lax.axis_index("seq")
    owner = lax.axis_index("fsdp")
    floor = owner // 2
    core = owner % 2
    toks, width = tokens.shape[1:]
    hidden_all = w_fc.shape[1]
    own = width // nf
    heads = H // ns
    local = width // ns
    hw = hidden_all // (nf * ns)
    cols = nz * hw

    token_block = tokens[0]
    branch = cotangent[0]

    token_blocks = plane_gather(token_block)
    vectors = [gain_one, shift_one, bias_qv, bias_out, gain_two, shift_two, bias_fc, bias_proj]
    packed = jnp.concatenate([v.reshape(-1, own) for v in vectors], axis=0)
    lines = packed.shape[0]
    packed_rows = -(-packed.size // (3 * local))
    packed = jnp.pad(packed.reshape(-1), (0, 16 * (-(-packed_rows // 16)) * 3 * local - packed.size))
    mine_qkv = pick(w_qkv.reshape(own, 3, ns, local), me, 2).reshape(own, 3 * local)
    sent_qkv = jnp.concatenate([mine_qkv, packed.reshape(-1, 3 * local)], axis=0)
    got_qkv = jnp.stack([sent_qkv] + [swap(sent_qkv, "fsdp", 2 * k) for k in range(1, nz)])
    got_qkv = xor_take(by_core(core, got_qkv, swap(got_qkv, "fsdp", 1), 1), floor, 0)
    qkv_mat = got_qkv[:, :, :own].reshape(width, 3 * local)
    small = got_qkv[:, :, own:].reshape(nf, -1)[:, : lines * own].reshape(nf, lines, own)
    at = 0
    full = []
    for v in vectors:
        count = v.shape[0] // own
        full.append(small[:, at : at + count].reshape(-1).astype(F32))
        at += count
    gain_a, shift_a, qv_vec, out_vec, gain_b, shift_b, fc_vec, proj_vec = full

    fc_cut = w_fc.reshape(own, nz, 2, ns, hw)
    fc_mine = pick(fc_cut, core, 2)
    fc_other = swap(pick(fc_cut, 1 - core, 2).reshape(own, -1), "fsdp", 1)
    fc_rows = by_core(core, fc_mine.reshape(own, -1), fc_other, 0).reshape(2 * own, nz, ns, hw)
    fc_rows = xor_take(xor_take(fc_rows, floor, 1), me, 2)
    proj_rows = xor_take(w_proj.reshape(ns, hw, width), me, 0)
    out_cols = xor_take(w_out.reshape(own, ns, local), me, 1)
    proj_parts = width // cols
    out_parts = max(1, cols // local)

    def share(q, k):
        fc = jnp.concatenate([fc_rows[:, j ^ k, q] for j in range(nz)], axis=1)
        proj = [proj_rows[q][:, i * cols : (i + 1) * cols] for i in range(proj_parts)]
        out = out_cols[:, q]
        if out_parts > 1:
            step = own // out_parts
            out = jnp.concatenate([out[i * step : (i + 1) * step] for i in range(out_parts)], axis=1)
        return fc, proj, out

    def message(k):
        fc, proj, out = share(0, k)
        return jnp.concatenate([fc, *proj, out.reshape(-1, cols)], axis=0)

    got = [swap(message(k), "fsdp", 2 * k) for k in range(1, nz)]
    rows_each = got[0].shape[0]
    planes = plane_gather(jnp.concatenate(got, axis=0))

    def parts_of(q, k):
        if k == 0:
            fc, proj, out = share(q, 0)
            return fc, jnp.concatenate(proj, axis=1), out_cols[:, q]
        block = planes[q][(k - 1) * rows_each : k * rows_each]
        fc = block[: 2 * own]
        proj = jnp.concatenate(
            [block[2 * own + i * hw : 2 * own + (i + 1) * hw] for i in range(proj_parts)], axis=1
        )
        out = block[2 * own + proj_parts * hw :]
        if out_parts > 1:
            out = jnp.concatenate(
                [out[:, i * local : (i + 1) * local] for i in range(out_parts)], axis=0
            )
        else:
            out = out.reshape(own, local)
        return fc, proj, out

    pieces = [[parts_of(q, k) for k in range(nz)] for q in range(ns)]
    out_half = jnp.stack(
        [jnp.stack([pieces[q][k][2] for q in range(ns)], axis=1) for k in range(nz)]
    )
    out_half = xor_take(out_half, me, 2).reshape(nz, own, width)
    out_both = by_core(core, out_half, swap(out_half, "fsdp", 1), 1)
    out_mat = xor_take(out_both, floor, 0).reshape(ns, local, width)
    out_mat = xor_take(out_mat, me, 0).reshape(width, width)
    fc_mat = jnp.concatenate(
        [jnp.concatenate([pieces[q][k][0] for k in range(nz)], axis=0) for q in range(ns)], axis=1
    )
    proj_mat = jnp.concatenate([pieces[q][k][1] for q in range(ns) for k in range(nz)], axis=0)
    fc_bias = pick(fc_vec.reshape(nz, 2, ns, hw), core, 1)
    fc_bias = xor_take(xor_take(fc_bias, floor, 0), me, 1).transpose(1, 0, 2).reshape(-1)

    all_tokens = jnp.concatenate(token_blocks, axis=0).astype(F32)
    unit_all, _ = norm_stats(all_tokens)
    first = (unit_all * gain_a + shift_a).astype(BF)
    bias_all = jnp.concatenate(
        [
            pick(qv_vec.reshape(2, ns, local)[0], me, 0),
            jnp.zeros((local,), F32),
            pick(qv_vec.reshape(2, ns, local)[1], me, 0),
        ]
    )
    qkv = (jnp.dot(first, qkv_mat, preferred_element_type=F32) + bias_all).astype(BF)
    lens = jnp.concatenate([prompt_lens, cont_lens[0], me.reshape(1)]).astype(jnp.int32)
    mixed_heads, norms = attend_forward(lens, qkv, heads)

    def to_tokens(values):
        return jnp.concatenate(
            [values[:toks]]
            + [swap(values[k * toks : (k + 1) * toks], "seq", k) for k in range(1, ns)],
            axis=1,
        )

    def to_heads(values):
        return jnp.concatenate(
            [values[:, :local]]
            + [swap(values[:, k * local : (k + 1) * local], "seq", k) for k in range(1, ns)],
            axis=0,
        )

    mixed = to_tokens(mixed_heads)
    hidden = token_block.astype(F32) + jnp.dot(mixed, out_mat, preferred_element_type=F32) + out_vec
    unit_two, scale_two = norm_stats(hidden)
    second = (unit_two * gain_b + shift_b).astype(BF)

    second_both = jnp.concatenate([second, swap(second, "fsdp", 1)], axis=0)
    second_both = xor_blocks(second_both, floor, nz, 1)
    branch_both = jnp.concatenate([branch, swap(branch, "fsdp", 1)], axis=0)
    pre = jnp.dot(second_both, fc_mat, preferred_element_type=F32) + fc_bias
    act_full, bend = gelu_both(pre)
    act = act_full.astype(BF)
    grad_act = nt(branch_both, proj_mat)
    grad_pre = (grad_act * bend).astype(BF)
    grad_second_both = nt(grad_pre, fc_mat)
    grad_second = grad_second_both[:toks] + swap(
        grad_second_both[toks:].astype(BF), "fsdp", 1
    ).astype(F32)
    grad_second = xor_blocks(grad_second, floor, nz, 1)
    out_sum = jnp.dot(act, proj_mat, preferred_element_type=F32)
    result = hidden + out_sum[:toks] + proj_vec
    result = result + swap(out_sum[toks:].astype(BF), "fsdp", 1).astype(F32)
    output = result.astype(BF)[None]

    grad_hidden = branch.astype(F32) + norm_pull(unit_two, scale_two, grad_second * gain_b)
    grad_attn = grad_hidden.astype(BF)
    grad_mixed = nt(grad_attn, out_mat).astype(BF)
    grad_heads = to_heads(grad_mixed)

    backward = attend_backward(lens, qkv, mixed_heads, norms, grad_heads, heads)
    grad_q, grad_k, grad_v = (
        jnp.concatenate([part[i] for part in backward], axis=1) for i in range(3)
    )
    grad_qkv = jnp.concatenate([grad_q, grad_k, grad_v], axis=1)
    grad_first_part = nt(grad_qkv, qkv_mat).astype(BF)
    grad_first = plane_scatter(
        [grad_first_part[k * toks : (k + 1) * toks] for k in range(ns)]
    )
    unit_one, scale_one = norm_stats(token_block.astype(F32))
    input_grad = (grad_hidden + norm_pull(unit_one, scale_one, grad_first * gain_a))[None]

    span = nz * hw
    grad_fc = [tn(second_both, grad_pre[:, q * span : (q + 1) * span]).astype(BF) for q in range(ns)]
    grad_proj = [tn(act[:, q * span : (q + 1) * span], branch_both).astype(BF) for q in range(ns)]
    fc_sum = plane_scatter(grad_fc)
    proj_sum = plane_scatter(grad_proj)

    def fc_for(k):
        block = fc_sum[k * 2 * own : (k + 1) * 2 * own].reshape(2 * own, nz, hw)
        return jnp.concatenate([block[:, j ^ k] for j in range(nz)], axis=1)

    def proj_for(k):
        block = proj_sum[k * hw : (k + 1) * hw]
        return jnp.concatenate(
            [block[:, i * span : (i + 1) * span] for i in range(proj_parts)], axis=0
        )

    both_sum = jnp.concatenate([fc_for(0), proj_for(0)], axis=0)
    for k in range(1, nz):
        sent = jnp.concatenate([fc_for(k), proj_for(k)], axis=0).astype(BF)
        both_sum = both_sum + swap(sent, "fsdp", 2 * k).astype(F32)
    fc_owned = both_sum[: 2 * own].reshape(2, own, span)
    fc_kept = pick(fc_owned, core, 0).astype(BF)
    fc_moved = swap(pick(fc_owned, 1 - core, 0).astype(BF), "fsdp", 1)
    final = jnp.concatenate([fc_kept, fc_moved, both_sum[2 * own :].astype(BF)], axis=0)
    finals = plane_gather(final)
    fc_kept_all = jnp.stack([v[:own].reshape(own, nz, hw) for v in finals], axis=2)
    fc_moved_all = jnp.stack([v[own : 2 * own].reshape(own, nz, hw) for v in finals], axis=2)
    grad_w_fc = by_core(core, fc_kept_all, fc_moved_all, 2)
    grad_w_fc = xor_take(xor_take(grad_w_fc, floor, 1), me, 3).reshape(own, hidden_all).astype(F32)
    grad_w_proj = jnp.stack(
        [
            jnp.concatenate(
                [v[2 * own + i * hw : 2 * own + (i + 1) * hw] for i in range(proj_parts)], axis=1
            )
            for v in finals
        ]
    )
    grad_w_proj = xor_take(grad_w_proj, me, 0).reshape(ns * hw, width).astype(F32)

    grad_out = tn(mixed, grad_attn).astype(BF).reshape(ns, local, width)
    grad_out = xor_take(grad_out, me, 0).reshape(nz, 2, own, width)
    grad_out = xor_take(grad_out, floor, 0)
    out_kept = pick(grad_out, core, 1).astype(F32) + swap(
        pick(grad_out, 1 - core, 1), "fsdp", 1
    ).astype(F32)
    out_owned = out_kept[0]
    for k in range(1, nz):
        out_owned = out_owned + swap(out_kept[k].astype(BF), "fsdp", 2 * k).astype(F32)
    bit = 1
    while bit < ns:
        out_owned = out_owned + swap(out_owned.astype(BF), "seq", bit).astype(F32)
        bit *= 2
    grad_w_out = out_owned

    grad_in = tn(first, grad_qkv).astype(BF).reshape(nz, 2, own, 3 * local)
    grad_in = xor_take(grad_in, floor, 0)
    in_kept = pick(grad_in, core, 1).astype(F32) + swap(
        pick(grad_in, 1 - core, 1), "fsdp", 1
    ).astype(F32)
    in_owned = in_kept[0]
    for k in range(1, nz):
        in_owned = in_owned + swap(in_kept[k].astype(BF), "fsdp", 2 * k).astype(F32)
    in_owned = in_owned.astype(BF)
    in_blocks = jnp.stack(
        [in_owned.reshape(own, 3, local)]
        + [swap(in_owned, "seq", k).reshape(own, 3, local) for k in range(1, ns)],
        axis=2,
    )
    grad_w_qkv = xor_take(in_blocks, me, 2).reshape(own, 3 * width).astype(F32)

    def placed(values, parts):
        slots = jnp.arange(parts)[:, None] == me
        return jnp.where(slots, values[None, :], 0.0).reshape(-1)

    part_f32 = grad_first_part.astype(F32)
    fc_bias_grad = jnp.sum(grad_pre.astype(F32), axis=0).reshape(ns, nz, hw).transpose(1, 0, 2)
    fc_bias_grad = xor_take(xor_take(fc_bias_grad, floor, 0), me, 1)
    fc_bias_grad = jnp.where(
        (jnp.arange(2) == core)[None, :, None, None], fc_bias_grad[:, None], 0.0
    ).reshape(-1)
    vector_grads = [
        jnp.sum(part_f32 * unit_all, axis=0),
        jnp.sum(part_f32, axis=0),
        placed(jnp.sum(grad_q.astype(F32), axis=0), ns),
        placed(jnp.sum(grad_v.astype(F32), axis=0), ns),
        jnp.sum(grad_attn.astype(F32), axis=0),
        jnp.sum(grad_second * unit_two, axis=0),
        jnp.sum(grad_second, axis=0),
        fc_bias_grad,
        jnp.sum(branch.astype(F32), axis=0),
    ]
    vector_sum = jnp.concatenate([v.reshape(-1, width) for v in vector_grads], axis=0)
    for axis, size in (("seq", ns), ("fsdp", nf)):
        bit = 1
        while bit < size:
            vector_sum = vector_sum + swap(vector_sum, axis, bit)
            bit *= 2
    vector_sum = vector_sum.reshape(-1)
    outs = []
    at = 0
    for v in vectors:
        count = v.shape[0]
        outs.append(lax.dynamic_slice_in_dim(vector_sum, at + owner * count, count))
        at += nf * count
    (g_gain_one, g_shift_one, g_bias_qv, g_bias_out, g_gain_two, g_shift_two, g_bias_fc, g_bias_proj) = outs

    return (
        output,
        input_grad,
        g_gain_one,
        g_shift_one,
        grad_w_qkv,
        g_bias_qv,
        grad_w_out,
        g_bias_out,
        g_gain_two,
        g_shift_two,
        grad_w_fc,
        g_bias_fc,
        grad_w_proj,
        g_bias_proj,
    )


UPPER = (0, 2, 1, 3)


def hidden_at(q, half, size):
    return half * 4 * size + (UPPER[q] if half == 0 else q) * size


def start_all(copies, sems):
    made = [
        pltpu.make_async_copy(source, target, sems.at[i]) for i, (source, target) in enumerate(copies)
    ]
    for copy in made:
        copy.start()
    return made


def aligned(value, size):
    return pl.multiple_of(value, size)


def pack_kernel(hw, place, fc_ref, proj_ref, out_mat_ref, mine_ref, other_ref, share_ref):
    me, core = place[0], place[2]
    for q in range(4):
        for z in range(4):
            target = hidden_at(q, z // 2, 2 * hw) + (z % 2) * hw
            for out_ref, which in ((mine_ref, core), (other_ref, 1 - core)):
                source = aligned(z * 8 * hw + which * 4 * hw + (me ^ q) * hw, hw)
                out_ref[:, target : target + hw] = fc_ref[:, pl.ds(source, hw)]
    share_ref[...] = proj_ref[...]
    other_ref[:, 16 * hw :] = out_mat_ref[...]


def pack(place, w_fc, w_proj, w_out):
    own, hidden_all = w_fc.shape
    hw, width = w_proj.shape[0] // 4, w_proj.shape[1]

    def whole(shape):
        return pl.BlockSpec(shape, lambda i, place: (0, 0))

    half = jax.ShapeDtypeStruct((own, hidden_all // 2), BF)
    more = jax.ShapeDtypeStruct((own, hidden_all // 2 + width), BF)
    return pl.pallas_call(
        functools.partial(pack_kernel, hw),
        out_shape=(half, more, jax.ShapeDtypeStruct((hw, width), BF)),
        grid_spec=pltpu.PrefetchScalarGridSpec(
            num_scalar_prefetch=1,
            grid=(1,),
            in_specs=[
                whole((own, hidden_all)),
                pl.BlockSpec((hw, width), lambda i, place: (place[0], 0)),
                whole(w_out.shape),
            ],
            out_specs=(whole(half.shape), whole(more.shape), whole((hw, width))),
        ),
        cost_estimate=cost(3),
        name="pack_shares",
    )(place, w_fc, w_proj, w_out)


def join_kernel(place, m0, m1, o0, o1, mine_out, l0, l1, out_ref):
    core = place[2]
    own, chunk = m0.shape
    part = mine_out.shape[0]
    for refs, which in (((m0, m1), core), ((o0, o1), 1 - core)):
        rows = pl.ds(aligned(which * own, own), own)
        for half in range(2):
            out_ref[rows, half * chunk : (half + 1) * chunk] = refs[half][...]
    wide = 2 * chunk
    for parts, which in (
        ((mine_out[:, :wide], mine_out[:, wide:]), core),
        ((l0[...], l1[...]), 1 - core),
    ):
        for half in range(2):
            rows = pl.ds(aligned(2 * own + which * 2 * part + half * part, part), part)
            out_ref[rows, :] = parts[half]


def join(place, mine, other, w_out):
    own, hidden = mine.shape
    chunk = hidden // 8
    part = own // 4
    rows = 2 * own + 4 * part
    pieces = [
        pl.BlockSpec((own, chunk), lambda i, place, at=hidden_at(0, half, 1): (0, at))
        for half in range(2)
    ]
    quarters = [
        pl.BlockSpec((part, 2 * chunk), lambda i, place, at=4 + half: (place[0], at))
        for half in range(2)
    ]
    return pl.pallas_call(
        join_kernel,
        out_shape=jax.ShapeDtypeStruct((rows, 2 * chunk), BF),
        grid_spec=pltpu.PrefetchScalarGridSpec(
            num_scalar_prefetch=1,
            grid=(1,),
            in_specs=pieces * 2
            + [pl.BlockSpec((part, w_out.shape[1]), lambda i, place: (place[0], 0))]
            + quarters,
            out_specs=pl.BlockSpec((rows, 2 * chunk), lambda i, place: (0, 0)),
        ),
        cost_estimate=cost(2),
        name="join_rows",
    )(place, mine, mine, other, other, w_out, other, other)


def joined_kernel(*refs):
    at = 0
    for ref in refs[:-1]:
        refs[-1][at : at + ref.shape[0], :] = ref[...]
        at += ref.shape[0]


def joined(parts):
    rows = sum(part.shape[0] for part in parts)
    return pl.pallas_call(
        joined_kernel,
        out_shape=jax.ShapeDtypeStruct((rows, parts[0].shape[1]), parts[0].dtype),
        cost_estimate=cost(1),
        name="joined",
    )(*parts)


def project_kernel(
    place, own_ref, one_ref, two_ref, up_ref, low_ref, kept_ref, moved_ref, gain_ref, shift_ref,
    bias_ref, first_ref, unit_ref, qkv_ref, turned_ref, toks, mat, sems,
):
    step = pl.program_id(0)
    floor, core = place[1], place[2]
    block = own_ref.shape[0]
    half = block // 2
    own = mat.shape[0] // 8

    def copies():
        made = [
            (own_ref, toks.at[pl.ds(0, block), :]),
            (one_ref, toks.at[pl.ds(block, block), :]),
            (two_ref, toks.at[pl.ds(2 * block, block), :]),
            (up_ref, toks.at[pl.ds(3 * block, half), :]),
            (low_ref, toks.at[pl.ds(3 * block + half, half), :]),
        ]
        for k in range(4):
            for ref, which in ((kept_ref, core), (moved_ref, 1 - core)):
                row = aligned((floor ^ k) * 2 * own + which * own, own)
                made.append((ref.at[k, pl.ds(0, own), :], mat.at[pl.ds(row, own), :]))
        return made

    @pl.when(step == 0)
    def _():
        for copy in start_all(copies(), sems):
            copy.wait()

    rows = first_ref.shape[0]
    values = toks[pl.ds(aligned(step * rows, rows), rows), :].astype(F32)
    unit, _ = norm_stats(values)
    first = (unit * gain_ref[...] + shift_ref[...]).astype(BF)
    first_ref[...] = first
    unit_ref[...] = unit.astype(BF)
    qkv_ref[...] = (nn(first, mat[...]) + bias_ref[...]).astype(BF)

    @pl.when(step == pl.num_programs(0) - 1)
    def _():
        turned_ref[...] = mat[...].T


def project(place, blocks, kept, moved, gain, shift, bias):
    block, width = blocks[0].shape
    outs = kept.shape[2]
    total = 4 * block
    rows = 256
    raw = pl.BlockSpec(memory_space=pl.ANY)

    def line(size):
        return pl.BlockSpec((1, size), lambda i, place: (0, 0))

    def tile(size):
        return pl.BlockSpec((rows, size), lambda i, place: (i, 0))

    return pl.pallas_call(
        project_kernel,
        out_shape=(
            jax.ShapeDtypeStruct((total, width), BF),
            jax.ShapeDtypeStruct((total, width), BF),
            jax.ShapeDtypeStruct((total, outs), BF),
            jax.ShapeDtypeStruct((outs, width), BF),
        ),
        grid_spec=pltpu.PrefetchScalarGridSpec(
            num_scalar_prefetch=1,
            grid=(total // rows,),
            in_specs=[raw] * 7 + [line(width), line(width), line(outs)],
            out_specs=(
                tile(width),
                tile(width),
                tile(outs),
                pl.BlockSpec((outs, width), lambda i, place: (0, 0)),
            ),
            scratch_shapes=[
                pltpu.VMEM((total, width), BF),
                pltpu.VMEM((width, outs), BF),
                pltpu.SemaphoreType.DMA((13,)),
            ],
        ),
        cost_estimate=cost(12),
        name="project",
    )(place, *blocks, kept, moved, gain, shift, bias)


def out_mat_kernel(part, place, *refs):
    (mine_ref, other_ref), shares, (mat_ref, sems) = refs[:2], refs[2:6], refs[6:]
    me, floor, core = place[0], place[1], place[2]
    own, width = mine_ref.shape
    wide = width // 2
    rows_each = 2 * own + 4 * part
    made = []
    for source, which in (
        (mine_ref, core),
        (other_ref.at[:, pl.ds(other_ref.shape[1] - width, width)], 1 - core),
    ):
        row = aligned(floor * 2 * own + which * own, own)
        made.append((source, mat_ref.at[pl.ds(row, own), :]))
    for q in range(4):
        for k in range(1, 4):
            for which in range(2):
                row = aligned((floor ^ k) * 2 * own + which * own + (me ^ q) * part, part)
                for half in range(2):
                    at = (k - 1) * rows_each + 2 * own + which * 2 * part + half * part
                    made.append(
                        (
                            shares[q].at[pl.ds(at, part), :],
                            mat_ref.at[pl.ds(row, part), pl.ds(half * wide, wide)],
                        )
                    )
    for copy in start_all(made, sems):
        copy.wait()


def out_matrix(place, mine, other, shares):
    width = mine.shape[1]
    return pl.pallas_call(
        functools.partial(out_mat_kernel, mine.shape[0] // 4),
        out_shape=jax.ShapeDtypeStruct((width, width), BF),
        grid_spec=pltpu.PrefetchScalarGridSpec(
            num_scalar_prefetch=1,
            grid=(1,),
            in_specs=[pl.BlockSpec(memory_space=pl.ANY)] * 6,
            out_specs=pl.BlockSpec((width, width), lambda i, place: (0, 0)),
            scratch_shapes=[pltpu.SemaphoreType.DMA((50,))],
        ),
        cost_estimate=cost(3),
        name="out_matrix",
    )(place, mine, other, *shares)


def attn_out_kernel(place, *refs):
    mixed_refs, (mat_ref, token_ref, bias_ref, gain_ref, shift_ref) = refs[:4], refs[4:9]
    hidden_ref, second_ref, mixed_ref, mixed, sems = refs[9:]
    step = pl.program_id(0)
    me = place[0]
    local = mixed_refs[0].shape[1]
    block = mixed.shape[0]

    @pl.when(step == 0)
    def _():
        made = []
        for k, ref in enumerate(mixed_refs):
            lanes = pl.ds(aligned((me ^ k) * local, local), local)
            made.append((ref.at[pl.ds(0, block), :], mixed.at[:, lanes]))
        for copy in start_all(made, sems):
            copy.wait()

    rows = hidden_ref.shape[0]
    here = mixed[pl.ds(aligned(step * rows, rows), rows), :]
    mixed_ref[...] = here
    hidden = token_ref[...].astype(F32) + nn(here, mat_ref[...]) + bias_ref[...]
    hidden_ref[...] = hidden
    unit, _ = norm_stats(hidden)
    second_ref[...] = (unit * gain_ref[...] + shift_ref[...]).astype(BF)


def attn_out(place, mixed, mat, tokens, bias, gain, shift):
    block, width = tokens.shape
    rows = 256
    raw = pl.BlockSpec(memory_space=pl.ANY)
    line = pl.BlockSpec((1, width), lambda i, place: (0, 0))
    tile = pl.BlockSpec((rows, width), lambda i, place: (i, 0))
    return pl.pallas_call(
        attn_out_kernel,
        out_shape=(
            jax.ShapeDtypeStruct((block, width), F32),
            jax.ShapeDtypeStruct((block, width), BF),
            jax.ShapeDtypeStruct((block, width), BF),
        ),
        grid_spec=pltpu.PrefetchScalarGridSpec(
            num_scalar_prefetch=1,
            grid=(block // rows,),
            in_specs=[raw] * 4
            + [pl.BlockSpec((width, width), lambda i, place: (0, 0)), tile, line, line, line],
            out_specs=(tile, tile, tile),
            scratch_shapes=[pltpu.VMEM((block, width), BF), pltpu.SemaphoreType.DMA((4,))],
        ),
        cost_estimate=cost(5),
        name="attn_out",
    )(place, *mixed, mat, tokens, bias, gain, shift)


def feed_kernel(
    hw, place, second_oth, second_own, branch_oth, branch_own, bias_a, bias_b, mine_ref, other_ref,
    a0, a1, a2, a3, proj_ref, b0, b1, b2, b_up, b_low, act_a, act_b, slope_a, slope_b, out_own, out_oth, back_own, back_oth, sum_a, sum_b,
    fc, proj, fc_turned, proj_turned, total, back, sems,
):
    step = pl.program_id(0)
    me, floor, core = place[0], place[1], place[2]
    own = mine_ref.shape[0]
    chunk = 2 * hw
    rows_each = a0.shape[0] // 3

    def copies(q):
        made = []
        for ref, which in ((mine_ref, core), (other_ref, 1 - core)):
            row = aligned(floor * 2 * own + which * own, own)
            for half in range(2):
                made.append(
                    (
                        ref.at[:, pl.ds(hidden_at(q, half, chunk), chunk)],
                        fc.at[q, pl.ds(row, own), pl.ds(half * chunk, chunk)],
                    )
                )
        for k in range(1, 4):
            row = aligned((floor ^ k) * 2 * own, 2 * own)
            source = (a0, a1, a2, a3)[q].at[pl.ds((k - 1) * rows_each, 2 * own), :]
            made.append((source, fc.at[q, pl.ds(row, 2 * own), :]))
        cut = hw // 2
        for k in range(4):
            row = aligned((floor ^ k) * hw, hw)
            if k == 0:
                made.append((proj_ref.at[pl.ds(aligned((me ^ q) * hw, hw), hw), :], proj.at[q, pl.ds(row, hw), :]))
            elif q < 3:
                source = (b0, b1, b2)[q].at[pl.ds((k - 1) * hw, hw), :]
                made.append((source, proj.at[q, pl.ds(row, hw), :]))
            else:
                for i in range(2):
                    at = (k - 1) * hw + i * cut
                    source = (b_up if at < 3 * cut else b_low).at[pl.ds(at % (3 * cut), cut), :]
                    made.append((source, proj.at[q, pl.ds(aligned(row + i * cut, cut), cut), :]))
        return [
            pltpu.make_async_copy(source, target, sems.at[q, i])
            for i, (source, target) in enumerate(made)
        ]

    @pl.when(step == 0)
    def _():
        for q in range(4):
            for copy in copies(q):
                copy.start()

    for q in range(4):

        @pl.when(step == q)
        def _():
            for copy in copies(q):
                copy.wait()

    fc_turned[...] = fc[step].T
    proj_turned[...] = proj[step].T
    bias = jnp.concatenate([bias_a[...], bias_b[...]], axis=1)
    rows = second_own.shape[0]
    both = 2 * rows
    partial = None
    for start, second_ref, branch_ref in ((0, second_oth, branch_oth), (rows, second_own, branch_own)):
        here = slice(start, start + rows)
        pre = nn(second_ref[...], fc[step]) + bias
        value, bend = gelu_both(pre)
        act = value.astype(BF)
        act_a[here, :] = act[:, :chunk]
        act_b[here, :] = act[:, chunk:]
        slope_full = nn(branch_ref[...], proj_turned[...]) * bend
        slope = slope_full.astype(BF)
        slope_a[here, :] = slope[:, :chunk]
        slope_b[here, :] = slope[:, chunk:]
        more = jnp.sum(slope_full, axis=0, keepdims=True)
        partial = more if partial is None else partial + more
        out_part = nn(act, proj[step])
        back_part = nn(slope, fc_turned[...])

        @pl.when(step == 0)
        def _():
            total[here, :] = out_part
            back[here, :] = back_part

        @pl.when(step > 0)
        def _():
            total[here, :] += out_part
            back[here, :] += back_part

    sum_a[...] = partial[:, :chunk]
    sum_b[...] = partial[:, chunk:]

    @pl.when(step == 3)
    def _():
        half = both // 2
        out_oth[...] = total[:half].astype(BF)
        back_oth[...] = back[:half].astype(BF)
        out_own[...] = total[half:]
        back_own[...] = back[half:]


def feed(place, second, branch, bias, mine, other, shares, w_proj, proj_shares):
    both, width = 2 * second[0].shape[0], second[0].shape[1]
    hidden = mine.shape[1]
    hw = hidden // 16
    chunk = 2 * hw
    raw = pl.BlockSpec(memory_space=pl.ANY)

    def whole(height):
        return pl.BlockSpec((height, width), lambda i, place: (0, 0))

    def upper(height):
        return pl.BlockSpec((height, chunk), lambda i, place: (0, (i % 2) * 2 + i // 2))

    def lower(height, first=0):
        return pl.BlockSpec((height, chunk), lambda i, place: (0, first + i))

    half = jax.ShapeDtypeStruct((both, hidden // 2), BF)
    line = jax.ShapeDtypeStruct((1, hidden // 2), F32)
    return pl.pallas_call(
        functools.partial(feed_kernel, hw),
        out_shape=(
            half,
            half,
            half,
            half,
            jax.ShapeDtypeStruct((both // 2, width), F32),
            jax.ShapeDtypeStruct((both // 2, width), BF),
            jax.ShapeDtypeStruct((both // 2, width), F32),
            jax.ShapeDtypeStruct((both // 2, width), BF),
            line,
            line,
        ),
        grid_spec=pltpu.PrefetchScalarGridSpec(
            num_scalar_prefetch=1,
            grid=(4,),
            in_specs=[whole(both // 2)] * 4 + [upper(1), lower(1, 4)] + [raw] * 12,
            out_specs=(upper(both), lower(both), upper(both), lower(both))
            + (whole(both // 2),) * 4
            + (upper(1), lower(1)),
            scratch_shapes=[
                pltpu.VMEM((4, width, 2 * chunk), BF),
                pltpu.VMEM((4, 2 * chunk, width), BF),
                pltpu.VMEM((2 * chunk, width), BF),
                pltpu.VMEM((width, 2 * chunk), BF),
                pltpu.VMEM((both, width), F32),
                pltpu.VMEM((both, width), F32),
                pltpu.SemaphoreType.DMA((4, 14)),
            ],
        ),
        cost_estimate=cost(35),
        name="feed",
    )(place, *second, *branch, bias, bias, mine, other, *shares, w_proj, *proj_shares)


def mixed_back_kernel(
    place, own_ref, oth_ref, hidden_ref, branch_ref, gain_ref, mat_ref,
    full_ref, low_ref, g0, g1, g2, g3, sums_ref,
):
    step = pl.program_id(0)
    me = place[0]
    local = g0.shape[1]
    slope = own_ref[...] + oth_ref[...].astype(F32)
    unit, scale = norm_stats(hidden_ref[...])
    full = branch_ref[...].astype(F32) + norm_pull(unit, scale, slope * gain_ref[...])
    low = full.astype(BF)
    full_ref[...] = full
    low_ref[...] = low
    for k, ref in enumerate((g0, g1, g2, g3)):
        rows = pl.ds(aligned((me ^ k) * local, local), local)
        ref[...] = nt(low, mat_ref[rows, :]).astype(BF)
    sums = jnp.concatenate(
        [
            jnp.sum(low.astype(F32), axis=0, keepdims=True),
            jnp.sum(slope * unit, axis=0, keepdims=True),
            jnp.sum(slope, axis=0, keepdims=True),
            jnp.sum(branch_ref[...].astype(F32), axis=0, keepdims=True),
        ],
        axis=0,
    )

    @pl.when(step == 0)
    def _():
        sums_ref[...] = sums

    @pl.when(step > 0)
    def _():
        sums_ref[...] += sums


def mixed_back(place, own, oth, hidden, branch, gain, mat):
    block, width = own.shape
    local = width // 4
    rows = block // 2

    def tile(size):
        return pl.BlockSpec((rows, size), lambda i, place: (i, 0))

    def whole(height):
        return pl.BlockSpec((height, width), lambda i, place: (0, 0))

    return pl.pallas_call(
        mixed_back_kernel,
        out_shape=(
            jax.ShapeDtypeStruct((block, width), F32),
            jax.ShapeDtypeStruct((block, width), BF),
        )
        + (jax.ShapeDtypeStruct((block, local), BF),) * 4
        + (jax.ShapeDtypeStruct((4, width), F32),),
        grid_spec=pltpu.PrefetchScalarGridSpec(
            num_scalar_prefetch=1,
            grid=(block // rows,),
            in_specs=[tile(width)] * 4 + [whole(1), whole(width)],
            out_specs=(tile(width), tile(width)) + (tile(local),) * 4 + (whole(4),),
        ),
        cost_estimate=cost(7),
        name="mixed_back",
    )(place, own, oth, hidden, branch, gain, mat)


def first_back_kernel(tiles, parts, place, *refs):
    step = pl.program_id(0)
    count = len(tiles) // 2
    grad_refs, (unit_ref, mat_ref), refs = refs[:parts], refs[parts : parts + 2], refs[parts + 2 :]
    out_refs, sums_ref = refs[:count], refs[count]
    part = nn(jnp.concatenate([ref[...] for ref in grad_refs], axis=1), mat_ref[...])
    low = part.astype(BF)
    for i in range(count):

        @pl.when(step // 2 == i)
        def _():
            out_refs[i][...] = low

    sums = jnp.concatenate(
        [
            jnp.sum(part * unit_ref[...].astype(F32), axis=0, keepdims=True),
            jnp.sum(part, axis=0, keepdims=True),
        ],
        axis=0,
    )

    @pl.when(step == 0)
    def _():
        sums_ref[...] = sums

    @pl.when(step > 0)
    def _():
        sums_ref[...] += sums


def first_back(tiles, grads, unit, mat):
    outs, width = mat.shape
    rows = 256
    table = jnp.asarray(tiles, jnp.int32)

    def at(i, place):
        return (place[i], 0)

    return pl.pallas_call(
        functools.partial(first_back_kernel, tiles, len(grads)),
        out_shape=tuple(jax.ShapeDtypeStruct((2 * rows, width), BF) for _ in tiles[::2])
        + (jax.ShapeDtypeStruct((2, width), F32),),
        grid_spec=pltpu.PrefetchScalarGridSpec(
            num_scalar_prefetch=1,
            grid=(len(tiles),),
            in_specs=[pl.BlockSpec((rows, grad.shape[1]), at) for grad in grads]
            + [
                pl.BlockSpec((rows, width), at),
                pl.BlockSpec((outs, width), lambda i, place: (0, 0)),
            ],
            out_specs=tuple(
                pl.BlockSpec((rows, width), lambda i, place, g=g: (jnp.clip(i - 2 * g, 0, 1), 0))
                for g in range(len(tiles) // 2)
            )
            + (pl.BlockSpec((2, width), lambda i, place: (0, 0)),),
        ),
        cost_estimate=cost(5),
        name="first_back",
    )(table, *grads, unit, mat)


def gather_fc_kernel(place, fa, xa, la, fb, yb, lb, o0, o1, o2, o3, fc):
    floor = place[1]
    chunk = fc.shape[1] // 2
    fc[:, :chunk] = fa[...].astype(F32) + xa[...].astype(F32) + la[...].astype(F32)
    fc[:, chunk:] = fb[...].astype(F32) + yb[...].astype(F32) + lb[...].astype(F32)
    rows = fc.shape[0] // 4
    for k, out in enumerate((o0, o1, o2, o3)):
        out[...] = fc[pl.ds(aligned((floor ^ k) * rows, rows), rows), :].astype(BF)


def gather_proj_kernel(place, pa, xp, lpa, pb, yp, lpb, o0, o1, o2, o3, proj):
    floor = place[1]
    chunk = proj.shape[0] // 2
    proj[:chunk, :] = pa[...].astype(F32) + xp[...].astype(F32) + lpa[...].astype(F32)
    proj[chunk:, :] = pb[...].astype(F32) + yp[...].astype(F32) + lpb[...].astype(F32)
    rows = proj.shape[0] // 4
    for k, out in enumerate((o0, o1, o2, o3)):
        out[...] = proj[pl.ds(aligned((floor ^ k) * rows, rows), rows), :].astype(BF)


def gather_sum(place, kernel, parts, shape, block):
    out = jax.ShapeDtypeStruct((shape[0] // 4, shape[1]), BF)
    return pl.pallas_call(
        kernel,
        out_shape=(out,) * 4,
        grid_spec=pltpu.PrefetchScalarGridSpec(
            num_scalar_prefetch=1,
            grid=(1,),
            in_specs=[pl.BlockSpec(block, lambda i, place: (0, 0))] * 6,
            out_specs=(pl.BlockSpec(out.shape, lambda i, place: (0, 0)),) * 4,
            scratch_shapes=[pltpu.VMEM(shape, F32)],
        ),
        cost_estimate=cost(3),
        name="gather_sum",
    )(place, *parts)


def spread_fc_kernel(place, *refs):
    me, core = place[0], place[2]
    finals, fc_ref = refs[:4], refs[4]
    own = fc_ref.shape[0]
    hw = finals[0].shape[1] // 4
    for q in range(4):
        for part, which in ((0, core), (1, 1 - core)):
            for z in range(4):
                lanes = pl.ds(aligned(z * 8 * hw + which * 4 * hw + (me ^ q) * hw, hw), hw)
                block = finals[q][part * own : (part + 1) * own, z * hw : (z + 1) * hw]
                fc_ref[:, lanes] = block.astype(F32)


def spread_proj_kernel(place, *refs):
    me = place[0]
    finals, proj_ref = refs[:4], refs[4]
    hw = finals[0].shape[0]
    for q in range(4):
        proj_ref[pl.ds(aligned((me ^ q) * hw, hw), hw), :] = finals[q][...].astype(F32)


def spread(place, kernel, finals, shape):
    def whole(shape):
        return pl.BlockSpec(shape, lambda i, place: (0, 0))

    return pl.pallas_call(
        kernel,
        out_shape=jax.ShapeDtypeStruct(shape, F32),
        grid_spec=pltpu.PrefetchScalarGridSpec(
            num_scalar_prefetch=1,
            grid=(1,),
            in_specs=[whole(finals[0].shape)] * 4,
            out_specs=whole(shape),
        ),
        cost_estimate=cost(2),
        name="spread",
    )(place, *finals)


def last_kernel(
    keep_ref, got_x, got_y, last_y, last_x, token_ref, hidden_ref, gain_ref, out_ref
):
    def finish(got, last):
        slope = keep_ref[...].astype(F32) + got[...].astype(F32) + last[...].astype(F32)
        unit, scale = norm_stats(token_ref[...].astype(F32))
        out_ref[...] = hidden_ref[...] + norm_pull(unit, scale, slope * gain_ref[...])

    @pl.when(pl.program_id(0) == 0)
    def _():
        finish(got_x, last_y)

    @pl.when(pl.program_id(0) == 1)
    def _():
        finish(got_y, last_x)


def body_aligned(
    tokens,
    prompt_lens,
    cont_lens,
    gain_one,
    shift_one,
    w_qkv,
    bias_qv,
    w_out,
    bias_out,
    gain_two,
    shift_two,
    w_fc,
    bias_fc,
    w_proj,
    bias_proj,
    cotangent,
):
    ns = nz = 4
    nf = 8
    me = lax.axis_index("seq")
    owner = lax.axis_index("fsdp")
    floor = owner // 2
    core = owner % 2
    place = jnp.stack([me, floor, core]).astype(jnp.int32)
    toks, width = tokens.shape[1:]
    own = width // nf
    heads = H // ns
    local = width // ns
    hw = w_fc.shape[1] // (nf * ns)
    token_block = tokens[0]
    branch = cotangent[0]

    half = toks // 2
    vectors = [gain_one, shift_one, bias_qv, bias_out, gain_two, shift_two, bias_fc, bias_proj]
    packed = jnp.concatenate([v.reshape(-1, own) for v in vectors], axis=0)
    lines = packed.shape[0]
    packed = jnp.pad(packed.reshape(-1), (0, 16 * 3 * local - packed.size)).reshape(16, 3 * local)
    mine_qkv = pick(w_qkv.reshape(own, 3, ns, local), me, 2).reshape(own, 3 * local)
    sent_qkv = jnp.concatenate([mine_qkv, packed], axis=0)
    tok_one = swap(token_block, "seq", 1)
    tok_two = swap(token_block, "seq", 2)
    got_qkv = [swap(sent_qkv, "fsdp", 2 * k) for k in range(1, nz)]
    fc_mine, fc_sent, proj_share = pack(place, after(w_fc, sent_qkv), w_proj, w_out)
    fc_other = swap(fc_sent, "fsdp", 1)
    fc_share = join(place, fc_mine, fc_other, w_out)

    tok_one, tok_two, got_qkv, fc_share, proj_share = lax.optimization_barrier(
        (tok_one, tok_two, got_qkv, fc_share, proj_share)
    )
    tok_up = swap(tok_two[:half], "seq", 1)
    tok_low = swap(tok_one[half:], "seq", 2)
    kept_qkv = jnp.stack([sent_qkv, *got_qkv])
    moved_qkv = swap(kept_qkv, "fsdp", 1)
    moved_qkv, fc_share = lax.optimization_barrier((moved_qkv, fc_share))
    fc_got = [swap(fc_share, "fsdp", 2 * k) for k in range(1, nz)]

    small = by_core(core, kept_qkv[:, own : own + 2], moved_qkv[:, own : own + 2], 1)
    small = xor_take(small, floor, 0).reshape(nf, -1).reshape(nf, lines, own)
    at = 0
    full = []
    for v in vectors:
        count = v.shape[0] // own
        full.append(small[:, at : at + count].reshape(1, -1).astype(F32))
        at += count
    gain_a, shift_a, qv_vec, out_vec, gain_b, shift_b, fc_vec, proj_vec = full
    qv_mine = pick(qv_vec.reshape(2, ns, local), me, 1)
    bias_all = jnp.concatenate([qv_mine[0], jnp.zeros((local,), F32), qv_mine[1]]).reshape(1, -1)
    fc_bias = xor_take(pick(fc_vec.reshape(nz, 2, ns, hw), core, 1), me, 1)
    order = [(q, 0) for q in (0, 2, 1, 3)] + [(q, 1) for q in range(4)]
    fc_bias = jnp.concatenate(
        [fc_bias[2 * part : 2 * part + 2, q].reshape(1, -1) for q, part in order], axis=1
    )

    first, unit_all, qkv, qkv_turned = project(
        place, (token_block, tok_one, tok_two, tok_up, tok_low), kept_qkv, moved_qkv, gain_a, shift_a,
        bias_all,
    )
    lens = jnp.concatenate([prompt_lens, cont_lens[0], me.reshape(1)]).astype(jnp.int32)

    qkv, fc_got, proj_share = lax.optimization_barrier((qkv, fc_got, proj_share))
    fc_zero = joined(fc_got)
    fc_one = swap(fc_zero, "seq", 1)
    fc_two = swap(fc_zero, "seq", 2)
    proj_got = [swap(proj_share, "fsdp", 2 * k) for k in range(1, nz)]
    ends = {}

    def between(lens, mixed, arrays):
        (mixed, arrays, one, two, got, ends["branch"]) = lax.optimization_barrier(
            (mixed, arrays, fc_one, fc_two, proj_got, branch)
        )
        ends["branch_got"] = swap(ends["branch"], "fsdp", 1)
        cut = one.shape[0] // 2
        ends["fc"] = (one, two, swap(two[:cut], "seq", 1), swap(one[cut:], "seq", 2))
        ends["proj"] = joined(got)
        return lens, mixed, arrays

    mixed_heads, norms = attend_forward(lens, qkv, heads, between)
    fc_one, fc_two, fc_up, fc_low = ends["fc"]
    proj_zero = ends["proj"]

    mixed_heads, fc_up, fc_low, proj_zero, branch_got = lax.optimization_barrier(
        (mixed_heads, fc_up, fc_low, proj_zero, ends["branch_got"])
    )
    branch_both = jnp.concatenate([branch_got, branch], axis=0)
    mixed_blocks = [mixed_heads] + [
        swap(mixed_heads[k * toks : (k + 1) * toks], "seq", k) for k in range(1, ns)
    ]
    fc_three = joined([fc_up, fc_low])
    shares = (fc_zero, fc_one, fc_two, fc_three)
    proj_one = swap(proj_zero, "seq", 1)
    proj_two = swap(proj_zero, "seq", 2)
    cut = proj_one.shape[0] // 2
    proj_three = swap(proj_two[:cut], "seq", 1), swap(proj_one[cut:], "seq", 2)
    out_mat = out_matrix(place, w_out, fc_other, shares)
    mixed_blocks, branch_both, out_mat = lax.optimization_barrier((mixed_blocks, branch_both, out_mat))
    hidden, second, mixed = attn_out(
        place, mixed_blocks, out_mat, token_block, out_vec, gain_b, shift_b
    )

    second_got = swap(second, "fsdp", 1)
    *hiddens, out_own, out_oth, back_own, back_oth, sum_upper, sum_lower = feed(
        place, (second_got, second), (branch_got, branch), fc_bias, fc_mine, fc_other,
        shares, w_proj, (proj_zero, proj_one, proj_two, *proj_three),
    )
    back_got = swap(back_oth, "fsdp", 1)
    out_got = swap(out_oth, "fsdp", 1)
    grad_hidden, grad_attn, *grad_blocks, sums_two = mixed_back(
        place, back_own, back_got, hidden, branch, gain_b, out_mat
    )

    def added(left, right):
        return (left.astype(F32) + right.astype(F32)).astype(BF)

    def halves(values, index):
        pair = values.reshape(2, values.shape[0] // 2, values.shape[1])
        return pick(pair, index, 0).astype(F32), pick(pair, 1 - index, 0).astype(BF)

    def core_halves(grad):
        cut = grad.reshape(nz, 2, own, -1)
        mine, sent = pick(cut, core, 1), pick(cut, 1 - core, 1)
        return mine.reshape(nz * own, -1), sent.reshape(nz * own, -1)

    edge = 4 * hw
    chunk = 2 * hw
    head_got = [swap(grad_blocks[k], "seq", k) for k in range(1, ns)]
    hiddens, branch_late, second_late, second_got, mixed_late, attn_late = after(
        (hiddens, branch_both, second, second_got, mixed, grad_attn), grad_blocks
    )
    acts, slopes = (
        [v[:, i * edge : (i + 1) * edge] for v in pair for i in range(2)]
        for pair in (hiddens[:2], hiddens[2:])
    )
    wo_mine, wo_sent = core_halves(tn(mixed_late, attn_late).astype(BF))
    second_both = jnp.concatenate([second_got, second_late], axis=0)

    head_x = head_got[0]
    acts, slopes, second_both, branch_late, wo_sent, head_x, out_got = after(
        (acts, slopes, second_both, branch_late, wo_sent, head_x, out_got)
    )
    proj_grads = [tn(v, branch_late).astype(BF) if i % 2 else None for i, v in enumerate(acts)]
    proj_x = swap(proj_grads[1], "seq", 1)
    proj_y = swap(proj_grads[3], "seq", 2)
    wo_got = swap(wo_sent, "fsdp", 1)
    fc_grads = [None] * 4
    for i in (1, 3, 0, 2):
        fc_grads[i] = tn(second_both, slopes[i]).astype(BF)
    for i in (0, 2):
        proj_grads[i] = tn(acts[i], branch_late).astype(BF)
    output = (hidden + out_own + proj_vec + out_got.astype(F32)).astype(BF)

    grad_heads = jnp.concatenate([grad_blocks[0], head_x, *head_got[1:]], axis=0)
    grad_heads, fc_grads, proj_keep, wo_got, output = after(
        (grad_heads, fc_grads, proj_grads[::2], wo_got, output)
    )
    fc_x = swap(fc_grads[1], "seq", 1)
    fc_y = swap(fc_grads[3], "seq", 2)
    wo_keep, wo_sent = halves(wo_mine.astype(F32) + wo_got.astype(F32), floor // 2)
    wo_far = swap(wo_sent, "fsdp", 4)
    back = {}

    def between_back(lens, parts, grad):
        parts, grad, x, y, far = after((parts, grad, proj_x, proj_y, wo_far))
        back["proj"] = (
            x,
            y,
            swap(added(proj_keep[1][chunk:], y[chunk:]), "seq", 1),
            swap(added(proj_keep[0][chunk:], x[chunk:]), "seq", 2),
        )
        keep, sent = halves(wo_keep + far.astype(F32), floor % 2)
        back["out"] = keep, swap(sent, "fsdp", 2)
        return lens, parts, grad

    backward = attend_backward(lens, qkv, mixed_heads, norms, grad_heads, heads, between_back)
    proj_x, proj_y, proj_last_x, proj_last_y = back["proj"]
    wo_keep, wo_near = back["out"]

    backward, fc_x, fc_y, proj_x, proj_y, proj_last_x, proj_last_y, wo_near = after(
        (backward, fc_x, fc_y, proj_x, proj_y, proj_last_x, proj_last_y, wo_near)
    )
    fc_far = [added(fc_grads[0][:, chunk:], fc_x[:, chunk:]), added(fc_grads[2][:, chunk:], fc_y[:, chunk:])]
    fc_last_y = swap(fc_far[0], "seq", 2)
    fc_last_x = swap(fc_far[1], "seq", 1)
    wo_sum = wo_keep + wo_near.astype(F32)
    wo_got = swap(wo_sum.astype(BF), "seq", 1)
    backward = after(backward, fc_far)
    parts = [part[i] for i in range(3) for part in backward]
    sent_x, sent_y, sums_early = first_back((2, 6, 5, 7), parts, unit_all, qkv_turned)

    sent_x, sent_y, parts, fc_last_x, fc_last_y, proj_x, proj_y = after(
        (sent_x, sent_y, parts, fc_last_x, fc_last_y, proj_x, proj_y)
    )
    got_x = swap(sent_x, "seq", 1)
    got_y = swap(sent_y, "seq", 2)
    cuts = gather_sum(
        place, gather_proj_kernel,
        (proj_keep[0], proj_x, proj_last_y, proj_keep[1], proj_y, proj_last_x),
        (4 * hw, width), (chunk, width),
    )
    cuts, wo_got = after((cuts, wo_got))
    cuts_proj = [swap(cuts[k], "fsdp", 2 * k) for k in range(1, nz)]
    grad_proj_kept = cuts[0]
    fc_grads = after(fc_grads, cuts)
    cuts = gather_sum(
        place, gather_fc_kernel,
        (fc_grads[0], fc_x, fc_last_y, fc_grads[2], fc_y, fc_last_x),
        (width, 4 * hw), (width, chunk),
    )

    parts = after(parts, cuts)
    far_late, kept_late, sums_late = first_back((4, 3, 0, 1), parts, unit_all, qkv_turned)
    cuts_proj, cuts, far_late = after((cuts_proj, cuts, far_late))
    cuts_fc = [swap(cuts[k], "fsdp", 2 * k) for k in range(1, nz)]
    fc_kept = cuts[0]

    got_x, got_y, far_late, parts = after((got_x, got_y, far_late, parts))
    far_y = added(far_late[:half], got_x[half:])
    far_x = added(far_late[half:], got_y[half:])
    last_y = swap(far_y, "seq", 2)
    last_x = swap(far_x, "seq", 1)
    parts, first_late, cuts_proj = after((parts, first, cuts_proj), far_x, far_y)
    grad_qkv = jnp.concatenate(parts, axis=1)
    wi_grad = tn(first_late, grad_qkv).astype(BF)
    proj_owned = grad_proj_kept.astype(F32)
    for part in cuts_proj:
        proj_owned = proj_owned + part.astype(F32)
    proj_owned = proj_owned.astype(BF)

    def placed(values):
        slots = jnp.arange(ns)[:, None] == me
        return jnp.where(slots, values[None, :], 0.0).reshape(-1)

    spots = {}
    for i, (q, part) in enumerate(order):
        here = (sum_upper, sum_lower)[part][0, (i % 4) * chunk : (i % 4 + 1) * chunk]
        spots[q, part] = here.reshape(2, hw)
    fc_bias_grad = jnp.stack(
        [jnp.concatenate([spots[q, 0], spots[q, 1]], axis=0) for q in range(ns)], axis=1
    )
    fc_bias_grad = xor_take(fc_bias_grad, me, 1)
    fc_bias_grad = jnp.where(
        (jnp.arange(2) == core)[None, :, None, None], fc_bias_grad[:, None], 0.0
    ).reshape(-1)
    sums_one = sums_early + sums_late
    qkv_sum = jnp.sum(grad_qkv.astype(F32), axis=0)
    vector_grads = [
        sums_one[0],
        sums_one[1],
        jnp.concatenate([placed(qkv_sum[:local]), placed(qkv_sum[2 * local :])]),
        sums_two[0],
        sums_two[1],
        sums_two[2],
        fc_bias_grad,
        sums_two[3],
    ]
    by_owner = jnp.concatenate([v.reshape(nf, -1) for v in vector_grads], axis=1)
    by_owner = by_owner.reshape(nz, 2, -1, 3 * local)
    lines = by_owner.shape[2]
    tall = own + 16
    by_owner = jnp.pad(by_owner, ((0, 0), (0, 0), (0, 16 - lines), (0, 0)))
    wi_cut = jnp.concatenate([wi_grad.reshape(nz, 2, own, 3 * local), by_owner.astype(BF)], axis=2)
    wi_mine = pick(wi_cut, core, 1).reshape(nz * tall, 3 * local)
    wi_sent = pick(wi_cut, 1 - core, 1).reshape(nz * tall, 3 * local)
    last_x, last_y, cuts_fc, wi_sent, proj_owned, wo_sum, wo_got = after(
        (last_x, last_y, cuts_fc, wi_sent, proj_owned, wo_sum, wo_got)
    )
    wi_got = swap(wi_sent, "fsdp", 1)
    fc_owned = fc_kept.astype(F32)
    for part in cuts_fc:
        fc_owned = fc_owned + part.astype(F32)
    fc_mine, fc_sent = halves(fc_owned, core)
    fc_got = swap(fc_sent, "fsdp", 1)
    wo_sum = wo_sum + wo_got.astype(F32)

    wi_got, fc_got = after((wi_got, fc_got))
    wi_keep, wi_sent = halves(wi_mine.astype(F32) + wi_got.astype(F32), floor // 2)
    wi_far = swap(wi_sent, "fsdp", 4)
    fc_final = jnp.concatenate([fc_mine.astype(BF), fc_got], axis=0)
    fc_finals = [fc_final] + [swap(fc_final, "seq", k) for k in range(1, ns)]
    last_x, last_y, kept_late = after((last_x, last_y, kept_late), fc_final, wi_sent)
    ends_at = pl.BlockSpec((half, width), lambda i: (i, 0))
    one_end = pl.BlockSpec((half, width), lambda i: (0, 0))
    input_grad = pl.pallas_call(
        last_kernel,
        out_shape=jax.ShapeDtypeStruct((toks, width), F32),
        grid=(2,),
        in_specs=[ends_at] + [one_end] * 4 + [ends_at] * 2 + [pl.BlockSpec((1, width), lambda i: (0, 0))],
        out_specs=ends_at,
        cost_estimate=cost(5),
        name="last",
    )(kept_late, got_x, got_y, last_y, last_x, token_block, grad_hidden, gain_a)

    fc_finals, input_grad, wo_sum, proj_owned = after((fc_finals, input_grad, wo_sum, proj_owned))
    input_grad = input_grad[None]
    proj_finals = [proj_owned] + [swap(proj_owned, "seq", k) for k in range(1, ns)]
    wo_got = swap(wo_sum.astype(BF), "seq", 2)
    grad_w_fc = spread(place, spread_fc_kernel, fc_finals, (own, 32 * hw))

    wi_far, grad_w_fc = after((wi_far, grad_w_fc))
    wi_keep, wi_sent = halves(wi_keep + wi_far.astype(F32), floor % 2)
    wi_near = swap(wi_sent, "fsdp", 2)

    wi_near, proj_finals = after((wi_near, proj_finals))
    wi_owned = wi_keep + wi_near.astype(F32)
    wi_low = wi_owned.astype(BF)
    wi_finals = [wi_low] + [swap(wi_low, "seq", k) for k in range(1, ns)]
    grad_w_proj = spread(place, spread_proj_kernel, proj_finals, (4 * hw, width))
    wo_got, grad_w_proj = after((wo_got, grad_w_proj))
    grad_w_out = wo_sum + wo_got.astype(F32)
    wi_blocks = jnp.stack([v[:own].reshape(own, 3, local) for v in wi_finals], axis=2)
    grad_w_qkv = xor_take(wi_blocks, me, 2).reshape(own, 3 * width).astype(F32)
    output = output[None]
    vector_sum = wi_owned[own : own + lines]
    for v in wi_finals[1:]:
        vector_sum = vector_sum + v[own : own + lines].astype(F32)
    vector_sum = vector_sum.reshape(-1)
    outs = []
    at = 0
    for v in vectors:
        count = v.shape[0]
        outs.append(vector_sum[at : at + count])
        at += count
    (g_gain_one, g_shift_one, g_bias_qv, g_bias_out, g_gain_two, g_shift_two, g_bias_fc, g_bias_proj) = outs

    return (
        output,
        input_grad,
        g_gain_one,
        g_shift_one,
        grad_w_qkv,
        g_bias_qv,
        grad_w_out,
        g_bias_out,
        g_gain_two,
        g_shift_two,
        grad_w_fc,
        g_bias_fc,
        grad_w_proj,
        g_bias_proj,
    )


def body(*args):
    tokens, w_proj = args[0], args[13]
    fits = (
        lax.axis_size("seq") == 4
        and lax.axis_size("fsdp") == 8
        and tokens.shape[1:] == (512, 1024)
        and w_proj.shape == (512, 1024)
    )
    return body_aligned(*args) if fits else body_general(*args)


def solution(mesh):
    rows = P("fsdp", None)
    vec = P("fsdp")
    acts = P("fsdp", "seq", None)
    return jax.shard_map(
        body,
        mesh=mesh,
        in_specs=(
            acts, vec, rows, vec, vec, rows, vec, rows, vec, vec, vec, rows, vec, rows, vec, acts,
        ),
        out_specs=(
            acts, acts, vec, vec, rows, vec, rows, vec, vec, vec, rows, vec, rows, vec,
        ),
        check_vma=False,
    )
```
